32 devices in a mesh: dp: 4 (over z), seq: 8 (over y, x, core).
Axes of the slice: x: 2, y: 2, z: 4, core: 2. Of those that a mesh axis runs over, the one named last changes fastest.
Arguments:
- inputs: bfloat16 [8, 2048, 2048], P('dp', 'seq'), may hold values from -6 to 6
- teacher: bfloat16 [8, 2048, 2048], P('dp', 'seq'), may hold values from -6 to 6
- segment_ids: int32 [8, 2048], P('dp', 'seq'), may hold values from 0 to 15, never falling along the last dimension, each value on 1 to 1024 neighbouring positions
- summary_start: int32 [8], P('dp'), may hold values from 0 to 1998, as said below
- valid_mask: int32 [8, 2048], P('dp', 'seq'), may hold values from 0 to 1, as said below
- attn_norm_gain: bfloat16 [2048], P(('dp', 'seq')), may hold values from 0.5 to 1.5
- attn_norm_bias: bfloat16 [2048], P(('dp', 'seq')), may hold values from -1.25 to 1.25
- query_weight: bfloat16 [2048, 2048], P(('dp', 'seq')), may hold values from -0.125 to 0.125
- query_bias: bfloat16 [2048], P(('dp', 'seq')), may hold values from -1.25 to 1.25
- key_weight: bfloat16 [2048, 2048], P(('dp', 'seq')), may hold values from -0.125 to 0.125
- value_weight: bfloat16 [2048, 2048], P(('dp', 'seq')), may hold values from -0.125 to 0.125
- value_bias: bfloat16 [2048], P(('dp', 'seq')), may hold values from -1.25 to 1.25
- out_weight: bfloat16 [2048, 2048], P(('dp', 'seq')), may hold values from -0.75 to 0.75
- out_bias: bfloat16 [2048], P(('dp', 'seq')), may hold values from -1.25 to 1.25
- mlp_norm_gain: bfloat16 [2048], P(('dp', 'seq')), may hold values from 0.5 to 1.5
- mlp_norm_bias: bfloat16 [2048], P(('dp', 'seq')), may hold values from -1.25 to 1.25
- up_weight: bfloat16 [2048, 8192], P(('dp', 'seq')), may hold values from -0.125 to 0.125
- up_bias: bfloat16 [8192], P(('dp', 'seq')), may hold values from -1.25 to 1.25
- down_weight: bfloat16 [8192, 2048], P(('dp', 'seq')), may hold values from -0.09375 to 0.09375
- down_bias: bfloat16 [2048], P(('dp', 'seq')), may hold values from -1.25 to 1.25
Outputs:
- output: bfloat16 [8, 2048, 2048], P('dp', 'seq')
- loss: float32 [], replicated
- grad_inputs: float32 [8, 2048, 2048], P('dp', 'seq')
- grad_attn_norm_gain: float32 [2048], P(('dp', 'seq'))
- grad_attn_norm_bias: float32 [2048], P(('dp', 'seq'))
- grad_query_weight: float32 [2048, 2048], P(('dp', 'seq'))
- grad_query_bias: float32 [2048], P(('dp', 'seq'))
- grad_key_weight: float32 [2048, 2048], P(('dp', 'seq'))
- grad_value_weight: float32 [2048, 2048], P(('dp', 'seq'))
- grad_value_bias: float32 [2048], P(('dp', 'seq'))
- grad_out_weight: float32 [2048, 2048], P(('dp', 'seq'))
- grad_out_bias: float32 [2048], P(('dp', 'seq'))
- grad_mlp_norm_gain: float32 [2048], P(('dp', 'seq'))
- grad_mlp_norm_bias: float32 [2048], P(('dp', 'seq'))
- grad_up_weight: float32 [2048, 8192], P(('dp', 'seq'))
- grad_up_bias: float32 [8192], P(('dp', 'seq'))
- grad_down_weight: float32 [8192, 2048], P(('dp', 'seq'))
- grad_down_bias: float32 [2048], P(('dp', 'seq'))
The draws below stay inside these ranges and needn't reach their ends.
Inputs may be any that keep to these rules, and one draw needn't show every extreme that they name: `segment_ids`: segment ids never fall along a sequence; a segment holds at most 1024 tokens. The summary tokens of sequence b are positions summary_start[b] to summary_start[b] + 49. `valid_mask`: position 0 of every sequence is counted.
All inputs are finite; a program needn't handle non-finite values.
Results may differ from the reference program's by a relative error of at most 0.013.
Values may be sent and summed in bfloat16 or wider, within the bound.
No kernel may reach another device: no remote copies, remote signals or barrier semaphores. Data moves between devices by JAX's collectives and lax.ppermute only.
A program may use at most 448 MiB of HBM per device.

```python
import math
import jax
import jax.numpy as jnp
import numpy as np
from jax import lax

D = 2048
FF = 8192
H = 32
HD = 64
SEQ_LEN = 2048
NSUM = 50
SEQS = 2
BATCH = 8
SHARD_LEN = 256


def draw_summary_start(key, part):
    key_one, key_two = jax.random.split(key)
    starts = jax.random.randint(key_one, (BATCH,), 0, SEQ_LEN - NSUM + 1)
    order = jax.random.permutation(key_two, BATCH)
    starts = starts.at[order[0]].set(SEQ_LEN - NSUM).at[order[1]].set(0)
    return starts.astype(jnp.int32)


def draw_valid_mask(key, part):
    row_index = jnp.arange(BATCH, dtype=jnp.int32)[:, None]
    place_index = jnp.arange(SEQ_LEN, dtype=jnp.int32)[None, :]
    seq_groups = SEQ_LEN // SHARD_LEN
    device = row_index // SEQS * seq_groups + place_index // SHARD_LEN
    last_device = BATCH // SEQS * seq_groups - 1
    cutoff = 250 + 500 * device // last_device
    ticket = jax.random.randint(key, (BATCH, SEQ_LEN), 0, 1000)
    valid_flag = (ticket < cutoff) | (place_index == 0)
    return valid_flag.astype(jnp.int32)


def block_levels(rng, dims, cuts, least, largest):
    level, own = 1.0, jax.random.fold_in(rng, 6)
    for dim, blocks in cuts:
        heights = jnp.exp(jax.random.uniform(jax.random.fold_in(own, dim), (blocks,), jnp.float32, least / len(cuts), largest / len(cuts)))
        level = level * jnp.repeat(heights, dims[dim] // blocks).reshape([-1 if axis == dim else 1 for axis in range(len(dims))])
    return level


def split_up(amount, total, limit, skew):
    portions = [(1 << 20) // math.isqrt(rank ** skew) + 1 for rank in range(2, amount + 1)]
    spare, counts = total - limit - (amount - 1), [1] * (amount - 1)
    while spare > 0:
        candidates = [i for i in range(amount - 1) if counts[i] < limit]
        mass, remaining = sum([portions[i] for i in candidates]), spare
        for i in candidates:
            addition = min(limit - counts[i], max(1, remaining * portions[i] // mass), spare)
            counts[i] = counts[i] + addition
            spare = spare - addition
    return np.array([limit] + counts)


def uneven(rng, amount, total, most, slope):
    if amount == 2:
        one = jax.random.randint(rng, (), max(1, total - most), min(most, total - 1) + 1)
        return jnp.stack([one, total - one])
    tallies = jnp.asarray(split_up(amount, total, most, slope), jnp.int32)
    pairs = (amount - 1) // 2
    source_of, taker = tallies[1:1 + 2 * pairs:2], tallies[2:2 + 2 * pairs:2]
    margin = jnp.minimum(source_of - 1, most - taker)
    moved = jax.random.randint(jax.random.fold_in(rng, 1), (pairs,), 0, 1 << 20) % (margin + 1)
    tallies = tallies.at[1:1 + 2 * pairs:2].set(source_of - moved).at[2:2 + 2 * pairs:2].set(taker + moved)
    return tallies[jax.random.permutation(jax.random.fold_in(rng, 2), amount)]


def noise(rng, dims, spread, limit, cuts=(), kind=jnp.bfloat16):
    drawn = jax.random.normal(rng, dims, jnp.float32) * spread
    if len(cuts) > 0:
        drawn = block_levels(rng, dims, cuts, -0.22, 0.18) * drawn
    return jnp.clip(drawn, min=-limit, max=limit).astype(kind)


def setup_inputs(seed: int = 0) -> dict:
    keys = jax.random.split(jax.random.key(seed), 21)
    inputs = noise(keys[0], (BATCH, SEQ_LEN, D), 1.0, 6.0, ((0, 4), (1, 8)))
    teacher = noise(keys[1], (BATCH, SEQ_LEN, D), 1.0, 6.0, ((0, 4), (1, 8)))
    segment_ids = jax.vmap(lambda own: jnp.searchsorted(jnp.cumsum(uneven(own, max(4, SEQ_LEN // 128), SEQ_LEN, SEQ_LEN // 2, 2)), jnp.arange(SEQ_LEN), side="right"))(jax.random.split(keys[2], BATCH)).reshape((BATCH, SEQ_LEN)).astype(jnp.int32)
    summary_start = draw_summary_start(jax.random.fold_in(keys[20], 71), 0)
    valid_mask = draw_valid_mask(jax.random.fold_in(keys[20], 71), 0)
    attn_norm_gain = jnp.clip(1.0 + 0.1 * jax.random.normal(keys[5], (D,), jnp.float32), 0.5, 1.5).astype(jnp.bfloat16)
    attn_norm_bias = noise(keys[6], (D,), 0.2, 1.25, ((0, 32),))
    query_weight = noise(keys[7], (D, D), D ** -0.5, 0.125, ((0, 32),))
    query_bias = noise(keys[8], (D,), 0.2, 1.25, ((0, 32),))
    key_weight = noise(keys[9], (D, D), D ** -0.5, 0.125, ((0, 32),))
    value_weight = noise(keys[10], (D, D), D ** -0.5, 0.125, ((0, 32),))
    value_bias = noise(keys[11], (D,), 0.2, 1.25, ((0, 32),))
    out_weight = noise(keys[12], (D, D), (D // 32) ** -0.5, 0.75, ((0, 32),))
    out_bias = noise(keys[13], (D,), 0.2, 1.25, ((0, 32),))
    mlp_norm_gain = jnp.clip(1.0 + 0.1 * jax.random.normal(keys[14], (D,), jnp.float32), 0.5, 1.5).astype(jnp.bfloat16)
    mlp_norm_bias = noise(keys[15], (D,), 0.2, 1.25, ((0, 32),))
    up_weight = noise(keys[16], (D, FF), D ** -0.5, 0.125, ((0, 32),))
    up_bias = noise(keys[17], (FF,), 0.2, 1.25, ((0, 32),))
    down_weight = noise(keys[18], (FF, D), (FF // 2) ** -0.5, 0.09375, ((0, 32),))
    down_bias = noise(keys[19], (D,), 0.2, 1.25, ((0, 32),))
    return {"inputs": inputs, "teacher": teacher, "segment_ids": segment_ids, "summary_start": summary_start, "valid_mask": valid_mask, "attn_norm_gain": attn_norm_gain, "attn_norm_bias": attn_norm_bias, "query_weight": query_weight, "query_bias": query_bias, "key_weight": key_weight, "value_weight": value_weight, "value_bias": value_bias, "out_weight": out_weight, "out_bias": out_bias, "mlp_norm_gain": mlp_norm_gain, "mlp_norm_bias": mlp_norm_bias, "up_weight": up_weight, "up_bias": up_bias, "down_weight": down_weight, "down_bias": down_bias}


NORM_EPS = 1e-05
NEG_FILL = -1e+30

@jax.custom_vjp
def low(v):
    return lax.optimization_barrier(v.astype(jnp.bfloat16)).astype(jnp.float32)

@jax.custom_vjp
def low_back(v):
    return v

def low_keep(v):
    return (low(v), None)

def low_pass(kept, grad):
    return (grad,)

def back_keep(v):
    return (v, None)

def back_low(kept, grad):
    return (low(grad),)
low.defvjp(low_keep, low_pass)
low_back.defvjp(back_keep, back_low)

def product(left_in, right_in):
    return jnp.dot(left_in, right_in, precision=lax.Precision.HIGHEST)

def layer_norm(values, gain_in, shift_in):
    center = values - lax.optimization_barrier(jnp.mean(values, axis=-1, keepdims=True))
    inverse = lax.rsqrt(lax.optimization_barrier(jnp.mean(center * center, axis=-1, keepdims=True)) + NORM_EPS)
    return center * inverse * gain_in + shift_in

def attention(queries, key_rows, values, segments, summary_from):
    seq_group = queries.shape[0]
    block_rows = min(512, SEQ_LEN)
    blocks = SEQ_LEN // block_rows
    key_places = jnp.arange(SEQ_LEN, dtype=jnp.int32)
    key_heads = key_rows.reshape(seq_group, SEQ_LEN, H, HD)
    value_heads = values.reshape(seq_group, SEQ_LEN, H, HD)

    def attend_block(block_args):
        query_block, block_first = block_args
        query_places = block_first + jnp.arange(block_rows, dtype=jnp.int32)
        query_segments = lax.dynamic_slice_in_dim(segments, block_first, block_rows, 1)
        query_heads = query_block.reshape(seq_group, block_rows, H, HD)
        scores = low_back(jnp.einsum('gqhd,gkhd->ghqk', query_heads, key_heads, precision=lax.Precision.HIGHEST))
        in_summary = (query_places[None, :] >= summary_from[:, None]) & (query_places[None, :] < summary_from[:, None] + NSUM)
        allowed = (key_places[None, None, :] <= query_places[None, :, None]) & ((query_segments[:, :, None] == segments[:, None, :]) | in_summary[:, :, None])
        scores = jnp.where(allowed[:, None], scores, NEG_FILL)
        attn_probs = low(jax.nn.softmax(scores, axis=-1))
        mixed_out = jnp.einsum('ghqk,gkhd->gqhd', attn_probs, value_heads, precision=lax.Precision.HIGHEST)
        return mixed_out.reshape(seq_group, block_rows, H * HD)
    query_blocks = queries.reshape(seq_group, blocks, block_rows, H * HD).transpose(1, 0, 2, 3)
    firsts = jnp.arange(blocks, dtype=jnp.int32) * block_rows
    mixed_all = lax.map(jax.checkpoint(attend_block), (query_blocks, firsts))
    return mixed_all.transpose(1, 0, 2, 3).reshape(seq_group * SEQ_LEN, H * HD)

def layer_forward(params, inputs_group, segments, summary_from):
    gain_one, shift_one, w_query, b_query, w_key, w_value, b_value, w_out, b_out, gain_two, shift_two, w_up, b_up, w_down, b_down = params
    seq_group = inputs_group.shape[0]
    flat_rows = inputs_group.reshape(seq_group * SEQ_LEN, D)
    ready_one = low(layer_norm(flat_rows, gain_one, shift_one))
    query_rows = (product(ready_one, w_query) + b_query) * HD ** (-0.5)
    key_rows = product(ready_one, w_key)
    value_rows = product(ready_one, w_value) + b_value
    attended = attention(low(low_back(query_rows)).reshape(seq_group, SEQ_LEN, D), low(low_back(key_rows)).reshape(seq_group, SEQ_LEN, D), low(low_back(value_rows)).reshape(seq_group, SEQ_LEN, D), segments, summary_from)
    branch = low_back(product(low(low_back(attended)), w_out) + b_out)
    hidden = flat_rows + branch
    ready_two = low(layer_norm(hidden, gain_two, shift_two))
    active = low(jax.nn.relu(low_back(product(ready_two, w_up) + b_up)))
    return hidden + low_back(product(active, w_down) + b_down)

def reference(inputs, teacher, segment_ids, summary_start, valid_mask, attn_norm_gain, attn_norm_bias, query_weight, query_bias, key_weight, value_weight, value_bias, out_weight, out_bias, mlp_norm_gain, mlp_norm_bias, up_weight, up_bias, down_weight, down_bias):
    params = tuple((weight_in.astype(jnp.float32) for weight_in in (attn_norm_gain, attn_norm_bias, query_weight, query_bias, key_weight, value_weight, value_bias, out_weight, out_bias, mlp_norm_gain, mlp_norm_bias, up_weight, up_bias, down_weight, down_bias)))
    valid_float = valid_mask.astype(jnp.float32)
    count_all = jnp.sum(valid_float)
    factor = BATCH * SEQ_LEN / (2.0 * count_all)
    seq_group = min(BATCH, max(1, 4096 // SEQ_LEN))
    rounds = BATCH // seq_group

    def regroup(values):
        return values.reshape((rounds, seq_group) + values.shape[1:])

    def one_round(carried, slices):
        grads_sum, error_total = carried
        inputs_group, teacher_group, segments, summary_from, valid_group = slices

        def objective(params_in, inputs_in):
            result = layer_forward(params_in, inputs_in, segments, summary_from)
            misfit = result - teacher_group.reshape(-1, D)
            squares = jnp.sum(lax.optimization_barrier(jnp.sum(misfit * misfit, axis=-1)) * valid_group.reshape(-1))
            return (squares * factor, (result, squares))
        value_out, pullback, aux_out = jax.vjp(objective, params, inputs_group, has_aux=True)
        grad_params, grad_group = pullback(jnp.ones_like(value_out))
        result, squares = aux_out
        new_grads = jax.tree.map(jnp.add, grads_sum, grad_params)
        return ((new_grads, error_total + squares), (result, grad_group))
    start_grads = jax.tree.map(jnp.zeros_like, params)
    (grads_all, error_all), (results, grad_groups) = lax.scan(one_round, (start_grads, jnp.float32(0.0)), (regroup(inputs.astype(jnp.float32)), regroup(teacher.astype(jnp.float32)), regroup(segment_ids), regroup(summary_start), regroup(valid_float)))
    output = results.reshape(BATCH, SEQ_LEN, D).astype(jnp.bfloat16)
    loss_value = error_all / (count_all * D)
    grad_inputs = grad_groups.reshape(BATCH, SEQ_LEN, D)
    return (output, loss_value, grad_inputs, grads_all[0], grads_all[1], grads_all[2], grads_all[3], grads_all[4], grads_all[5], grads_all[6], grads_all[7], grads_all[8], grads_all[9], grads_all[10], grads_all[11], grads_all[12], grads_all[13], grads_all[14])
```

```python
import functools

import jax
import jax.numpy as jnp
from jax import lax
from jax.experimental import pallas as pl
from jax.experimental.pallas import tpu as pltpu
from jax.sharding import PartitionSpec as P

HD = 64
NSUM = 50
NORM_EPS = 1e-05
NEG_FILL = -1e30
BF = jnp.bfloat16
F32 = jnp.float32


def dot(left_in, right_in):
    return jnp.dot(left_in, right_in, preferred_element_type=F32)


def dot_tn(left_in, right_in):
    return lax.dot_general(left_in, right_in, (((0,), (0,)), ((), ())), preferred_element_type=F32)


def dot_nt(left_in, right_in):
    return lax.dot_general(left_in, right_in, (((1,), (1,)), ((), ())), preferred_element_type=F32)


def norm_core(values):
    center = values - jnp.mean(values, axis=-1, keepdims=True)
    inverse = lax.rsqrt(jnp.mean(center * center, axis=-1, keepdims=True) + NORM_EPS)
    return center * inverse, inverse


def norm_back(grad_out, normed, inverse, gain_in):
    grad_normed = grad_out * gain_in
    inner_one = jnp.mean(grad_normed, axis=-1, keepdims=True)
    inner_two = jnp.mean(grad_normed * normed, axis=-1, keepdims=True)
    grad_in = inverse * (grad_normed - inner_one - normed * inner_two)
    return grad_in, jnp.sum(grad_out * normed, axis=0), jnp.sum(grad_out, axis=0)


def swap(values, mask):
    n = lax.axis_size("seq")
    return lax.ppermute(values, "seq", [(i, i ^ mask) for i in range(n)])


def gather_rows(own):
    n = lax.axis_size("seq")
    if n == 8:
        half = own.shape[0] // 2
        from_two, from_four = swap(own, 2), swap(own, 4)
        six_top, six_end = swap(from_four[:half], 2), swap(from_two[half:], 4)
        same = jnp.concatenate([own, from_two, from_four, six_top, six_end], axis=0)
    else:
        same, step = own, 2
        while step < n:
            same = jnp.concatenate([same, swap(same, step)], axis=0)
            step *= 2
    return same, swap(same, 1)


def scatter_rows(even_blocks, odd_part):
    n = lax.axis_size("seq")
    blocks = even_blocks(swap(odd_part, 1))
    if n == 8:
        zero, two, four, six = blocks
        half = zero.shape[0] // 2
        six = six.astype(BF)
        to_four = swap(six[:half], 2)
        to_two = swap(six[half:], 4)
        two_top = swap(two[:half].astype(BF), 2)
        four_end = swap(four[half:].astype(BF), 4)
        two_end = swap((two[half:] + to_two.astype(F32)).astype(BF), 2)
        four_top = swap((four[:half] + to_four.astype(F32)).astype(BF), 4)
        top = zero[:half] + two_top.astype(F32) + four_top.astype(F32)
        end = zero[half:] + two_end.astype(F32) + four_end.astype(F32)
        return jnp.concatenate([top, end], axis=0)
    step = n // 2
    while step > 1:
        keep = len(blocks) // 2
        sent = [swap(block.astype(BF), step).astype(F32) for block in blocks[keep:]]
        blocks = [block + got for block, got in zip(blocks[:keep], sent)]
        step //= 2
    return blocks[0]


def place_of(k, n):
    return (k >> 1) + (k & 1) * (n // 2)


def natural_order(pieces):
    n = len(pieces)
    index = lax.axis_index("seq")
    stacked = jnp.stack(pieces)
    return [lax.dynamic_index_in_dim(stacked, other ^ index, 0, keepdims=False) for other in range(n)]


def visible_scores(q_head, k_block, first, q_place, key_start, length):
    scores = dot_nt(q_head, k_block)
    k_place = key_start + lax.broadcasted_iota(jnp.int32, (1, length), 1)
    allowed = (k_place >= first) & (k_place <= q_place)
    return jnp.where(allowed, scores, NEG_FILL)


def storage_row(block, place, blocks, length):
    k = block ^ place
    return pl.multiple_of(((k >> 1) + (k & 1) * (blocks // 2)) * length, length)


def fold(values, op):
    out = values[:, :128]
    for start in range(128, values.shape[1], 128):
        out = op(out, values[:, start : start + 128])
    return out


def attend_forward_kernel(
    place_ref, low_ref, q_ref, k_ref, v_ref, first_ref, o_ref, lse_ref, s_scr, m_scr, l_scr, *, heads, length, blocks
):
    i = pl.program_id(0)
    place = place_ref[0]
    low = low_ref[i]
    width = heads * HD
    lanes = lax.broadcasted_iota(jnp.int32, (length, width), 1) // HD
    q_all = q_ref[...]
    q_heads = [jnp.where(lanes == h, q_all, jnp.zeros_like(q_all)) for h in range(heads)]
    first = first_ref[...]
    q_place = i * length + lax.broadcasted_iota(jnp.int32, (length, 1), 0)
    m_scr[...] = jnp.full_like(m_scr, NEG_FILL)
    l_scr[...] = jnp.zeros_like(l_scr)

    def score_step(j, carry):
        k_block = k_ref[pl.ds(storage_row(j, place, blocks, length), length), :]
        cols = pl.ds(pl.multiple_of(j * length, length), length)
        for h in range(heads):
            scores = visible_scores(q_heads[h], k_block, first, q_place, j * length, length)
            s_scr[h, :, cols] = scores
            m_scr[h] = jnp.maximum(m_scr[h], fold(scores, jnp.maximum))
        return carry

    lax.fori_loop(low, i + 1, score_step, 0)
    tops = [jnp.max(m_scr[h], axis=-1, keepdims=True) for h in range(heads)]

    def exp_step(j, carry):
        cols = pl.ds(pl.multiple_of(j * length, length), length)
        for h in range(heads):
            raised = jnp.exp(s_scr[h, :, cols] - tops[h])
            s_scr[h, :, cols] = raised
            l_scr[h] = l_scr[h] + fold(raised, jnp.add)
        return carry

    lax.fori_loop(low, i + 1, exp_step, 0)
    totals = [jnp.sum(l_scr[h], axis=-1, keepdims=True) for h in range(heads)]
    scales = [1.0 / total for total in totals]

    def mix_step(j, acc):
        v_block = v_ref[pl.ds(storage_row(j, place, blocks, length), length), :]
        cols = pl.ds(pl.multiple_of(j * length, length), length)
        for h in range(heads):
            probs = (s_scr[h, :, cols] * scales[h]).astype(BF)
            acc = acc + jnp.where(lanes == h, dot(probs, v_block), 0.0)
        return acc

    mixed = lax.fori_loop(low, i + 1, mix_step, jnp.zeros((length, width), F32))
    o_ref[...] = mixed.astype(BF)
    cols = lax.broadcasted_iota(jnp.int32, (length, 128), 1)
    lse = jnp.zeros((length, 128), F32)
    for h in range(heads):
        lse = jnp.where(cols == h, tops[h] + jnp.log(totals[h]), lse)
    lse_ref[...] = lse


def attend_backward_kernel(
    place_ref, low_ref, q_ref, go_ref, o_ref, lse_ref, k_ref, v_ref, first_ref, grad_ref, kt_scr, vt_scr, *, heads, length, blocks
):
    i = pl.program_id(0)
    place = place_ref[0]
    low = low_ref[i]
    width = heads * HD
    lanes = lax.broadcasted_iota(jnp.int32, (length, width), 1) // HD
    first = first_ref[...]
    q_place = i * length + lax.broadcasted_iota(jnp.int32, (length, 1), 0)
    q_all, go_all = q_ref[...], go_ref[...]
    inner_all = go_all.astype(F32) * o_ref[...].astype(F32)
    q_turned, go_turned = q_all.astype(F32).T.astype(BF), go_all.astype(F32).T.astype(BF)
    lse_all = lse_ref[...]
    q_heads, go_heads, inner, lse = [], [], [], []
    for h in range(heads):
        mine = lanes == h
        q_heads.append(jnp.where(mine, q_all, jnp.zeros_like(q_all)))
        go_heads.append(jnp.where(mine, go_all, jnp.zeros_like(go_all)))
        inner.append(jnp.sum(jnp.where(mine, inner_all, 0.0), axis=-1, keepdims=True))
        lse.append(lse_all[:, h : h + 1])

    @pl.when(i == 0)
    def _():
        kt_scr[...] = jnp.zeros_like(kt_scr)
        vt_scr[...] = jnp.zeros_like(vt_scr)

    def step(j, acc):
        rows = pl.ds(storage_row(j, place, blocks, length), length)
        k_block, v_block = k_ref[rows, :], v_ref[rows, :]
        for h in range(heads):
            scores = visible_scores(q_heads[h], k_block, first, q_place, j * length, length)
            probs = jnp.exp(scores - lse[h])
            grad_probs = dot_nt(go_heads[h], v_block)
            grad_scores = (probs * (grad_probs - inner[h])).astype(BF)
            part = slice(h * HD, (h + 1) * HD)
            vt_scr[part, rows] = vt_scr[part, rows] + dot(go_turned[part, :], probs.astype(BF))
            kt_scr[part, rows] = kt_scr[part, rows] + dot(q_turned[part, :], grad_scores)
            acc = acc + jnp.where(lanes == h, dot(grad_scores, k_block), 0.0)
        return acc

    grad_q = lax.fori_loop(low, i + 1, step, jnp.zeros((length, width), F32))
    own_rows = pl.ds(storage_row(i, place, blocks, length), length)
    grad_ref[own_rows, 0:width] = (grad_q.astype(BF).astype(F32) * (HD**-0.5)).astype(BF)

    @pl.when(i == blocks - 1)
    def _():
        for j in range(blocks):
            rows = slice(j * length, (j + 1) * length)
            grad_ref[rows, width : 2 * width] = kt_scr[:, rows].T.astype(BF)
            grad_ref[rows, 2 * width : 3 * width] = vt_scr[:, rows].T.astype(BF)


def storage_map(length, blocks, column):
    def index(i, place_ref, low_ref):
        k = i ^ place_ref[0]
        return ((k >> 1) + (k & 1) * (blocks // 2), column)

    return index


def attend_cost(rows, width, products):
    return pl.CostEstimate(
        flops=products * rows * rows * 256 * (width // HD), bytes_accessed=8 * rows * width * 2, transcendentals=rows * rows
    )


def attend_forward(place, low, qkv, first, length):
    rows, triple = qkv.shape
    width, blocks = triple // 3, rows // length
    heads = width // HD
    return pl.pallas_call(
        functools.partial(attend_forward_kernel, heads=heads, length=length, blocks=blocks),
        grid_spec=pltpu.PrefetchScalarGridSpec(
            num_scalar_prefetch=2,
            grid=(blocks,),
            in_specs=[
                pl.BlockSpec((length, width), storage_map(length, blocks, 0)),
                pl.BlockSpec((rows, width), lambda i, p, w: (0, 1)),
                pl.BlockSpec((rows, width), lambda i, p, w: (0, 2)),
                pl.BlockSpec((length, 1), lambda i, p, w: (i, 0)),
            ],
            out_specs=[
                pl.BlockSpec((length, width), storage_map(length, blocks, 0)),
                pl.BlockSpec((length, 128), storage_map(length, blocks, 0)),
            ],
            scratch_shapes=[
                pltpu.VMEM((heads, length, rows), F32),
                pltpu.VMEM((heads, length, 128), F32),
                pltpu.VMEM((heads, length, 128), F32),
            ],
        ),
        out_shape=[jax.ShapeDtypeStruct((rows, width), BF), jax.ShapeDtypeStruct((rows, 128), F32)],
        compiler_params=pltpu.CompilerParams(dimension_semantics=("arbitrary",), vmem_limit_bytes=40 << 20),
        cost_estimate=attend_cost(rows, width, 2),
        name="attend_forward",
    )(place, low, qkv, qkv, qkv, first)


def attend_backward(place, low, qkv, grad_out, mixed, lse, first, length):
    rows, triple = qkv.shape
    width, blocks = triple // 3, rows // length
    heads = width // HD
    return pl.pallas_call(
        functools.partial(attend_backward_kernel, heads=heads, length=length, blocks=blocks),
        grid_spec=pltpu.PrefetchScalarGridSpec(
            num_scalar_prefetch=2,
            grid=(blocks,),
            in_specs=[
                pl.BlockSpec((length, width), storage_map(length, blocks, 0)),
                pl.BlockSpec((length, width), storage_map(length, blocks, 0)),
                pl.BlockSpec((length, width), storage_map(length, blocks, 0)),
                pl.BlockSpec((length, 128), storage_map(length, blocks, 0)),
                pl.BlockSpec((rows, width), lambda i, p, w: (0, 1)),
                pl.BlockSpec((rows, width), lambda i, p, w: (0, 2)),
                pl.BlockSpec((length, 1), lambda i, p, w: (i, 0)),
            ],
            out_specs=pl.BlockSpec((rows, triple), lambda i, p, w: (0, 0)),
            scratch_shapes=[pltpu.VMEM((width, rows), F32), pltpu.VMEM((width, rows), F32)],
        ),
        out_shape=jax.ShapeDtypeStruct((rows, triple), BF),
        compiler_params=pltpu.CompilerParams(dimension_semantics=("arbitrary",), vmem_limit_bytes=40 << 20),
        cost_estimate=attend_cost(rows, width, 5),
        name="attend_backward",
    )(place, low, qkv, grad_out, mixed, lse, qkv, qkv, first)


def local(
    inputs,
    teacher,
    segment_ids,
    summary_start,
    valid_mask,
    attn_norm_gain,
    attn_norm_bias,
    query_weight,
    query_bias,
    key_weight,
    value_weight,
    value_bias,
    out_weight,
    out_bias,
    mlp_norm_gain,
    mlp_norm_bias,
    up_weight,
    up_bias,
    down_weight,
    down_bias,
):
    seqs, length = segment_ids.shape
    width = inputs.shape[-1]
    hidden_units = up_weight.shape[1]
    n, groups = lax.axis_size("seq"), lax.axis_size("dp")
    place, group = lax.axis_index("seq"), lax.axis_index("dp")
    both = ("dp", "seq")
    seq_len = length * n
    tokens_all = seqs * seq_len * groups
    scale = HD**-0.5
    own_rows = query_weight.shape[0]
    own_hidden = up_bias.shape[0]
    head_cols = width // n
    blocks = range(n)

    valid = valid_mask.astype(F32)
    small = [attn_norm_gain, attn_norm_bias, out_bias, mlp_norm_gain, mlp_norm_bias, down_bias, query_bias, value_bias, up_bias]
    sizes = [v.shape[0] for v in small]
    packed = jnp.concatenate([v.astype(F32) for v in small] + [segment_ids.astype(F32).reshape(-1), jnp.sum(valid).reshape(1)])
    packed = lax.all_gather(packed, both, axis=0, tiled=False)
    parts, at = [], 0
    for size in sizes:
        parts.append(packed[:, at : at + size])
        at += size
    gain_one, shift_one, b_out, gain_two, shift_two, b_down = [part.reshape(-1) for part in parts[:6]]
    b_query, b_value = [lax.dynamic_slice_in_dim(part.reshape(-1), place * head_cols, head_cols) for part in parts[6:8]]
    b_up = lax.dynamic_index_in_dim(parts[8].reshape(groups, n, -1), place, 1, keepdims=False).reshape(-1)
    ids = packed[:, at : at + seqs * length].reshape(groups, n, seqs, length)
    ids = lax.dynamic_index_in_dim(ids, group, 0, keepdims=False).transpose(1, 0, 2).reshape(seqs, seq_len)
    total_count = jnp.sum(packed[:, at + seqs * length])

    qkv_cut = jnp.concatenate(
        [w.reshape(own_rows, n, head_cols).transpose(1, 0, 2) for w in (query_weight, key_weight, value_weight)], axis=2
    )
    qkv_cut = lax.all_to_all(qkv_cut, "seq", split_axis=0, concat_axis=0, tiled=True)
    w_qkv = lax.all_gather(qkv_cut.reshape(n * own_rows, 3 * head_cols), "dp", axis=0, tiled=True)
    w_out = lax.all_gather(out_weight, both, axis=0, tiled=True)
    up_cut = up_weight.reshape(own_rows, groups, n, own_hidden).transpose(2, 0, 1, 3).reshape(n, own_rows, groups * own_hidden)
    up_cut = lax.all_to_all(up_cut, "seq", split_axis=0, concat_axis=0, tiled=True)
    w_up = lax.all_gather(up_cut.reshape(n * own_rows, groups * own_hidden), "dp", axis=0, tiled=True)
    w_down = lax.all_gather(down_weight, "dp", axis=0, tiled=True)
    b_qkv = jnp.concatenate([b_query, jnp.zeros_like(b_query), b_value])
    s_qkv = jnp.concatenate([jnp.full((head_cols,), scale, F32), jnp.ones((2 * head_cols,), F32)])

    place_arr = place.reshape(1).astype(jnp.int32)
    positions = jnp.arange(seq_len, dtype=jnp.int32)

    state = []
    for b in range(seqs):
        rows = inputs[b].astype(F32)
        normed, inverse = norm_core(rows)
        ready = (normed * gain_one + shift_one).astype(BF)
        first = jnp.sum((ids[b][None, :] < ids[b][:, None]).astype(jnp.int32), axis=1)
        in_summary = (positions >= summary_start[b]) & (positions < summary_start[b] + NSUM)
        first = jnp.where(in_summary, 0, first)
        low = jnp.min(first.reshape(n, length), axis=1) // length
        even, odd = gather_rows(ready)
        qkv = jnp.concatenate([((dot(part, w_qkv) + b_qkv) * s_qkv).astype(BF) for part in (even, odd)], axis=0)
        mixed, lse = attend_forward(place_arr, low, qkv, first.reshape(seq_len, 1), length)
        pieces = [
            swap(mixed[place_of(k, n) * length : (place_of(k, n) + 1) * length], k) if k else mixed[:length] for k in blocks
        ]
        attended = jnp.concatenate(natural_order(pieces), axis=1)
        hidden = rows + (dot(attended, w_out) + b_out)
        normed_two, inverse_two = norm_core(hidden)
        ready_two = (normed_two * gain_two + shift_two).astype(BF)
        even_two, odd_two = gather_rows(ready_two)
        act_even = jnp.maximum(dot(even_two, w_up) + b_up, 0.0).astype(BF)
        act_odd = jnp.maximum(dot(odd_two, w_up) + b_up, 0.0).astype(BF)

        def down_blocks(got, act=act_even):
            return [
                dot(act[m * length : (m + 1) * length], w_down) + got[m * length : (m + 1) * length].astype(F32)
                for m in range(n // 2)
            ]

        result = hidden + (scatter_rows(down_blocks, dot(act_odd, w_down).astype(BF)) + b_down)
        misfit = result - teacher[b].astype(F32)
        local_sq = jnp.sum(jnp.sum(misfit * misfit, axis=-1) * valid[b])
        grad_result = misfit * (valid[b] * (tokens_all / total_count))[:, None]
        state.append(
            dict(
                normed=normed, inverse=inverse, first=first, low=low, even=even, odd=odd, qkv=qkv, mixed=mixed, lse=lse,
                attended=attended, normed_two=normed_two, inverse_two=inverse_two, even_two=even_two, odd_two=odd_two,
                act_even=act_even, act_odd=act_odd, result=result, local_sq=local_sq, grad_result=grad_result,
            )
        )

    def total(terms):
        out = terms[0]
        for term in terms[1:]:
            out = out + term
        return out

    for st in state:
        low_grad = st["grad_result"].astype(BF)
        st["g_b_down"] = jnp.sum(low_grad.astype(F32), axis=0)
        g_even, g_odd = gather_rows(low_grad)
        st["g_w_down"] = dot_tn(st["act_even"], g_even) + dot_tn(st["act_odd"], g_odd)
        pre_even = jnp.where(st["act_even"] > 0, dot_nt(g_even, w_down), 0.0).astype(BF)
        pre_odd = jnp.where(st["act_odd"] > 0, dot_nt(g_odd, w_down), 0.0).astype(BF)
        st["g_w_up"] = dot_tn(st["even_two"], pre_even) + dot_tn(st["odd_two"], pre_odd)
        st["g_b_up"] = jnp.sum(pre_even.astype(F32), axis=0) + jnp.sum(pre_odd.astype(F32), axis=0)

        def up_blocks(got, pre=pre_even):
            return [
                dot_nt(pre[m * length : (m + 1) * length], w_up) + got[m * length : (m + 1) * length].astype(F32)
                for m in range(n // 2)
            ]

        grad_ready = scatter_rows(up_blocks, dot_nt(pre_odd, w_up).astype(BF))
        grad_norm, st["g_gain_two"], st["g_shift_two"] = norm_back(grad_ready, st["normed_two"], st["inverse_two"], gain_two)
        grad_hidden = st["grad_result"] + grad_norm
        branch = grad_hidden.astype(BF)
        st["g_w_out"] = dot_tn(st["attended"], branch)
        st["g_b_out"] = jnp.sum(branch.astype(F32), axis=0)
        grad_att = dot_nt(branch, w_out).astype(BF)
        pieces = []
        for k in blocks:
            piece = lax.dynamic_slice_in_dim(grad_att, (place ^ k) * head_cols, head_cols, axis=1)
            pieces.append(swap(piece, k) if k else piece)
        grad_mixed = jnp.concatenate([pieces[k] for k in list(range(0, n, 2)) + list(range(1, n, 2))], axis=0)
        grad_qkv = attend_backward(
            place_arr, st["low"], st["qkv"], grad_mixed, st["mixed"], st["lse"], st["first"].reshape(seq_len, 1), length
        )
        half = seq_len // 2
        gq_even, gq_odd = grad_qkv[:half], grad_qkv[half:]
        st["g_w_qkv"] = dot_tn(st["even"], gq_even) + dot_tn(st["odd"], gq_odd)
        st["g_b_qkv"] = jnp.sum(grad_qkv.astype(F32), axis=0)

        def qkv_blocks(got, pre=gq_even):
            return [
                dot_nt(pre[m * length : (m + 1) * length], w_qkv) + got[m * length : (m + 1) * length].astype(F32)
                for m in range(n // 2)
            ]

        grad_ready_one = scatter_rows(qkv_blocks, dot_nt(gq_odd, w_qkv).astype(BF))
        grad_norm, st["g_gain_one"], st["g_shift_one"] = norm_back(grad_ready_one, st["normed"], st["inverse"], gain_one)
        st["grad_inputs"] = grad_hidden + grad_norm

    def summed(name):
        return total([st[name] for st in state])

    g_down = lax.psum_scatter(summed("g_w_down").astype(BF), "dp", scatter_dimension=0, tiled=True).astype(F32)
    g_up = lax.psum_scatter(summed("g_w_up").astype(BF), "dp", scatter_dimension=0, tiled=True)
    g_up = lax.all_to_all(g_up.reshape(n, own_rows, groups * own_hidden), "seq", split_axis=0, concat_axis=0, tiled=True)
    g_up = g_up.reshape(n, own_rows, groups, own_hidden).transpose(1, 2, 0, 3).reshape(own_rows, hidden_units).astype(F32)
    g_out = lax.psum_scatter(summed("g_w_out").astype(BF), both, scatter_dimension=0, tiled=True).astype(F32)
    g_qkv = lax.psum_scatter(summed("g_w_qkv").astype(BF), "dp", scatter_dimension=0, tiled=True)
    g_qkv = lax.all_to_all(g_qkv.reshape(n, own_rows, 3 * head_cols), "seq", split_axis=0, concat_axis=0, tiled=True)
    g_qkv = g_qkv.reshape(n, own_rows, 3, head_cols).transpose(2, 1, 0, 3).reshape(3, own_rows, width).astype(F32)

    g_b_qkv = summed("g_b_qkv").reshape(3, head_cols)
    own_bias = jnp.zeros((2, width), F32)
    own_bias = lax.dynamic_update_slice(own_bias, jnp.stack([g_b_qkv[0], g_b_qkv[2]]), (0, place * head_cols))
    g_b_up = summed("g_b_up").reshape(groups, 1, own_hidden)
    spread_up = lax.dynamic_update_slice_in_dim(jnp.zeros((groups, n, own_hidden), F32), g_b_up, place, 1)
    names = ("g_gain_one", "g_shift_one", "g_b_out", "g_gain_two", "g_shift_two", "g_b_down")
    vectors = jnp.concatenate([jnp.stack([summed(name) for name in names]), own_bias], axis=0)
    count = vectors.shape[0]
    vectors = vectors.reshape(count, groups * n, own_rows).transpose(1, 0, 2).reshape(groups * n, count * own_rows)
    sq = jnp.broadcast_to(summed("local_sq"), (groups * n, 1))
    tail = jnp.concatenate([vectors, spread_up.reshape(groups * n, own_hidden), sq], axis=1)
    tail = lax.psum_scatter(tail, both, scatter_dimension=0, tiled=True)[0]
    vectors = tail[: count * own_rows].reshape(count, own_rows)
    g_b_query, g_b_value, g_b_up = vectors[6], vectors[7], tail[count * own_rows : -1]
    mean_loss = tail[-1] / (total_count * width)
    return (
        jnp.stack([st["result"].astype(BF) for st in state]),
        mean_loss,
        jnp.stack([st["grad_inputs"] for st in state]),
        vectors[0],
        vectors[1],
        g_qkv[0],
        g_b_query,
        g_qkv[1],
        g_qkv[2],
        g_b_value,
        g_out,
        vectors[2],
        vectors[3],
        vectors[4],
        g_up,
        g_b_up,
        g_down,
        vectors[5],
    )


def solution(mesh):
    rows3, rows2, flat, mat = P("dp", "seq", None), P("dp", "seq"), P(("dp", "seq")), P(("dp", "seq"), None)
    placed = (
        rows3, rows3, rows2, P("dp"), rows2, flat, flat, mat, flat, mat, mat, flat, mat, flat, flat, flat, mat, flat, mat, flat,
    )
    out = (rows3, P(), rows3, flat, flat, mat, flat, mat, mat, flat, mat, flat, flat, flat, mat, flat, mat, flat)
    return jax.shard_map(local, mesh=mesh, in_specs=placed, out_specs=out, check_vma=False)
```

```python
import functools

import jax
import jax.numpy as jnp
from jax import lax
from jax.experimental import pallas as pl
from jax.experimental.pallas import tpu as pltpu
from jax.sharding import PartitionSpec as P

HD = 64
NSUM = 50
NORM_EPS = 1e-05
NEG_FILL = -1e30
BF = jnp.bfloat16
F32 = jnp.float32


def dot(left_in, right_in):
    return jnp.dot(left_in, right_in, preferred_element_type=F32)


def dot_tn(left_in, right_in):
    return lax.dot_general(left_in, right_in, (((0,), (0,)), ((), ())), preferred_element_type=F32)


def dot_nt(left_in, right_in):
    return lax.dot_general(left_in, right_in, (((1,), (1,)), ((), ())), preferred_element_type=F32)


def norm_core(values):
    center = values - jnp.mean(values, axis=-1, keepdims=True)
    inverse = lax.rsqrt(jnp.mean(center * center, axis=-1, keepdims=True) + NORM_EPS)
    return center * inverse, inverse


def norm_back(grad_out, normed, inverse, gain_in):
    grad_normed = grad_out * gain_in
    inner_one = jnp.mean(grad_normed, axis=-1, keepdims=True)
    inner_two = jnp.mean(grad_normed * normed, axis=-1, keepdims=True)
    grad_in = inverse * (grad_normed - inner_one - normed * inner_two)
    return grad_in, jnp.sum(grad_out * normed, axis=0), jnp.sum(grad_out, axis=0)


def swap(values, mask):
    n = lax.axis_size("seq")
    return lax.ppermute(values, "seq", [(i, i ^ mask) for i in range(n)])


def gather_rows(own):
    n = lax.axis_size("seq")
    if n == 8:
        half = own.shape[0] // 2
        from_two, from_four = swap(own, 2), swap(own, 4)
        six_top, six_end = swap(from_four[:half], 2), swap(from_two[half:], 4)
        same = jnp.concatenate([own, from_two, from_four, six_top, six_end], axis=0)
    else:
        same, step = own, 2
        while step < n:
            same = jnp.concatenate([same, swap(same, step)], axis=0)
            step *= 2
    return same, swap(same, 1)


def scatter_rows(even_blocks, odd_part):
    n = lax.axis_size("seq")
    blocks = even_blocks(swap(odd_part, 1))
    if n == 8:
        zero, two, four, six = blocks
        half = zero.shape[0] // 2
        six = six.astype(BF)
        to_four = swap(six[:half], 2)
        to_two = swap(six[half:], 4)
        two_top = swap(two[:half].astype(BF), 2)
        four_end = swap(four[half:].astype(BF), 4)
        two_end = swap((two[half:] + to_two.astype(F32)).astype(BF), 2)
        four_top = swap((four[:half] + to_four.astype(F32)).astype(BF), 4)
        top = zero[:half] + two_top.astype(F32) + four_top.astype(F32)
        end = zero[half:] + two_end.astype(F32) + four_end.astype(F32)
        return jnp.concatenate([top, end], axis=0)
    step = n // 2
    while step > 1:
        keep = len(blocks) // 2
        sent = [swap(block.astype(BF), step).astype(F32) for block in blocks[keep:]]
        blocks = [block + got for block, got in zip(blocks[:keep], sent)]
        step //= 2
    return blocks[0]


def exchange(values, axis, bit):
    size = lax.axis_size(axis)
    return lax.ppermute(values, axis, [(i, i ^ bit) for i in range(size)])


def gather_small(vector):
    length = -(-vector.shape[0] // 1024) * 1024
    held = jnp.pad(vector, (0, length - vector.shape[0])).reshape(1, 8, length // 8)
    for axis in ("seq", "dp"):
        bit, index = 1, lax.axis_index(axis)
        while bit < lax.axis_size(axis):
            other = exchange(held, axis, bit)
            upper = (index & bit) != 0
            held = jnp.concatenate([jnp.where(upper, other, held), jnp.where(upper, held, other)], axis=0)
            bit *= 2
    return held.reshape(held.shape[0], length)[:, : vector.shape[0]]


def scatter_small(table):
    count, width = table.shape
    length = -(-width // 1024) * 1024
    held = jnp.pad(table, ((0, 0), (0, length - width))).reshape(count, 8, length // 8)
    for axis in ("dp", "seq"):
        bit, index = lax.axis_size(axis) // 2, lax.axis_index(axis)
        while bit > 0:
            half = held.shape[0] // 2
            upper = (index & bit) != 0
            sent = jnp.where(upper, held[:half], held[half:])
            held = jnp.where(upper, held[half:], held[:half]) + exchange(sent, axis, bit)
            bit //= 2
    return held.reshape(length)[:width]


def after(value, *earlier):
    return lax.optimization_barrier((value, *earlier))[0]


def weight_grad_kernel(*refs):
    count = (len(refs) - 1) // 2
    total = dot_tn(refs[0][...], refs[count][...])
    for part in range(1, count):
        total = total + dot_tn(refs[part][...], refs[count + part][...])
    refs[-1][...] = total.astype(BF)


def weight_grad(lefts, rights, left_tile, right_tile):
    rows, left_width = lefts[0].shape
    right_width = rights[0].shape[1]
    left_tile, right_tile = min(left_tile, left_width), min(right_tile, right_width)
    count = len(lefts)
    return pl.pallas_call(
        weight_grad_kernel,
        grid=(right_width // right_tile, left_width // left_tile),
        in_specs=[pl.BlockSpec((rows, left_tile), lambda j, i: (0, i))] * count
        + [pl.BlockSpec((rows, right_tile), lambda j, i: (0, j))] * count,
        out_specs=pl.BlockSpec((left_tile, right_tile), lambda j, i: (i, j)),
        out_shape=jax.ShapeDtypeStruct((left_width, right_width), BF),
        compiler_params=pltpu.CompilerParams(dimension_semantics=("arbitrary", "arbitrary"), vmem_limit_bytes=48 << 20),
        cost_estimate=pl.CostEstimate(
            flops=2 * count * rows * left_width * right_width,
            bytes_accessed=2 * count * rows * (left_width + right_width) + 2 * left_width * right_width,
            transcendentals=0,
        ),
        name="weight_grad",
    )(*lefts, *rights)


def visible_scores(q_head, k_block, first, q_place, key_start, length):
    scores = dot_nt(q_head, k_block)
    k_place = key_start + lax.broadcasted_iota(jnp.int32, (1, length), 1)
    allowed = (k_place >= first) & (k_place <= q_place)
    return jnp.where(allowed, scores, NEG_FILL)


def storage_row(block, place, blocks, length):
    k = block ^ place
    return pl.multiple_of(((k >> 1) + (k & 1) * (blocks // 2)) * length, length)


def fold(values, op):
    out = values[:, :128]
    for start in range(128, values.shape[1], 128):
        out = op(out, values[:, start : start + 128])
    return out


def attend_forward_kernel(
    place_ref, low_ref, q_ref, k_ref, v_ref, first_ref, o_ref, lse_ref, s_scr, m_scr, l_scr, *, heads, length, blocks
):
    i = pl.program_id(0)
    place = place_ref[0]
    low = low_ref[i]
    width = heads * HD
    lanes = lax.broadcasted_iota(jnp.int32, (length, width), 1) // HD
    q_all = q_ref[...]
    q_heads = [jnp.where(lanes == h, q_all, jnp.zeros_like(q_all)) for h in range(heads)]
    first = first_ref[...]
    q_place = i * length + lax.broadcasted_iota(jnp.int32, (length, 1), 0)
    m_scr[...] = jnp.full_like(m_scr, NEG_FILL)
    l_scr[...] = jnp.zeros_like(l_scr)

    def score_step(j, carry):
        k_block = k_ref[pl.ds(storage_row(j, place, blocks, length), length), :]
        cols = pl.ds(pl.multiple_of(j * length, length), length)
        for h in range(heads):
            scores = visible_scores(q_heads[h], k_block, first, q_place, j * length, length)
            s_scr[h, :, cols] = scores
            m_scr[h] = jnp.maximum(m_scr[h], fold(scores, jnp.maximum))
        return carry

    lax.fori_loop(low, i + 1, score_step, 0)
    tops = [jnp.max(m_scr[h], axis=-1, keepdims=True) for h in range(heads)]

    def exp_step(j, carry):
        cols = pl.ds(pl.multiple_of(j * length, length), length)
        for h in range(heads):
            raised = jnp.exp(s_scr[h, :, cols] - tops[h])
            s_scr[h, :, cols] = raised
            l_scr[h] = l_scr[h] + fold(raised, jnp.add)
        return carry

    lax.fori_loop(low, i + 1, exp_step, 0)
    totals = [jnp.sum(l_scr[h], axis=-1, keepdims=True) for h in range(heads)]
    scales = [1.0 / total for total in totals]

    def mix_step(j, acc):
        v_block = v_ref[pl.ds(storage_row(j, place, blocks, length), length), :]
        cols = pl.ds(pl.multiple_of(j * length, length), length)
        for h in range(heads):
            probs = (s_scr[h, :, cols] * scales[h]).astype(BF)
            acc = acc + jnp.where(lanes == h, dot(probs, v_block), 0.0)
        return acc

    mixed = lax.fori_loop(low, i + 1, mix_step, jnp.zeros((length, width), F32))
    o_ref[...] = mixed.astype(BF)
    cols = lax.broadcasted_iota(jnp.int32, (length, 128), 1)
    lse = jnp.zeros((length, 128), F32)
    for h in range(heads):
        lse = jnp.where(cols == h, tops[h] + jnp.log(totals[h]), lse)
    lse_ref[...] = lse


def attend_backward_kernel(
    place_ref, low_ref, q_ref, go_ref, o_ref, lse_ref, k_ref, v_ref, first_ref, grad_ref, kt_scr, vt_scr, *, heads, length, blocks
):
    i = pl.program_id(0)
    place = place_ref[0]
    low = low_ref[i]
    width = heads * HD
    lanes = lax.broadcasted_iota(jnp.int32, (length, width), 1) // HD
    first = first_ref[...]
    q_place = i * length + lax.broadcasted_iota(jnp.int32, (length, 1), 0)
    q_all, go_all = q_ref[...], go_ref[...]
    inner_all = go_all.astype(F32) * o_ref[...].astype(F32)
    q_turned, go_turned = q_all.astype(F32).T.astype(BF), go_all.astype(F32).T.astype(BF)
    lse_all = lse_ref[...]
    q_heads, go_heads, inner, lse = [], [], [], []
    for h in range(heads):
        mine = lanes == h
        q_heads.append(jnp.where(mine, q_all, jnp.zeros_like(q_all)))
        go_heads.append(jnp.where(mine, go_all, jnp.zeros_like(go_all)))
        inner.append(jnp.sum(jnp.where(mine, inner_all, 0.0), axis=-1, keepdims=True))
        lse.append(lse_all[:, h : h + 1])

    @pl.when(i == 0)
    def _():
        kt_scr[...] = jnp.zeros_like(kt_scr)
        vt_scr[...] = jnp.zeros_like(vt_scr)

    def step(j, acc):
        rows = pl.ds(storage_row(j, place, blocks, length), length)
        k_block, v_block = k_ref[rows, :], v_ref[rows, :]
        for h in range(heads):
            scores = visible_scores(q_heads[h], k_block, first, q_place, j * length, length)
            probs = jnp.exp(scores - lse[h])
            grad_probs = dot_nt(go_heads[h], v_block)
            grad_scores = (probs * (grad_probs - inner[h])).astype(BF)
            part = slice(h * HD, (h + 1) * HD)
            vt_scr[part, rows] = vt_scr[part, rows] + dot(go_turned[part, :], probs.astype(BF))
            kt_scr[part, rows] = kt_scr[part, rows] + dot(q_turned[part, :], grad_scores)
            acc = acc + jnp.where(lanes == h, dot(grad_scores, k_block), 0.0)
        return acc

    grad_q = lax.fori_loop(low, i + 1, step, jnp.zeros((length, width), F32))
    own_rows = pl.ds(storage_row(i, place, blocks, length), length)
    grad_ref[own_rows, 0:width] = (grad_q.astype(BF).astype(F32) * (HD**-0.5)).astype(BF)

    @pl.when(i == blocks - 1)
    def _():
        for j in range(blocks):
            rows = slice(j * length, (j + 1) * length)
            grad_ref[rows, width : 2 * width] = kt_scr[:, rows].T.astype(BF)
            grad_ref[rows, 2 * width : 3 * width] = vt_scr[:, rows].T.astype(BF)


def storage_map(length, blocks, column):
    def index(i, place_ref, low_ref):
        k = i ^ place_ref[0]
        return ((k >> 1) + (k & 1) * (blocks // 2), column)

    return index


def attend_cost(rows, width, products):
    return pl.CostEstimate(
        flops=products * rows * rows * 256 * (width // HD), bytes_accessed=8 * rows * width * 2, transcendentals=rows * rows
    )


def attend_forward(place, low, qkv, first, length):
    rows, triple = qkv.shape
    width, blocks = triple // 3, rows // length
    heads = width // HD
    return pl.pallas_call(
        functools.partial(attend_forward_kernel, heads=heads, length=length, blocks=blocks),
        grid_spec=pltpu.PrefetchScalarGridSpec(
            num_scalar_prefetch=2,
            grid=(blocks,),
            in_specs=[
                pl.BlockSpec((length, width), storage_map(length, blocks, 0)),
                pl.BlockSpec((rows, width), lambda i, p, w: (0, 1)),
                pl.BlockSpec((rows, width), lambda i, p, w: (0, 2)),
                pl.BlockSpec((length, 1), lambda i, p, w: (i, 0)),
            ],
            out_specs=[
                pl.BlockSpec((length, width), lambda i, p, w: (i, 0)),
                pl.BlockSpec((length, 128), lambda i, p, w: (i, 0)),
            ],
            scratch_shapes=[
                pltpu.VMEM((heads, length, rows), F32),
                pltpu.VMEM((heads, length, 128), F32),
                pltpu.VMEM((heads, length, 128), F32),
            ],
        ),
        out_shape=[jax.ShapeDtypeStruct((rows, width), BF), jax.ShapeDtypeStruct((rows, 128), F32)],
        compiler_params=pltpu.CompilerParams(dimension_semantics=("arbitrary",), vmem_limit_bytes=40 << 20),
        cost_estimate=attend_cost(rows, width, 6),
        name="attend_forward",
    )(place, low, qkv, qkv, qkv, first)


def attend_backward(place, low, qkv, grad_out, mixed, lse, first, length):
    rows, triple = qkv.shape
    width, blocks = triple // 3, rows // length
    heads = width // HD
    return pl.pallas_call(
        functools.partial(attend_backward_kernel, heads=heads, length=length, blocks=blocks),
        grid_spec=pltpu.PrefetchScalarGridSpec(
            num_scalar_prefetch=2,
            grid=(blocks,),
            in_specs=[
                pl.BlockSpec((length, width), storage_map(length, blocks, 0)),
                pl.BlockSpec((length, width), lambda i, p, w: (i, 0)),
                pl.BlockSpec((length, width), lambda i, p, w: (i, 0)),
                pl.BlockSpec((length, 128), lambda i, p, w: (i, 0)),
                pl.BlockSpec((rows, width), lambda i, p, w: (0, 1)),
                pl.BlockSpec((rows, width), lambda i, p, w: (0, 2)),
                pl.BlockSpec((length, 1), lambda i, p, w: (i, 0)),
            ],
            out_specs=pl.BlockSpec((rows, triple), lambda i, p, w: (0, 0)),
            scratch_shapes=[pltpu.VMEM((width, rows), F32), pltpu.VMEM((width, rows), F32)],
        ),
        out_shape=jax.ShapeDtypeStruct((rows, triple), BF),
        compiler_params=pltpu.CompilerParams(dimension_semantics=("arbitrary",), vmem_limit_bytes=40 << 20),
        cost_estimate=attend_cost(rows, width, 10),
        name="attend_backward",
    )(place, low, qkv, grad_out, mixed, lse, qkv, qkv, first)


def local(
    inputs,
    teacher,
    segment_ids,
    summary_start,
    valid_mask,
    attn_norm_gain,
    attn_norm_bias,
    query_weight,
    query_bias,
    key_weight,
    value_weight,
    value_bias,
    out_weight,
    out_bias,
    mlp_norm_gain,
    mlp_norm_bias,
    up_weight,
    up_bias,
    down_weight,
    down_bias,
):
    seqs, length = segment_ids.shape
    width = inputs.shape[-1]
    hidden_units = up_weight.shape[1]
    n, groups = lax.axis_size("seq"), lax.axis_size("dp")
    place, group = lax.axis_index("seq"), lax.axis_index("dp")
    both = ("dp", "seq")
    seq_len = length * n
    tokens_all = seqs * seq_len * groups
    scale = HD**-0.5
    own_rows = query_weight.shape[0]
    own_hidden = up_bias.shape[0]
    head_cols = width // n

    valid = valid_mask.astype(F32)
    small = [attn_norm_gain, attn_norm_bias, out_bias, mlp_norm_gain, mlp_norm_bias, down_bias, query_bias, value_bias, up_bias]
    sizes = [v.shape[0] for v in small]
    packed = jnp.concatenate([v.astype(F32) for v in small] + [segment_ids.astype(F32).reshape(-1), jnp.sum(valid).reshape(1)])
    packed = gather_small(packed)
    parts, at = [], 0
    for size in sizes:
        parts.append(packed[:, at : at + size])
        at += size
    gain_one, shift_one, b_out, gain_two, shift_two, b_down = [part.reshape(-1) for part in parts[:6]]
    b_query, b_value = [lax.dynamic_slice_in_dim(part.reshape(-1), place * head_cols, head_cols) for part in parts[6:8]]
    b_up = lax.dynamic_index_in_dim(parts[8].reshape(groups, n, -1), place, 1, keepdims=False).reshape(-1)
    ids = packed[:, at : at + seqs * length].reshape(groups, n, seqs, length)
    ids = lax.dynamic_index_in_dim(ids, group, 0, keepdims=False).transpose(1, 0, 2).reshape(seqs, seq_len)
    total_count = jnp.sum(packed[:, at + seqs * length])

    qkv_cut = jnp.concatenate(
        [w.reshape(own_rows, n, head_cols).transpose(1, 0, 2) for w in (query_weight, key_weight, value_weight)], axis=2
    )
    qkv_cut = lax.all_to_all(qkv_cut, "seq", split_axis=0, concat_axis=0, tiled=True)
    w_qkv = lax.all_gather(qkv_cut.reshape(n * own_rows, 3 * head_cols), "dp", axis=0, tiled=True)
    w_out = lax.all_gather(out_weight, both, axis=0, tiled=True)
    up_cut = up_weight.reshape(own_rows, groups, n, own_hidden).transpose(2, 0, 1, 3).reshape(n, own_rows, groups * own_hidden)
    up_cut = lax.all_to_all(up_cut, "seq", split_axis=0, concat_axis=0, tiled=True)
    w_up = lax.all_gather(up_cut.reshape(n * own_rows, groups * own_hidden), "dp", axis=0, tiled=True)
    w_down = lax.all_gather(down_weight, "dp", axis=0, tiled=True)
    b_qkv = jnp.concatenate([b_query, jnp.zeros_like(b_query), b_value])
    s_qkv = jnp.concatenate([jnp.full((head_cols,), scale, F32), jnp.ones((2 * head_cols,), F32)])

    place_arr = place.reshape(1).astype(jnp.int32)
    positions = jnp.arange(seq_len, dtype=jnp.int32)

    def out_of(value):
        return lax.all_to_all(value, "seq", split_axis=0, concat_axis=0, tiled=True)

    def block_products(left, function):
        def run(got):
            cuts = [slice(m * length, (m + 1) * length) for m in range(n // 2)]
            return [function(left[cut]) + got[cut].astype(F32) for cut in cuts]

        return run

    def add_all(terms):
        out = terms[0]
        for term in terms[1:]:
            out = out + term
        return out

    state = [dict() for _ in range(seqs)]

    def start(b):
        st = state[b]
        st["rows"] = inputs[b].astype(F32)
        st["normed"], st["inverse"] = norm_core(st["rows"])
        ready = (st["normed"] * gain_one + shift_one).astype(BF)
        first = jnp.sum((ids[b][None, :] < ids[b][:, None]).astype(jnp.int32), axis=1)
        in_summary = (positions >= summary_start[b]) & (positions < summary_start[b] + NSUM)
        first = jnp.where(in_summary, 0, first)
        st["low"] = jnp.min(first.reshape(n, length), axis=1) // length
        st["first"] = first.reshape(seq_len, 1)
        st["even"], st["odd"] = gather_rows(ready)

    def project(b, *earlier):
        st = state[b]
        parts = [after(st["even"], *earlier) if earlier else st["even"], st["odd"]]
        st["qkv"] = jnp.concatenate([((dot(part, w_qkv) + b_qkv) * s_qkv).astype(BF) for part in parts], axis=0)

    def attend(b, *earlier):
        st = state[b]
        qkv = after(st["qkv"], *earlier) if earlier else st["qkv"]
        st["mixed"], st["lse"] = attend_forward(place_arr, st["low"], qkv, st["first"], length)
        moved = out_of(st["mixed"].reshape(n, length, head_cols))
        st["attended"] = moved.transpose(1, 0, 2).reshape(length, width)

    def middle(b):
        st = state[b]
        st["hidden"] = st["rows"] + (dot(st["attended"], w_out) + b_out)
        st["normed_two"], st["inverse_two"] = norm_core(st["hidden"])
        st["ready_two"] = (st["normed_two"] * gain_two + shift_two).astype(BF)
        st["even_two"], st["odd_two"] = gather_rows(st["ready_two"])

    def up(b):
        st = state[b]
        st["act_even"] = jnp.maximum(dot(st["even_two"], w_up) + b_up, 0.0).astype(BF)
        st["act_odd"] = jnp.maximum(dot(st["odd_two"], w_up) + b_up, 0.0).astype(BF)

    def down(b, *earlier):
        st = state[b]
        act_odd = after(st["act_odd"], *earlier) if earlier else st["act_odd"]
        odd = dot(act_odd, w_down).astype(BF)
        summed = scatter_rows(block_products(st["act_even"], lambda rows: dot(rows, w_down)), odd)
        st["result"] = st["hidden"] + (summed + b_down)
        misfit = st["result"] - teacher[b].astype(F32)
        st["local_sq"] = jnp.sum(jnp.sum(misfit * misfit, axis=-1) * valid[b])
        st["grad_result"] = misfit * (valid[b] * (tokens_all / total_count))[:, None]
        low_grad = st["grad_result"].astype(BF)
        st["g_b_down"] = jnp.sum(low_grad.astype(F32), axis=0)
        st["gm_even"], st["gm_odd"] = gather_rows(low_grad)

    def mlp_back(b):
        st = state[b]
        st["pre_odd"] = jnp.where(st["act_odd"] > 0, dot_nt(st["gm_odd"], w_down), 0.0).astype(BF)
        odd = dot_nt(st["pre_odd"], w_up).astype(BF)
        st["pre_even"] = jnp.where(st["act_even"] > 0, dot_nt(st["gm_even"], w_down), 0.0).astype(BF)
        st["grad_ready"] = scatter_rows(block_products(st["pre_even"], lambda rows: dot_nt(rows, w_up)), odd)
        st["g_b_up"] = jnp.sum(st["pre_even"].astype(F32), axis=0) + jnp.sum(st["pre_odd"].astype(F32), axis=0)

    def branch_back(b, *earlier):
        st = state[b]
        grad_ready = after(st["grad_ready"], *earlier) if earlier else st["grad_ready"]
        grad_norm, st["g_gain_two"], st["g_shift_two"] = norm_back(grad_ready, st["normed_two"], st["inverse_two"], gain_two)
        st["grad_hidden"] = st["grad_result"] + grad_norm
        st["branch"] = st["grad_hidden"].astype(BF)
        st["g_b_out"] = jnp.sum(st["branch"].astype(F32), axis=0)
        grad_att = dot_nt(st["branch"], w_out).astype(BF).reshape(length, n, head_cols).transpose(1, 0, 2)
        st["grad_mixed"] = out_of(grad_att).reshape(seq_len, head_cols)

    def attend_back(b, *earlier):
        st = state[b]
        grad_mixed = after(st["grad_mixed"], *earlier) if earlier else st["grad_mixed"]
        st["grad_qkv"] = attend_backward(
            place_arr, st["low"], st["qkv"], grad_mixed, st["mixed"], st["lse"], st["first"], length
        )
        st["g_b_qkv"] = jnp.sum(st["grad_qkv"].astype(F32), axis=0)

    def project_back(b):
        st = state[b]
        half = seq_len // 2
        even, odd = st["grad_qkv"][:half], st["grad_qkv"][half:]
        st["grad_ready_one"] = scatter_rows(
            block_products(even, lambda rows: dot_nt(rows, w_qkv)), dot_nt(odd, w_qkv).astype(BF)
        )

    def finish(b):
        st = state[b]
        grad_norm, st["g_gain_one"], st["g_shift_one"] = norm_back(
            st["grad_ready_one"], st["normed"], st["inverse"], gain_one
        )
        st["grad_inputs"] = st["grad_hidden"] + grad_norm

    every = range(seqs)
    for b in every:
        start(b)
    for b in every:
        if b == 0:
            project(b)
            attend(b)
        else:
            project(b, state[b - 1]["mixed"])
            middle(b - 1)
            attend(b, state[b - 1]["ready_two"])
            up(b - 1)
    middle(seqs - 1)
    for b in range(seqs - 1):
        down(b, state[b + 1]["ready_two"])
    up(seqs - 1)
    down(seqs - 1)
    for b in every:
        mlp_back(b)

    lefts = [st[name] for st in state for name in ("act_even", "act_odd")]
    rights = [st[name] for st in state for name in ("gm_even", "gm_odd")]
    g_w_down = weight_grad(lefts, rights, 256, 1024)
    g_down = lax.psum_scatter(g_w_down, "dp", scatter_dimension=0, tiled=True).astype(F32)
    lefts = [st[name] for st in state for name in ("even_two", "odd_two")]
    rights = [st[name] for st in state for name in ("pre_even", "pre_odd")]
    g_w_up = weight_grad(lefts, rights, 512, 1024)
    g_up = lax.psum_scatter(g_w_up, "dp", scatter_dimension=0, tiled=True)
    for b in every:
        branch_back(b, g_w_down, g_w_up)

    turned = [
        st["attended"].reshape(length, groups, n, own_rows).transpose(2, 0, 1, 3).reshape(n, length, groups * own_rows)
        for st in state
    ]

    def out_block(k):
        return add_all(
            [dot_tn(lax.dynamic_index_in_dim(t, place ^ k, 0, keepdims=False), st["branch"]) for t, st in zip(turned, state)]
        )

    out_odd = jnp.concatenate([out_block(k).astype(BF) for k in range(1, n, 2)], axis=0)
    out_rows = groups * own_rows
    g_out = scatter_rows(
        lambda got: [out_block(2 * m) + got[m * out_rows : (m + 1) * out_rows].astype(F32) for m in range(n // 2)], out_odd
    )
    g_out = lax.psum_scatter(g_out.astype(BF), "dp", scatter_dimension=0, tiled=True).astype(F32)
    for b in every:
        if b:
            attend_back(b, state[b - 1]["grad_qkv"])
        else:
            attend_back(b)
        project_back(b)
    half = seq_len // 2
    lefts = [st[name] for st in state for name in ("even", "odd")]
    rights = [part for st in state for part in (st["grad_qkv"][:half], st["grad_qkv"][half:])]
    g_w_qkv = weight_grad(lefts, rights, 1024, 768)
    g_qkv = lax.psum_scatter(g_w_qkv, "dp", scatter_dimension=0, tiled=True)
    for b in every:
        finish(b)

    def summed(name):
        return add_all([st[name] for st in state])

    g_up = out_of(g_up.reshape(n, own_rows, groups * own_hidden))
    g_up = g_up.reshape(n, own_rows, groups, own_hidden).transpose(1, 2, 0, 3).reshape(own_rows, hidden_units).astype(F32)
    g_qkv = out_of(g_qkv.reshape(n, own_rows, 3 * head_cols))
    g_qkv = g_qkv.reshape(n, own_rows, 3, head_cols).transpose(2, 1, 0, 3).reshape(3, own_rows, width).astype(F32)

    g_b_qkv = summed("g_b_qkv").reshape(3, head_cols)
    own_bias = jnp.zeros((2, width), F32)
    own_bias = lax.dynamic_update_slice(own_bias, jnp.stack([g_b_qkv[0], g_b_qkv[2]]), (0, place * head_cols))
    g_b_up = summed("g_b_up").reshape(groups, 1, own_hidden)
    spread_up = lax.dynamic_update_slice_in_dim(jnp.zeros((groups, n, own_hidden), F32), g_b_up, place, 1)
    names = ("g_gain_one", "g_shift_one", "g_b_out", "g_gain_two", "g_shift_two", "g_b_down")
    vectors = jnp.concatenate([jnp.stack([summed(name) for name in names]), own_bias], axis=0)
    count = vectors.shape[0]
    vectors = vectors.reshape(count, groups * n, own_rows).transpose(1, 0, 2).reshape(groups * n, count * own_rows)
    sq = jnp.broadcast_to(summed("local_sq"), (groups * n, 1))
    tail = jnp.concatenate([vectors, spread_up.reshape(groups * n, own_hidden), sq], axis=1)
    tail = scatter_small(tail)
    vectors = tail[: count * own_rows].reshape(count, own_rows)
    g_b_query, g_b_value, g_b_up = vectors[6], vectors[7], tail[count * own_rows : -1]
    mean_loss = tail[-1] / (total_count * width)
    return (
        jnp.stack([st["result"].astype(BF) for st in state]),
        mean_loss,
        jnp.stack([st["grad_inputs"] for st in state]),
        vectors[0],
        vectors[1],
        g_qkv[0],
        g_b_query,
        g_qkv[1],
        g_qkv[2],
        g_b_value,
        g_out,
        vectors[2],
        vectors[3],
        vectors[4],
        g_up,
        g_b_up,
        g_down,
        vectors[5],
    )


def solution(mesh):
    rows3, rows2, flat, mat = P("dp", "seq", None), P("dp", "seq"), P(("dp", "seq")), P(("dp", "seq"), None)
    placed = (
        rows3, rows3, rows2, P("dp"), rows2, flat, flat, mat, flat, mat, mat, flat, mat, flat, flat, flat, mat, flat, mat, flat,
    )
    out = (rows3, P(), rows3, flat, flat, mat, flat, mat, mat, flat, mat, flat, flat, flat, mat, flat, mat, flat)
    return jax.shard_map(local, mesh=mesh, in_specs=placed, out_specs=out, check_vma=False)
```

```python
import functools
import types

import jax
import jax.numpy as jnp
from jax import lax
from jax.experimental import pallas as pl
from jax.experimental.pallas import tpu as pltpu
from jax.sharding import PartitionSpec as P

HD = 64
NSUM = 50
NORM_EPS = 1e-05
NEG_FILL = -1e30
BF = jnp.bfloat16
F32 = jnp.float32


def dot(left_in, right_in):
    return jnp.dot(left_in, right_in, preferred_element_type=F32)


def dot_tn(left_in, right_in):
    return lax.dot_general(left_in, right_in, (((0,), (0,)), ((), ())), preferred_element_type=F32)


def dot_nt(left_in, right_in):
    return lax.dot_general(left_in, right_in, (((1,), (1,)), ((), ())), preferred_element_type=F32)


def norm_core(values):
    center = values - jnp.mean(values, axis=-1, keepdims=True)
    inverse = lax.rsqrt(jnp.mean(center * center, axis=-1, keepdims=True) + NORM_EPS)
    return center * inverse, inverse


def norm_back(grad_out, normed, inverse, gain_in):
    grad_normed = grad_out * gain_in
    inner_one = jnp.mean(grad_normed, axis=-1, keepdims=True)
    inner_two = jnp.mean(grad_normed * normed, axis=-1, keepdims=True)
    grad_in = inverse * (grad_normed - inner_one - normed * inner_two)
    return grad_in, jnp.sum(grad_out * normed, axis=0), jnp.sum(grad_out, axis=0)


def swap(values, mask):
    n = lax.axis_size("seq")
    return lax.ppermute(values, "seq", [(i, i ^ mask) for i in range(n)])


def gather_start(own):
    n = lax.axis_size("seq")
    return (swap(own, 2), swap(own, 4)) if n == 8 else ()


def gather_end(own, came):
    n = lax.axis_size("seq")
    if n == 8:
        half = own.shape[0] // 2
        from_two, from_four = came
        six_top, six_end = swap(from_four[:half], 2), swap(from_two[half:], 4)
        same = jnp.concatenate([own, from_two, from_four, six_top, six_end], axis=0)
    else:
        same, step = own, 2
        while step < n:
            same = jnp.concatenate([same, swap(same, step)], axis=0)
            step *= 2
    return same, swap(same, 1)


def gather_rows(own):
    return gather_end(own, gather_start(own))


def scatter_start(blocks):
    if lax.axis_size("seq") != 8:
        return ()
    six = blocks[3].astype(BF)
    half = six.shape[0] // 2
    return swap(six[:half], 2), swap(six[half:], 4)


def scatter_end(blocks, came):
    n = lax.axis_size("seq")
    if n == 8:
        zero, two, four, _ = blocks
        half = zero.shape[0] // 2
        to_four, to_two = came
        four = jnp.concatenate([four[:half] + to_four.astype(F32), four[half:]], axis=0).astype(BF)
        two = jnp.concatenate([two[:half], two[half:] + to_two.astype(F32)], axis=0).astype(BF)
        return zero + swap(two, 2).astype(F32) + swap(four, 4).astype(F32)
    step = n // 2
    while step > 1:
        keep = len(blocks) // 2
        sent = [swap(block.astype(BF), step).astype(F32) for block in blocks[keep:]]
        blocks = [block.astype(F32) + got for block, got in zip(blocks[:keep], sent)]
        step //= 2
    return blocks[0]


def scatter_rows(blocks):
    return scatter_end(blocks, scatter_start(blocks))


def scatter_groups(rows):
    bit, index = lax.axis_size("dp") // 2, lax.axis_index("dp")
    while bit > 0:
        half = rows.shape[0] // 2
        upper = (index & bit) != 0
        sent = jnp.where(upper, rows[:half], rows[half:]).astype(BF)
        rows = jnp.where(upper, rows[half:], rows[:half]) + exchange(sent, "dp", bit).astype(F32)
        bit //= 2
    return rows


def exchange(values, axis, bit):
    size = lax.axis_size(axis)
    return lax.ppermute(values, axis, [(i, i ^ bit) for i in range(size)])


def gather_small(vector):
    length = -(-vector.shape[0] // 1024) * 1024
    held = jnp.pad(vector, (0, length - vector.shape[0])).reshape(1, 8, length // 8)
    for axis in ("seq", "dp"):
        bit, index = 1, lax.axis_index(axis)
        while bit < lax.axis_size(axis):
            other = exchange(held, axis, bit)
            upper = (index & bit) != 0
            held = jnp.concatenate([jnp.where(upper, other, held), jnp.where(upper, held, other)], axis=0)
            bit *= 2
    return held.reshape(held.shape[0], length)[:, : vector.shape[0]]


def scatter_small(table):
    count, width = table.shape
    length = -(-width // 1024) * 1024
    held = jnp.pad(table, ((0, 0), (0, length - width))).reshape(count, 8, length // 8)
    for axis in ("dp", "seq"):
        bit, index = lax.axis_size(axis) // 2, lax.axis_index(axis)
        while bit > 0:
            half = held.shape[0] // 2
            upper = (index & bit) != 0
            sent = jnp.where(upper, held[:half], held[half:])
            held = jnp.where(upper, held[half:], held[:half]) + exchange(sent, axis, bit)
            bit //= 2
    return held.reshape(length)[:width]


def trade(pieces):
    n = lax.axis_size("seq")
    index = lax.axis_index("seq")
    came = [lax.dynamic_index_in_dim(pieces, index ^ k, 0, keepdims=False) for k in range(n)]
    came = jnp.stack([swap(piece, k) if k else piece for k, piece in enumerate(came)])
    return jnp.stack([lax.dynamic_index_in_dim(came, other ^ index, 0, keepdims=False) for other in range(n)])


def after(value, *earlier):
    return lax.optimization_barrier((value, *earlier))[0]


def after_all(values, *earlier):
    return lax.optimization_barrier((values, *earlier))[0]


def natural_rows(pieces):
    n = lax.axis_size("seq")
    index = lax.axis_index("seq")
    came = []
    for other in range(n):
        k = other ^ index
        came.append(lax.dynamic_index_in_dim(pieces, (k >> 1) + (k & 1) * (n // 2), 0, keepdims=False))
    return came


def weight_grad_kernel(*refs):
    count = (len(refs) - 1) // 2
    total = dot_tn(refs[0][...], refs[count][...])
    for part in range(1, count):
        total = total + dot_tn(refs[part][...], refs[count + part][...])
    refs[-1][...] = total.astype(BF)


def weight_grad(lefts, rights, left_tile, right_tile):
    rows, left_width = lefts[0].shape
    right_width = rights[0].shape[1]
    left_tile, right_tile = min(left_tile, left_width), min(right_tile, right_width)
    count = len(lefts)
    return pl.pallas_call(
        weight_grad_kernel,
        grid=(right_width // right_tile, left_width // left_tile),
        in_specs=[pl.BlockSpec((rows, left_tile), lambda j, i: (0, i))] * count
        + [pl.BlockSpec((rows, right_tile), lambda j, i: (0, j))] * count,
        out_specs=pl.BlockSpec((left_tile, right_tile), lambda j, i: (i, j)),
        out_shape=jax.ShapeDtypeStruct((left_width, right_width), BF),
        compiler_params=pltpu.CompilerParams(dimension_semantics=("arbitrary", "arbitrary"), vmem_limit_bytes=48 << 20),
        cost_estimate=SMALL_COST,
        name="weight_grad",
    )(*lefts, *rights)


def tile_dot(left, right, turned):
    return dot_nt(left, right) if turned else dot(left, right)


def plain_kernel(left_ref, right_ref, out_ref, *, turned):
    out_ref[...] = tile_dot(left_ref[...], right_ref[...], turned).astype(out_ref.dtype)


def project_kernel(left_ref, right_ref, bias_ref, scale_ref, out_ref):
    out_ref[...] = ((dot(left_ref[...], right_ref[...]) + bias_ref[...]) * scale_ref[...]).astype(BF)


def up_kernel(left_ref, right_ref, bias_ref, out_ref):
    out_ref[...] = jnp.maximum(dot(left_ref[...], right_ref[...]) + bias_ref[...], 0.0).astype(BF)


def masked_kernel(left_ref, right_ref, act_ref, out_ref, sums_ref):
    grad = jnp.where(act_ref[...] > 0, dot_nt(left_ref[...], right_ref[...]), 0.0).astype(BF)
    out_ref[...] = grad
    part = jnp.sum(grad.astype(F32).reshape(-1, 8, grad.shape[1]), axis=0)

    @pl.when(pl.program_id(1) == 0)
    def _():
        sums_ref[...] = part

    @pl.when(pl.program_id(1) > 0)
    def _():
        sums_ref[...] = sums_ref[...] + part


def blocks_kernel(left_ref, right_ref, got_ref, *out_refs, turned):
    count = len(out_refs)
    total = tile_dot(left_ref[...], right_ref[...], turned) + got_ref[...].astype(F32)
    for m in range(count):

        @pl.when(pl.program_id(1) == count - 1 - m)
        def _(m=m):
            out_refs[m][...] = total.astype(out_refs[m].dtype)


SMALL_COST = pl.CostEstimate(flops=1, bytes_accessed=1, transcendentals=0)


def tiled(kernel, name, left, right, turned, extras, outs, row_tile, col_tile, row_of=lambda m: m):
    rows, depth = left.shape
    cols = right.shape[0] if turned else right.shape[1]
    row_tile, col_tile = min(row_tile, rows), min(col_tile, cols)
    kinds = {
        "both": pl.BlockSpec((row_tile, col_tile), lambda j, m: (row_of(m), j)),
        "vector": pl.BlockSpec((1, col_tile), lambda j, m: (0, j)),
        "sums": pl.BlockSpec((8, col_tile), lambda j, m: (0, j)),
        "block": pl.BlockSpec((row_tile, col_tile), lambda j, m: (0, j)),
    }
    shapes = {"both": (rows, cols), "sums": (8, cols), "block": (row_tile, cols)}
    right_spec = (
        pl.BlockSpec((col_tile, depth), lambda j, m: (j, 0)) if turned else pl.BlockSpec((depth, col_tile), lambda j, m: (0, j))
    )
    return pl.pallas_call(
        kernel,
        grid=(cols // col_tile, rows // row_tile),
        in_specs=[pl.BlockSpec((row_tile, depth), lambda j, m: (row_of(m), 0)), right_spec] + [kinds[k] for k, _ in extras],
        out_specs=[kinds[k] for k, _ in outs],
        out_shape=[jax.ShapeDtypeStruct(shapes[k], dtype) for k, dtype in outs],
        compiler_params=pltpu.CompilerParams(dimension_semantics=("arbitrary", "arbitrary"), vmem_limit_bytes=40 << 20),
        cost_estimate=SMALL_COST,
        name=name,
    )(left, right, *[value for _, value in extras])


def plain_product(left, right, turned=False):
    kernel = functools.partial(plain_kernel, turned=turned)
    return tiled(kernel, "product", left, right, turned, [], [("both", BF)], 256, 1024)[0]


def project_product(left, right, bias, scale):
    extras = [("vector", bias.reshape(1, -1)), ("vector", scale.reshape(1, -1))]
    return tiled(project_kernel, "project", left, right, False, extras, [("both", BF)], 256, 768)[0]


def up_product(left, right, bias):
    return tiled(up_kernel, "up", left, right, False, [("vector", bias.reshape(1, -1))], [("both", BF)], 256, 512)[0]


def masked_product(left, right, act):
    outs = [("both", BF), ("sums", F32)]
    return tiled(masked_kernel, "masked_product", left, right, True, [("both", act)], outs, 256, 512)


def block_products(left, right, got, count, turned=False):
    kernel = functools.partial(blocks_kernel, turned=turned)
    outs = [("block", F32)] * (count - 1) + [("block", BF)]
    return tiled(
        kernel, "block_products", left, right, turned, [("both", got)], outs, left.shape[0] // count, 1024, lambda m: count - 1 - m
    )


def visible_scores(q_head, k_block, first, q_place, key_start, length):
    scores = dot_nt(q_head, k_block)
    k_place = key_start + lax.broadcasted_iota(jnp.int32, (1, length), 1)
    allowed = (k_place >= first) & (k_place <= q_place)
    return jnp.where(allowed, scores, NEG_FILL)


def storage_row(block, place, blocks, length):
    k = block ^ place
    return pl.multiple_of(((k >> 1) + (k & 1) * (blocks // 2)) * length, length)


def fold(values, op):
    out = values[:, :128]
    for start in range(128, values.shape[1], 128):
        out = op(out, values[:, start : start + 128])
    return out


def attend_forward_kernel(
    place_ref, low_ref, q_ref, k_ref, v_ref, first_ref, o_ref, lse_ref, s_scr, m_scr, l_scr, *, heads, length, blocks
):
    i = pl.program_id(0)
    place = place_ref[0]
    low = low_ref[i]
    width = heads * HD
    lanes = lax.broadcasted_iota(jnp.int32, (length, width), 1) // HD
    q_all = q_ref[...]
    q_heads = [jnp.where(lanes == h, q_all, jnp.zeros_like(q_all)) for h in range(heads)]
    first = first_ref[...]
    q_place = i * length + lax.broadcasted_iota(jnp.int32, (length, 1), 0)
    m_scr[...] = jnp.full_like(m_scr, NEG_FILL)
    l_scr[...] = jnp.zeros_like(l_scr)

    def score_step(j, carry):
        k_block = k_ref[pl.ds(storage_row(j, place, blocks, length), length), :]
        cols = pl.ds(pl.multiple_of(j * length, length), length)
        for h in range(heads):
            scores = visible_scores(q_heads[h], k_block, first, q_place, j * length, length)
            s_scr[h, :, cols] = scores
            m_scr[h] = jnp.maximum(m_scr[h], fold(scores, jnp.maximum))
        return carry

    lax.fori_loop(low, i + 1, score_step, 0)
    tops = [jnp.max(m_scr[h], axis=-1, keepdims=True) for h in range(heads)]

    def exp_step(j, carry):
        cols = pl.ds(pl.multiple_of(j * length, length), length)
        for h in range(heads):
            raised = jnp.exp(s_scr[h, :, cols] - tops[h])
            s_scr[h, :, cols] = raised
            l_scr[h] = l_scr[h] + fold(raised, jnp.add)
        return carry

    lax.fori_loop(low, i + 1, exp_step, 0)
    totals = [jnp.sum(l_scr[h], axis=-1, keepdims=True) for h in range(heads)]
    scales = [1.0 / total for total in totals]

    def mix_step(j, acc):
        v_block = v_ref[pl.ds(storage_row(j, place, blocks, length), length), :]
        cols = pl.ds(pl.multiple_of(j * length, length), length)
        for h in range(heads):
            probs = (s_scr[h, :, cols] * scales[h]).astype(BF)
            acc = acc + jnp.where(lanes == h, dot(probs, v_block), 0.0)
        return acc

    mixed = lax.fori_loop(low, i + 1, mix_step, jnp.zeros((length, width), F32))
    o_ref[...] = mixed.astype(BF)
    cols = lax.broadcasted_iota(jnp.int32, (length, 128), 1)
    lse = jnp.zeros((length, 128), F32)
    for h in range(heads):
        lse = jnp.where(cols == h, tops[h] + jnp.log(totals[h]), lse)
    lse_ref[...] = lse


def attend_backward_kernel(
    place_ref, low_ref, q_ref, go_ref, o_ref, lse_ref, k_ref, v_ref, first_ref, grad_ref, kt_scr, vt_scr, *, heads, length, blocks
):
    i = pl.program_id(0)
    place = place_ref[0]
    low = low_ref[i]
    width = heads * HD
    lanes = lax.broadcasted_iota(jnp.int32, (length, width), 1) // HD
    first = first_ref[...]
    q_place = i * length + lax.broadcasted_iota(jnp.int32, (length, 1), 0)
    q_all, go_all = q_ref[...], go_ref[...]
    inner_all = go_all.astype(F32) * o_ref[...].astype(F32)
    q_turned, go_turned = q_all.astype(F32).T.astype(BF), go_all.astype(F32).T.astype(BF)
    lse_all = lse_ref[...]
    q_heads, go_heads, inner, lse = [], [], [], []
    for h in range(heads):
        mine = lanes == h
        q_heads.append(jnp.where(mine, q_all, jnp.zeros_like(q_all)))
        go_heads.append(jnp.where(mine, go_all, jnp.zeros_like(go_all)))
        inner.append(jnp.sum(jnp.where(mine, inner_all, 0.0), axis=-1, keepdims=True))
        lse.append(lse_all[:, h : h + 1])

    @pl.when(i == 0)
    def _():
        kt_scr[...] = jnp.zeros_like(kt_scr)
        vt_scr[...] = jnp.zeros_like(vt_scr)

    def step(j, acc):
        rows = pl.ds(storage_row(j, place, blocks, length), length)
        k_block, v_block = k_ref[rows, :], v_ref[rows, :]
        for h in range(heads):
            scores = visible_scores(q_heads[h], k_block, first, q_place, j * length, length)
            probs = jnp.exp(scores - lse[h])
            grad_probs = dot_nt(go_heads[h], v_block)
            grad_scores = (probs * (grad_probs - inner[h])).astype(BF)
            part = slice(h * HD, (h + 1) * HD)
            vt_scr[part, rows] = vt_scr[part, rows] + dot(go_turned[part, :], probs.astype(BF))
            kt_scr[part, rows] = kt_scr[part, rows] + dot(q_turned[part, :], grad_scores)
            acc = acc + jnp.where(lanes == h, dot(grad_scores, k_block), 0.0)
        return acc

    grad_q = lax.fori_loop(low, i + 1, step, jnp.zeros((length, width), F32))
    own_rows = pl.ds(storage_row(i, place, blocks, length), length)
    grad_ref[own_rows, 0:width] = (grad_q.astype(BF).astype(F32) * (HD**-0.5)).astype(BF)

    @pl.when(i == blocks - 1)
    def _():
        for j in range(blocks):
            rows = slice(j * length, (j + 1) * length)
            grad_ref[rows, width : 2 * width] = kt_scr[:, rows].T.astype(BF)
            grad_ref[rows, 2 * width : 3 * width] = vt_scr[:, rows].T.astype(BF)


def storage_map(length, blocks, column):
    def index(i, place_ref, low_ref):
        k = i ^ place_ref[0]
        return ((k >> 1) + (k & 1) * (blocks // 2), column)

    return index


def attend_forward(place, low, qkv, first, length):
    rows, triple = qkv.shape
    width, blocks = triple // 3, rows // length
    heads = width // HD
    return pl.pallas_call(
        functools.partial(attend_forward_kernel, heads=heads, length=length, blocks=blocks),
        grid_spec=pltpu.PrefetchScalarGridSpec(
            num_scalar_prefetch=2,
            grid=(blocks,),
            in_specs=[
                pl.BlockSpec((length, width), storage_map(length, blocks, 0)),
                pl.BlockSpec((rows, width), lambda i, p, w: (0, 1)),
                pl.BlockSpec((rows, width), lambda i, p, w: (0, 2)),
                pl.BlockSpec((length, 1), lambda i, p, w: (i, 0)),
            ],
            out_specs=[
                pl.BlockSpec((length, width), lambda i, p, w: (i, 0)),
                pl.BlockSpec((length, 128), lambda i, p, w: (i, 0)),
            ],
            scratch_shapes=[
                pltpu.VMEM((heads, length, rows), F32),
                pltpu.VMEM((heads, length, 128), F32),
                pltpu.VMEM((heads, length, 128), F32),
            ],
        ),
        out_shape=[jax.ShapeDtypeStruct((rows, width), BF), jax.ShapeDtypeStruct((rows, 128), F32)],
        compiler_params=pltpu.CompilerParams(dimension_semantics=("arbitrary",), vmem_limit_bytes=40 << 20),
        cost_estimate=SMALL_COST,
        name="attend_forward",
    )(place, low, qkv, qkv, qkv, first)


def attend_backward(place, low, qkv, grad_out, mixed, lse, first, length):
    rows, triple = qkv.shape
    width, blocks = triple // 3, rows // length
    heads = width // HD
    return pl.pallas_call(
        functools.partial(attend_backward_kernel, heads=heads, length=length, blocks=blocks),
        grid_spec=pltpu.PrefetchScalarGridSpec(
            num_scalar_prefetch=2,
            grid=(blocks,),
            in_specs=[
                pl.BlockSpec((length, width), storage_map(length, blocks, 0)),
                pl.BlockSpec((length, width), lambda i, p, w: (i, 0)),
                pl.BlockSpec((length, width), lambda i, p, w: (i, 0)),
                pl.BlockSpec((length, 128), lambda i, p, w: (i, 0)),
                pl.BlockSpec((rows, width), lambda i, p, w: (0, 1)),
                pl.BlockSpec((rows, width), lambda i, p, w: (0, 2)),
                pl.BlockSpec((length, 1), lambda i, p, w: (i, 0)),
            ],
            out_specs=pl.BlockSpec((rows, triple), lambda i, p, w: (0, 0)),
            scratch_shapes=[pltpu.VMEM((width, rows), F32), pltpu.VMEM((width, rows), F32)],
        ),
        out_shape=jax.ShapeDtypeStruct((rows, triple), BF),
        compiler_params=pltpu.CompilerParams(dimension_semantics=("arbitrary",), vmem_limit_bytes=40 << 20),
        cost_estimate=SMALL_COST,
        name="attend_backward",
    )(place, low, qkv, grad_out, mixed, lse, qkv, qkv, first)


def local(
    inputs,
    teacher,
    segment_ids,
    summary_start,
    valid_mask,
    attn_norm_gain,
    attn_norm_bias,
    query_weight,
    query_bias,
    key_weight,
    value_weight,
    value_bias,
    out_weight,
    out_bias,
    mlp_norm_gain,
    mlp_norm_bias,
    up_weight,
    up_bias,
    down_weight,
    down_bias,
):
    seqs, length = segment_ids.shape
    width = inputs.shape[-1]
    hidden_units = up_weight.shape[1]
    n, groups = lax.axis_size("seq"), lax.axis_size("dp")
    place, group = lax.axis_index("seq"), lax.axis_index("dp")
    both = ("dp", "seq")
    seq_len = length * n
    tokens_all = seqs * seq_len * groups
    scale = HD**-0.5
    own_rows = query_weight.shape[0]
    own_hidden = up_bias.shape[0]
    head_cols = width // n

    valid = valid_mask.astype(F32)
    small = [attn_norm_gain, attn_norm_bias, out_bias, mlp_norm_gain, mlp_norm_bias, down_bias, query_bias, value_bias, up_bias]
    sizes = [v.shape[0] for v in small]
    packed = jnp.concatenate([v.astype(F32) for v in small] + [segment_ids.astype(F32).reshape(-1), jnp.sum(valid).reshape(1)])
    packed = gather_small(packed)
    parts, at = [], 0
    for size in sizes:
        parts.append(packed[:, at : at + size])
        at += size
    gain_one, shift_one, b_out, gain_two, shift_two, b_down = [part.reshape(-1) for part in parts[:6]]
    b_query, b_value = [lax.dynamic_slice_in_dim(part.reshape(-1), place * head_cols, head_cols) for part in parts[6:8]]
    b_up = lax.dynamic_index_in_dim(parts[8].reshape(groups, n, -1), place, 1, keepdims=False).reshape(-1)
    ids = packed[:, at : at + seqs * length].reshape(groups, n, seqs, length)
    ids = lax.dynamic_index_in_dim(ids, group, 0, keepdims=False).transpose(1, 0, 2).reshape(seqs, seq_len)
    total_count = jnp.sum(packed[:, at + seqs * length])

    qkv_cut = jnp.concatenate(
        [w.reshape(own_rows, n, head_cols).transpose(1, 0, 2) for w in (query_weight, key_weight, value_weight)], axis=2
    )
    qkv_cut = trade(qkv_cut)
    w_qkv = lax.all_gather(qkv_cut.reshape(n * own_rows, 3 * head_cols), "dp", axis=0, tiled=True)
    gathered = [gather_rows(after(inputs[0], qkv_cut))]
    for b in range(1, seqs):
        own = after(inputs[b], packed, gathered[-1][0])
        gathered.append(gather_end(own, after_all(gather_start(own), w_qkv)))
    out_even, out_odd = gather_rows(lax.all_gather(out_weight, "dp", axis=0, tiled=True))
    w_out = natural_rows(jnp.concatenate([out_even, out_odd], axis=0).reshape(n, groups, own_rows, width))
    w_out = jnp.stack(w_out, axis=1).reshape(width, width)
    up_cut = up_weight.reshape(own_rows, groups, n, own_hidden).transpose(2, 0, 1, 3).reshape(n, own_rows, groups * own_hidden)
    up_cut = lax.all_to_all(up_cut, "seq", split_axis=0, concat_axis=0, tiled=True)
    w_up = lax.all_gather(up_cut.reshape(n * own_rows, groups * own_hidden), "dp", axis=0, tiled=True)
    w_down = lax.all_gather(down_weight, "dp", axis=0, tiled=True)
    b_qkv = jnp.concatenate([b_query, jnp.zeros_like(b_query), b_value])
    s_qkv = jnp.concatenate([jnp.full((head_cols,), scale, F32), jnp.ones((2 * head_cols,), F32)])

    place_arr = place.reshape(1).astype(jnp.int32)
    positions = jnp.arange(seq_len, dtype=jnp.int32)

    def out_of(value):
        return lax.all_to_all(value, "seq", split_axis=0, concat_axis=0, tiled=True)

    def add_all(terms):
        out = terms[0]
        for term in terms[1:]:
            out = out + term
        return out

    state = [types.SimpleNamespace() for _ in range(seqs)]

    def start(b):
        st = state[b]
        st.rows = inputs[b].astype(F32)
        st.normed, st.inverse = norm_core(st.rows)
        first = jnp.sum((ids[b][None, :] < ids[b][:, None]).astype(jnp.int32), axis=1)
        in_summary = (positions >= summary_start[b]) & (positions < summary_start[b] + NSUM)
        first = jnp.where(in_summary, 0, first)
        st.low = jnp.min(first.reshape(n, length), axis=1) // length
        st.first = first.reshape(seq_len, 1)
        st.even, st.odd = [
            (norm_core(part.astype(F32))[0] * gain_one + shift_one).astype(BF) for part in gathered[b]
        ]

    def project(b, *earlier):
        st = state[b]
        parts = [after(st.even, *earlier) if earlier else st.even, st.odd]
        st.qkv = jnp.concatenate([project_product(part, w_qkv, b_qkv, s_qkv) for part in parts], axis=0)

    def attend(b, *earlier):
        st = state[b]
        qkv = after(st.qkv, *earlier) if earlier else st.qkv
        st.mixed, st.lse = attend_forward(place_arr, st.low, qkv, st.first, length)

    def send_mixed(b, *earlier):
        st = state[b]
        mixed = after(st.mixed, *earlier) if earlier else st.mixed
        st.attended = out_of(mixed.reshape(n, length, head_cols)).transpose(1, 0, 2).reshape(length, width)

    def middle(b):
        st = state[b]
        st.hidden = st.rows + (dot(st.attended, w_out) + b_out)
        st.normed_two, st.inverse_two = norm_core(st.hidden)
        st.ready_two = (st.normed_two * gain_two + shift_two).astype(BF)
        st.came_two = gather_start(st.ready_two)

    def up(b, *earlier):
        st = state[b]
        st.even_two, st.odd_two = gather_end(st.ready_two, st.came_two)
        even, odd = after_all((st.even_two, st.odd_two), *earlier) if earlier else (st.even_two, st.odd_two)
        st.act_odd = up_product(odd, w_up, b_up)
        st.act_even = up_product(even, w_up, b_up)

    def down(b, *earlier):
        st = state[b]
        act_odd = after(st.act_odd, *earlier) if earlier else st.act_odd
        got = swap(plain_product(act_odd, w_down), 1)
        st.down_sums = block_products(st.act_even, w_down, got, n // 2)
        summed = scatter_rows(st.down_sums)
        st.result = st.hidden + (summed + b_down)
        misfit = st.result - teacher[b].astype(F32)
        st.local_sq = jnp.sum(jnp.sum(misfit * misfit, axis=-1) * valid[b])
        st.grad_result = misfit * (valid[b] * (tokens_all / total_count))[:, None]
        low_grad = st.grad_result.astype(BF)
        st.g_b_down = jnp.sum(low_grad.astype(F32), axis=0)
        st.gm_even, st.gm_odd = gather_rows(low_grad)

    def mlp_back(b, *earlier):
        st = state[b]
        gm_even, gm_odd = after_all((st.gm_even, st.gm_odd), *earlier) if earlier else (st.gm_even, st.gm_odd)
        st.pre_odd, sums_odd = masked_product(gm_odd, w_down, st.act_odd)
        got = swap(plain_product(st.pre_odd, w_up, turned=True), 1)
        st.pre_even, sums_even = masked_product(gm_even, w_down, st.act_even)
        st.up_sums = block_products(st.pre_even, w_up, got, n // 2, turned=True)
        st.grad_ready = scatter_rows(st.up_sums)
        st.g_b_up = jnp.sum(sums_even + sums_odd, axis=0)

    def branch_back(b, *earlier):
        st = state[b]
        grad_ready = after(st.grad_ready, *earlier) if earlier else st.grad_ready
        grad_norm, st.g_gain_two, st.g_shift_two = norm_back(grad_ready, st.normed_two, st.inverse_two, gain_two)
        st.grad_hidden = st.grad_result + grad_norm
        st.branch = st.grad_hidden.astype(BF)
        st.g_b_out = jnp.sum(st.branch.astype(F32), axis=0)
        st.grad_att = dot_nt(st.branch, w_out).astype(BF).reshape(length, n, head_cols).transpose(1, 0, 2)
        st.grad_mixed = out_of(st.grad_att).reshape(seq_len, head_cols)

    def attend_back(b, *earlier):
        st = state[b]
        grad_mixed = after(st.grad_mixed, *earlier) if earlier else st.grad_mixed
        st.grad_qkv = attend_backward(
            place_arr, st.low, st.qkv, grad_mixed, st.mixed, st.lse, st.first, length
        )
        st.g_b_qkv = jnp.sum(st.grad_qkv.astype(F32), axis=0)

    def project_back_odd(b, *earlier):
        st = state[b]
        odd = st.grad_qkv[seq_len // 2 :]
        odd = after(odd, *earlier) if earlier else odd
        st.odd_sum = plain_product(odd, w_qkv, turned=True)
        st.got = swap(st.odd_sum, 1)

    def project_back_even(b, *earlier):
        st = state[b]
        even = st.grad_qkv[: seq_len // 2]
        even = after(even, *earlier) if earlier else even
        st.even_sums = block_products(even, w_qkv, st.got, n // 2, turned=True)
        st.came_one = scatter_start(st.even_sums)
        st.grad_ready_one = scatter_end(st.even_sums, st.came_one)

    def finish(b):
        st = state[b]
        grad_norm, st.g_gain_one, st.g_shift_one = norm_back(
            st.grad_ready_one, st.normed, st.inverse, gain_one
        )
        st.grad_inputs = st.grad_hidden + grad_norm

    every = range(seqs)
    for b in every:
        start(b)
    project(0)
    attend(0)
    send_mixed(0)
    for b in range(1, seqs):
        project(b, state[b - 1].mixed)
        middle(b - 1)
        attend(b, state[b - 1].ready_two)
        send_mixed(b, *state[b - 1].came_two)
        up(b - 1)
    middle(seqs - 1)
    for b in range(seqs - 1):
        down(b, state[b + 1].ready_two)
        up(b + 1, *state[b].down_sums)
    down(seqs - 1)
    mlp_back(0)
    for b in range(1, seqs):
        mlp_back(b, *state[b - 1].up_sums)
    lefts = [part for st in state for part in (st.act_even, st.act_odd)]
    rights = [part for st in state for part in (st.gm_even, st.gm_odd)]
    lefts[0] = after(lefts[0], *state[-1].up_sums)
    g_w_down = weight_grad(lefts, rights, 256, 1024)
    g_down = lax.psum_scatter(g_w_down, "dp", scatter_dimension=0, tiled=True)
    lefts = [part for st in state for part in (st.even_two, st.odd_two)]
    rights = [part for st in state for part in (st.pre_even, st.pre_odd)]
    lefts[0] = after(lefts[0], g_w_down)
    g_w_up = weight_grad(lefts, rights, 512, 1024)
    g_up = lax.psum_scatter(g_w_up, "dp", scatter_dimension=0, tiled=True)
    for b in every:
        branch_back(b, g_w_down, g_w_up)

    turned = [
        st.attended.reshape(length, groups, n, own_rows).transpose(2, 0, 1, 3).reshape(n, length, groups * own_rows)
        for st in state
    ]

    def out_block(k):
        return add_all(
            [dot_tn(lax.dynamic_index_in_dim(t, place ^ k, 0, keepdims=False), st.branch) for t, st in zip(turned, state)]
        )

    out_odd = jnp.concatenate([out_block(k).astype(BF) for k in range(1, n, 2)], axis=0)
    out_got = swap(out_odd, 1)
    out_rows = groups * own_rows
    attend_back(0, out_odd, *[st.grad_att for st in state])
    project_back_odd(0)
    out_got = after(out_got, state[0].odd_sum)
    out_even = [out_block(2 * m) + out_got[m * out_rows : (m + 1) * out_rows].astype(F32) for m in range(n // 2)]
    project_back_even(0, *out_even)
    g_out = scatter_groups(scatter_rows(out_even))
    for b in range(1, seqs):
        attend_back(b, *state[b - 1].even_sums)
        project_back_odd(b, *state[b - 1].came_one)
    half = seq_len // 2
    lefts = [part for st in state for part in (st.even, st.odd)]
    rights = [part for st in state for part in (st.grad_qkv[:half], st.grad_qkv[half:])]
    g_w_qkv = weight_grad(lefts, rights, 1024, 768)
    g_qkv = lax.psum_scatter(g_w_qkv, "dp", scatter_dimension=0, tiled=True)
    for b in range(1, seqs):
        project_back_even(b, g_w_qkv)
    for b in every:
        finish(b)

    def summed(name):
        return add_all([getattr(st, name) for st in state])

    g_down = after(g_down, g_w_qkv).astype(F32)
    g_up = out_of(after(g_up, g_w_qkv).reshape(n, own_rows, groups * own_hidden))
    g_up = g_up.reshape(n, own_rows, groups, own_hidden).transpose(1, 2, 0, 3).reshape(own_rows, hidden_units).astype(F32)
    g_qkv = out_of(g_qkv.reshape(n, own_rows, 3 * head_cols))
    g_qkv = g_qkv.reshape(n, own_rows, 3, head_cols).transpose(2, 1, 0, 3).reshape(3, own_rows, width).astype(F32)

    g_b_qkv = summed("g_b_qkv").reshape(3, head_cols)
    own_bias = jnp.zeros((2, width), F32)
    own_bias = lax.dynamic_update_slice(own_bias, jnp.stack([g_b_qkv[0], g_b_qkv[2]]), (0, place * head_cols))
    g_b_up = summed("g_b_up").reshape(groups, 1, own_hidden)
    spread_up = lax.dynamic_update_slice_in_dim(jnp.zeros((groups, n, own_hidden), F32), g_b_up, place, 1)
    names = ("g_gain_one", "g_shift_one", "g_b_out", "g_gain_two", "g_shift_two", "g_b_down")
    vectors = jnp.concatenate([jnp.stack([summed(name) for name in names]), own_bias], axis=0)
    count = vectors.shape[0]
    vectors = vectors.reshape(count, groups * n, own_rows).transpose(1, 0, 2).reshape(groups * n, count * own_rows)
    sq = jnp.broadcast_to(summed("local_sq"), (groups * n, 1))
    tail = jnp.concatenate([vectors, spread_up.reshape(groups * n, own_hidden), sq], axis=1)
    tail = scatter_small(tail)
    vectors = tail[: count * own_rows].reshape(count, own_rows)
    g_b_query, g_b_value, g_b_up = vectors[6], vectors[7], tail[count * own_rows : -1]
    mean_loss = tail[-1] / (total_count * width)
    return (
        jnp.stack([st.result.astype(BF) for st in state]),
        mean_loss,
        jnp.stack([st.grad_inputs for st in state]),
        vectors[0],
        vectors[1],
        g_qkv[0],
        g_b_query,
        g_qkv[1],
        g_qkv[2],
        g_b_value,
        g_out,
        vectors[2],
        vectors[3],
        vectors[4],
        g_up,
        g_b_up,
        g_down,
        vectors[5],
    )


def solution(mesh):
    rows3, rows2, flat, mat = P("dp", "seq", None), P("dp", "seq"), P(("dp", "seq")), P(("dp", "seq"), None)
    placed = (
        rows3, rows3, rows2, P("dp"), rows2, flat, flat, mat, flat, mat, mat, flat, mat, flat, flat, flat, mat, flat, mat, flat,
    )
    out = (rows3, P(), rows3, flat, flat, mat, flat, mat, mat, flat, mat, flat, flat, flat, mat, flat, mat, flat)
    return jax.shard_map(local, mesh=mesh, in_specs=placed, out_specs=out, check_vma=False)
```

```python
import functools
import types

import jax
import jax.numpy as jnp
from jax import lax
from jax.experimental import pallas as pl
from jax.experimental.pallas import tpu as pltpu
from jax.sharding import PartitionSpec as P

HD = 64
NSUM = 50
NORM_EPS = 1e-05
NEG_FILL = -1e30
BF = jnp.bfloat16
F32 = jnp.float32


def dot(left_in, right_in):
    return jnp.dot(left_in, right_in, preferred_element_type=F32)


def dot_tn(left_in, right_in):
    return lax.dot_general(left_in, right_in, (((0,), (0,)), ((), ())), preferred_element_type=F32)


def dot_nt(left_in, right_in):
    return lax.dot_general(left_in, right_in, (((1,), (1,)), ((), ())), preferred_element_type=F32)


def norm_core(values):
    center = values - jnp.mean(values, axis=-1, keepdims=True)
    inverse = lax.rsqrt(jnp.mean(center * center, axis=-1, keepdims=True) + NORM_EPS)
    return center * inverse, inverse


def norm_back(grad_out, normed, inverse, gain_in):
    grad_normed = grad_out * gain_in
    inner_one = jnp.mean(grad_normed, axis=-1, keepdims=True)
    inner_two = jnp.mean(grad_normed * normed, axis=-1, keepdims=True)
    grad_in = inverse * (grad_normed - inner_one - normed * inner_two)
    return grad_in, jnp.sum(grad_out * normed, axis=0), jnp.sum(grad_out, axis=0)


def swap(values, mask):
    n = lax.axis_size("seq")
    return lax.ppermute(values, "seq", [(i, i ^ mask) for i in range(n)])


def gather_start(own):
    return (swap(own, 2), swap(own, 4)) if lax.axis_size("seq") == 8 else ()


def gather_relay(own, came):
    if lax.axis_size("seq") != 8:
        return ()
    half = own.shape[0] // 2
    return swap(came[1][:half], 2), swap(came[0][half:], 4)


def gather_join(own, came, relayed):
    if lax.axis_size("seq") == 8:
        return jnp.concatenate([own, *came, *relayed], axis=0)
    same, step = own, 2
    while step < lax.axis_size("seq"):
        same = jnp.concatenate([same, swap(same, step)], axis=0)
        step *= 2
    return same


def gather_rows(own):
    came = gather_start(own)
    same = gather_join(own, came, gather_relay(own, came))
    return same, swap(same, 1)


def scatter_start(blocks):
    if lax.axis_size("seq") != 8:
        return ()
    six = blocks[3].astype(BF)
    half = six.shape[0] // 2
    return swap(six[:half], 2), swap(six[half:], 4)


def scatter_relay(blocks, came):
    if lax.axis_size("seq") != 8:
        return ()
    _, two, four, _ = blocks
    half = two.shape[0] // 2
    to_four, to_two = came
    four = jnp.concatenate([four[:half] + to_four.astype(F32), four[half:]], axis=0).astype(BF)
    two = jnp.concatenate([two[:half], two[half:] + to_two.astype(F32)], axis=0).astype(BF)
    return swap(two, 2), swap(four, 4)


def scatter_join(blocks, relayed):
    n = lax.axis_size("seq")
    if n == 8:
        return blocks[0] + relayed[0].astype(F32) + relayed[1].astype(F32)
    step = n // 2
    while step > 1:
        keep = len(blocks) // 2
        sent = [swap(block.astype(BF), step).astype(F32) for block in blocks[keep:]]
        blocks = [block.astype(F32) + got for block, got in zip(blocks[:keep], sent)]
        step //= 2
    return blocks[0]


def scatter_groups(rows):
    bit, index = lax.axis_size("dp") // 2, lax.axis_index("dp")
    while bit > 0:
        half = rows.shape[0] // 2
        upper = (index & bit) != 0
        sent = jnp.where(upper, rows[:half], rows[half:]).astype(BF)
        rows = jnp.where(upper, rows[half:], rows[:half]) + exchange(sent, "dp", bit).astype(F32)
        bit //= 2
    return rows


def exchange(values, axis, bit):
    size = lax.axis_size(axis)
    return lax.ppermute(values, axis, [(i, i ^ bit) for i in range(size)])


def gather_small(vector):
    length = -(-vector.shape[0] // 1024) * 1024
    held = jnp.pad(vector, (0, length - vector.shape[0])).reshape(1, 8, length // 8)
    for axis in ("dp", "seq"):
        bit, index = 1, lax.axis_index(axis)
        while bit < lax.axis_size(axis):
            other = exchange(held, axis, bit)
            upper = (index & bit) != 0
            held = jnp.concatenate([jnp.where(upper, other, held), jnp.where(upper, held, other)], axis=0)
            bit *= 2
    held = held.reshape(lax.axis_size("seq"), lax.axis_size("dp"), length).transpose(1, 0, 2)
    return held.reshape(-1, length)[:, : vector.shape[0]]


def gather_groups(rows):
    bit, index = 1, lax.axis_index("dp")
    held = rows[None]
    while bit < lax.axis_size("dp"):
        other = exchange(held, "dp", bit)
        upper = (index & bit) != 0
        held = jnp.concatenate([jnp.where(upper, other, held), jnp.where(upper, held, other)], axis=0)
        bit *= 2
    return held.reshape(-1, rows.shape[1])


def scatter_small(table):
    count, width = table.shape
    length = -(-width // 1024) * 1024
    held = jnp.pad(table, ((0, 0), (0, length - width))).reshape(count, 8, length // 8)
    for axis in ("dp", "seq"):
        bit, index = lax.axis_size(axis) // 2, lax.axis_index(axis)
        while bit > 0:
            half = held.shape[0] // 2
            upper = (index & bit) != 0
            sent = jnp.where(upper, held[:half], held[half:])
            held = jnp.where(upper, held[half:], held[:half]) + exchange(sent, axis, bit)
            bit //= 2
    return held.reshape(length)[:width]


def after(value, *earlier):
    return lax.optimization_barrier((value, *earlier))[0]


class Order:
    def __init__(self):
        self.last = ()

    def tie(self, value):
        if not jax.tree.leaves(value) or not jax.tree.leaves(self.last):
            return value
        return lax.optimization_barrier((value, self.last))[0]

    def mark(self, value):
        if jax.tree.leaves(value):
            self.last = value
        return value

    def pause(self, value):
        return self.mark(self.tie(value))


def weight_grad_kernel(*refs):
    count = (len(refs) - 1) // 2
    total = dot_tn(refs[0][...], refs[count][...])
    for part in range(1, count):
        total = total + dot_tn(refs[part][...], refs[count + part][...])
    refs[-1][...] = total.astype(BF)


def weight_grad(lefts, rights, left_tile, right_tile):
    rows, left_width = lefts[0].shape
    right_width = rights[0].shape[1]
    left_tile, right_tile = min(left_tile, left_width), min(right_tile, right_width)
    count = len(lefts)
    return pl.pallas_call(
        weight_grad_kernel,
        grid=(right_width // right_tile, left_width // left_tile),
        in_specs=[pl.BlockSpec((rows, left_tile), lambda j, i: (0, i))] * count
        + [pl.BlockSpec((rows, right_tile), lambda j, i: (0, j))] * count,
        out_specs=pl.BlockSpec((left_tile, right_tile), lambda j, i: (i, j)),
        out_shape=jax.ShapeDtypeStruct((left_width, right_width), BF),
        compiler_params=pltpu.CompilerParams(dimension_semantics=("arbitrary", "arbitrary"), vmem_limit_bytes=48 << 20),
        cost_estimate=light_cost(2 * count * rows * left_width * right_width),
        name="weight_grad",
    )(*lefts, *rights)


def tile_dot(left, right, turned):
    return dot_nt(left, right) if turned else dot(left, right)


def plain_kernel(left_ref, right_ref, out_ref, *, turned):
    out_ref[...] = tile_dot(left_ref[...], right_ref[...], turned).astype(out_ref.dtype)


def project_kernel(left_ref, right_ref, bias_ref, scale_ref, out_ref):
    out_ref[...] = ((dot(left_ref[...], right_ref[...]) + bias_ref[...]) * scale_ref[...]).astype(BF)


def up_kernel(left_ref, right_ref, bias_ref, out_ref):
    out_ref[...] = jnp.maximum(dot(left_ref[...], right_ref[...]) + bias_ref[...], 0.0).astype(BF)


def masked_kernel(left_ref, right_ref, act_ref, out_ref, sums_ref):
    grad = jnp.where(act_ref[...] > 0, dot_nt(left_ref[...], right_ref[...]), 0.0).astype(BF)
    out_ref[...] = grad
    part = jnp.sum(grad.astype(F32).reshape(-1, 8, grad.shape[1]), axis=0)

    @pl.when(pl.program_id(1) == 0)
    def _():
        sums_ref[...] = part

    @pl.when(pl.program_id(1) > 0)
    def _():
        sums_ref[...] = sums_ref[...] + part


def blocks_kernel(left_ref, right_ref, got_ref, *out_refs, turned):
    count = len(out_refs)
    total = tile_dot(left_ref[...], right_ref[...], turned) + got_ref[...].astype(F32)
    for m in range(count):

        @pl.when(pl.program_id(1) == count - 1 - m)
        def _(m=m):
            out_refs[m][...] = total.astype(out_refs[m].dtype)


def light_cost(flops):
    return pl.CostEstimate(flops=int(flops) // 8, bytes_accessed=1, transcendentals=0)


def tiled(kernel, name, left, right, turned, extras, outs, row_tile, col_tile, row_of=lambda m: m):
    rows, depth = left.shape
    cols = right.shape[0] if turned else right.shape[1]
    row_tile, col_tile = min(row_tile, rows), min(col_tile, cols)
    kinds = {
        "both": pl.BlockSpec((row_tile, col_tile), lambda j, m: (row_of(m), j)),
        "vector": pl.BlockSpec((1, col_tile), lambda j, m: (0, j)),
        "sums": pl.BlockSpec((8, col_tile), lambda j, m: (0, j)),
        "block": pl.BlockSpec((row_tile, col_tile), lambda j, m: (0, j)),
    }
    shapes = {"both": (rows, cols), "sums": (8, cols), "block": (row_tile, cols)}
    right_spec = (
        pl.BlockSpec((col_tile, depth), lambda j, m: (j, 0)) if turned else pl.BlockSpec((depth, col_tile), lambda j, m: (0, j))
    )
    return pl.pallas_call(
        kernel,
        grid=(cols // col_tile, rows // row_tile),
        in_specs=[pl.BlockSpec((row_tile, depth), lambda j, m: (row_of(m), 0)), right_spec] + [kinds[k] for k, _ in extras],
        out_specs=[kinds[k] for k, _ in outs],
        out_shape=[jax.ShapeDtypeStruct(shapes[k], dtype) for k, dtype in outs],
        compiler_params=pltpu.CompilerParams(dimension_semantics=("arbitrary", "arbitrary"), vmem_limit_bytes=40 << 20),
        cost_estimate=light_cost(2 * rows * cols * depth),
        name=name,
    )(left, right, *[value for _, value in extras])


def plain_product(left, right, turned=False):
    kernel = functools.partial(plain_kernel, turned=turned)
    return tiled(kernel, "product", left, right, turned, [], [("both", BF)], 256, 1024)[0]


def project_product(left, right, bias, scale):
    extras = [("vector", bias.reshape(1, -1)), ("vector", scale.reshape(1, -1))]
    return tiled(project_kernel, "project", left, right, False, extras, [("both", BF)], 256, 768)[0]


def up_product(left, right, bias):
    return tiled(up_kernel, "up", left, right, False, [("vector", bias.reshape(1, -1))], [("both", BF)], 256, 512)[0]


def masked_product(left, right, act):
    outs = [("both", BF), ("sums", F32)]
    return tiled(masked_kernel, "masked_product", left, right, True, [("both", act)], outs, 256, 512)


def block_products(left, right, got, count, turned=False):
    kernel = functools.partial(blocks_kernel, turned=turned)
    outs = [("block", F32)] * (count - 1) + [("block", BF)]
    return tiled(
        kernel, "block_products", left, right, turned, [("both", got)], outs, left.shape[0] // count, 1024, lambda m: count - 1 - m
    )


def visible_scores(q_head, k_block, first, q_place, key_start, length):
    scores = dot_nt(q_head, k_block)
    k_place = key_start + lax.broadcasted_iota(jnp.int32, (1, length), 1)
    allowed = (k_place >= first) & (k_place <= q_place)
    return jnp.where(allowed, scores, NEG_FILL)


def storage_row(block, place, blocks, length):
    k = block ^ place
    return pl.multiple_of(((k >> 1) + (k & 1) * (blocks // 2)) * length, length)


def fold(values, op):
    out = values[:, :128]
    for start in range(128, values.shape[1], 128):
        out = op(out, values[:, start : start + 128])
    return out


def attend_forward_kernel(
    place_ref, low_ref, q_ref, k_ref, v_ref, first_ref, o_ref, lse_ref, s_scr, m_scr, l_scr, *, heads, length, blocks
):
    i = pl.program_id(0)
    place = place_ref[0]
    low = low_ref[i]
    width = heads * HD
    lanes = lax.broadcasted_iota(jnp.int32, (length, width), 1) // HD
    q_all = q_ref[...]
    q_heads = [jnp.where(lanes == h, q_all, jnp.zeros_like(q_all)) for h in range(heads)]
    first = first_ref[...]
    q_place = i * length + lax.broadcasted_iota(jnp.int32, (length, 1), 0)
    m_scr[...] = jnp.full_like(m_scr, NEG_FILL)
    l_scr[...] = jnp.zeros_like(l_scr)

    def score_step(j, carry):
        k_block = k_ref[pl.ds(storage_row(j, place, blocks, length), length), :]
        cols = pl.ds(pl.multiple_of(j * length, length), length)
        for h in range(heads):
            scores = visible_scores(q_heads[h], k_block, first, q_place, j * length, length)
            s_scr[h, :, cols] = scores
            m_scr[h] = jnp.maximum(m_scr[h], fold(scores, jnp.maximum))
        return carry

    lax.fori_loop(low, i + 1, score_step, 0)
    tops = [jnp.max(m_scr[h], axis=-1, keepdims=True) for h in range(heads)]

    def exp_step(j, carry):
        cols = pl.ds(pl.multiple_of(j * length, length), length)
        for h in range(heads):
            raised = jnp.exp(s_scr[h, :, cols] - tops[h])
            s_scr[h, :, cols] = raised
            l_scr[h] = l_scr[h] + fold(raised, jnp.add)
        return carry

    lax.fori_loop(low, i + 1, exp_step, 0)
    totals = [jnp.sum(l_scr[h], axis=-1, keepdims=True) for h in range(heads)]
    scales = [1.0 / total for total in totals]

    def mix_step(j, acc):
        v_block = v_ref[pl.ds(storage_row(j, place, blocks, length), length), :]
        cols = pl.ds(pl.multiple_of(j * length, length), length)
        for h in range(heads):
            probs = (s_scr[h, :, cols] * scales[h]).astype(BF)
            acc = acc + jnp.where(lanes == h, dot(probs, v_block), 0.0)
        return acc

    mixed = lax.fori_loop(low, i + 1, mix_step, jnp.zeros((length, width), F32))
    o_ref[...] = mixed.astype(BF)
    cols = lax.broadcasted_iota(jnp.int32, (length, 128), 1)
    lse = jnp.zeros((length, 128), F32)
    for h in range(heads):
        lse = jnp.where(cols == h, tops[h] + jnp.log(totals[h]), lse)
    lse_ref[...] = lse


def attend_backward_kernel(
    place_ref, low_ref, q_ref, go_ref, o_ref, lse_ref, k_ref, v_ref, first_ref, grad_ref, kt_scr, vt_scr, *, heads, length, blocks
):
    i = pl.program_id(0)
    place = place_ref[0]
    low = low_ref[i]
    width = heads * HD
    lanes = lax.broadcasted_iota(jnp.int32, (length, width), 1) // HD
    first = first_ref[...]
    q_place = i * length + lax.broadcasted_iota(jnp.int32, (length, 1), 0)
    q_all, go_all = q_ref[...], go_ref[...]
    inner_all = go_all.astype(F32) * o_ref[...].astype(F32)
    q_turned, go_turned = q_all.astype(F32).T.astype(BF), go_all.astype(F32).T.astype(BF)
    lse_all = lse_ref[...]
    q_heads, go_heads, inner, lse = [], [], [], []
    for h in range(heads):
        mine = lanes == h
        q_heads.append(jnp.where(mine, q_all, jnp.zeros_like(q_all)))
        go_heads.append(jnp.where(mine, go_all, jnp.zeros_like(go_all)))
        inner.append(jnp.sum(jnp.where(mine, inner_all, 0.0), axis=-1, keepdims=True))
        lse.append(lse_all[:, h : h + 1])

    @pl.when(i == 0)
    def _():
        kt_scr[...] = jnp.zeros_like(kt_scr)
        vt_scr[...] = jnp.zeros_like(vt_scr)

    def step(j, acc):
        rows = pl.ds(storage_row(j, place, blocks, length), length)
        k_block, v_block = k_ref[rows, :], v_ref[rows, :]
        for h in range(heads):
            scores = visible_scores(q_heads[h], k_block, first, q_place, j * length, length)
            probs = jnp.exp(scores - lse[h])
            grad_probs = dot_nt(go_heads[h], v_block)
            grad_scores = (probs * (grad_probs - inner[h])).astype(BF)
            part = slice(h * HD, (h + 1) * HD)
            vt_scr[part, rows] = vt_scr[part, rows] + dot(go_turned[part, :], probs.astype(BF))
            kt_scr[part, rows] = kt_scr[part, rows] + dot(q_turned[part, :], grad_scores)
            acc = acc + jnp.where(lanes == h, dot(grad_scores, k_block), 0.0)
        return acc

    grad_q = lax.fori_loop(low, i + 1, step, jnp.zeros((length, width), F32))
    own_rows = pl.ds(storage_row(i, place, blocks, length), length)
    grad_ref[own_rows, 0:width] = (grad_q.astype(BF).astype(F32) * (HD**-0.5)).astype(BF)

    @pl.when(i == blocks - 1)
    def _():
        for j in range(blocks):
            rows = slice(j * length, (j + 1) * length)
            grad_ref[rows, width : 2 * width] = kt_scr[:, rows].T.astype(BF)
            grad_ref[rows, 2 * width : 3 * width] = vt_scr[:, rows].T.astype(BF)


def storage_map(length, blocks, column):
    def index(i, place_ref, low_ref):
        k = i ^ place_ref[0]
        return ((k >> 1) + (k & 1) * (blocks // 2), column)

    return index


def attend_forward(place, low, qkv, first, length):
    rows, triple = qkv.shape
    width, blocks = triple // 3, rows // length
    heads = width // HD
    return pl.pallas_call(
        functools.partial(attend_forward_kernel, heads=heads, length=length, blocks=blocks),
        grid_spec=pltpu.PrefetchScalarGridSpec(
            num_scalar_prefetch=2,
            grid=(blocks,),
            in_specs=[
                pl.BlockSpec((length, width), storage_map(length, blocks, 0)),
                pl.BlockSpec((rows, width), lambda i, p, w: (0, 1)),
                pl.BlockSpec((rows, width), lambda i, p, w: (0, 2)),
                pl.BlockSpec((length, 1), lambda i, p, w: (i, 0)),
            ],
            out_specs=[
                pl.BlockSpec((length, width), lambda i, p, w: (i, 0)),
                pl.BlockSpec((length, 128), lambda i, p, w: (i, 0)),
            ],
            scratch_shapes=[
                pltpu.VMEM((heads, length, rows), F32),
                pltpu.VMEM((heads, length, 128), F32),
                pltpu.VMEM((heads, length, 128), F32),
            ],
        ),
        out_shape=[jax.ShapeDtypeStruct((rows, width), BF), jax.ShapeDtypeStruct((rows, 128), F32)],
        compiler_params=pltpu.CompilerParams(dimension_semantics=("arbitrary",), vmem_limit_bytes=40 << 20),
        cost_estimate=light_cost(24 * rows * rows * width),
        name="attend_forward",
    )(place, low, qkv, qkv, qkv, first)


def attend_backward(place, low, qkv, grad_out, mixed, lse, first, length):
    rows, triple = qkv.shape
    width, blocks = triple // 3, rows // length
    heads = width // HD
    return pl.pallas_call(
        functools.partial(attend_backward_kernel, heads=heads, length=length, blocks=blocks),
        grid_spec=pltpu.PrefetchScalarGridSpec(
            num_scalar_prefetch=2,
            grid=(blocks,),
            in_specs=[
                pl.BlockSpec((length, width), storage_map(length, blocks, 0)),
                pl.BlockSpec((length, width), lambda i, p, w: (i, 0)),
                pl.BlockSpec((length, width), lambda i, p, w: (i, 0)),
                pl.BlockSpec((length, 128), lambda i, p, w: (i, 0)),
                pl.BlockSpec((rows, width), lambda i, p, w: (0, 1)),
                pl.BlockSpec((rows, width), lambda i, p, w: (0, 2)),
                pl.BlockSpec((length, 1), lambda i, p, w: (i, 0)),
            ],
            out_specs=pl.BlockSpec((rows, triple), lambda i, p, w: (0, 0)),
            scratch_shapes=[pltpu.VMEM((width, rows), F32), pltpu.VMEM((width, rows), F32)],
        ),
        out_shape=jax.ShapeDtypeStruct((rows, triple), BF),
        compiler_params=pltpu.CompilerParams(dimension_semantics=("arbitrary",), vmem_limit_bytes=40 << 20),
        cost_estimate=light_cost(36 * rows * rows * width),
        name="attend_backward",
    )(place, low, qkv, grad_out, mixed, lse, qkv, qkv, first)


def local(
    inputs,
    teacher,
    segment_ids,
    summary_start,
    valid_mask,
    attn_norm_gain,
    attn_norm_bias,
    query_weight,
    query_bias,
    key_weight,
    value_weight,
    value_bias,
    out_weight,
    out_bias,
    mlp_norm_gain,
    mlp_norm_bias,
    up_weight,
    up_bias,
    down_weight,
    down_bias,
):
    seqs, length = segment_ids.shape
    width = inputs.shape[-1]
    hidden_units = up_weight.shape[1]
    n, groups = lax.axis_size("seq"), lax.axis_size("dp")
    place, group = lax.axis_index("seq"), lax.axis_index("dp")
    both = ("dp", "seq")
    seq_len = length * n
    tokens_all = seqs * seq_len * groups
    scale = HD**-0.5
    own_rows = query_weight.shape[0]
    own_hidden = up_bias.shape[0]
    head_cols = width // n

    valid = valid_mask.astype(F32)
    small = [attn_norm_gain, attn_norm_bias, out_bias, mlp_norm_gain, mlp_norm_bias, down_bias, query_bias, value_bias, up_bias]
    sizes = [v.shape[0] for v in small]
    packed = jnp.concatenate([v.astype(F32) for v in small] + [segment_ids.astype(F32).reshape(-1), jnp.sum(valid).reshape(1)])
    packed = gather_small(packed)
    parts, at = [], 0
    for size in sizes:
        parts.append(packed[:, at : at + size])
        at += size
    gain_one, shift_one, b_out, gain_two, shift_two, b_down = [part.reshape(-1) for part in parts[:6]]
    b_query, b_value = [lax.dynamic_slice_in_dim(part.reshape(-1), place * head_cols, head_cols) for part in parts[6:8]]
    b_up = lax.dynamic_index_in_dim(parts[8].reshape(groups, n, -1), place, 1, keepdims=False).reshape(-1)
    ids = packed[:, at : at + seqs * length].reshape(groups, n, seqs, length)
    ids = lax.dynamic_index_in_dim(ids, group, 0, keepdims=False).transpose(1, 0, 2).reshape(seqs, seq_len)
    total_count = jnp.sum(packed[:, at + seqs * length])

    def out_of(value):
        return lax.all_to_all(value, "seq", split_axis=0, concat_axis=0, tiled=True)

    qkv_cut = jnp.concatenate(
        [w.reshape(own_rows, n, head_cols).transpose(1, 0, 2) for w in (query_weight, key_weight, value_weight)], axis=2
    )
    up_cut = up_weight.reshape(own_rows, groups, n, own_hidden).transpose(2, 0, 1, 3).reshape(n, own_rows, groups * own_hidden)
    b_qkv = jnp.concatenate([b_query, jnp.zeros_like(b_query), b_value])
    s_qkv = jnp.concatenate([jnp.full((head_cols,), scale, F32), jnp.ones((2 * head_cols,), F32)])

    place_arr = place.reshape(1).astype(jnp.int32)
    positions = jnp.arange(seq_len, dtype=jnp.int32)

    def add_all(terms):
        out = terms[0]
        for term in terms[1:]:
            out = out + term
        return out

    state = [types.SimpleNamespace() for _ in range(seqs)]

    order = Order()

    def spans(b):
        st = state[b]
        first = jnp.sum((ids[b][None, :] < ids[b][:, None]).astype(jnp.int32), axis=1)
        in_summary = (positions >= summary_start[b]) & (positions < summary_start[b] + NSUM)
        first = jnp.where(in_summary, 0, first)
        st.low = jnp.min(first.reshape(n, length), axis=1) // length
        st.first = first.reshape(seq_len, 1)

    def ready(rows):
        return (norm_core(rows.astype(F32))[0] * gain_one + shift_one).astype(BF)

    def project(b):
        st = state[b]
        even, odd = order.tie((st.even, st.odd))
        parts = [project_product(part, w_qkv, b_qkv, s_qkv) for part in (even, odd)]
        st.qkv = order.mark(jnp.concatenate(parts, axis=0))

    def attend(b):
        st = state[b]
        qkv = order.tie(st.qkv)
        st.mixed, st.lse = attend_forward(place_arr, st.low, qkv, st.first, length)
        order.mark(st.mixed)

    def send_mixed(b):
        st = state[b]
        st.moved = out_of(st.mixed.reshape(n, length, head_cols))

    def middle(b):
        st = state[b]
        attended = order.tie(st.moved)
        st.attended = attended.transpose(1, 0, 2).reshape(length, width)
        rows = inputs[b].astype(F32)
        st.hidden = rows + (dot(st.attended, w_out) + b_out)
        st.normed_two, st.inverse_two = norm_core(st.hidden)
        st.own_two = order.mark((st.normed_two * gain_two + shift_two).astype(BF))
        st.came_two = gather_start(st.own_two)

    def up_even(b):
        st = state[b]
        st.act_even = order.mark(up_product(order.tie(st.even_two), w_up, b_up))

    def up_odd(b):
        st = state[b]
        st.act_odd = order.mark(up_product(order.tie(st.odd_two), w_up, b_up))

    def relay(b, own, came):
        st = state[b]
        came = order.pause(getattr(st, came))
        return came, gather_relay(getattr(st, own), came)

    def join(b, own, came_relayed):
        same = order.mark(gather_join(getattr(state[b], own), *order.tie(came_relayed)))
        return same, swap(same, 1)

    def down_odd(b):
        st = state[b]
        st.down_got = swap(order.mark(plain_product(order.tie(st.act_odd), w_down)), 1)

    def down_even(b):
        st = state[b]
        st.down_sums = order.mark(block_products(st.act_even, w_down, order.tie(st.down_got), n // 2))
        st.down_came = scatter_start(st.down_sums)

    def pass_on(b, sums, came):
        st = state[b]
        came = order.pause(getattr(st, came))
        return scatter_relay(getattr(st, sums), came)

    def misfit(b):
        st = state[b]
        summed = scatter_join(st.down_sums, order.tie(st.down_sent))
        st.result = st.hidden + (summed + b_down)
        error = st.result - teacher[b].astype(F32)
        st.local_sq = jnp.sum(jnp.sum(error * error, axis=-1) * valid[b])
        st.grad_result = error * (valid[b] * (tokens_all / total_count))[:, None]
        st.own_grad = order.mark(st.grad_result.astype(BF))
        st.g_b_down = jnp.sum(st.own_grad.astype(F32), axis=0)
        st.came_grad = gather_start(st.own_grad)

    def act_back_even(b):
        st = state[b]
        st.pre_even, st.sums_even = masked_product(order.tie(st.gm_even), w_down, st.act_even)
        order.mark(st.pre_even)

    def act_back_odd(b):
        st = state[b]
        st.pre_odd, st.sums_odd = masked_product(order.tie(st.gm_odd), w_down, st.act_odd)
        order.mark(st.pre_odd)

    def up_back_odd(b):
        st = state[b]
        st.up_got = swap(order.mark(plain_product(order.tie(st.pre_odd), w_up, turned=True)), 1)

    def up_back_even(b):
        st = state[b]
        st.up_sums = order.mark(block_products(st.pre_even, w_up, order.tie(st.up_got), n // 2, turned=True))
        st.up_came = scatter_start(st.up_sums)

    def branch_back(b):
        st = state[b]
        grad_ready = scatter_join(st.up_sums, order.tie(st.up_sent))
        grad_norm, st.g_gain_two, st.g_shift_two = norm_back(grad_ready, st.normed_two, st.inverse_two, gain_two)
        st.grad_hidden = st.grad_result + grad_norm
        st.branch = st.grad_hidden.astype(BF)
        st.g_b_out = jnp.sum(st.branch.astype(F32), axis=0)
        grad_att = dot_nt(st.branch, w_out).astype(BF).reshape(length, n, head_cols).transpose(1, 0, 2)
        st.grad_mixed = out_of(order.mark(grad_att)).reshape(seq_len, head_cols)

    def attend_back(b):
        st = state[b]
        st.grad_qkv = attend_backward(
            place_arr, st.low, st.qkv, order.tie(st.grad_mixed), st.mixed, st.lse, st.first, length
        )
        order.mark(st.grad_qkv)
        st.g_b_qkv = jnp.sum(st.grad_qkv.astype(F32), axis=0)

    def project_back_odd(b):
        st = state[b]
        odd = order.tie(st.grad_qkv)[seq_len // 2 :]
        st.one_got = swap(order.mark(plain_product(odd, w_qkv, turned=True)), 1)

    def project_back_even(b):
        st = state[b]
        st.one_sums = block_products(st.grad_qkv[: seq_len // 2], w_qkv, order.tie(st.one_got), n // 2, turned=True)
        order.mark(st.one_sums)
        st.one_came = scatter_start(st.one_sums)

    def finish(b):
        st = state[b]
        grad_ready = scatter_join(st.one_sums, order.tie(st.one_sent))
        normed, inverse = norm_core(inputs[b].astype(F32))
        grad_norm, st.g_gain_one, st.g_shift_one = norm_back(grad_ready, normed, inverse, gain_one)
        st.grad_inputs = order.mark(st.grad_hidden + grad_norm)

    every, later = range(seqs), range(1, seqs)

    def whole_out_weight(own, came, relayed):
        whole = jnp.zeros((groups, n, own_rows, width), BF)
        half = groups // 2
        same = [(0, own, 0), (2, came[0], 0), (4, came[1], 0), (6, relayed[0], 0), (6, relayed[1], half)]
        other = [(k + 1, swap(piece, 1), first) for k, piece, first in same]
        for k, piece, first in same + other:
            whole = lax.dynamic_update_slice(whole, piece.reshape(-1, 1, own_rows, width), (first, place ^ k, 0, 0))
        return whole.reshape(width, width)

    def zero_after(value):
        return jnp.minimum(jnp.abs(value[0, 0].astype(F32)), 0.0).astype(jnp.int32)

    for b in every:
        spans(b)
    st = state[0]
    st.own = inputs[0]
    st.came = gather_start(st.own)
    qkv_cut = order.pause(out_of(qkv_cut))
    w_qkv = lax.all_gather(qkv_cut.reshape(n * own_rows, 3 * head_cols), "dp", axis=0, tiled=True)
    st = state[0]
    came_relayed = relay(0, "own", "came")
    for b in later:
        state[b].own = lax.dynamic_index_in_dim(inputs, b + zero_after(came_relayed[0][0] if n == 8 else packed), 0, keepdims=False)
        state[b].came = gather_start(state[b].own)
    up_cut = order.pause(out_of(after(up_cut, qkv_cut)))
    raw_even, raw_odd = join(0, "own", came_relayed)
    st.even, st.odd = ready(raw_even), ready(raw_odd)
    if n == 8:
        own_out = order.pause(gather_groups(out_weight))
        out_came = gather_start(own_out)
    else:
        w_out = lax.all_gather(after(out_weight, up_cut), both, axis=0, tiled=True)
    w_up = lax.all_gather(up_cut.reshape(n * own_rows, groups * own_hidden), "dp", axis=0, tiled=True)
    w_down = lax.all_gather(after(down_weight, up_cut), "dp", axis=0, tiled=True)
    w_qkv = order.pause(w_qkv)
    came_relayed = [relay(b, "own", "came") for b in later]
    project(0)
    for b in later:
        st = state[b]
        raw_even, raw_odd = join(b, "own", came_relayed[b - 1])
        st.even, st.odd = ready(raw_even), ready(raw_odd)
    if n == 8:
        out_came = order.pause(out_came)
        out_relayed = gather_relay(own_out, out_came)
    attend(0)
    if n == 8:
        w_out = whole_out_weight(own_out, out_came, order.pause(out_relayed))
    send_mixed(0)
    for b in later:
        project(b)
    middle(0)
    for b in later:
        last, st = state[b - 1], state[b]
        attend(b)
        came_relayed = relay(b - 1, "own_two", "came_two")
        send_mixed(b)
        last.even_two, last.odd_two = join(b - 1, "own_two", came_relayed)
        up_even(b - 1)
        middle(b)
        up_odd(b - 1)
        came_relayed = relay(b, "own_two", "came_two")
        down_odd(b - 1)
        st.even_two, st.odd_two = join(b, "own_two", came_relayed)
        up_even(b)
        down_even(b - 1)
        up_odd(b)
        last.down_sent = pass_on(b - 1, "down_sums", "down_came")
        down_odd(b)
        down_even(b)
        misfit(b - 1)
        st.down_sent = pass_on(b, "down_sums", "down_came")
        came_relayed = relay(b - 1, "own_grad", "came_grad")
        misfit(b)
        last.gm_even, last.gm_odd = join(b - 1, "own_grad", came_relayed)
        act_back_even(b - 1)
        act_back_odd(b - 1)
        up_back_odd(b - 1)
        came_relayed = relay(b, "own_grad", "came_grad")
        up_back_even(b - 1)
        st.gm_even, st.gm_odd = join(b, "own_grad", came_relayed)
        act_back_even(b)
        last.up_sent = pass_on(b - 1, "up_sums", "up_came")
        act_back_odd(b)
        up_back_odd(b)
        up_back_even(b)
    lefts = [part for st in state for part in (st.even_two, st.odd_two)]
    rights = [part for st in state for part in (st.pre_even, st.pre_odd)]
    g_w_up = order.mark(weight_grad(order.tie(lefts), rights, 512, 1024))
    g_up = lax.psum_scatter(g_w_up, "dp", scatter_dimension=0, tiled=True)
    for b in later:
        state[b].up_sent = pass_on(b, "up_sums", "up_came")
    branch_back(0)
    lefts = [part for st in state for part in (st.act_even, st.act_odd)]
    rights = [part for st in state for part in (st.gm_even, st.gm_odd)]
    g_w_down = order.mark(weight_grad(order.tie(lefts), rights, 256, 1024))
    g_down = lax.psum_scatter(g_w_down, "dp", scatter_dimension=0, tiled=True)
    for b in later:
        branch_back(b)
    turned = [
        st.attended.reshape(length, groups, n, own_rows).transpose(2, 0, 1, 3).reshape(n, length, groups * own_rows)
        for st in state
    ]

    def out_block(k):
        return add_all(
            [dot_tn(lax.dynamic_index_in_dim(t, place ^ k, 0, keepdims=False), st.branch) for t, st in zip(turned, state)]
        )

    out_rows = groups * own_rows
    attend_back(0)
    project_back_odd(0)
    turned = order.tie(turned)
    out_odd = order.mark(jnp.concatenate([out_block(k).astype(BF) for k in range(1, n, 2)], axis=0))
    out_got = swap(out_odd, 1)
    project_back_even(0)
    for b in later:
        attend_back(b)
        state[b - 1].one_sent = pass_on(b - 1, "one_sums", "one_came")
        project_back_odd(b)
    half = seq_len // 2
    lefts = [part for st in state for part in (st.even, st.odd)]
    rights = [part for st in state for part in (st.grad_qkv[:half], st.grad_qkv[half:])]
    g_w_qkv = order.mark(weight_grad(order.tie(lefts), rights, 1024, 768))
    g_qkv = lax.psum_scatter(g_w_qkv, "dp", scatter_dimension=0, tiled=True)
    for b in later:
        order.pause(state[b - 1].one_sent)
        project_back_even(b)
    out_got = order.tie(out_got)
    out_sums = [out_block(2 * m) + out_got[m * out_rows : (m + 1) * out_rows].astype(F32) for m in range(n // 2)]
    order.mark(out_sums)
    out_came = scatter_start(out_sums)
    for b in later:
        state[b].one_sent = pass_on(b, "one_sums", "one_came")
        finish(b - 1)
    out_sent = scatter_relay(out_sums, order.pause(out_came))
    for b in later:
        finish(b)
    g_out = scatter_groups(scatter_join(out_sums, order.tie(out_sent)))

    def summed(name):
        return add_all([after(getattr(st, name), g_w_qkv) for st in state])

    g_down = after(g_down, g_w_qkv).astype(F32)
    g_up = out_of(after(g_up, g_w_qkv).reshape(n, own_rows, groups * own_hidden))
    g_up = g_up.reshape(n, own_rows, groups, own_hidden).transpose(1, 2, 0, 3).reshape(own_rows, hidden_units).astype(F32)
    g_qkv = out_of(g_qkv.reshape(n, own_rows, 3 * head_cols))
    g_qkv = g_qkv.reshape(n, own_rows, 3, head_cols).transpose(2, 1, 0, 3).reshape(3, own_rows, width).astype(F32)

    g_b_qkv = summed("g_b_qkv").reshape(3, head_cols)
    own_bias = jnp.zeros((2, width), F32)
    own_bias = lax.dynamic_update_slice(own_bias, jnp.stack([g_b_qkv[0], g_b_qkv[2]]), (0, place * head_cols))
    g_b_up = jnp.sum(summed("sums_even") + summed("sums_odd"), axis=0).reshape(groups, 1, own_hidden)
    spread_up = lax.dynamic_update_slice_in_dim(jnp.zeros((groups, n, own_hidden), F32), g_b_up, place, 1)
    names = ("g_gain_one", "g_shift_one", "g_b_out", "g_gain_two", "g_shift_two", "g_b_down")
    vectors = jnp.concatenate([jnp.stack([summed(name) for name in names]), own_bias], axis=0)
    count = vectors.shape[0]
    vectors = vectors.reshape(count, groups * n, own_rows).transpose(1, 0, 2).reshape(groups * n, count * own_rows)
    sq = jnp.broadcast_to(summed("local_sq"), (groups * n, 1))
    tail = jnp.concatenate([vectors, spread_up.reshape(groups * n, own_hidden), sq], axis=1)
    tail = scatter_small(tail)
    vectors = tail[: count * own_rows].reshape(count, own_rows)
    g_b_query, g_b_value, g_b_up = vectors[6], vectors[7], tail[count * own_rows : -1]
    mean_loss = tail[-1] / (total_count * width)
    return (
        jnp.stack([st.result.astype(BF) for st in state]),
        mean_loss,
        jnp.stack([st.grad_inputs for st in state]),
        vectors[0],
        vectors[1],
        g_qkv[0],
        g_b_query,
        g_qkv[1],
        g_qkv[2],
        g_b_value,
        g_out,
        vectors[2],
        vectors[3],
        vectors[4],
        g_up,
        g_b_up,
        g_down,
        vectors[5],
    )


def solution(mesh):
    rows3, rows2, flat, mat = P("dp", "seq", None), P("dp", "seq"), P(("dp", "seq")), P(("dp", "seq"), None)
    placed = (
        rows3, rows3, rows2, P("dp"), rows2, flat, flat, mat, flat, mat, mat, flat, mat, flat, flat, flat, mat, flat, mat, flat,
    )
    out = (rows3, P(), rows3, flat, flat, mat, flat, mat, mat, flat, mat, flat, flat, flat, mat, flat, mat, flat)
    return jax.shard_map(local, mesh=mesh, in_specs=placed, out_specs=out, check_vma=False)
```

```python
import functools
import types

import jax
import jax.numpy as jnp
from jax import lax
from jax.experimental import pallas as pl
from jax.experimental.pallas import tpu as pltpu
from jax.sharding import PartitionSpec as P

HD = 64
NSUM = 50
NORM_EPS = 1e-05
NEG_FILL = -1e30
VMEM_GRANT = 30 << 20
BF = jnp.bfloat16
F32 = jnp.float32


def dot(left_in, right_in):
    return jnp.dot(left_in, right_in, preferred_element_type=F32)


def dot_tn(left_in, right_in):
    return lax.dot_general(left_in, right_in, (((0,), (0,)), ((), ())), preferred_element_type=F32)


def dot_nt(left_in, right_in):
    return lax.dot_general(left_in, right_in, (((1,), (1,)), ((), ())), preferred_element_type=F32)


def norm_core(values):
    center = values - jnp.mean(values, axis=-1, keepdims=True)
    inverse = lax.rsqrt(jnp.mean(center * center, axis=-1, keepdims=True) + NORM_EPS)
    return center * inverse, inverse


def norm_back(grad_out, normed, inverse, gain_in):
    grad_normed = grad_out * gain_in
    inner_one = jnp.mean(grad_normed, axis=-1, keepdims=True)
    inner_two = jnp.mean(grad_normed * normed, axis=-1, keepdims=True)
    grad_in = inverse * (grad_normed - inner_one - normed * inner_two)
    return grad_in, jnp.sum(grad_out * normed, axis=0), jnp.sum(grad_out, axis=0)


def swap(values, mask):
    n = lax.axis_size("seq")
    return lax.ppermute(values, "seq", [(i, i ^ mask) for i in range(n)])


def gather_start(own):
    return (swap(own, 2), swap(own, 4)) if lax.axis_size("seq") == 8 else ()


def gather_relay(own, came):
    if lax.axis_size("seq") != 8:
        return ()
    half = own.shape[0] // 2
    return swap(came[1][:half], 2), swap(came[0][half:], 4)


def gather_join(own, came, relayed):
    if lax.axis_size("seq") == 8:
        return jnp.concatenate([own, *came, *relayed], axis=0)
    same, step = own, 2
    while step < lax.axis_size("seq"):
        same = jnp.concatenate([same, swap(same, step)], axis=0)
        step *= 2
    return same


def gather_rows(own):
    came = gather_start(own)
    same = gather_join(own, came, gather_relay(own, came))
    return same, swap(same, 1)


def scatter_start(blocks):
    if lax.axis_size("seq") != 8:
        return ()
    six = blocks[3].astype(BF)
    half = six.shape[0] // 2
    return swap(six[:half], 2), swap(six[half:], 4)


def scatter_relay(blocks, came):
    if lax.axis_size("seq") != 8:
        return ()
    _, two, four, _ = blocks
    half, width = two.shape[0] // 2, two.shape[1]
    which = lax.broadcasted_iota(jnp.int32, (2, half, width), 0)

    def with_half(block, part, side):
        part = jnp.where(which == side, part.astype(F32)[None], 0.0)
        return (block.reshape(2, half, width) + part).astype(BF).reshape(2 * half, width)

    return swap(with_half(two, came[1], 1), 2), swap(with_half(four, came[0], 0), 4)


def scatter_join(blocks, relayed):
    n = lax.axis_size("seq")
    if n == 8:
        return blocks[0] + relayed[0].astype(F32) + relayed[1].astype(F32)
    step = n // 2
    while step > 1:
        keep = len(blocks) // 2
        sent = [swap(block.astype(BF), step).astype(F32) for block in blocks[keep:]]
        blocks = [block.astype(F32) + got for block, got in zip(blocks[:keep], sent)]
        step //= 2
    return blocks[0]


def scatter_groups(rows):
    bit, index = lax.axis_size("dp") // 2, lax.axis_index("dp")
    while bit > 0:
        half = rows.shape[0] // 2
        upper = (index & bit) != 0
        sent = jnp.where(upper, rows[:half], rows[half:]).astype(BF)
        rows = jnp.where(upper, rows[half:], rows[:half]) + exchange(sent, "dp", bit).astype(F32)
        bit //= 2
    return rows


def exchange(values, axis, bit):
    size = lax.axis_size(axis)
    return lax.ppermute(values, axis, [(i, i ^ bit) for i in range(size)])


class Order:
    def __init__(self):
        self.last = ()

    def tie(self, value):
        if not jax.tree.leaves(value) or not jax.tree.leaves(self.last):
            return value
        return lax.optimization_barrier((value, self.last))[0]

    def mark(self, value):
        if jax.tree.leaves(value):
            self.last = value
        return value

    def pause(self, value):
        return self.mark(self.tie(value))


def doubling(held, axes):
    for axis in axes:
        bit, index = 1, lax.axis_index(axis)
        while bit < lax.axis_size(axis):
            other = yield exchange(held, axis, bit)
            upper = (index & bit) != 0
            held = jnp.concatenate([jnp.where(upper, other, held), jnp.where(upper, held, other)], axis=0)
            bit *= 2
    return held


class Steps:
    def __init__(self, order, generator):
        self.order, self.generator, self.flight, self.result = order, generator, next(generator), None

    def step(self, count=1):
        for _ in range(count):
            if self.flight is None:
                return
            try:
                self.flight = self.generator.send(self.order.pause(self.flight))
            except StopIteration as stop:
                self.flight, self.result = None, stop.value

    def finish(self):
        while self.flight is not None:
            self.step()
        return self.result


def scatter_small(table):
    count, width = table.shape
    length = -(-width // 1024) * 1024
    held = jnp.pad(table, ((0, 0), (0, length - width))).reshape(count, 8, length // 8)
    for axis in ("dp", "seq"):
        bit, index = lax.axis_size(axis) // 2, lax.axis_index(axis)
        while bit > 0:
            half = held.shape[0] // 2
            upper = (index & bit) != 0
            sent = jnp.where(upper, held[:half], held[half:])
            held = jnp.where(upper, held[half:], held[:half]) + exchange(sent, axis, bit)
            bit //= 2
    return held.reshape(length)[:width]


def after(value, *earlier):
    return lax.optimization_barrier((value, *earlier))[0]


def weight_grad_kernel(*refs):
    count = (len(refs) - 1) // 2
    total = dot_tn(refs[0][...], refs[count][...])
    for part in range(1, count):
        total = total + dot_tn(refs[part][...], refs[count + part][...])
    refs[-1][...] = total.astype(BF)


def weight_grad(lefts, rights, left_tile, right_tile):
    rows, left_width = lefts[0].shape
    right_width = rights[0].shape[1]
    left_tile, right_tile = min(left_tile, left_width), min(right_tile, right_width)
    count = len(lefts)
    return pl.pallas_call(
        weight_grad_kernel,
        grid=(right_width // right_tile, left_width // left_tile),
        in_specs=[pl.BlockSpec((rows, left_tile), lambda j, i: (0, i))] * count
        + [pl.BlockSpec((rows, right_tile), lambda j, i: (0, j))] * count,
        out_specs=pl.BlockSpec((left_tile, right_tile), lambda j, i: (i, j)),
        out_shape=jax.ShapeDtypeStruct((left_width, right_width), BF),
        compiler_params=pltpu.CompilerParams(dimension_semantics=("arbitrary", "arbitrary"), vmem_limit_bytes=VMEM_GRANT),
        cost_estimate=light_cost(2 * count * rows * left_width * right_width),
        name="weight_grad",
    )(*lefts, *rights)


def tile_dot(left, right, turned):
    return dot_nt(left, right) if turned else dot(left, right)


def plain_kernel(left_ref, right_ref, out_ref, *, turned):
    out_ref[...] = tile_dot(left_ref[...], right_ref[...], turned).astype(out_ref.dtype)


def project_kernel(left_ref, right_ref, bias_ref, scale_ref, out_ref):
    out_ref[...] = ((dot(left_ref[...], right_ref[...]) + bias_ref[...]) * scale_ref[...]).astype(BF)


def up_kernel(left_ref, right_ref, bias_ref, out_ref):
    out_ref[...] = jnp.maximum(dot(left_ref[...], right_ref[...]) + bias_ref[...], 0.0).astype(BF)


def masked_kernel(left_ref, right_ref, act_ref, out_ref, sums_ref):
    grad = jnp.where(act_ref[...] > 0, dot_nt(left_ref[...], right_ref[...]), 0.0).astype(BF)
    out_ref[...] = grad
    part = jnp.sum(grad.astype(F32).reshape(-1, 8, grad.shape[1]), axis=0)

    @pl.when(pl.program_id(1) == 0)
    def _():
        sums_ref[...] = part

    @pl.when(pl.program_id(1) > 0)
    def _():
        sums_ref[...] = sums_ref[...] + part


def blocks_kernel(left_ref, right_ref, got_ref, *out_refs, turned):
    rows = out_refs[0].shape[0]
    for m in range(len(out_refs) - 1, -1, -1):
        cut = slice(m * rows, (m + 1) * rows)
        total = tile_dot(left_ref[cut, :], right_ref[...], turned) + got_ref[cut, :].astype(F32)
        out_refs[m][...] = total.astype(out_refs[m].dtype)


def light_cost(flops):
    return pl.CostEstimate(flops=int(flops) // 8, bytes_accessed=1, transcendentals=0)


def tiled(kernel, name, left, right, turned, extras, outs, row_tile, col_tile, parts=1):
    rows, depth = left.shape
    cols = right.shape[0] if turned else right.shape[1]
    row_tile, col_tile = min(row_tile, rows), min(col_tile, cols)
    kinds = {
        "both": pl.BlockSpec((row_tile, col_tile), lambda j, m: (m, j)),
        "vector": pl.BlockSpec((1, col_tile), lambda j, m: (0, j)),
        "sums": pl.BlockSpec((8, col_tile), lambda j, m: (0, j)),
        "block": pl.BlockSpec((rows // parts, col_tile), lambda j, m: (0, j)),
    }
    shapes = {"both": (rows, cols), "sums": (8, cols), "block": (rows // parts, cols)}
    right_spec = (
        pl.BlockSpec((col_tile, depth), lambda j, m: (j, 0)) if turned else pl.BlockSpec((depth, col_tile), lambda j, m: (0, j))
    )
    return pl.pallas_call(
        kernel,
        grid=(cols // col_tile, rows // row_tile),
        in_specs=[pl.BlockSpec((row_tile, depth), lambda j, m: (m, 0)), right_spec] + [kinds[k] for k, _ in extras],
        out_specs=[kinds[k] for k, _ in outs],
        out_shape=[jax.ShapeDtypeStruct(shapes[k], dtype) for k, dtype in outs],
        compiler_params=pltpu.CompilerParams(dimension_semantics=("arbitrary", "arbitrary"), vmem_limit_bytes=VMEM_GRANT),
        cost_estimate=light_cost(2 * rows * cols * depth),
        name=name,
    )(left, right, *[value for _, value in extras])


def plain_product(left, right, turned=False):
    kernel = functools.partial(plain_kernel, turned=turned)
    return tiled(kernel, "product", left, right, turned, [], [("both", BF)], 1024, 256)[0]


def project_product(left, right, bias, scale):
    extras = [("vector", bias.reshape(1, -1)), ("vector", scale.reshape(1, -1))]
    return tiled(project_kernel, "project", left, right, False, extras, [("both", BF)], 1024, 256)[0]


def up_product(left, right, bias):
    return tiled(up_kernel, "up", left, right, False, [("vector", bias.reshape(1, -1))], [("both", BF)], 1024, 256)[0]


def masked_product(left, right, act):
    outs = [("both", BF), ("sums", F32)]
    return tiled(masked_kernel, "masked_product", left, right, True, [("both", act)], outs, 1024, 256)


def block_products(left, right, got, count, turned=False):
    kernel = functools.partial(blocks_kernel, turned=turned)
    outs = [("block", F32)] * (count - 1) + [("block", BF)]
    return tiled(
        kernel, "block_products", left, right, turned, [("both", got)], outs, left.shape[0], 256, count
    )


def visible_scores(q_head, k_block, first, q_place, key_start, length):
    scores = dot_nt(q_head, k_block)
    k_place = key_start + lax.broadcasted_iota(jnp.int32, (1, length), 1)
    allowed = (k_place >= first) & (k_place <= q_place)
    return jnp.where(allowed, scores, NEG_FILL)


def storage_row(block, place, blocks, length):
    k = block ^ place
    return pl.multiple_of(((k >> 1) + (k & 1) * (blocks // 2)) * length, length)


def spread_heads(source_ref, target_ref, lanes, heads, length, blocks):
    def one(m, carry):
        rows = source_ref[pl.ds(pl.multiple_of(m * length, length), length), :]
        for h in range(heads):
            target = pl.ds(pl.multiple_of((m * heads + h) * length, length), length)
            target_ref[target, :] = jnp.where(lanes == h, rows, jnp.zeros_like(rows))
        return carry

    lax.fori_loop(0, blocks, one, 0)


def fold(values, op):
    out = values[:, :128]
    for start in range(128, values.shape[1], 128):
        out = op(out, values[:, start : start + 128])
    return out


def attend_forward_kernel(
    place_ref, low_ref, q_ref, k_ref, v_ref, first_ref, o_ref, lse_ref, s_scr, m_scr, l_scr, v_scr, *, heads, length, blocks
):
    i = pl.program_id(0)
    place = place_ref[0]
    low = low_ref[i]
    width = heads * HD
    lanes = lax.broadcasted_iota(jnp.int32, (length, width), 1) // HD
    q_all = q_ref[...]
    q_heads = [jnp.where(lanes == h, q_all, jnp.zeros_like(q_all)) for h in range(heads)]
    first = first_ref[...]
    q_place = i * length + lax.broadcasted_iota(jnp.int32, (length, 1), 0)
    m_scr[...] = jnp.full_like(m_scr, NEG_FILL)
    l_scr[...] = jnp.zeros_like(l_scr)

    @pl.when(i == 0)
    def _():
        spread_heads(v_ref, v_scr, lanes, heads, length, blocks)

    def score_step(j, carry):
        k_block = k_ref[pl.ds(storage_row(j, place, blocks, length), length), :]
        cols = pl.ds(pl.multiple_of(j * length, length), length)
        for h in range(heads):
            scores = visible_scores(q_heads[h], k_block, first, q_place, j * length, length)
            s_scr[h, :, cols] = scores
            m_scr[h] = jnp.maximum(m_scr[h], fold(scores, jnp.maximum))
        return carry

    lax.fori_loop(low, i + 1, score_step, 0)
    tops = [jnp.max(m_scr[h], axis=-1, keepdims=True) for h in range(heads)]

    def exp_step(j, carry):
        cols = pl.ds(pl.multiple_of(j * length, length), length)
        for h in range(heads):
            raised = jnp.exp(s_scr[h, :, cols] - tops[h])
            s_scr[h, :, cols] = raised
            l_scr[h] = l_scr[h] + fold(raised, jnp.add)
        return carry

    lax.fori_loop(low, i + 1, exp_step, 0)
    totals = [jnp.sum(l_scr[h], axis=-1, keepdims=True) for h in range(heads)]
    scales = [1.0 / total for total in totals]

    def mix_step(j, acc):
        rows = pl.ds(pl.multiple_of(storage_row(j, place, blocks, length) * heads, heads * length), heads * length)
        cols = pl.ds(pl.multiple_of(j * length, length), length)
        probs = [(s_scr[h, :, cols] * scales[h]).astype(BF) for h in range(heads)]
        return acc + dot(jnp.concatenate(probs, axis=1), v_scr[rows, :])

    mixed = lax.fori_loop(low, i + 1, mix_step, jnp.zeros((length, width), F32))
    o_ref[...] = mixed.astype(BF)
    cols = lax.broadcasted_iota(jnp.int32, (length, 128), 1)
    lse = jnp.zeros((length, 128), F32)
    for h in range(heads):
        lse = jnp.where(cols == h, tops[h] + jnp.log(totals[h]), lse)
    lse_ref[...] = lse


def attend_backward_kernel(
    place_ref, low_ref, q_ref, go_ref, o_ref, lse_ref, k_ref, v_ref, first_ref, grad_ref, kt_scr, vt_scr, k_scr, *, heads, length,
    blocks
):
    i = pl.program_id(0)
    place = place_ref[0]
    low = low_ref[i]
    width = heads * HD
    lanes = lax.broadcasted_iota(jnp.int32, (length, width), 1) // HD
    first = first_ref[...]
    q_place = i * length + lax.broadcasted_iota(jnp.int32, (length, 1), 0)
    q_all, go_all = q_ref[...], go_ref[...]
    inner_all = go_all.astype(F32) * o_ref[...].astype(F32)
    q_turned, go_turned = q_all.astype(F32).T.astype(BF), go_all.astype(F32).T.astype(BF)
    lse_all = lse_ref[...]
    q_heads, go_heads, inner, lse = [], [], [], []
    for h in range(heads):
        mine = lanes == h
        q_heads.append(jnp.where(mine, q_all, jnp.zeros_like(q_all)))
        go_heads.append(jnp.where(mine, go_all, jnp.zeros_like(go_all)))
        inner.append(jnp.sum(jnp.where(mine, inner_all, 0.0), axis=-1, keepdims=True))
        lse.append(lse_all[:, h : h + 1])

    @pl.when(i == 0)
    def _():
        kt_scr[...] = jnp.zeros_like(kt_scr)
        vt_scr[...] = jnp.zeros_like(vt_scr)
        spread_heads(k_ref, k_scr, lanes, heads, length, blocks)

    def step(j, acc):
        start = storage_row(j, place, blocks, length)
        rows = pl.ds(start, length)
        k_block, v_block = k_ref[rows, :], v_ref[rows, :]
        k_place = j * length + lax.broadcasted_iota(jnp.int32, (1, length), 1)
        allowed = (k_place >= first) & (k_place <= q_place)
        every = range(heads)
        scores = [dot_nt(q_heads[h], k_block) for h in every]
        grad_probs = [dot_nt(go_heads[h], v_block) for h in every]
        probs = [jnp.exp(jnp.where(allowed, scores[h] - lse[h], NEG_FILL)) for h in every]
        grad_scores = [(probs[h] * (grad_probs[h] - inner[h])).astype(BF) for h in every]
        for h in every:
            part = slice(h * HD, (h + 1) * HD)
            vt_scr[part, rows] = vt_scr[part, rows] + dot(go_turned[part, :], probs[h].astype(BF))
            kt_scr[part, rows] = kt_scr[part, rows] + dot(q_turned[part, :], grad_scores[h])
        spread = pl.ds(pl.multiple_of(start * heads, heads * length), heads * length)
        return acc + dot(jnp.concatenate(grad_scores, axis=1), k_scr[spread, :])

    grad_q = lax.fori_loop(low, i + 1, step, jnp.zeros((length, width), F32))
    own_rows = pl.ds(storage_row(i, place, blocks, length), length)
    grad_ref[own_rows, 0:width] = (grad_q.astype(BF).astype(F32) * (HD**-0.5)).astype(BF)

    @pl.when(i == blocks - 1)
    def _():
        for j in range(blocks):
            rows = slice(j * length, (j + 1) * length)
            grad_ref[rows, width : 2 * width] = kt_scr[:, rows].T.astype(BF)
            grad_ref[rows, 2 * width : 3 * width] = vt_scr[:, rows].T.astype(BF)


def storage_map(length, blocks, column):
    def index(i, place_ref, low_ref):
        k = i ^ place_ref[0]
        return ((k >> 1) + (k & 1) * (blocks // 2), column)

    return index


def attend_forward(place, low, qkv, first, length):
    rows, triple = qkv.shape
    width, blocks = triple // 3, rows // length
    heads = width // HD
    return pl.pallas_call(
        functools.partial(attend_forward_kernel, heads=heads, length=length, blocks=blocks),
        grid_spec=pltpu.PrefetchScalarGridSpec(
            num_scalar_prefetch=2,
            grid=(blocks,),
            in_specs=[
                pl.BlockSpec((length, width), storage_map(length, blocks, 0)),
                pl.BlockSpec((rows, width), lambda i, p, w: (0, 1)),
                pl.BlockSpec((rows, width), lambda i, p, w: (0, 2)),
                pl.BlockSpec((length, 1), lambda i, p, w: (i, 0)),
            ],
            out_specs=[
                pl.BlockSpec((length, width), lambda i, p, w: (i, 0)),
                pl.BlockSpec((length, 128), lambda i, p, w: (i, 0)),
            ],
            scratch_shapes=[
                pltpu.VMEM((heads, length, rows), F32),
                pltpu.VMEM((heads, length, 128), F32),
                pltpu.VMEM((heads, length, 128), F32),
                pltpu.VMEM((heads * rows, width), BF),
            ],
        ),
        out_shape=[jax.ShapeDtypeStruct((rows, width), BF), jax.ShapeDtypeStruct((rows, 128), F32)],
        compiler_params=pltpu.CompilerParams(dimension_semantics=("arbitrary",), vmem_limit_bytes=VMEM_GRANT),
        cost_estimate=light_cost(24 * rows * rows * width),
        name="attend_forward",
    )(place, low, qkv, qkv, qkv, first)


def attend_backward(place, low, qkv, grad_out, mixed, lse, first, length):
    rows, triple = qkv.shape
    width, blocks = triple // 3, rows // length
    heads = width // HD
    return pl.pallas_call(
        functools.partial(attend_backward_kernel, heads=heads, length=length, blocks=blocks),
        grid_spec=pltpu.PrefetchScalarGridSpec(
            num_scalar_prefetch=2,
            grid=(blocks,),
            in_specs=[
                pl.BlockSpec((length, width), storage_map(length, blocks, 0)),
                pl.BlockSpec((length, width), lambda i, p, w: (i, 0)),
                pl.BlockSpec((length, width), lambda i, p, w: (i, 0)),
                pl.BlockSpec((length, 128), lambda i, p, w: (i, 0)),
                pl.BlockSpec((rows, width), lambda i, p, w: (0, 1)),
                pl.BlockSpec((rows, width), lambda i, p, w: (0, 2)),
                pl.BlockSpec((length, 1), lambda i, p, w: (i, 0)),
            ],
            out_specs=pl.BlockSpec((rows, triple), lambda i, p, w: (0, 0)),
            scratch_shapes=[
                pltpu.VMEM((width, rows), F32),
                pltpu.VMEM((width, rows), F32),
                pltpu.VMEM((heads * rows, width), BF),
            ],
        ),
        out_shape=jax.ShapeDtypeStruct((rows, triple), BF),
        compiler_params=pltpu.CompilerParams(dimension_semantics=("arbitrary",), vmem_limit_bytes=VMEM_GRANT),
        cost_estimate=light_cost(36 * rows * rows * width),
        name="attend_backward",
    )(place, low, qkv, grad_out, mixed, lse, qkv, qkv, first)


def local(
    inputs,
    teacher,
    segment_ids,
    summary_start,
    valid_mask,
    attn_norm_gain,
    attn_norm_bias,
    query_weight,
    query_bias,
    key_weight,
    value_weight,
    value_bias,
    out_weight,
    out_bias,
    mlp_norm_gain,
    mlp_norm_bias,
    up_weight,
    up_bias,
    down_weight,
    down_bias,
):
    seqs, length = segment_ids.shape
    width = inputs.shape[-1]
    hidden_units = up_weight.shape[1]
    n, groups = lax.axis_size("seq"), lax.axis_size("dp")
    place, group = lax.axis_index("seq"), lax.axis_index("dp")
    both = ("dp", "seq")
    seq_len = length * n
    tokens_all = seqs * seq_len * groups
    scale = HD**-0.5
    own_rows = query_weight.shape[0]
    own_hidden = up_bias.shape[0]
    head_cols = width // n

    def out_of(value):
        return lax.all_to_all(value, "seq", split_axis=0, concat_axis=0, tiled=True)

    valid = valid_mask.astype(F32)
    small = [attn_norm_gain, attn_norm_bias, out_bias, mlp_norm_gain, mlp_norm_bias, down_bias, query_bias, value_bias, up_bias]
    sizes = [v.shape[0] for v in small]
    packed = jnp.concatenate([v.astype(F32) for v in small] + [segment_ids.astype(F32).reshape(-1), jnp.sum(valid).reshape(1)])
    packed_length = packed.shape[0]
    padded = -(-packed_length // 1024) * 1024
    packed = jnp.pad(packed, (0, padded - packed_length)).reshape(1, 8, padded // 8)
    order = Order()
    out_steps = Steps(order, doubling(out_weight[None], ("dp",))) if n == 8 else None
    cut = jnp.concatenate(
        [w.reshape(own_rows, n, head_cols).transpose(1, 0, 2) for w in (query_weight, key_weight, value_weight)], axis=2
    )
    qkv_cut = out_of(cut)
    small_steps = Steps(order, doubling(after(packed, cut), ("dp", "seq")))
    if n == 8:
        out_steps.step()
    small_steps.step(3)
    qkv_cut = order.pause(qkv_cut)
    w_qkv = lax.all_gather(qkv_cut.reshape(n * own_rows, 3 * head_cols), "dp", axis=0, tiled=True)

    def zero_after(value):
        return jnp.minimum(jnp.abs(value.reshape(-1)[0].astype(F32)), 0.0).astype(jnp.int32)

    def rows_after(b, value):
        return lax.dynamic_index_in_dim(inputs, b + zero_after(value), 0, keepdims=False)

    state = [types.SimpleNamespace() for _ in range(seqs)]
    state[0].own = rows_after(0, qkv_cut)
    state[0].came = gather_start(state[0].own)
    packed = small_steps.finish().reshape(n, groups, padded).transpose(1, 0, 2).reshape(groups * n, padded)
    if n == 8:
        own_out = out_steps.finish().reshape(-1, width)
    parts, at = [], 0
    for size in sizes:
        parts.append(packed[:, at : at + size])
        at += size
    gain_one, shift_one, b_out, gain_two, shift_two, b_down = [part.reshape(-1) for part in parts[:6]]
    b_query, b_value = [lax.dynamic_slice_in_dim(part.reshape(-1), place * head_cols, head_cols) for part in parts[6:8]]
    b_up = lax.dynamic_index_in_dim(parts[8].reshape(groups, n, -1), place, 1, keepdims=False).reshape(-1)
    ids = packed[:, at : at + seqs * length].reshape(groups, n, seqs, length)
    ids = lax.dynamic_index_in_dim(ids, group, 0, keepdims=False).transpose(1, 0, 2).reshape(seqs, seq_len)
    total_count = jnp.sum(packed[:, at + seqs * length])

    up_cut = up_weight.reshape(own_rows, groups, n, own_hidden).transpose(2, 0, 1, 3).reshape(n, own_rows, groups * own_hidden)
    b_qkv = jnp.concatenate([b_query, jnp.zeros_like(b_query), b_value])
    s_qkv = jnp.concatenate([jnp.full((head_cols,), scale, F32), jnp.ones((2 * head_cols,), F32)])

    place_arr = place.reshape(1).astype(jnp.int32)
    positions = jnp.arange(seq_len, dtype=jnp.int32)

    def add_all(terms):
        out = terms[0]
        for term in terms[1:]:
            out = out + term
        return out


    def spans(b):
        st = state[b]
        first = jnp.sum((ids[b][None, :] < ids[b][:, None]).astype(jnp.int32), axis=1)
        in_summary = (positions >= summary_start[b]) & (positions < summary_start[b] + NSUM)
        first = jnp.where(in_summary, 0, first)
        st.low = jnp.min(first.reshape(n, length), axis=1) // length
        st.first = first.reshape(seq_len, 1)

    def ready(rows):
        return (norm_core(rows.astype(F32))[0] * gain_one + shift_one).astype(BF)

    def project(b):
        st = state[b]
        even, odd = order.tie((st.even, st.odd))
        parts = [project_product(part, w_qkv, b_qkv, s_qkv) for part in (even, odd)]
        st.qkv = order.mark(jnp.concatenate(parts, axis=0))

    def attend(b):
        st = state[b]
        qkv = order.tie(st.qkv)
        st.mixed, st.lse = attend_forward(place_arr, st.low, qkv, st.first, length)
        order.mark(st.mixed)

    def send_mixed(b):
        st = state[b]
        st.moved = out_of(st.mixed.reshape(n, length, head_cols))

    def middle(b):
        st = state[b]
        attended = order.tie(st.moved)
        st.attended = attended.transpose(1, 0, 2).reshape(length, width)
        rows = inputs[b].astype(F32)
        st.hidden = rows + (dot(st.attended, w_out) + b_out)
        st.normed_two, st.inverse_two = norm_core(st.hidden)
        st.own_two = order.mark((st.normed_two * gain_two + shift_two).astype(BF))
        st.came_two = gather_start(st.own_two)

    def up_even(b):
        st = state[b]
        st.act_even = order.mark(up_product(order.tie(st.even_two), w_up, b_up))

    def up_odd(b):
        st = state[b]
        st.act_odd = order.mark(up_product(order.tie(st.odd_two), w_up, b_up))

    def relay(b, own, came):
        st = state[b]
        came = order.pause(getattr(st, came))
        return came, gather_relay(getattr(st, own), came)

    def join(b, own, came_relayed):
        same = order.mark(gather_join(getattr(state[b], own), *order.tie(came_relayed)))
        return same, swap(same, 1)

    def down_odd(b):
        st = state[b]
        st.down_got = swap(order.mark(plain_product(order.tie(st.act_odd), w_down)), 1)

    def down_even(b):
        st = state[b]
        st.down_sums = order.mark(block_products(st.act_even, w_down, order.tie(st.down_got), n // 2))
        st.down_came = scatter_start(st.down_sums)

    def pass_on(b, sums, came):
        st = state[b]
        came = order.pause(getattr(st, came))
        return scatter_relay(getattr(st, sums), came)

    def misfit(b):
        st = state[b]
        summed = scatter_join(st.down_sums, order.tie(st.down_sent))
        st.result = st.hidden + (summed + b_down)
        error = st.result - teacher[b].astype(F32)
        st.local_sq = jnp.sum(jnp.sum(error * error, axis=-1) * valid[b])
        st.grad_result = error * (valid[b] * (tokens_all / total_count))[:, None]
        st.own_grad = order.mark(st.grad_result.astype(BF))
        st.g_b_down = jnp.sum(st.own_grad.astype(F32), axis=0)
        st.came_grad = gather_start(st.own_grad)

    def act_back_even(b):
        st = state[b]
        st.pre_even, st.sums_even = masked_product(order.tie(st.gm_even), w_down, st.act_even)
        order.mark(st.pre_even)

    def act_back_odd(b):
        st = state[b]
        st.pre_odd, st.sums_odd = masked_product(order.tie(st.gm_odd), w_down, st.act_odd)
        order.mark(st.pre_odd)

    def up_back_odd(b):
        st = state[b]
        st.up_got = swap(order.mark(plain_product(order.tie(st.pre_odd), w_up, turned=True)), 1)

    def up_back_even(b):
        st = state[b]
        st.up_sums = order.mark(block_products(st.pre_even, w_up, order.tie(st.up_got), n // 2, turned=True))
        st.up_came = scatter_start(st.up_sums)

    def branch_back(b):
        st = state[b]
        grad_ready = scatter_join(st.up_sums, order.tie(st.up_sent))
        grad_norm, st.g_gain_two, st.g_shift_two = norm_back(grad_ready, st.normed_two, st.inverse_two, gain_two)
        st.grad_hidden = st.grad_result + grad_norm
        st.branch = st.grad_hidden.astype(BF)
        st.g_b_out = jnp.sum(st.branch.astype(F32), axis=0)
        grad_att = dot_nt(st.branch, w_out).astype(BF).reshape(length, n, head_cols).transpose(1, 0, 2)
        st.grad_mixed = out_of(order.mark(grad_att)).reshape(seq_len, head_cols)

    def attend_back(b):
        st = state[b]
        st.grad_qkv = attend_backward(
            place_arr, st.low, st.qkv, order.tie(st.grad_mixed), st.mixed, st.lse, st.first, length
        )
        order.mark(st.grad_qkv)
        st.g_b_qkv = jnp.sum(st.grad_qkv.astype(F32), axis=0)

    def project_back_odd(b):
        st = state[b]
        odd = order.tie(st.grad_qkv)[seq_len // 2 :]
        st.one_got = swap(order.mark(plain_product(odd, w_qkv, turned=True)), 1)

    def project_back_even(b):
        st = state[b]
        st.one_sums = block_products(st.grad_qkv[: seq_len // 2], w_qkv, order.tie(st.one_got), n // 2, turned=True)
        order.mark(st.one_sums)
        st.one_came = scatter_start(st.one_sums)

    def finish(b):
        st = state[b]
        grad_ready = scatter_join(st.one_sums, order.tie(st.one_sent))
        normed, inverse = norm_core(inputs[b].astype(F32))
        grad_norm, st.g_gain_one, st.g_shift_one = norm_back(grad_ready, normed, inverse, gain_one)
        st.grad_inputs = order.mark(st.grad_hidden + grad_norm)

    every, later = range(seqs), range(1, seqs)

    def whole_out_weight(own, came, relayed):
        whole = jnp.zeros((groups, n, own_rows, width), BF)
        half = groups // 2
        same = [(0, own, 0), (2, came[0], 0), (4, came[1], 0), (6, relayed[0], 0), (6, relayed[1], half)]
        other = [(k + 1, swap(piece, 1), first) for k, piece, first in same]
        for k, piece, first in same + other:
            whole = lax.dynamic_update_slice(whole, piece.reshape(-1, 1, own_rows, width), (first, place ^ k, 0, 0))
        return whole.reshape(width, width)

    def make_ready(b, raw_even, raw_odd):
        st = state[b]
        st.even = order.mark(ready(order.tie(raw_even)))
        st.odd = order.mark(ready(order.tie(raw_odd)))

    for b in every:
        spans(b)
    came_relayed = relay(0, "own", "came")
    for b in later:
        state[b].own = rows_after(b, came_relayed[0][0] if n == 8 else packed)
        state[b].came = gather_start(state[b].own)
    up_cut = order.pause(out_of(after(up_cut, qkv_cut)))
    w_up = lax.all_gather(up_cut.reshape(n * own_rows, groups * own_hidden), "dp", axis=0, tiled=True)
    w_down = lax.all_gather(after(down_weight, up_cut), "dp", axis=0, tiled=True)
    raw = join(0, "own", came_relayed)
    if n == 8:
        own_out = order.tie(own_out)
        out_came = gather_start(own_out)
    else:
        w_out = lax.all_gather(after(out_weight, up_cut), both, axis=0, tiled=True)
    make_ready(0, *raw)
    w_qkv = order.pause(w_qkv)
    project(0)
    came_relayed = [relay(b, "own", "came") for b in later]
    if n == 8:
        out_came = order.pause(out_came)
        out_relayed = gather_relay(own_out, out_came)
    attend(0)
    send_mixed(0)
    raw = [join(b, "own", came_relayed[b - 1]) for b in later]
    if n == 8:
        w_out = whole_out_weight(own_out, out_came, order.pause(out_relayed))
    middle(0)
    for b in later:
        last, st = state[b - 1], state[b]
        make_ready(b, *raw[b - 1])
        project(b)
        came_relayed = relay(b - 1, "own_two", "came_two")
        attend(b)
        send_mixed(b)
        last.even_two, last.odd_two = join(b - 1, "own_two", came_relayed)
        up_even(b - 1)
        middle(b)
        up_odd(b - 1)
        came_relayed = relay(b, "own_two", "came_two")
        down_odd(b - 1)
        st.even_two, st.odd_two = join(b, "own_two", came_relayed)
        up_even(b)
        down_even(b - 1)
        up_odd(b)
        last.down_sent = pass_on(b - 1, "down_sums", "down_came")
        down_odd(b)
        down_even(b)
        misfit(b - 1)
        st.down_sent = pass_on(b, "down_sums", "down_came")
        came_relayed = relay(b - 1, "own_grad", "came_grad")
        misfit(b)
        last.gm_even, last.gm_odd = join(b - 1, "own_grad", came_relayed)
        act_back_even(b - 1)
        act_back_odd(b - 1)
        up_back_odd(b - 1)
        came_relayed = relay(b, "own_grad", "came_grad")
        up_back_even(b - 1)
        st.gm_even, st.gm_odd = join(b, "own_grad", came_relayed)
        act_back_even(b)
        last.up_sent = pass_on(b - 1, "up_sums", "up_came")
        act_back_odd(b)
        up_back_odd(b)
        up_back_even(b)
    lefts = [part for st in state for part in (st.even_two, st.odd_two)]
    rights = [part for st in state for part in (st.pre_even, st.pre_odd)]
    g_w_up = order.mark(weight_grad(order.tie(lefts), rights, 512, 1024))
    g_up = lax.psum_scatter(g_w_up, "dp", scatter_dimension=0, tiled=True)
    for b in later:
        state[b].up_sent = pass_on(b, "up_sums", "up_came")
    branch_back(0)
    lefts = [part for st in state for part in (st.act_even, st.act_odd)]
    rights = [part for st in state for part in (st.gm_even, st.gm_odd)]
    g_w_down = order.mark(weight_grad(order.tie(lefts), rights, 256, 1024))
    g_down = lax.psum_scatter(g_w_down, "dp", scatter_dimension=0, tiled=True)
    for b in later:
        branch_back(b)
    turned = [
        st.attended.reshape(length, groups, n, own_rows).transpose(2, 0, 1, 3).reshape(n, length, groups * own_rows)
        for st in state
    ]

    def out_block(k):
        return add_all(
            [dot_tn(lax.dynamic_index_in_dim(t, place ^ k, 0, keepdims=False), st.branch) for t, st in zip(turned, state)]
        )

    out_rows = groups * own_rows
    half = seq_len // 2
    attend_back(0)
    project_back_odd(0)
    turned = order.tie(turned)
    out_odd = order.mark(jnp.concatenate([out_block(k).astype(BF) for k in range(1, n, 2)], axis=0))
    out_got = swap(out_odd, 1)
    project_back_even(0)
    out_got = order.tie(out_got)
    out_sums = [out_block(2 * m) + out_got[m * out_rows : (m + 1) * out_rows].astype(F32) for m in range(n // 2)]
    order.mark(out_sums)
    out_came = scatter_start(out_sums)
    for b in later:
        attend_back(b)
        state[b - 1].one_sent = pass_on(b - 1, "one_sums", "one_came")
    out_sent = scatter_relay(out_sums, order.pause(out_came))
    for b in later:
        project_back_odd(b)
    lefts = [part for st in state for part in (st.even, st.odd)]
    rights = [part for st in state for part in (st.grad_qkv[:half], st.grad_qkv[half:])]
    g_w_qkv = order.mark(weight_grad(order.tie(lefts), rights, 1024, 768))
    g_qkv = lax.psum_scatter(g_w_qkv, "dp", scatter_dimension=0, tiled=True)
    for b in later:
        project_back_even(b)
        finish(b - 1)
    out_sum = order.mark(scatter_join(out_sums, order.tie(out_sent)))
    for b in later:
        state[b].one_sent = pass_on(b, "one_sums", "one_came")
    g_out = scatter_groups(out_sum)
    g_up = out_of(order.tie(g_up).reshape(n, own_rows, groups * own_hidden))
    for b in later:
        finish(b)

    def summed(name):
        return add_all([after(getattr(st, name), g_w_qkv) for st in state])

    g_down = order.tie(g_down).astype(F32)
    g_up = g_up.reshape(n, own_rows, groups, own_hidden).transpose(1, 2, 0, 3).reshape(own_rows, hidden_units).astype(F32)
    g_qkv = out_of(g_qkv.reshape(n, own_rows, 3 * head_cols))
    g_qkv = g_qkv.reshape(n, own_rows, 3, head_cols).transpose(2, 1, 0, 3).reshape(3, own_rows, width).astype(F32)

    g_b_qkv = summed("g_b_qkv").reshape(3, head_cols)
    own_bias = jnp.zeros((2, width), F32)
    own_bias = lax.dynamic_update_slice(own_bias, jnp.stack([g_b_qkv[0], g_b_qkv[2]]), (0, place * head_cols))
    g_b_up = jnp.sum(summed("sums_even") + summed("sums_odd"), axis=0).reshape(groups, 1, own_hidden)
    spread_up = lax.dynamic_update_slice_in_dim(jnp.zeros((groups, n, own_hidden), F32), g_b_up, place, 1)
    names = ("g_gain_one", "g_shift_one", "g_b_out", "g_gain_two", "g_shift_two", "g_b_down")
    vectors = jnp.concatenate([jnp.stack([summed(name) for name in names]), own_bias], axis=0)
    count = vectors.shape[0]
    vectors = vectors.reshape(count, groups * n, own_rows).transpose(1, 0, 2).reshape(groups * n, count * own_rows)
    sq = jnp.broadcast_to(summed("local_sq"), (groups * n, 1))
    tail = jnp.concatenate([vectors, spread_up.reshape(groups * n, own_hidden), sq], axis=1)
    tail = scatter_small(tail)
    vectors = tail[: count * own_rows].reshape(count, own_rows)
    g_b_query, g_b_value, g_b_up = vectors[6], vectors[7], tail[count * own_rows : -1]
    mean_loss = tail[-1] / (total_count * width)
    return (
        jnp.stack([st.result.astype(BF) for st in state]),
        mean_loss,
        jnp.stack([st.grad_inputs for st in state]),
        vectors[0],
        vectors[1],
        g_qkv[0],
        g_b_query,
        g_qkv[1],
        g_qkv[2],
        g_b_value,
        g_out,
        vectors[2],
        vectors[3],
        vectors[4],
        g_up,
        g_b_up,
        g_down,
        vectors[5],
    )


def solution(mesh):
    rows3, rows2, flat, mat = P("dp", "seq", None), P("dp", "seq"), P(("dp", "seq")), P(("dp", "seq"), None)
    placed = (
        rows3, rows3, rows2, P("dp"), rows2, flat, flat, mat, flat, mat, mat, flat, mat, flat, flat, flat, mat, flat, mat, flat,
    )
    out = (rows3, P(), rows3, flat, flat, mat, flat, mat, mat, flat, mat, flat, flat, flat, mat, flat, mat, flat)
    return jax.shard_map(local, mesh=mesh, in_specs=placed, out_specs=out, check_vma=False)
```

```python
import functools
import types

import jax
import jax.numpy as jnp
from jax import lax
from jax.experimental import pallas as pl
from jax.experimental.pallas import tpu as pltpu
from jax.sharding import PartitionSpec as P

HD = 64
NSUM = 50
NORM_EPS = 1e-05
NEG_FILL = -1e30
PRODUCT_GRANT, LARGE_GRANT = 30 << 20, 56 << 20
BF = jnp.bfloat16
F32 = jnp.float32


def dot(left_in, right_in):
    return jnp.dot(left_in, right_in, preferred_element_type=F32)


def dot_tn(left_in, right_in):
    return lax.dot_general(left_in, right_in, (((0,), (0,)), ((), ())), preferred_element_type=F32)


def dot_nt(left_in, right_in):
    return lax.dot_general(left_in, right_in, (((1,), (1,)), ((), ())), preferred_element_type=F32)


def norm_core(values):
    center = values - jnp.mean(values, axis=-1, keepdims=True)
    inverse = lax.rsqrt(jnp.mean(center * center, axis=-1, keepdims=True) + NORM_EPS)
    return center * inverse, inverse


def norm_back(grad_out, normed, inverse, gain_in):
    grad_normed = grad_out * gain_in
    inner_one = jnp.mean(grad_normed, axis=-1, keepdims=True)
    inner_two = jnp.mean(grad_normed * normed, axis=-1, keepdims=True)
    grad_in = inverse * (grad_normed - inner_one - normed * inner_two)
    return grad_in, jnp.sum(grad_out * normed, axis=0), jnp.sum(grad_out, axis=0)


def swap(values, mask):
    n = lax.axis_size("seq")
    return lax.ppermute(values, "seq", [(i, i ^ mask) for i in range(n)])


def gather_start(own):
    return (swap(own, 2), swap(own, 4)) if lax.axis_size("seq") == 8 else ()


def gather_relay(own, came):
    if lax.axis_size("seq") != 8:
        return ()
    half = own.shape[0] // 2
    return swap(came[1][:half], 2), swap(came[0][half:], 4)


def gather_join(own, came, relayed):
    if lax.axis_size("seq") == 8:
        return jnp.concatenate([own, *came, *relayed], axis=0)
    same, step = own, 2
    while step < lax.axis_size("seq"):
        same = jnp.concatenate([same, swap(same, step)], axis=0)
        step *= 2
    return same


def gather_rows(own):
    came = gather_start(own)
    same = gather_join(own, came, gather_relay(own, came))
    return same, swap(same, 1)


def scatter_start(blocks):
    if lax.axis_size("seq") != 8:
        return ()
    six = blocks[3].astype(BF)
    half = six.shape[0] // 2
    return swap(six[:half], 2), swap(six[half:], 4)


def scatter_relay(blocks, came):
    if lax.axis_size("seq") != 8:
        return ()
    _, two, four, _ = blocks
    half, width = two.shape[0] // 2, two.shape[1]
    which = lax.broadcasted_iota(jnp.int32, (2, half, width), 0)

    def with_half(block, part, side):
        part = jnp.where(which == side, part.astype(F32)[None], 0.0)
        return (block.reshape(2, half, width) + part).astype(BF).reshape(2 * half, width)

    return swap(with_half(two, came[1], 1), 2), swap(with_half(four, came[0], 0), 4)


def scatter_join(blocks, relayed):
    n = lax.axis_size("seq")
    if n == 8:
        return blocks[0] + relayed[0].astype(F32) + relayed[1].astype(F32)
    step = n // 2
    while step > 1:
        keep = len(blocks) // 2
        sent = [swap(block.astype(BF), step).astype(F32) for block in blocks[keep:]]
        blocks = [block.astype(F32) + got for block, got in zip(blocks[:keep], sent)]
        step //= 2
    return blocks[0]


def scatter_groups(rows):
    bit, index = lax.axis_size("dp") // 2, lax.axis_index("dp")
    while bit > 0:
        half = rows.shape[0] // 2
        upper = (index & bit) != 0
        sent = jnp.where(upper, rows[:half], rows[half:]).astype(BF)
        rows = jnp.where(upper, rows[half:], rows[:half]) + exchange(sent, "dp", bit).astype(F32)
        bit //= 2
    return rows


def exchange(values, axis, bit):
    size = lax.axis_size(axis)
    return lax.ppermute(values, axis, [(i, i ^ bit) for i in range(size)])


class Order:
    def __init__(self):
        self.last = ()

    def tie(self, value):
        if not jax.tree.leaves(value) or not jax.tree.leaves(self.last):
            return value
        return lax.optimization_barrier((value, self.last))[0]

    def mark(self, value):
        if jax.tree.leaves(value):
            self.last = value
        return value

    def pause(self, value):
        return self.mark(self.tie(value))


def doubling(held, axes):
    for axis in axes:
        bit, index = 1, lax.axis_index(axis)
        while bit < lax.axis_size(axis):
            other = yield exchange(held, axis, bit)
            upper = (index & bit) != 0
            held = jnp.concatenate([jnp.where(upper, other, held), jnp.where(upper, held, other)], axis=0)
            bit *= 2
    return held


def line_gather(own):
    size, index = lax.axis_size("dp"), lax.axis_index("dp")
    below, above = [], []
    to_right, to_left = own, own
    for _ in range(size - 1):
        flight = (
            lax.ppermute(to_right, "dp", [(i, i + 1) for i in range(size - 1)]),
            lax.ppermute(to_left, "dp", [(i + 1, i) for i in range(size - 1)]),
        )
        to_right, to_left = yield flight
        below.insert(0, to_right)
        above.append(to_left)
    rows = jnp.concatenate(below + [own] + above, axis=0)
    return lax.dynamic_slice_in_dim(rows, (size - 1 - index) * own.shape[0], size * own.shape[0], axis=0)


def line_scatter(parts):
    size, index = lax.axis_size("dp"), lax.axis_index("dp")

    def part(which):
        return lax.dynamic_index_in_dim(parts, jnp.clip(which, 0, size - 1), 0, keepdims=False)

    right = left = None
    for step in range(size - 1):
        far = size - 1 - step
        up, down = part(index + far), part(index - far)
        if step:
            up, down = (up.astype(F32) + right.astype(F32)).astype(BF), (down.astype(F32) + left.astype(F32)).astype(BF)
        flight = (
            lax.ppermute(up, "dp", [(i, i + 1) for i in range(size - far)]),
            lax.ppermute(down, "dp", [(i, i - 1) for i in range(far, size)]),
        )
        right, left = yield flight
    return part(index).astype(F32) + right.astype(F32) + left.astype(F32)


class Steps:
    def __init__(self, order, generator):
        self.order, self.generator, self.flight, self.result = order, generator, next(generator), None

    def step(self, count=1):
        for _ in range(count):
            if self.flight is None:
                return
            try:
                self.flight = self.generator.send(self.order.pause(self.flight))
            except StopIteration as stop:
                self.flight, self.result = None, stop.value

    def finish(self):
        while self.flight is not None:
            self.step()
        return self.result


def scatter_small(table):
    count, width = table.shape
    length = -(-width // 1024) * 1024
    held = jnp.pad(table, ((0, 0), (0, length - width))).reshape(count, 8, length // 8)
    for axis in ("dp", "seq"):
        bit, index = lax.axis_size(axis) // 2, lax.axis_index(axis)
        while bit > 0:
            half = held.shape[0] // 2
            upper = (index & bit) != 0
            sent = jnp.where(upper, held[:half], held[half:])
            held = jnp.where(upper, held[half:], held[:half]) + exchange(sent, axis, bit)
            bit //= 2
    return held.reshape(length)[:width]


def after(value, *earlier):
    return lax.optimization_barrier((value, *earlier))[0]


def weight_grad_kernel(*refs):
    count = (len(refs) - 1) // 2
    total = dot_tn(refs[0][...], refs[count][...])
    for part in range(1, count):
        total = total + dot_tn(refs[part][...], refs[count + part][...])
    refs[-1][...] = total.astype(BF)


def weight_grad(lefts, rights, left_tile, right_tile):
    rows, left_width = lefts[0].shape
    right_width = rights[0].shape[1]
    left_tile, right_tile = min(left_tile, left_width), min(right_tile, right_width)
    count = len(lefts)
    return pl.pallas_call(
        weight_grad_kernel,
        grid=(right_width // right_tile, left_width // left_tile),
        in_specs=[pl.BlockSpec((rows, left_tile), lambda j, i: (0, i))] * count
        + [pl.BlockSpec((rows, right_tile), lambda j, i: (0, j))] * count,
        out_specs=pl.BlockSpec((left_tile, right_tile), lambda j, i: (i, j)),
        out_shape=jax.ShapeDtypeStruct((left_width, right_width), BF),
        compiler_params=pltpu.CompilerParams(dimension_semantics=("arbitrary", "arbitrary"), vmem_limit_bytes=LARGE_GRANT),
        cost_estimate=light_cost(2 * count * rows * left_width * right_width),
        name="weight_grad",
    )(*lefts, *rights)


def tile_dot(left, right, turned):
    return dot_nt(left, right) if turned else dot(left, right)


def plain_kernel(left_ref, right_ref, out_ref, *, turned):
    out_ref[...] = tile_dot(left_ref[...], right_ref[...], turned).astype(out_ref.dtype)


def project_kernel(left_ref, right_ref, bias_ref, scale_ref, out_ref):
    out_ref[...] = ((dot(left_ref[...], right_ref[...]) + bias_ref[...]) * scale_ref[...]).astype(BF)


def up_kernel(left_ref, right_ref, bias_ref, out_ref):
    out_ref[...] = jnp.maximum(dot(left_ref[...], right_ref[...]) + bias_ref[...], 0.0).astype(BF)


def masked_kernel(left_ref, right_ref, act_ref, out_ref, sums_ref):
    grad = jnp.where(act_ref[...] > 0, dot_nt(left_ref[...], right_ref[...]), 0.0).astype(BF)
    out_ref[...] = grad
    part = jnp.sum(grad.astype(F32).reshape(-1, 8, grad.shape[1]), axis=0)

    @pl.when(pl.program_id(1) == 0)
    def _():
        sums_ref[...] = part

    @pl.when(pl.program_id(1) > 0)
    def _():
        sums_ref[...] = sums_ref[...] + part


def blocks_kernel(left_ref, right_ref, got_ref, *out_refs, turned):
    rows = out_refs[0].shape[0]
    for m in range(len(out_refs) - 1, -1, -1):
        cut = slice(m * rows, (m + 1) * rows)
        total = tile_dot(left_ref[cut, :], right_ref[...], turned) + got_ref[cut, :].astype(F32)
        out_refs[m][...] = total.astype(out_refs[m].dtype)


def light_cost(flops):
    return pl.CostEstimate(flops=int(flops) // 8, bytes_accessed=1, transcendentals=0)


def tiled(kernel, name, left, right, turned, extras, outs, row_tile, col_tile, parts=1):
    rows, depth = left.shape
    cols = right.shape[0] if turned else right.shape[1]
    row_tile, col_tile = min(row_tile, rows), min(col_tile, cols)
    kinds = {
        "both": pl.BlockSpec((row_tile, col_tile), lambda j, m: (m, j)),
        "vector": pl.BlockSpec((1, col_tile), lambda j, m: (0, j)),
        "sums": pl.BlockSpec((8, col_tile), lambda j, m: (0, j)),
        "block": pl.BlockSpec((rows // parts, col_tile), lambda j, m: (0, j)),
    }
    shapes = {"both": (rows, cols), "sums": (8, cols), "block": (rows // parts, cols)}
    right_spec = (
        pl.BlockSpec((col_tile, depth), lambda j, m: (j, 0)) if turned else pl.BlockSpec((depth, col_tile), lambda j, m: (0, j))
    )
    return pl.pallas_call(
        kernel,
        grid=(cols // col_tile, rows // row_tile),
        in_specs=[pl.BlockSpec((row_tile, depth), lambda j, m: (m, 0)), right_spec] + [kinds[k] for k, _ in extras],
        out_specs=[kinds[k] for k, _ in outs],
        out_shape=[jax.ShapeDtypeStruct(shapes[k], dtype) for k, dtype in outs],
        compiler_params=pltpu.CompilerParams(dimension_semantics=("arbitrary", "arbitrary"), vmem_limit_bytes=PRODUCT_GRANT),
        cost_estimate=light_cost(2 * rows * cols * depth),
        name=name,
    )(left, right, *[value for _, value in extras])


def plain_product(left, right, turned=False):
    kernel = functools.partial(plain_kernel, turned=turned)
    return tiled(kernel, "product", left, right, turned, [], [("both", BF)], 1024, 256)[0]


def project_product(left, right, bias, scale):
    extras = [("vector", bias.reshape(1, -1)), ("vector", scale.reshape(1, -1))]
    return tiled(project_kernel, "project", left, right, False, extras, [("both", BF)], 1024, 256)[0]


def up_product(left, right, bias):
    return tiled(up_kernel, "up", left, right, False, [("vector", bias.reshape(1, -1))], [("both", BF)], 1024, 256)[0]


def masked_product(left, right, act):
    outs = [("both", BF), ("sums", F32)]
    return tiled(masked_kernel, "masked_product", left, right, True, [("both", act)], outs, 1024, 256)


def block_products(left, right, got, count, turned=False):
    kernel = functools.partial(blocks_kernel, turned=turned)
    outs = [("block", F32)] * (count - 1) + [("block", BF)]
    return tiled(
        kernel, "block_products", left, right, turned, [("both", got)], outs, left.shape[0], 256, count
    )


def visible_scores(q_head, k_block, first, q_place, key_start, length):
    scores = dot_nt(q_head, k_block)
    k_place = key_start + lax.broadcasted_iota(jnp.int32, (1, length), 1)
    allowed = (k_place >= first) & (k_place <= q_place)
    return jnp.where(allowed, scores, NEG_FILL)


def storage_row(block, place, blocks, length):
    k = block ^ place
    return pl.multiple_of(((k >> 1) + (k & 1) * (blocks // 2)) * length, length)


def spread_heads(source_ref, target_ref, lanes, heads, length, blocks):
    def one(m, carry):
        rows = source_ref[pl.ds(pl.multiple_of(m * length, length), length), :]
        for h in range(heads):
            target = pl.ds(pl.multiple_of((m * heads + h) * length, length), length)
            target_ref[target, :] = jnp.where(lanes == h, rows, jnp.zeros_like(rows))
        return carry

    lax.fori_loop(0, blocks, one, 0)


def fold(values, op):
    out = values[:, :128]
    for start in range(128, values.shape[1], 128):
        out = op(out, values[:, start : start + 128])
    return out


def attend_forward_kernel(
    place_ref, low_ref, q_ref, k_ref, v_ref, first_ref, o_ref, lse_ref, s_scr, m_scr, l_scr, v_scr, *, heads, length, blocks
):
    i = pl.program_id(0)
    place = place_ref[0]
    low = low_ref[i]
    width = heads * HD
    lanes = lax.broadcasted_iota(jnp.int32, (length, width), 1) // HD
    q_all = q_ref[...]
    q_heads = [jnp.where(lanes == h, q_all, jnp.zeros_like(q_all)) for h in range(heads)]
    first = first_ref[...]
    q_place = i * length + lax.broadcasted_iota(jnp.int32, (length, 1), 0)
    m_scr[...] = jnp.full_like(m_scr, NEG_FILL)
    l_scr[...] = jnp.zeros_like(l_scr)

    @pl.when(i == 0)
    def _():
        spread_heads(v_ref, v_scr, lanes, heads, length, blocks)

    def score_step(j, carry):
        k_block = k_ref[pl.ds(storage_row(j, place, blocks, length), length), :]
        cols = pl.ds(pl.multiple_of(j * length, length), length)
        for h in range(heads):
            scores = visible_scores(q_heads[h], k_block, first, q_place, j * length, length)
            s_scr[h, :, cols] = scores
            m_scr[h] = jnp.maximum(m_scr[h], fold(scores, jnp.maximum))
        return carry

    lax.fori_loop(low, i + 1, score_step, 0)
    tops = [jnp.max(m_scr[h], axis=-1, keepdims=True) for h in range(heads)]

    def exp_step(j, carry):
        cols = pl.ds(pl.multiple_of(j * length, length), length)
        for h in range(heads):
            raised = jnp.exp(s_scr[h, :, cols] - tops[h])
            s_scr[h, :, cols] = raised
            l_scr[h] = l_scr[h] + fold(raised, jnp.add)
        return carry

    lax.fori_loop(low, i + 1, exp_step, 0)
    totals = [jnp.sum(l_scr[h], axis=-1, keepdims=True) for h in range(heads)]
    scales = [1.0 / total for total in totals]

    def mix_step(j, acc):
        rows = pl.ds(pl.multiple_of(storage_row(j, place, blocks, length) * heads, heads * length), heads * length)
        cols = pl.ds(pl.multiple_of(j * length, length), length)
        probs = [(s_scr[h, :, cols] * scales[h]).astype(BF) for h in range(heads)]
        return acc + dot(jnp.concatenate(probs, axis=1), v_scr[rows, :])

    mixed = lax.fori_loop(low, i + 1, mix_step, jnp.zeros((length, width), F32))
    o_ref[...] = mixed.astype(BF)
    cols = lax.broadcasted_iota(jnp.int32, (length, 128), 1)
    lse = jnp.zeros((length, 128), F32)
    for h in range(heads):
        lse = jnp.where(cols == h, tops[h] + jnp.log(totals[h]), lse)
    lse_ref[...] = lse


def attend_backward_kernel(
    place_ref, low_ref, q_ref, go_ref, o_ref, lse_ref, k_ref, v_ref, first_ref, grad_ref, kt_scr, vt_scr, k_scr, *, heads, length,
    blocks
):
    i = pl.program_id(0)
    place = place_ref[0]
    low = low_ref[i]
    width = heads * HD
    lanes = lax.broadcasted_iota(jnp.int32, (length, width), 1) // HD
    first = first_ref[...]
    q_place = i * length + lax.broadcasted_iota(jnp.int32, (length, 1), 0)
    q_all, go_all = q_ref[...], go_ref[...]
    inner_all = go_all.astype(F32) * o_ref[...].astype(F32)
    q_turned, go_turned = q_all.astype(F32).T.astype(BF), go_all.astype(F32).T.astype(BF)
    lse_all = lse_ref[...]
    q_heads, go_heads, inner, lse = [], [], [], []
    for h in range(heads):
        mine = lanes == h
        q_heads.append(jnp.where(mine, q_all, jnp.zeros_like(q_all)))
        go_heads.append(jnp.where(mine, go_all, jnp.zeros_like(go_all)))
        inner.append(jnp.sum(jnp.where(mine, inner_all, 0.0), axis=-1, keepdims=True))
        lse.append(lse_all[:, h : h + 1])

    @pl.when(i == 0)
    def _():
        kt_scr[...] = jnp.zeros_like(kt_scr)
        vt_scr[...] = jnp.zeros_like(vt_scr)
        spread_heads(k_ref, k_scr, lanes, heads, length, blocks)

    def step(j, acc):
        start = storage_row(j, place, blocks, length)
        rows = pl.ds(start, length)
        k_block, v_block = k_ref[rows, :], v_ref[rows, :]
        k_place = j * length + lax.broadcasted_iota(jnp.int32, (1, length), 1)
        allowed = (k_place >= first) & (k_place <= q_place)
        every = range(heads)
        scores = [dot_nt(q_heads[h], k_block) for h in every]
        grad_probs = [dot_nt(go_heads[h], v_block) for h in every]
        probs = [jnp.exp(jnp.where(allowed, scores[h] - lse[h], NEG_FILL)) for h in every]
        grad_scores = [(probs[h] * (grad_probs[h] - inner[h])).astype(BF) for h in every]
        for h in every:
            part = slice(h * HD, (h + 1) * HD)
            vt_scr[part, rows] = vt_scr[part, rows] + dot(go_turned[part, :], probs[h].astype(BF))
            kt_scr[part, rows] = kt_scr[part, rows] + dot(q_turned[part, :], grad_scores[h])
        spread = pl.ds(pl.multiple_of(start * heads, heads * length), heads * length)
        return acc + dot(jnp.concatenate(grad_scores, axis=1), k_scr[spread, :])

    grad_q = lax.fori_loop(low, i + 1, step, jnp.zeros((length, width), F32))
    own_rows = pl.ds(storage_row(i, place, blocks, length), length)
    grad_ref[own_rows, 0:width] = (grad_q.astype(BF).astype(F32) * (HD**-0.5)).astype(BF)

    @pl.when(i == blocks - 1)
    def _():
        for j in range(blocks):
            rows = slice(j * length, (j + 1) * length)
            grad_ref[rows, width : 2 * width] = kt_scr[:, rows].T.astype(BF)
            grad_ref[rows, 2 * width : 3 * width] = vt_scr[:, rows].T.astype(BF)


def storage_map(length, blocks, column):
    def index(i, place_ref, low_ref):
        k = i ^ place_ref[0]
        return ((k >> 1) + (k & 1) * (blocks // 2), column)

    return index


def attend_forward(place, low, qkv, first, length):
    rows, triple = qkv.shape
    width, blocks = triple // 3, rows // length
    heads = width // HD
    return pl.pallas_call(
        functools.partial(attend_forward_kernel, heads=heads, length=length, blocks=blocks),
        grid_spec=pltpu.PrefetchScalarGridSpec(
            num_scalar_prefetch=2,
            grid=(blocks,),
            in_specs=[
                pl.BlockSpec((length, width), storage_map(length, blocks, 0)),
                pl.BlockSpec((rows, width), lambda i, p, w: (0, 1)),
                pl.BlockSpec((rows, width), lambda i, p, w: (0, 2)),
                pl.BlockSpec((length, 1), lambda i, p, w: (i, 0)),
            ],
            out_specs=[
                pl.BlockSpec((length, width), lambda i, p, w: (i, 0)),
                pl.BlockSpec((length, 128), lambda i, p, w: (i, 0)),
            ],
            scratch_shapes=[
                pltpu.VMEM((heads, length, rows), F32),
                pltpu.VMEM((heads, length, 128), F32),
                pltpu.VMEM((heads, length, 128), F32),
                pltpu.VMEM((heads * rows, width), BF),
            ],
        ),
        out_shape=[jax.ShapeDtypeStruct((rows, width), BF), jax.ShapeDtypeStruct((rows, 128), F32)],
        compiler_params=pltpu.CompilerParams(dimension_semantics=("arbitrary",), vmem_limit_bytes=LARGE_GRANT),
        cost_estimate=light_cost(24 * rows * rows * width),
        name="attend_forward",
    )(place, low, qkv, qkv, qkv, first)


def attend_backward(place, low, qkv, grad_out, mixed, lse, first, length):
    rows, triple = qkv.shape
    width, blocks = triple // 3, rows // length
    heads = width // HD
    return pl.pallas_call(
        functools.partial(attend_backward_kernel, heads=heads, length=length, blocks=blocks),
        grid_spec=pltpu.PrefetchScalarGridSpec(
            num_scalar_prefetch=2,
            grid=(blocks,),
            in_specs=[
                pl.BlockSpec((length, width), storage_map(length, blocks, 0)),
                pl.BlockSpec((length, width), lambda i, p, w: (i, 0)),
                pl.BlockSpec((length, width), lambda i, p, w: (i, 0)),
                pl.BlockSpec((length, 128), lambda i, p, w: (i, 0)),
                pl.BlockSpec((rows, width), lambda i, p, w: (0, 1)),
                pl.BlockSpec((rows, width), lambda i, p, w: (0, 2)),
                pl.BlockSpec((length, 1), lambda i, p, w: (i, 0)),
            ],
            out_specs=pl.BlockSpec((rows, triple), lambda i, p, w: (0, 0)),
            scratch_shapes=[
                pltpu.VMEM((width, rows), F32),
                pltpu.VMEM((width, rows), F32),
                pltpu.VMEM((heads * rows, width), BF),
            ],
        ),
        out_shape=jax.ShapeDtypeStruct((rows, triple), BF),
        compiler_params=pltpu.CompilerParams(dimension_semantics=("arbitrary",), vmem_limit_bytes=LARGE_GRANT),
        cost_estimate=light_cost(36 * rows * rows * width),
        name="attend_backward",
    )(place, low, qkv, grad_out, mixed, lse, qkv, qkv, first)


def local(
    inputs,
    teacher,
    segment_ids,
    summary_start,
    valid_mask,
    attn_norm_gain,
    attn_norm_bias,
    query_weight,
    query_bias,
    key_weight,
    value_weight,
    value_bias,
    out_weight,
    out_bias,
    mlp_norm_gain,
    mlp_norm_bias,
    up_weight,
    up_bias,
    down_weight,
    down_bias,
):
    seqs, length = segment_ids.shape
    width = inputs.shape[-1]
    hidden_units = up_weight.shape[1]
    n, groups = lax.axis_size("seq"), lax.axis_size("dp")
    place, group = lax.axis_index("seq"), lax.axis_index("dp")
    both = ("dp", "seq")
    seq_len = length * n
    tokens_all = seqs * seq_len * groups
    scale = HD**-0.5
    own_rows = query_weight.shape[0]
    own_hidden = up_bias.shape[0]
    head_cols = width // n

    def out_of(value):
        return lax.all_to_all(value, "seq", split_axis=0, concat_axis=0, tiled=True)

    valid = valid_mask.astype(F32)
    order = Order()
    near = n == 8 and groups == 4
    out_steps = Steps(order, doubling(out_weight[None], ("dp",))) if near else None
    cut = jnp.concatenate(
        [w.reshape(own_rows, n, head_cols).transpose(1, 0, 2) for w in (query_weight, key_weight, value_weight)], axis=2
    )
    qkv_cut = out_of(cut)
    small = [attn_norm_gain, attn_norm_bias, out_bias, mlp_norm_gain, mlp_norm_bias, down_bias, query_bias, value_bias, up_bias]
    pieces = [v.astype(F32) for v in small] + [segment_ids.astype(F32).reshape(-1), jnp.sum(valid).reshape(1)]
    starts, lines = [], []
    for piece in pieces:
        starts.append(sum(line.shape[0] for line in lines))
        short = -piece.shape[0] % 128
        lines.append(jnp.pad(piece, (0, short)).reshape(-1, 128))
    used = sum(line.shape[0] for line in lines)
    packed = jnp.pad(jnp.concatenate(lines, axis=0), ((0, -used % 8), (0, 0)))[None]
    small_steps = Steps(order, doubling(after(packed, cut), ("dp", "seq")))
    if near:
        out_steps.step()
    small_steps.step(3)
    qkv_cut = order.pause(qkv_cut).reshape(n * own_rows, 3 * head_cols)
    if near:
        qkv_steps = Steps(order, line_gather(qkv_cut))
    else:
        w_qkv = lax.all_gather(qkv_cut, "dp", axis=0, tiled=True)
    packed = small_steps.finish().reshape(n, groups, -1, 128).transpose(1, 0, 2, 3).reshape(groups * n, -1, 128)

    def zero_after(value):
        return jnp.minimum(jnp.abs(value.reshape(-1)[0].astype(F32)), 0.0).astype(jnp.int32)

    def rows_after(b, value):
        return lax.dynamic_index_in_dim(inputs, b + zero_after(value), 0, keepdims=False)

    state = [types.SimpleNamespace() for _ in range(seqs)]
    state[0].own = rows_after(0, packed)
    state[0].came = gather_start(state[0].own)
    parts = []
    for piece, at in zip(pieces, starts):
        count = -(-piece.shape[0] // 128)
        parts.append(packed[:, at : at + count].reshape(groups * n, -1)[:, : piece.shape[0]])
    gain_one, shift_one, b_out, gain_two, shift_two, b_down = [part.reshape(-1) for part in parts[:6]]
    b_query, b_value = [lax.dynamic_slice_in_dim(part.reshape(-1), place * head_cols, head_cols) for part in parts[6:8]]
    b_up = lax.dynamic_index_in_dim(parts[8].reshape(groups, n, -1), place, 1, keepdims=False).reshape(-1)
    ids = lax.dynamic_index_in_dim(parts[9].reshape(groups, n, seqs, length), group, 0, keepdims=False)
    ids = ids.transpose(1, 0, 2).reshape(seqs, seq_len)
    total_count = jnp.sum(parts[10])

    up_cut = up_weight.reshape(own_rows, groups, n, own_hidden).transpose(2, 0, 1, 3).reshape(n, own_rows, groups * own_hidden)
    b_qkv = jnp.concatenate([b_query, jnp.zeros_like(b_query), b_value])
    s_qkv = jnp.concatenate([jnp.full((head_cols,), scale, F32), jnp.ones((2 * head_cols,), F32)])

    place_arr = place.reshape(1).astype(jnp.int32)
    positions = jnp.arange(seq_len, dtype=jnp.int32)

    def add_all(terms):
        out = terms[0]
        for term in terms[1:]:
            out = out + term
        return out


    def spans(b):
        st = state[b]
        first = jnp.sum((ids[b][None, :] < ids[b][:, None]).astype(jnp.int32), axis=1)
        in_summary = (positions >= summary_start[b]) & (positions < summary_start[b] + NSUM)
        first = jnp.where(in_summary, 0, first)
        st.low = jnp.min(first.reshape(n, length), axis=1) // length
        st.first = first.reshape(seq_len, 1)

    def ready(rows):
        return (norm_core(rows.astype(F32))[0] * gain_one + shift_one).astype(BF)

    def project(b):
        st = state[b]
        even, odd = order.tie((st.even, st.odd))
        parts = [project_product(part, w_qkv, b_qkv, s_qkv) for part in (even, odd)]
        st.qkv = order.mark(jnp.concatenate(parts, axis=0))

    def attend(b):
        st = state[b]
        qkv = order.tie(st.qkv)
        st.mixed, st.lse = attend_forward(place_arr, st.low, qkv, st.first, length)
        order.mark(st.mixed)

    def send_mixed(b):
        st = state[b]
        st.moved = out_of(st.mixed.reshape(n, length, head_cols))

    def middle(b):
        st = state[b]
        attended = order.tie(st.moved)
        st.attended = attended.transpose(1, 0, 2).reshape(length, width)
        rows = inputs[b].astype(F32)
        st.hidden = rows + (dot(st.attended, w_out) + b_out)
        st.normed_two, st.inverse_two = norm_core(st.hidden)
        st.own_two = order.mark((st.normed_two * gain_two + shift_two).astype(BF))
        st.came_two = gather_start(st.own_two)

    def up_even(b):
        st = state[b]
        st.act_even = order.mark(up_product(order.tie(st.even_two), w_up, b_up))

    def up_odd(b):
        st = state[b]
        st.act_odd = order.mark(up_product(order.tie(st.odd_two), w_up, b_up))

    def relay(b, own, came):
        st = state[b]
        came = order.pause(getattr(st, came))
        return came, gather_relay(getattr(st, own), came)

    def join(b, own, came_relayed):
        same = order.mark(gather_join(getattr(state[b], own), *order.tie(came_relayed)))
        return same, swap(same, 1)

    def down_odd(b):
        st = state[b]
        st.down_got = swap(order.mark(plain_product(order.tie(st.act_odd), w_down)), 1)

    def down_even(b):
        st = state[b]
        st.down_sums = order.mark(block_products(st.act_even, w_down, order.tie(st.down_got), n // 2))
        st.down_came = scatter_start(st.down_sums)

    def pass_on(b, sums, came):
        st = state[b]
        came = order.pause(getattr(st, came))
        return scatter_relay(getattr(st, sums), came)

    def misfit(b):
        st = state[b]
        summed = scatter_join(st.down_sums, order.tie(st.down_sent))
        st.result = st.hidden + (summed + b_down)
        error = st.result - teacher[b].astype(F32)
        st.local_sq = jnp.sum(jnp.sum(error * error, axis=-1) * valid[b])
        st.grad_result = error * (valid[b] * (tokens_all / total_count))[:, None]
        st.own_grad = order.mark(st.grad_result.astype(BF))
        st.g_b_down = jnp.sum(st.own_grad.astype(F32), axis=0)
        st.came_grad = gather_start(st.own_grad)

    def act_back_even(b):
        st = state[b]
        st.pre_even, st.sums_even = masked_product(order.tie(st.gm_even), w_down, st.act_even)
        order.mark(st.pre_even)

    def act_back_odd(b):
        st = state[b]
        st.pre_odd, st.sums_odd = masked_product(order.tie(st.gm_odd), w_down, st.act_odd)
        order.mark(st.pre_odd)

    def up_back_odd(b):
        st = state[b]
        st.up_got = swap(order.mark(plain_product(order.tie(st.pre_odd), w_up, turned=True)), 1)

    def up_back_even(b):
        st = state[b]
        st.up_sums = order.mark(block_products(st.pre_even, w_up, order.tie(st.up_got), n // 2, turned=True))
        st.up_came = scatter_start(st.up_sums)

    def branch_back(b):
        st = state[b]
        grad_ready = scatter_join(st.up_sums, order.tie(st.up_sent))
        grad_norm, st.g_gain_two, st.g_shift_two = norm_back(grad_ready, st.normed_two, st.inverse_two, gain_two)
        st.grad_hidden = st.grad_result + grad_norm
        st.branch = st.grad_hidden.astype(BF)
        st.g_b_out = jnp.sum(st.branch.astype(F32), axis=0)
        grad_att = dot_nt(st.branch, w_out).astype(BF).reshape(length, n, head_cols).transpose(1, 0, 2)
        st.grad_mixed = out_of(order.mark(grad_att)).reshape(seq_len, head_cols)

    def attend_back(b):
        st = state[b]
        st.grad_qkv = attend_backward(
            place_arr, st.low, st.qkv, order.tie(st.grad_mixed), st.mixed, st.lse, st.first, length
        )
        order.mark(st.grad_qkv)
        st.g_b_qkv = jnp.sum(st.grad_qkv.astype(F32), axis=0)

    def project_back_odd(b):
        st = state[b]
        odd = order.tie(st.grad_qkv)[seq_len // 2 :]
        st.one_got = swap(order.mark(plain_product(odd, w_qkv, turned=True)), 1)

    def project_back_even(b):
        st = state[b]
        st.one_sums = block_products(st.grad_qkv[: seq_len // 2], w_qkv, order.tie(st.one_got), n // 2, turned=True)
        order.mark(st.one_sums)
        st.one_came = scatter_start(st.one_sums)

    def finish(b):
        st = state[b]
        grad_ready = scatter_join(st.one_sums, order.tie(st.one_sent))
        normed, inverse = norm_core(inputs[b].astype(F32))
        grad_norm, st.g_gain_one, st.g_shift_one = norm_back(grad_ready, normed, inverse, gain_one)
        st.grad_inputs = order.mark(st.grad_hidden + grad_norm)

    every, later = range(seqs), range(1, seqs)

    def whole_out_weight(own, came, relayed):
        whole = jnp.zeros((groups, n, own_rows, width), BF)
        half = groups // 2
        same = [(0, own, 0), (2, came[0], 0), (4, came[1], 0), (6, relayed[0], 0), (6, relayed[1], half)]
        other = [(k + 1, swap(piece, 1), first) for k, piece, first in same]
        for k, piece, first in same + other:
            whole = lax.dynamic_update_slice(whole, piece.reshape(-1, 1, own_rows, width), (first, place ^ k, 0, 0))
        return whole.reshape(width, width)

    def make_ready(b, raw_even, raw_odd):
        st = state[b]
        st.even = order.mark(ready(order.tie(raw_even)))
        st.odd = order.mark(ready(order.tie(raw_odd)))

    for b in every:
        spans(b)
    if near:
        qkv_steps.step()
    came_relayed = relay(0, "own", "came")
    raw = join(0, "own", came_relayed)
    up_cut = out_of(after(up_cut, qkv_cut))
    if near:
        qkv_steps.step()
        own_out = out_steps.finish().reshape(-1, width)
    for b in later:
        state[b].own = rows_after(b, came_relayed[0][0] if near else packed)
        state[b].came = gather_start(state[b].own)
    up_cut = order.pause(up_cut)
    w_up = lax.all_gather(up_cut.reshape(n * own_rows, groups * own_hidden), "dp", axis=0, tiled=True)
    w_down = lax.all_gather(after(down_weight, up_cut), "dp", axis=0, tiled=True)
    if near:
        own_out = order.tie(own_out)
        out_came = gather_start(own_out)
    else:
        w_out = lax.all_gather(after(out_weight, up_cut), both, axis=0, tiled=True)
    make_ready(0, *raw)
    w_qkv = qkv_steps.finish() if near else order.pause(w_qkv)
    project(0)
    came_relayed = [relay(b, "own", "came") for b in later]
    if near:
        out_came = order.pause(out_came)
        out_relayed = gather_relay(own_out, out_came)
    attend(0)
    send_mixed(0)
    raw = [join(b, "own", came_relayed[b - 1]) for b in later]
    if near:
        w_out = whole_out_weight(own_out, out_came, order.pause(out_relayed))
    middle(0)
    for b in later:
        last, st = state[b - 1], state[b]
        make_ready(b, *raw[b - 1])
        project(b)
        came_relayed = relay(b - 1, "own_two", "came_two")
        attend(b)
        send_mixed(b)
        last.even_two, last.odd_two = join(b - 1, "own_two", came_relayed)
        up_even(b - 1)
        middle(b)
        up_odd(b - 1)
        came_relayed = relay(b, "own_two", "came_two")
        down_odd(b - 1)
        st.even_two, st.odd_two = join(b, "own_two", came_relayed)
        up_even(b)
        down_even(b - 1)
        up_odd(b)
        last.down_sent = pass_on(b - 1, "down_sums", "down_came")
        down_odd(b)
        down_even(b)
        misfit(b - 1)
        st.down_sent = pass_on(b, "down_sums", "down_came")
        came_relayed = relay(b - 1, "own_grad", "came_grad")
        misfit(b)
        last.gm_even, last.gm_odd = join(b - 1, "own_grad", came_relayed)
        act_back_even(b - 1)
        act_back_odd(b - 1)
        up_back_odd(b - 1)
        came_relayed = relay(b, "own_grad", "came_grad")
        up_back_even(b - 1)
        st.gm_even, st.gm_odd = join(b, "own_grad", came_relayed)
        act_back_even(b)
        last.up_sent = pass_on(b - 1, "up_sums", "up_came")
        act_back_odd(b)
        up_back_odd(b)
        up_back_even(b)
    lefts = [part for st in state for part in (st.even_two, st.odd_two)]
    rights = [part for st in state for part in (st.pre_even, st.pre_odd)]
    g_w_up = order.mark(weight_grad(order.tie(lefts), rights, 512, 1024))
    g_up = lax.psum_scatter(g_w_up, "dp", scatter_dimension=0, tiled=True)
    for b in later:
        state[b].up_sent = pass_on(b, "up_sums", "up_came")
    branch_back(0)
    lefts = [part for st in state for part in (st.act_even, st.act_odd)]
    rights = [part for st in state for part in (st.gm_even, st.gm_odd)]
    g_w_down = order.mark(weight_grad(order.tie(lefts), rights, 256, 1024))
    g_down = lax.psum_scatter(g_w_down, "dp", scatter_dimension=0, tiled=True)
    for b in later:
        branch_back(b)
    turned = [
        st.attended.reshape(length, groups, n, own_rows).transpose(2, 0, 1, 3).reshape(n, length, groups * own_rows)
        for st in state
    ]

    def out_block(k):
        return add_all(
            [dot_tn(lax.dynamic_index_in_dim(t, place ^ k, 0, keepdims=False), st.branch) for t, st in zip(turned, state)]
        )

    out_rows = groups * own_rows
    half = seq_len // 2
    turned = order.tie(turned)
    out_odd = order.mark(jnp.concatenate([out_block(k).astype(BF) for k in range(1, n, 2)], axis=0))
    out_got = swap(out_odd, 1)
    attend_back(0)
    out_got = order.tie(out_got)
    out_sums = [out_block(2 * m) + out_got[m * out_rows : (m + 1) * out_rows].astype(F32) for m in range(n // 2)]
    order.mark(out_sums)
    out_came = scatter_start(out_sums)
    project_back_odd(0)
    out_sent = scatter_relay(out_sums, order.pause(out_came))
    project_back_even(0)
    for b in later:
        attend_back(b)
        g_up, g_down = order.pause((g_up, g_down))
    out_sum = order.mark(scatter_join(out_sums, order.tie(out_sent)))
    for b in later:
        state[b - 1].one_sent = pass_on(b - 1, "one_sums", "one_came")
        project_back_odd(b)
    lefts = [part for st in state for part in (st.even, st.odd)]
    rights = [part for st in state for part in (st.grad_qkv[:half], st.grad_qkv[half:])]
    g_w_qkv = order.mark(weight_grad(order.tie(lefts), rights, 1024, 768))
    if near:
        qkv_steps = Steps(order, line_scatter(g_w_qkv.reshape(groups, n * own_rows, 3 * head_cols)))
    else:
        g_qkv = lax.psum_scatter(g_w_qkv, "dp", scatter_dimension=0, tiled=True)
    for b in later:
        project_back_even(b)
        finish(b - 1)
    if near:
        qkv_steps.step()
    for b in later:
        state[b].one_sent = pass_on(b, "one_sums", "one_came")
    g_up = out_of(order.tie(g_up).reshape(n, own_rows, groups * own_hidden))
    if near:
        qkv_steps.step()
    g_out = scatter_groups(out_sum)
    for b in later:
        finish(b)
    if near:
        g_qkv = qkv_steps.finish().astype(BF)

    def summed(name):
        return add_all([after(getattr(st, name), g_w_qkv) for st in state])

    g_down = order.tie(g_down).astype(F32)
    g_up = g_up.reshape(n, own_rows, groups, own_hidden).transpose(1, 2, 0, 3).reshape(own_rows, hidden_units).astype(F32)
    g_qkv = out_of(g_qkv.reshape(n, own_rows, 3 * head_cols))
    g_qkv = g_qkv.reshape(n, own_rows, 3, head_cols).transpose(2, 1, 0, 3).reshape(3, own_rows, width).astype(F32)

    g_b_qkv = summed("g_b_qkv").reshape(3, head_cols)
    own_bias = jnp.zeros((2, width), F32)
    own_bias = lax.dynamic_update_slice(own_bias, jnp.stack([g_b_qkv[0], g_b_qkv[2]]), (0, place * head_cols))
    g_b_up = jnp.sum(summed("sums_even") + summed("sums_odd"), axis=0).reshape(groups, 1, own_hidden)
    spread_up = lax.dynamic_update_slice_in_dim(jnp.zeros((groups, n, own_hidden), F32), g_b_up, place, 1)
    names = ("g_gain_one", "g_shift_one", "g_b_out", "g_gain_two", "g_shift_two", "g_b_down")
    vectors = jnp.concatenate([jnp.stack([summed(name) for name in names]), own_bias], axis=0)
    count = vectors.shape[0]
    vectors = vectors.reshape(count, groups * n, own_rows).transpose(1, 0, 2).reshape(groups * n, count * own_rows)
    sq = jnp.broadcast_to(summed("local_sq"), (groups * n, 1))
    tail = jnp.concatenate([vectors, spread_up.reshape(groups * n, own_hidden), sq], axis=1)
    tail = scatter_small(tail)
    vectors = tail[: count * own_rows].reshape(count, own_rows)
    g_b_query, g_b_value, g_b_up = vectors[6], vectors[7], tail[count * own_rows : -1]
    mean_loss = tail[-1] / (total_count * width)
    return (
        jnp.stack([st.result.astype(BF) for st in state]),
        mean_loss,
        jnp.stack([st.grad_inputs for st in state]),
        vectors[0],
        vectors[1],
        g_qkv[0],
        g_b_query,
        g_qkv[1],
        g_qkv[2],
        g_b_value,
        g_out,
        vectors[2],
        vectors[3],
        vectors[4],
        g_up,
        g_b_up,
        g_down,
        vectors[5],
    )


def solution(mesh):
    rows3, rows2, flat, mat = P("dp", "seq", None), P("dp", "seq"), P(("dp", "seq")), P(("dp", "seq"), None)
    placed = (
        rows3, rows3, rows2, P("dp"), rows2, flat, flat, mat, flat, mat, mat, flat, mat, flat, flat, flat, mat, flat, mat, flat,
    )
    out = (rows3, P(), rows3, flat, flat, mat, flat, mat, mat, flat, mat, flat, flat, flat, mat, flat, mat, flat)
    return jax.shard_map(local, mesh=mesh, in_specs=placed, out_specs=out, check_vma=False)
```

```python
import functools
import types

import jax
import jax.numpy as jnp
from jax import lax
from jax.experimental import pallas as pl
from jax.experimental.pallas import tpu as pltpu
from jax.sharding import PartitionSpec as P

HD = 64
NSUM = 50
NORM_EPS = 1e-05
NEG_FILL = -1e30
PRODUCT_GRANT, LARGE_GRANT = 30 << 20, 56 << 20
BF = jnp.bfloat16
F32 = jnp.float32


def dot(left_in, right_in):
    return jnp.dot(left_in, right_in, preferred_element_type=F32)


def dot_tn(left_in, right_in):
    return lax.dot_general(left_in, right_in, (((0,), (0,)), ((), ())), preferred_element_type=F32)


def dot_nt(left_in, right_in):
    return lax.dot_general(left_in, right_in, (((1,), (1,)), ((), ())), preferred_element_type=F32)


def norm_core(values):
    center = values - jnp.mean(values, axis=-1, keepdims=True)
    inverse = lax.rsqrt(jnp.mean(center * center, axis=-1, keepdims=True) + NORM_EPS)
    return center * inverse, inverse


def norm_back(grad_out, normed, inverse, gain_in):
    grad_normed = grad_out * gain_in
    inner_one = jnp.mean(grad_normed, axis=-1, keepdims=True)
    inner_two = jnp.mean(grad_normed * normed, axis=-1, keepdims=True)
    grad_in = inverse * (grad_normed - inner_one - normed * inner_two)
    return grad_in, jnp.sum(grad_out * normed, axis=0), jnp.sum(grad_out, axis=0)


def swap(values, mask):
    n = lax.axis_size("seq")
    return lax.ppermute(values, "seq", [(i, i ^ mask) for i in range(n)])


def gather_start(own):
    return (swap(own, 2), swap(own, 4)) if lax.axis_size("seq") == 8 else ()


def gather_relay(own, came):
    if lax.axis_size("seq") != 8:
        return ()
    half = own.shape[0] // 2
    return swap(came[1][:half], 2), swap(came[0][half:], 4)


def gather_join(own, came, relayed):
    if lax.axis_size("seq") == 8:
        return jnp.concatenate([own, *came, *relayed], axis=0)
    same, step = own, 2
    while step < lax.axis_size("seq"):
        same = jnp.concatenate([same, swap(same, step)], axis=0)
        step *= 2
    return same


def gather_rows(own):
    came = gather_start(own)
    same = gather_join(own, came, gather_relay(own, came))
    return same, swap(same, 1)


def scatter_start(blocks):
    if lax.axis_size("seq") != 8:
        return ()
    six = blocks[3].astype(BF)
    half = six.shape[0] // 2
    return swap(six[:half], 2), swap(six[half:], 4)


def scatter_halves(blocks, came):
    if lax.axis_size("seq") != 8:
        return ()
    _, two, four, _ = blocks
    half, width = two.shape[0] // 2, two.shape[1]
    which = lax.broadcasted_iota(jnp.int32, (2, half, width), 0)

    def with_half(block, part, side):
        part = jnp.where(which == side, part.astype(F32)[None], 0.0)
        return (block.reshape(2, half, width) + part).astype(BF).reshape(2 * half, width)

    return with_half(two, came[1], 1), with_half(four, came[0], 0)


def scatter_relay(halves):
    return (swap(halves[0], 2), swap(halves[1], 4)) if halves else ()


def scatter_join(blocks, relayed):
    n = lax.axis_size("seq")
    if n == 8:
        return blocks[0] + relayed[0].astype(F32) + relayed[1].astype(F32)
    step = n // 2
    while step > 1:
        keep = len(blocks) // 2
        sent = [swap(block.astype(BF), step).astype(F32) for block in blocks[keep:]]
        blocks = [block.astype(F32) + got for block, got in zip(blocks[:keep], sent)]
        step //= 2
    return blocks[0]


def scatter_groups(rows):
    bit, index = lax.axis_size("dp") // 2, lax.axis_index("dp")
    while bit > 0:
        half = rows.shape[0] // 2
        upper = (index & bit) != 0
        sent = jnp.where(upper, rows[:half], rows[half:]).astype(BF)
        rows = jnp.where(upper, rows[half:], rows[:half]) + exchange(sent, "dp", bit).astype(F32)
        bit //= 2
    return rows


def exchange(values, axis, bit):
    size = lax.axis_size(axis)
    return lax.ppermute(values, axis, [(i, i ^ bit) for i in range(size)])


class Order:
    def __init__(self):
        self.last = ()

    def tie(self, value):
        if not jax.tree.leaves(value) or not jax.tree.leaves(self.last):
            return value
        return lax.optimization_barrier((value, self.last))[0]

    def mark(self, value):
        if jax.tree.leaves(value):
            self.last = value
        return value

    def pause(self, value):
        return self.mark(self.tie(value))


def doubling(held, axes):
    for axis in axes:
        bit, index = 1, lax.axis_index(axis)
        while bit < lax.axis_size(axis):
            other = yield exchange(held, axis, bit)
            upper = (index & bit) != 0
            held = jnp.concatenate([jnp.where(upper, other, held), jnp.where(upper, held, other)], axis=0)
            bit *= 2
    return held


def line_scatter(parts):
    size, index = lax.axis_size("dp"), lax.axis_index("dp")

    def part(which):
        return lax.dynamic_index_in_dim(parts, jnp.clip(which, 0, size - 1), 0, keepdims=False)

    right = left = None
    for step in range(size - 1):
        far = size - 1 - step
        up, down = part(index + far), part(index - far)
        if step:
            up, down = (up.astype(F32) + right.astype(F32)).astype(BF), (down.astype(F32) + left.astype(F32)).astype(BF)
        flight = (
            lax.ppermute(up, "dp", [(i, i + 1) for i in range(size - far)]),
            lax.ppermute(down, "dp", [(i, i - 1) for i in range(far, size)]),
        )
        right, left = yield flight
    return part(index).astype(F32) + right.astype(F32) + left.astype(F32)


class Steps:
    def __init__(self, order, generator):
        self.order, self.generator, self.flight, self.result = order, generator, next(generator), None

    def step(self, count=1):
        for _ in range(count):
            if self.flight is None:
                return
            try:
                self.flight = self.generator.send(self.order.pause(self.flight))
            except StopIteration as stop:
                self.flight, self.result = None, stop.value

    def finish(self):
        while self.flight is not None:
            self.step()
        return self.result


def scatter_small(table):
    count, width = table.shape
    length = -(-width // 1024) * 1024
    held = jnp.pad(table, ((0, 0), (0, length - width))).reshape(count, 8, length // 8)
    for axis in ("dp", "seq"):
        bit, index = lax.axis_size(axis) // 2, lax.axis_index(axis)
        while bit > 0:
            half = held.shape[0] // 2
            upper = (index & bit) != 0
            sent = jnp.where(upper, held[:half], held[half:])
            held = jnp.where(upper, held[half:], held[:half]) + exchange(sent, axis, bit)
            bit //= 2
    return held.reshape(length)[:width]


def after(value, *earlier):
    return lax.optimization_barrier((value, *earlier))[0]


def weight_grad_kernel(*refs):
    count = (len(refs) - 1) // 2
    total = dot_tn(refs[0][...], refs[count][...])
    for part in range(1, count):
        total = total + dot_tn(refs[part][...], refs[count + part][...])
    refs[-1][...] = total.astype(BF)


def weight_grad(lefts, rights, left_tile, right_tile):
    rows, left_width = lefts[0].shape
    right_width = rights[0].shape[1]
    left_tile, right_tile = min(left_tile, left_width), min(right_tile, right_width)
    count = len(lefts)
    return pl.pallas_call(
        weight_grad_kernel,
        grid=(right_width // right_tile, left_width // left_tile),
        in_specs=[pl.BlockSpec((rows, left_tile), lambda j, i: (0, i))] * count
        + [pl.BlockSpec((rows, right_tile), lambda j, i: (0, j))] * count,
        out_specs=pl.BlockSpec((left_tile, right_tile), lambda j, i: (i, j)),
        out_shape=jax.ShapeDtypeStruct((left_width, right_width), BF),
        compiler_params=pltpu.CompilerParams(dimension_semantics=("arbitrary", "arbitrary"), vmem_limit_bytes=LARGE_GRANT),
        cost_estimate=light_cost(2 * count * rows * left_width * right_width),
        name="weight_grad",
    )(*lefts, *rights)


def tile_dot(left, right, turned):
    return dot_nt(left, right) if turned else dot(left, right)


def plain_kernel(left_ref, right_ref, out_ref, *, turned):
    out_ref[...] = tile_dot(left_ref[...], right_ref[...], turned).astype(out_ref.dtype)


def project_kernel(left_ref, right_ref, bias_ref, scale_ref, out_ref):
    out_ref[...] = ((dot(left_ref[...], right_ref[...]) + bias_ref[...]) * scale_ref[...]).astype(BF)


def up_kernel(left_ref, right_ref, bias_ref, out_ref):
    out_ref[...] = jnp.maximum(dot(left_ref[...], right_ref[...]) + bias_ref[...], 0.0).astype(BF)


def masked_kernel(left_ref, right_ref, act_ref, out_ref, sums_ref):
    grad = jnp.where(act_ref[...] > 0, dot_nt(left_ref[...], right_ref[...]), 0.0).astype(BF)
    out_ref[...] = grad
    part = jnp.sum(grad.astype(F32).reshape(-1, 8, grad.shape[1]), axis=0)

    @pl.when(pl.program_id(1) == 0)
    def _():
        sums_ref[...] = part

    @pl.when(pl.program_id(1) > 0)
    def _():
        sums_ref[...] = sums_ref[...] + part


def blocks_kernel(left_ref, right_ref, got_ref, *out_refs, turned):
    rows = out_refs[0].shape[0]
    for m in range(len(out_refs) - 1, -1, -1):
        cut = slice(m * rows, (m + 1) * rows)
        total = tile_dot(left_ref[cut, :], right_ref[...], turned) + got_ref[cut, :].astype(F32)
        out_refs[m][...] = total.astype(out_refs[m].dtype)


def light_cost(flops):
    return pl.CostEstimate(flops=int(flops) // 8, bytes_accessed=1, transcendentals=0)


def tiled(kernel, name, left, right, turned, extras, outs, row_tile, col_tile, parts=1):
    rows, depth = left.shape
    cols = right.shape[0] if turned else right.shape[1]
    row_tile, col_tile = min(row_tile, rows), min(col_tile, cols)
    kinds = {
        "both": pl.BlockSpec((row_tile, col_tile), lambda j, m: (m, j)),
        "vector": pl.BlockSpec((1, col_tile), lambda j, m: (0, j)),
        "sums": pl.BlockSpec((8, col_tile), lambda j, m: (0, j)),
        "block": pl.BlockSpec((rows // parts, col_tile), lambda j, m: (0, j)),
    }
    shapes = {"both": (rows, cols), "sums": (8, cols), "block": (rows // parts, cols)}
    right_spec = (
        pl.BlockSpec((col_tile, depth), lambda j, m: (j, 0)) if turned else pl.BlockSpec((depth, col_tile), lambda j, m: (0, j))
    )
    return pl.pallas_call(
        kernel,
        grid=(cols // col_tile, rows // row_tile),
        in_specs=[pl.BlockSpec((row_tile, depth), lambda j, m: (m, 0)), right_spec] + [kinds[k] for k, _ in extras],
        out_specs=[kinds[k] for k, _ in outs],
        out_shape=[jax.ShapeDtypeStruct(shapes[k], dtype) for k, dtype in outs],
        compiler_params=pltpu.CompilerParams(dimension_semantics=("arbitrary", "arbitrary"), vmem_limit_bytes=PRODUCT_GRANT),
        cost_estimate=light_cost(2 * rows * cols * depth),
        name=name,
    )(left, right, *[value for _, value in extras])


def plain_product(left, right, turned=False):
    kernel = functools.partial(plain_kernel, turned=turned)
    return tiled(kernel, "product", left, right, turned, [], [("both", BF)], 1024, 256)[0]


def project_product(left, right, bias, scale):
    extras = [("vector", bias.reshape(1, -1)), ("vector", scale.reshape(1, -1))]
    return tiled(project_kernel, "project", left, right, False, extras, [("both", BF)], 1024, 256)[0]


def up_product(left, right, bias):
    return tiled(up_kernel, "up", left, right, False, [("vector", bias.reshape(1, -1))], [("both", BF)], 1024, 256)[0]


def masked_product(left, right, act):
    outs = [("both", BF), ("sums", F32)]
    return tiled(masked_kernel, "masked_product", left, right, True, [("both", act)], outs, 1024, 256)


def block_products(left, right, got, count, turned=False):
    kernel = functools.partial(blocks_kernel, turned=turned)
    outs = [("block", F32)] * (count - 1) + [("block", BF)]
    return tiled(
        kernel, "block_products", left, right, turned, [("both", got)], outs, left.shape[0], 256, count
    )


def visible_scores(q_head, k_block, first, q_place, key_start, length):
    scores = dot_nt(q_head, k_block)
    k_place = key_start + lax.broadcasted_iota(jnp.int32, (1, length), 1)
    allowed = (k_place >= first) & (k_place <= q_place)
    return jnp.where(allowed, scores, NEG_FILL)


def storage_row(block, place, blocks, length):
    k = block ^ place
    return pl.multiple_of(((k >> 1) + (k & 1) * (blocks // 2)) * length, length)


def spread_heads(source_ref, target_ref, lanes, heads, length, blocks):
    def one(m, carry):
        rows = source_ref[pl.ds(pl.multiple_of(m * length, length), length), :]
        for h in range(heads):
            target = pl.ds(pl.multiple_of((m * heads + h) * length, length), length)
            target_ref[target, :] = jnp.where(lanes == h, rows, jnp.zeros_like(rows))
        return carry

    lax.fori_loop(0, blocks, one, 0)


def fold(values, op):
    out = values[:, :128]
    for start in range(128, values.shape[1], 128):
        out = op(out, values[:, start : start + 128])
    return out


def attend_forward_kernel(
    place_ref, low_ref, q_ref, k_ref, v_ref, first_ref, o_ref, lse_ref, s_scr, m_scr, l_scr, v_scr, *, heads, length, blocks
):
    i = pl.program_id(0)
    place = place_ref[0]
    low = low_ref[i]
    width = heads * HD
    lanes = lax.broadcasted_iota(jnp.int32, (length, width), 1) // HD
    q_all = q_ref[...]
    q_heads = [jnp.where(lanes == h, q_all, jnp.zeros_like(q_all)) for h in range(heads)]
    first = first_ref[...]
    q_place = i * length + lax.broadcasted_iota(jnp.int32, (length, 1), 0)
    m_scr[...] = jnp.full_like(m_scr, NEG_FILL)
    l_scr[...] = jnp.zeros_like(l_scr)

    @pl.when(i == 0)
    def _():
        spread_heads(v_ref, v_scr, lanes, heads, length, blocks)

    def score_step(j, carry):
        k_block = k_ref[pl.ds(storage_row(j, place, blocks, length), length), :]
        cols = pl.ds(pl.multiple_of(j * length, length), length)
        for h in range(heads):
            scores = visible_scores(q_heads[h], k_block, first, q_place, j * length, length)
            s_scr[h, :, cols] = scores
            m_scr[h] = jnp.maximum(m_scr[h], fold(scores, jnp.maximum))
        return carry

    lax.fori_loop(low, i + 1, score_step, 0)
    tops = [jnp.max(m_scr[h], axis=-1, keepdims=True) for h in range(heads)]

    def exp_step(j, carry):
        cols = pl.ds(pl.multiple_of(j * length, length), length)
        for h in range(heads):
            raised = jnp.exp(s_scr[h, :, cols] - tops[h])
            s_scr[h, :, cols] = raised
            l_scr[h] = l_scr[h] + fold(raised, jnp.add)
        return carry

    lax.fori_loop(low, i + 1, exp_step, 0)
    totals = [jnp.sum(l_scr[h], axis=-1, keepdims=True) for h in range(heads)]
    scales = [1.0 / total for total in totals]

    def mix_step(j, acc):
        rows = pl.ds(pl.multiple_of(storage_row(j, place, blocks, length) * heads, heads * length), heads * length)
        cols = pl.ds(pl.multiple_of(j * length, length), length)
        probs = [(s_scr[h, :, cols] * scales[h]).astype(BF) for h in range(heads)]
        return acc + dot(jnp.concatenate(probs, axis=1), v_scr[rows, :])

    mixed = lax.fori_loop(low, i + 1, mix_step, jnp.zeros((length, width), F32))
    o_ref[...] = mixed.astype(BF)
    cols = lax.broadcasted_iota(jnp.int32, (length, 128), 1)
    lse = jnp.zeros((length, 128), F32)
    for h in range(heads):
        lse = jnp.where(cols == h, tops[h] + jnp.log(totals[h]), lse)
    lse_ref[...] = lse


def attend_backward_kernel(
    place_ref, low_ref, q_ref, go_ref, o_ref, lse_ref, k_ref, v_ref, first_ref, grad_ref, kt_scr, vt_scr, k_scr, *, heads, length,
    blocks
):
    i = pl.program_id(0)
    place = place_ref[0]
    low = low_ref[i]
    width = heads * HD
    lanes = lax.broadcasted_iota(jnp.int32, (length, width), 1) // HD
    first = first_ref[...]
    q_place = i * length + lax.broadcasted_iota(jnp.int32, (length, 1), 0)
    q_all, go_all = q_ref[...], go_ref[...]
    inner_all = go_all.astype(F32) * o_ref[...].astype(F32)
    q_turned, go_turned = q_all.astype(F32).T.astype(BF), go_all.astype(F32).T.astype(BF)
    lse_all = lse_ref[...]
    q_heads, go_heads, inner, lse = [], [], [], []
    for h in range(heads):
        mine = lanes == h
        q_heads.append(jnp.where(mine, q_all, jnp.zeros_like(q_all)))
        go_heads.append(jnp.where(mine, go_all, jnp.zeros_like(go_all)))
        inner.append(jnp.sum(jnp.where(mine, inner_all, 0.0), axis=-1, keepdims=True))
        lse.append(lse_all[:, h : h + 1])

    @pl.when(i == 0)
    def _():
        kt_scr[...] = jnp.zeros_like(kt_scr)
        vt_scr[...] = jnp.zeros_like(vt_scr)
        spread_heads(k_ref, k_scr, lanes, heads, length, blocks)

    def step(j, acc):
        start = storage_row(j, place, blocks, length)
        rows = pl.ds(start, length)
        k_block, v_block = k_ref[rows, :], v_ref[rows, :]
        k_place = j * length + lax.broadcasted_iota(jnp.int32, (1, length), 1)
        allowed = (k_place >= first) & (k_place <= q_place)
        every = range(heads)
        scores = [dot_nt(q_heads[h], k_block) for h in every]
        grad_probs = [dot_nt(go_heads[h], v_block) for h in every]
        probs = [jnp.exp(jnp.where(allowed, scores[h] - lse[h], NEG_FILL)) for h in every]
        grad_scores = [(probs[h] * (grad_probs[h] - inner[h])).astype(BF) for h in every]
        for h in every:
            part = slice(h * HD, (h + 1) * HD)
            vt_scr[part, rows] = vt_scr[part, rows] + dot(go_turned[part, :], probs[h].astype(BF))
            kt_scr[part, rows] = kt_scr[part, rows] + dot(q_turned[part, :], grad_scores[h])
        spread = pl.ds(pl.multiple_of(start * heads, heads * length), heads * length)
        return acc + dot(jnp.concatenate(grad_scores, axis=1), k_scr[spread, :])

    grad_q = lax.fori_loop(low, i + 1, step, jnp.zeros((length, width), F32))
    own_rows = pl.ds(storage_row(i, place, blocks, length), length)
    grad_ref[own_rows, 0:width] = (grad_q.astype(BF).astype(F32) * (HD**-0.5)).astype(BF)

    @pl.when(i == blocks - 1)
    def _():
        for j in range(blocks):
            rows = slice(j * length, (j + 1) * length)
            grad_ref[rows, width : 2 * width] = kt_scr[:, rows].T.astype(BF)
            grad_ref[rows, 2 * width : 3 * width] = vt_scr[:, rows].T.astype(BF)


def storage_map(length, blocks, column):
    def index(i, place_ref, low_ref):
        k = i ^ place_ref[0]
        return ((k >> 1) + (k & 1) * (blocks // 2), column)

    return index


def attend_forward(place, low, qkv, first, length):
    rows, triple = qkv.shape
    width, blocks = triple // 3, rows // length
    heads = width // HD
    return pl.pallas_call(
        functools.partial(attend_forward_kernel, heads=heads, length=length, blocks=blocks),
        grid_spec=pltpu.PrefetchScalarGridSpec(
            num_scalar_prefetch=2,
            grid=(blocks,),
            in_specs=[
                pl.BlockSpec((length, width), storage_map(length, blocks, 0)),
                pl.BlockSpec((rows, width), lambda i, p, w: (0, 1)),
                pl.BlockSpec((rows, width), lambda i, p, w: (0, 2)),
                pl.BlockSpec((length, 1), lambda i, p, w: (i, 0)),
            ],
            out_specs=[
                pl.BlockSpec((length, width), lambda i, p, w: (i, 0)),
                pl.BlockSpec((length, 128), lambda i, p, w: (i, 0)),
            ],
            scratch_shapes=[
                pltpu.VMEM((heads, length, rows), F32),
                pltpu.VMEM((heads, length, 128), F32),
                pltpu.VMEM((heads, length, 128), F32),
                pltpu.VMEM((heads * rows, width), BF),
            ],
        ),
        out_shape=[jax.ShapeDtypeStruct((rows, width), BF), jax.ShapeDtypeStruct((rows, 128), F32)],
        compiler_params=pltpu.CompilerParams(dimension_semantics=("arbitrary",), vmem_limit_bytes=LARGE_GRANT),
        cost_estimate=light_cost(24 * rows * rows * width),
        name="attend_forward",
    )(place, low, qkv, qkv, qkv, first)


def attend_backward(place, low, qkv, grad_out, mixed, lse, first, length):
    rows, triple = qkv.shape
    width, blocks = triple // 3, rows // length
    heads = width // HD
    return pl.pallas_call(
        functools.partial(attend_backward_kernel, heads=heads, length=length, blocks=blocks),
        grid_spec=pltpu.PrefetchScalarGridSpec(
            num_scalar_prefetch=2,
            grid=(blocks,),
            in_specs=[
                pl.BlockSpec((length, width), storage_map(length, blocks, 0)),
                pl.BlockSpec((length, width), lambda i, p, w: (i, 0)),
                pl.BlockSpec((length, width), lambda i, p, w: (i, 0)),
                pl.BlockSpec((length, 128), lambda i, p, w: (i, 0)),
                pl.BlockSpec((rows, width), lambda i, p, w: (0, 1)),
                pl.BlockSpec((rows, width), lambda i, p, w: (0, 2)),
                pl.BlockSpec((length, 1), lambda i, p, w: (i, 0)),
            ],
            out_specs=pl.BlockSpec((rows, triple), lambda i, p, w: (0, 0)),
            scratch_shapes=[
                pltpu.VMEM((width, rows), F32),
                pltpu.VMEM((width, rows), F32),
                pltpu.VMEM((heads * rows, width), BF),
            ],
        ),
        out_shape=jax.ShapeDtypeStruct((rows, triple), BF),
        compiler_params=pltpu.CompilerParams(dimension_semantics=("arbitrary",), vmem_limit_bytes=LARGE_GRANT),
        cost_estimate=light_cost(36 * rows * rows * width),
        name="attend_backward",
    )(place, low, qkv, grad_out, mixed, lse, qkv, qkv, first)


def local(
    inputs,
    teacher,
    segment_ids,
    summary_start,
    valid_mask,
    attn_norm_gain,
    attn_norm_bias,
    query_weight,
    query_bias,
    key_weight,
    value_weight,
    value_bias,
    out_weight,
    out_bias,
    mlp_norm_gain,
    mlp_norm_bias,
    up_weight,
    up_bias,
    down_weight,
    down_bias,
):
    seqs, length = segment_ids.shape
    width = inputs.shape[-1]
    hidden_units = up_weight.shape[1]
    n, groups = lax.axis_size("seq"), lax.axis_size("dp")
    place, group = lax.axis_index("seq"), lax.axis_index("dp")
    both = ("dp", "seq")
    seq_len = length * n
    tokens_all = seqs * seq_len * groups
    scale = HD**-0.5
    own_rows = query_weight.shape[0]
    own_hidden = up_bias.shape[0]
    head_cols = width // n

    def out_of(value):
        return lax.all_to_all(value, "seq", split_axis=0, concat_axis=0, tiled=True)

    valid = valid_mask.astype(F32)
    order = Order()
    near = n == 8 and groups == 4
    out_steps = Steps(order, doubling(out_weight[None], ("dp",))) if near else None
    cut = jnp.concatenate(
        [w.reshape(own_rows, n, head_cols).transpose(1, 0, 2) for w in (query_weight, key_weight, value_weight)], axis=2
    )
    qkv_cut = out_of(cut)
    small = [attn_norm_gain, attn_norm_bias, out_bias, mlp_norm_gain, mlp_norm_bias, down_bias, query_bias, value_bias, up_bias]
    pieces = [v.astype(F32) for v in small] + [segment_ids.astype(F32).reshape(-1), jnp.sum(valid).reshape(1)]
    starts, lines = [], []
    for piece in pieces:
        starts.append(sum(line.shape[0] for line in lines))
        short = -piece.shape[0] % 128
        lines.append(jnp.pad(piece, (0, short)).reshape(-1, 128))
    used = sum(line.shape[0] for line in lines)
    packed = jnp.pad(jnp.concatenate(lines, axis=0), ((0, -used % 8), (0, 0)))[None]
    small_steps = Steps(order, doubling(after(packed, cut), ("dp", "seq")))
    if near:
        out_steps.step()
    small_steps.step(3)
    qkv_cut = order.pause(qkv_cut).reshape(n * own_rows, 3 * head_cols)
    w_qkv = lax.all_gather(qkv_cut, "dp", axis=0, tiled=True)
    small_steps.step(1)
    if near:
        own_out = out_steps.finish().reshape(-1, width)
    packed = small_steps.finish().reshape(n, groups, -1, 128).transpose(1, 0, 2, 3).reshape(groups * n, -1, 128)

    def zero_after(value):
        return jnp.minimum(jnp.abs(value.reshape(-1)[0].astype(F32)), 0.0).astype(jnp.int32)

    def rows_after(b, value):
        return lax.dynamic_index_in_dim(inputs, b + zero_after(value), 0, keepdims=False)

    state = [types.SimpleNamespace() for _ in range(seqs)]
    state[0].own = rows_after(0, packed)
    state[0].came = gather_start(state[0].own)
    parts = []
    for piece, at in zip(pieces, starts):
        count = -(-piece.shape[0] // 128)
        parts.append(packed[:, at : at + count].reshape(groups * n, -1)[:, : piece.shape[0]])
    gain_one, shift_one, b_out, gain_two, shift_two, b_down = [part.reshape(-1) for part in parts[:6]]
    b_query, b_value = [lax.dynamic_slice_in_dim(part.reshape(-1), place * head_cols, head_cols) for part in parts[6:8]]
    b_up = lax.dynamic_index_in_dim(parts[8].reshape(groups, n, -1), place, 1, keepdims=False).reshape(-1)
    ids = lax.dynamic_index_in_dim(parts[9].reshape(groups, n, seqs, length), group, 0, keepdims=False)
    ids = ids.transpose(1, 0, 2).reshape(seqs, seq_len)
    total_count = jnp.sum(parts[10])

    up_cut = up_weight.reshape(own_rows, groups, n, own_hidden).transpose(2, 0, 1, 3).reshape(n, own_rows, groups * own_hidden)
    b_qkv = jnp.concatenate([b_query, jnp.zeros_like(b_query), b_value])
    s_qkv = jnp.concatenate([jnp.full((head_cols,), scale, F32), jnp.ones((2 * head_cols,), F32)])

    place_arr = place.reshape(1).astype(jnp.int32)
    positions = jnp.arange(seq_len, dtype=jnp.int32)

    def add_all(terms):
        out = terms[0]
        for term in terms[1:]:
            out = out + term
        return out


    def spans(b):
        st = state[b]
        first = jnp.sum((ids[b][None, :] < ids[b][:, None]).astype(jnp.int32), axis=1)
        in_summary = (positions >= summary_start[b]) & (positions < summary_start[b] + NSUM)
        first = jnp.where(in_summary, 0, first)
        st.low = jnp.min(first.reshape(n, length), axis=1) // length
        st.first = first.reshape(seq_len, 1)

    def ready(rows):
        return (norm_core(rows.astype(F32))[0] * gain_one + shift_one).astype(BF)

    def project(b):
        st = state[b]
        even, odd = order.tie((st.even, st.odd))
        parts = [project_product(part, w_qkv, b_qkv, s_qkv) for part in (even, odd)]
        st.qkv = order.mark(jnp.concatenate(parts, axis=0))

    def attend(b):
        st = state[b]
        qkv = order.tie(st.qkv)
        st.mixed, st.lse = attend_forward(place_arr, st.low, qkv, st.first, length)
        order.mark(st.mixed)

    def send_mixed(b):
        st = state[b]
        st.moved = out_of(st.mixed.reshape(n, length, head_cols))

    def middle(b):
        st = state[b]
        attended = order.tie(st.moved)
        st.attended = attended.transpose(1, 0, 2).reshape(length, width)
        rows = inputs[b].astype(F32)
        st.hidden = rows + (dot(st.attended, w_out) + b_out)
        st.normed_two, st.inverse_two = norm_core(st.hidden)
        st.own_two = order.mark((st.normed_two * gain_two + shift_two).astype(BF))
        st.came_two = gather_start(st.own_two)

    def up_even(b):
        st = state[b]
        st.act_even = order.mark(up_product(order.tie(st.even_two), w_up, b_up))

    def up_odd(b):
        st = state[b]
        st.act_odd = order.mark(up_product(order.tie(st.odd_two), w_up, b_up))

    def relay(b, own, came):
        st = state[b]
        came = order.pause(getattr(st, came))
        return came, gather_relay(getattr(st, own), came)

    def join(b, own, came_relayed):
        same = order.mark(gather_join(getattr(state[b], own), *order.tie(came_relayed)))
        return same, swap(same, 1)

    def down_odd(b):
        st = state[b]
        st.down_got = swap(order.mark(plain_product(order.tie(st.act_odd), w_down)), 1)

    def down_even(b):
        st = state[b]
        st.down_sums = order.mark(block_products(st.act_even, w_down, order.tie(st.down_got), n // 2))
        st.down_came = scatter_start(st.down_sums)

    def pass_on(b, sums, came):
        st = state[b]
        came = order.pause(getattr(st, came))
        return scatter_relay(order.mark(scatter_halves(getattr(st, sums), came)))

    def misfit(b):
        st = state[b]
        summed = scatter_join(st.down_sums, order.tie(st.down_sent))
        st.result = st.hidden + (summed + b_down)
        error = st.result - teacher[b].astype(F32)
        st.local_sq = jnp.sum(jnp.sum(error * error, axis=-1) * valid[b])
        st.grad_result = error * (valid[b] * (tokens_all / total_count))[:, None]
        st.own_grad = order.mark(st.grad_result.astype(BF))
        st.g_b_down = jnp.sum(st.own_grad.astype(F32), axis=0)
        st.came_grad = gather_start(st.own_grad)

    def act_back_even(b):
        st = state[b]
        st.pre_even, st.sums_even = masked_product(order.tie(st.gm_even), w_down, st.act_even)
        order.mark(st.pre_even)

    def act_back_odd(b):
        st = state[b]
        st.pre_odd, st.sums_odd = masked_product(order.tie(st.gm_odd), w_down, st.act_odd)
        order.mark(st.pre_odd)

    def up_back_odd(b):
        st = state[b]
        st.up_got = swap(order.mark(plain_product(order.tie(st.pre_odd), w_up, turned=True)), 1)

    def up_back_even(b):
        st = state[b]
        st.up_sums = order.mark(block_products(st.pre_even, w_up, order.tie(st.up_got), n // 2, turned=True))
        st.up_came = scatter_start(st.up_sums)

    def branch_back(b):
        st = state[b]
        grad_ready = scatter_join(st.up_sums, order.tie(st.up_sent))
        grad_norm, st.g_gain_two, st.g_shift_two = norm_back(grad_ready, st.normed_two, st.inverse_two, gain_two)
        st.grad_hidden = st.grad_result + grad_norm
        st.branch = st.grad_hidden.astype(BF)
        st.g_b_out = jnp.sum(st.branch.astype(F32), axis=0)
        grad_att = dot_nt(st.branch, w_out).astype(BF).reshape(length, n, head_cols).transpose(1, 0, 2)
        st.grad_mixed = out_of(order.mark(grad_att)).reshape(seq_len, head_cols)

    def attend_back(b):
        st = state[b]
        st.grad_qkv = attend_backward(
            place_arr, st.low, st.qkv, order.tie(st.grad_mixed), st.mixed, st.lse, st.first, length
        )
        order.mark(st.grad_qkv)
        st.g_b_qkv = jnp.sum(st.grad_qkv.astype(F32), axis=0)

    def project_back_odd(b):
        st = state[b]
        odd = order.tie(st.grad_qkv)[seq_len // 2 :]
        st.one_got = swap(order.mark(plain_product(odd, w_qkv, turned=True)), 1)

    def project_back_even(b):
        st = state[b]
        st.one_sums = block_products(st.grad_qkv[: seq_len // 2], w_qkv, order.tie(st.one_got), n // 2, turned=True)
        order.mark(st.one_sums)
        st.one_came = scatter_start(st.one_sums)

    def finish(b):
        st = state[b]
        grad_ready = scatter_join(st.one_sums, order.tie(st.one_sent))
        normed, inverse = norm_core(inputs[b].astype(F32))
        grad_norm, st.g_gain_one, st.g_shift_one = norm_back(grad_ready, normed, inverse, gain_one)
        st.grad_inputs = order.mark(st.grad_hidden + grad_norm)

    every, later = range(seqs), range(1, seqs)

    def whole_out_weight(own, came, relayed):
        whole = jnp.zeros((groups, n, own_rows, width), BF)
        half = groups // 2
        same = [(0, own, 0), (2, came[0], 0), (4, came[1], 0), (6, relayed[0], 0), (6, relayed[1], half)]
        other = [(k + 1, swap(piece, 1), first) for k, piece, first in same]
        for k, piece, first in same + other:
            whole = lax.dynamic_update_slice(whole, piece.reshape(-1, 1, own_rows, width), (first, place ^ k, 0, 0))
        return whole.reshape(width, width)

    def make_ready(b, raw_even, raw_odd):
        st = state[b]
        st.even = order.mark(ready(order.tie(raw_even)))
        st.odd = order.mark(ready(order.tie(raw_odd)))

    for b in every:
        spans(b)
    came_relayed = relay(0, "own", "came")
    raw = join(0, "own", came_relayed)
    up_cut = out_of(after(up_cut, qkv_cut))
    for b in later:
        state[b].own = rows_after(b, came_relayed[0][0] if near else packed)
        state[b].came = gather_start(state[b].own)
    up_cut = order.pause(up_cut)
    w_up = lax.all_gather(up_cut.reshape(n * own_rows, groups * own_hidden), "dp", axis=0, tiled=True)
    w_down = lax.all_gather(after(down_weight, up_cut), "dp", axis=0, tiled=True)
    if near:
        own_out = order.tie(own_out)
        out_came = gather_start(own_out)
    else:
        w_out = lax.all_gather(after(out_weight, up_cut), both, axis=0, tiled=True)
    make_ready(0, *raw)
    w_qkv = order.pause(w_qkv)
    project(0)
    came_relayed = [relay(b, "own", "came") for b in later]
    if near:
        out_came = order.pause(out_came)
        out_relayed = gather_relay(own_out, out_came)
    attend(0)
    send_mixed(0)
    raw = [join(b, "own", came_relayed[b - 1]) for b in later]
    if near:
        w_out = whole_out_weight(own_out, out_came, order.pause(out_relayed))
    middle(0)
    for b in later:
        last, st = state[b - 1], state[b]
        make_ready(b, *raw[b - 1])
        project(b)
        came_relayed = relay(b - 1, "own_two", "came_two")
        attend(b)
        send_mixed(b)
        last.even_two, last.odd_two = join(b - 1, "own_two", came_relayed)
        up_even(b - 1)
        middle(b)
        up_odd(b - 1)
        came_relayed = relay(b, "own_two", "came_two")
        down_odd(b - 1)
        st.even_two, st.odd_two = join(b, "own_two", came_relayed)
        up_even(b)
        down_even(b - 1)
        up_odd(b)
        last.down_sent = pass_on(b - 1, "down_sums", "down_came")
        down_odd(b)
        down_even(b)
        misfit(b - 1)
        st.down_sent = pass_on(b, "down_sums", "down_came")
        came_relayed = relay(b - 1, "own_grad", "came_grad")
        misfit(b)
        last.gm_even, last.gm_odd = join(b - 1, "own_grad", came_relayed)
        act_back_even(b - 1)
        act_back_odd(b - 1)
        came_relayed = relay(b, "own_grad", "came_grad")
        up_back_odd(b - 1)
        up_back_even(b - 1)
        st.gm_even, st.gm_odd = join(b, "own_grad", came_relayed)
        act_back_even(b)
        last.up_sent = pass_on(b - 1, "up_sums", "up_came")
        act_back_odd(b)
        up_back_odd(b)
        up_back_even(b)
    lefts = [part for st in state for part in (st.even_two, st.odd_two)]
    rights = [part for st in state for part in (st.pre_even, st.pre_odd)]
    g_w_up = order.mark(weight_grad(order.tie(lefts), rights, 512, 1024))
    g_up = lax.psum_scatter(g_w_up, "dp", scatter_dimension=0, tiled=True)
    for b in later:
        state[b].up_sent = pass_on(b, "up_sums", "up_came")
    branch_back(0)
    lefts = [part for st in state for part in (st.act_even, st.act_odd)]
    rights = [part for st in state for part in (st.gm_even, st.gm_odd)]
    g_w_down = order.mark(weight_grad(order.tie(lefts), rights, 256, 1024))
    g_down = lax.psum_scatter(g_w_down, "dp", scatter_dimension=0, tiled=True)
    for b in later:
        branch_back(b)
    turned = [
        st.attended.reshape(length, groups, n, own_rows).transpose(2, 0, 1, 3).reshape(n, length, groups * own_rows)
        for st in state
    ]

    def out_block(k):
        return add_all(
            [dot_tn(lax.dynamic_index_in_dim(t, place ^ k, 0, keepdims=False), st.branch) for t, st in zip(turned, state)]
        )

    out_rows = groups * own_rows
    half = seq_len // 2
    turned = order.tie(turned)
    out_odd = order.mark(jnp.concatenate([out_block(k).astype(BF) for k in range(1, n, 2)], axis=0))
    out_got = swap(out_odd, 1)
    attend_back(0)
    out_got = order.tie(out_got)
    out_sums = [out_block(2 * m) + out_got[m * out_rows : (m + 1) * out_rows].astype(F32) for m in range(n // 2)]
    order.mark(out_sums)
    out_came = scatter_start(out_sums)
    project_back_odd(0)
    out_sent = scatter_relay(order.mark(scatter_halves(out_sums, order.pause(out_came))))
    project_back_even(0)
    for b in later:
        attend_back(b)
    g_up, g_down = order.pause((g_up, g_down))
    g_up = out_of(g_up.reshape(n, own_rows, groups * own_hidden))
    lefts = [part for st in state for part in (st.even, st.odd)]
    rights = [part for st in state for part in (st.grad_qkv[:half], st.grad_qkv[half:])]
    g_w_qkv = order.mark(weight_grad(order.tie(lefts), rights, 1024, 768))
    if near:
        qkv_steps = Steps(order, line_scatter(g_w_qkv.reshape(groups, n * own_rows, 3 * head_cols)))
    else:
        g_qkv = lax.psum_scatter(g_w_qkv, "dp", scatter_dimension=0, tiled=True)
    g_up = order.pause(g_up)
    for b in later:
        state[b - 1].one_sent = pass_on(b - 1, "one_sums", "one_came")
        project_back_odd(b)
    if near:
        qkv_steps.step()
    out_sum = order.mark(scatter_join(out_sums, order.tie(out_sent)))
    for b in later:
        project_back_even(b)
        finish(b - 1)
    if near:
        qkv_steps.step()
    for b in later:
        state[b].one_sent = pass_on(b, "one_sums", "one_came")
    g_out = scatter_groups(out_sum)
    if near:
        g_qkv = order.mark(qkv_steps.finish().astype(BF))
    g_qkv = out_of(g_qkv.reshape(n, own_rows, 3 * head_cols))
    for b in later:
        finish(b)

    def summed(name):
        return add_all([after(getattr(st, name), *state[-1].one_sums) for st in state])

    g_down = order.tie(g_down).astype(F32)
    g_up = g_up.reshape(n, own_rows, groups, own_hidden).transpose(1, 2, 0, 3).reshape(own_rows, hidden_units).astype(F32)
    g_qkv = g_qkv.reshape(n, own_rows, 3, head_cols).transpose(2, 1, 0, 3).reshape(3, own_rows, width).astype(F32)

    g_b_qkv = summed("g_b_qkv").reshape(3, head_cols)
    own_bias = jnp.zeros((2, width), F32)
    own_bias = lax.dynamic_update_slice(own_bias, jnp.stack([g_b_qkv[0], g_b_qkv[2]]), (0, place * head_cols))
    g_b_up = jnp.sum(summed("sums_even") + summed("sums_odd"), axis=0).reshape(groups, 1, own_hidden)
    spread_up = lax.dynamic_update_slice_in_dim(jnp.zeros((groups, n, own_hidden), F32), g_b_up, place, 1)
    names = ("g_gain_one", "g_shift_one", "g_b_out", "g_gain_two", "g_shift_two", "g_b_down")
    vectors = jnp.concatenate([jnp.stack([summed(name) for name in names]), own_bias], axis=0)
    count = vectors.shape[0]
    vectors = vectors.reshape(count, groups * n, own_rows).transpose(1, 0, 2).reshape(groups * n, count * own_rows)
    sq = jnp.broadcast_to(summed("local_sq"), (groups * n, 1))
    tail = jnp.concatenate([vectors, spread_up.reshape(groups * n, own_hidden), sq], axis=1)
    tail = scatter_small(tail)
    vectors = tail[: count * own_rows].reshape(count, own_rows)
    g_b_query, g_b_value, g_b_up = vectors[6], vectors[7], tail[count * own_rows : -1]
    mean_loss = tail[-1] / (total_count * width)
    return (
        jnp.stack([st.result.astype(BF) for st in state]),
        mean_loss,
        jnp.stack([st.grad_inputs for st in state]),
        vectors[0],
        vectors[1],
        g_qkv[0],
        g_b_query,
        g_qkv[1],
        g_qkv[2],
        g_b_value,
        g_out,
        vectors[2],
        vectors[3],
        vectors[4],
        g_up,
        g_b_up,
        g_down,
        vectors[5],
    )


def solution(mesh):
    rows3, rows2, flat, mat = P("dp", "seq", None), P("dp", "seq"), P(("dp", "seq")), P(("dp", "seq"), None)
    placed = (
        rows3, rows3, rows2, P("dp"), rows2, flat, flat, mat, flat, mat, mat, flat, mat, flat, flat, flat, mat, flat, mat, flat,
    )
    out = (rows3, P(), rows3, flat, flat, mat, flat, mat, mat, flat, mat, flat, flat, flat, mat, flat, mat, flat)
    return jax.shard_map(local, mesh=mesh, in_specs=placed, out_specs=out, check_vma=False)
```

```python
import functools
import types

import jax
import jax.numpy as jnp
from jax import lax
from jax.experimental import pallas as pl
from jax.experimental.pallas import tpu as pltpu
from jax.sharding import PartitionSpec as P

HD = 64
NSUM = 50
NORM_EPS = 1e-05
NEG_FILL = -1e30
PRODUCT_GRANT, LARGE_GRANT = 30 << 20, 56 << 20
BF = jnp.bfloat16
F32 = jnp.float32


def dot(left_in, right_in):
    return jnp.dot(left_in, right_in, preferred_element_type=F32)


def dot_tn(left_in, right_in):
    return lax.dot_general(left_in, right_in, (((0,), (0,)), ((), ())), preferred_element_type=F32)


def dot_nt(left_in, right_in):
    return lax.dot_general(left_in, right_in, (((1,), (1,)), ((), ())), preferred_element_type=F32)


def norm_core(values):
    center = values - jnp.mean(values, axis=-1, keepdims=True)
    inverse = lax.rsqrt(jnp.mean(center * center, axis=-1, keepdims=True) + NORM_EPS)
    return center * inverse, inverse


def norm_back(grad_out, normed, inverse, gain_in):
    grad_normed = grad_out * gain_in
    inner_one = jnp.mean(grad_normed, axis=-1, keepdims=True)
    inner_two = jnp.mean(grad_normed * normed, axis=-1, keepdims=True)
    grad_in = inverse * (grad_normed - inner_one - normed * inner_two)
    return grad_in, jnp.sum(grad_out * normed, axis=0), jnp.sum(grad_out, axis=0)


def swap(values, mask):
    n = lax.axis_size("seq")
    return lax.ppermute(values, "seq", [(i, i ^ mask) for i in range(n)])


def gather_start(own):
    return (swap(own, 2), swap(own, 4)) if lax.axis_size("seq") == 8 else ()


def gather_relay(own, came):
    if lax.axis_size("seq") != 8:
        return ()
    half = own.shape[0] // 2
    return swap(came[1][:half], 2), swap(came[0][half:], 4)


def gather_pieces(own, came, relayed):
    if lax.axis_size("seq") == 8:
        return [own, *came, *relayed]
    return [gather_join(own, came, relayed)]


def gather_join(own, came, relayed):
    if lax.axis_size("seq") == 8:
        return jnp.concatenate([own, *came, *relayed], axis=0)
    same, step = own, 2
    while step < lax.axis_size("seq"):
        same = jnp.concatenate([same, swap(same, step)], axis=0)
        step *= 2
    return same


def gather_rows(own):
    came = gather_start(own)
    same = gather_join(own, came, gather_relay(own, came))
    return same, swap(same, 1)


def scatter_start(blocks):
    if lax.axis_size("seq") != 8:
        return ()
    six = blocks[3].astype(BF)
    half = six.shape[0] // 2
    return swap(six[:half], 2), swap(six[half:], 4)


def scatter_halves(blocks, came):
    if lax.axis_size("seq") != 8:
        return ()
    _, two, four, _ = blocks
    half, width = two.shape[0] // 2, two.shape[1]
    which = lax.broadcasted_iota(jnp.int32, (2, half, width), 0)

    def with_half(block, part, side):
        part = jnp.where(which == side, part.astype(F32)[None], 0.0)
        return (block.reshape(2, half, width) + part).astype(BF).reshape(2 * half, width)

    return with_half(two, came[1], 1), with_half(four, came[0], 0)


def scatter_relay(halves):
    return (swap(halves[0], 2), swap(halves[1], 4)) if halves else ()


def scatter_join(blocks, relayed):
    n = lax.axis_size("seq")
    if n == 8:
        return blocks[0] + relayed[0].astype(F32) + relayed[1].astype(F32)
    step = n // 2
    while step > 1:
        keep = len(blocks) // 2
        sent = [swap(block.astype(BF), step).astype(F32) for block in blocks[keep:]]
        blocks = [block.astype(F32) + got for block, got in zip(blocks[:keep], sent)]
        step //= 2
    return blocks[0]


def scatter_groups(rows):
    bit, index = lax.axis_size("dp") // 2, lax.axis_index("dp")
    while bit > 0:
        half = rows.shape[0] // 2
        upper = (index & bit) != 0
        sent = jnp.where(upper, rows[:half], rows[half:]).astype(BF)
        other = yield exchange(sent, "dp", bit)
        rows = jnp.where(upper, rows[half:], rows[:half]) + other.astype(F32)
        bit //= 2
    return rows


def exchange(values, axis, bit):
    size = lax.axis_size(axis)
    return lax.ppermute(values, axis, [(i, i ^ bit) for i in range(size)])


class Order:
    def __init__(self):
        self.last = ()

    def tie(self, value):
        if not jax.tree.leaves(value) or not jax.tree.leaves(self.last):
            return value
        return lax.optimization_barrier((value, self.last))[0]

    def mark(self, value):
        if jax.tree.leaves(value):
            self.last = value
        return value

    def pause(self, value):
        return self.mark(self.tie(value))


def doubling(held, axes):
    for axis in axes:
        bit, index = 1, lax.axis_index(axis)
        while bit < lax.axis_size(axis):
            other = yield exchange(held, axis, bit)
            upper = (index & bit) != 0
            held = jnp.concatenate([jnp.where(upper, other, held), jnp.where(upper, held, other)], axis=0)
            bit *= 2
    return held


def line_gather(own):
    size, index = lax.axis_size("dp"), lax.axis_index("dp")
    below, above = [], []
    to_right, to_left = own, own
    for _ in range(size - 1):
        flight = (
            lax.ppermute(to_right, "dp", [(i, i + 1) for i in range(size - 1)]),
            lax.ppermute(to_left, "dp", [(i + 1, i) for i in range(size - 1)]),
        )
        to_right, to_left = yield flight
        below.insert(0, to_right)
        above.append(to_left)
    rows = jnp.concatenate(below + [own] + above, axis=0)
    return lax.dynamic_slice_in_dim(rows, (size - 1 - index) * own.shape[0], size * own.shape[0], axis=0)


def line_scatter(parts):
    size, index = lax.axis_size("dp"), lax.axis_index("dp")

    def part(which):
        return lax.dynamic_index_in_dim(parts, jnp.clip(which, 0, size - 1), 0, keepdims=False)

    right = left = None
    for step in range(size - 1):
        far = size - 1 - step
        up, down = part(index + far), part(index - far)
        if step:
            up, down = (up.astype(F32) + right.astype(F32)).astype(BF), (down.astype(F32) + left.astype(F32)).astype(BF)
        flight = (
            lax.ppermute(up, "dp", [(i, i + 1) for i in range(size - far)]),
            lax.ppermute(down, "dp", [(i, i - 1) for i in range(far, size)]),
        )
        right, left = yield flight
    return part(index).astype(F32) + right.astype(F32) + left.astype(F32)


class Steps:
    def __init__(self, order, generator):
        self.order, self.generator, self.flight, self.result = order, generator, next(generator), None

    def step(self, count=1):
        for _ in range(count):
            if self.flight is None:
                return
            try:
                self.flight = self.generator.send(self.order.pause(self.flight))
            except StopIteration as stop:
                self.flight, self.result = None, stop.value

    def finish(self):
        while self.flight is not None:
            self.step()
        return self.result


def scatter_small(table):
    count, width = table.shape
    length = -(-width // 1024) * 1024
    held = jnp.pad(table, ((0, 0), (0, length - width))).reshape(count, 8, length // 8)
    for axis in ("dp", "seq"):
        bit, index = lax.axis_size(axis) // 2, lax.axis_index(axis)
        while bit > 0:
            half = held.shape[0] // 2
            upper = (index & bit) != 0
            sent = jnp.where(upper, held[:half], held[half:])
            held = jnp.where(upper, held[half:], held[:half]) + exchange(sent, axis, bit)
            bit //= 2
    return held.reshape(length)[:width]


def after(value, *earlier):
    return lax.optimization_barrier((value, *earlier))[0]


def weight_grad_kernel(*refs):
    count = (len(refs) - 1) // 2
    total = dot_tn(refs[0][...], refs[count][...])
    for part in range(1, count):
        total = total + dot_tn(refs[part][...], refs[count + part][...])
    refs[-1][...] = total.astype(BF)


def weight_grad(lefts, rights, left_tile, right_tile):
    rows, left_width = lefts[0].shape
    right_width = rights[0].shape[1]
    left_tile, right_tile = min(left_tile, left_width), min(right_tile, right_width)
    count = len(lefts)
    return pl.pallas_call(
        weight_grad_kernel,
        grid=(right_width // right_tile, left_width // left_tile),
        in_specs=[pl.BlockSpec((rows, left_tile), lambda j, i: (0, i))] * count
        + [pl.BlockSpec((rows, right_tile), lambda j, i: (0, j))] * count,
        out_specs=pl.BlockSpec((left_tile, right_tile), lambda j, i: (i, j)),
        out_shape=jax.ShapeDtypeStruct((left_width, right_width), BF),
        compiler_params=pltpu.CompilerParams(dimension_semantics=("arbitrary", "arbitrary"), vmem_limit_bytes=LARGE_GRANT),
        cost_estimate=light_cost(2 * count * rows * left_width * right_width),
        name="weight_grad",
    )(*lefts, *rights)


def tile_dot(left, right, turned):
    return dot_nt(left, right) if turned else dot(left, right)


def plain_kernel(left_ref, right_ref, out_ref, *, turned):
    out_ref[...] = tile_dot(left_ref[...], right_ref[...], turned).astype(out_ref.dtype)


def project_kernel(left_ref, right_ref, bias_ref, scale_ref, out_ref):
    out_ref[...] = ((dot(left_ref[...], right_ref[...]) + bias_ref[...]) * scale_ref[...]).astype(BF)


def up_kernel(left_ref, right_ref, bias_ref, out_ref):
    out_ref[...] = jnp.maximum(dot(left_ref[...], right_ref[...]) + bias_ref[...], 0.0).astype(BF)


def masked_kernel(left_ref, right_ref, act_ref, out_ref, sums_ref):
    grad = jnp.where(act_ref[...] > 0, dot_nt(left_ref[...], right_ref[...]), 0.0).astype(BF)
    out_ref[...] = grad
    part = jnp.sum(grad.astype(F32).reshape(-1, 8, grad.shape[1]), axis=0)

    @pl.when(pl.program_id(1) == 0)
    def _():
        sums_ref[...] = part

    @pl.when(pl.program_id(1) > 0)
    def _():
        sums_ref[...] = sums_ref[...] + part


def blocks_kernel(left_ref, right_ref, got_ref, *out_refs, turned):
    rows = out_refs[0].shape[0]
    for m in range(len(out_refs) - 1, -1, -1):
        cut = slice(m * rows, (m + 1) * rows)
        total = tile_dot(left_ref[cut, :], right_ref[...], turned) + got_ref[cut, :].astype(F32)
        out_refs[m][...] = total.astype(out_refs[m].dtype)


def light_cost(flops):
    return pl.CostEstimate(flops=int(flops) // 8, bytes_accessed=1, transcendentals=0)


def tiled(kernel, name, left, right, turned, extras, outs, row_tile, col_tile, parts=1):
    rows, depth = left.shape
    cols = right.shape[0] if turned else right.shape[1]
    row_tile, col_tile = min(row_tile, rows), min(col_tile, cols)
    kinds = {
        "both": pl.BlockSpec((row_tile, col_tile), lambda j, m: (m, j)),
        "vector": pl.BlockSpec((1, col_tile), lambda j, m: (0, j)),
        "sums": pl.BlockSpec((8, col_tile), lambda j, m: (0, j)),
        "block": pl.BlockSpec((rows // parts, col_tile), lambda j, m: (0, j)),
    }
    shapes = {"both": (rows, cols), "sums": (8, cols), "block": (rows // parts, cols)}
    right_spec = (
        pl.BlockSpec((col_tile, depth), lambda j, m: (j, 0)) if turned else pl.BlockSpec((depth, col_tile), lambda j, m: (0, j))
    )
    return pl.pallas_call(
        kernel,
        grid=(cols // col_tile, rows // row_tile),
        in_specs=[pl.BlockSpec((row_tile, depth), lambda j, m: (m, 0)), right_spec] + [kinds[k] for k, _ in extras],
        out_specs=[kinds[k] for k, _ in outs],
        out_shape=[jax.ShapeDtypeStruct(shapes[k], dtype) for k, dtype in outs],
        compiler_params=pltpu.CompilerParams(dimension_semantics=("arbitrary", "arbitrary"), vmem_limit_bytes=PRODUCT_GRANT),
        cost_estimate=light_cost(2 * rows * cols * depth),
        name=name,
    )(left, right, *[value for _, value in extras])


def plain_product(left, right, turned=False):
    kernel = functools.partial(plain_kernel, turned=turned)
    return tiled(kernel, "product", left, right, turned, [], [("both", BF)], 1024, 256)[0]


def project_product(left, right, bias, scale):
    extras = [("vector", bias.reshape(1, -1)), ("vector", scale.reshape(1, -1))]
    return tiled(project_kernel, "project", left, right, False, extras, [("both", BF)], 1024, 256)[0]


def up_product(left, right, bias):
    return tiled(up_kernel, "up", left, right, False, [("vector", bias.reshape(1, -1))], [("both", BF)], 1024, 256)[0]


def masked_product(left, right, act):
    outs = [("both", BF), ("sums", F32)]
    return tiled(masked_kernel, "masked_product", left, right, True, [("both", act)], outs, 1024, 256)


def block_products(left, right, got, count, turned=False):
    kernel = functools.partial(blocks_kernel, turned=turned)
    outs = [("block", F32)] * (count - 1) + [("block", BF)]
    return tiled(
        kernel, "block_products", left, right, turned, [("both", got)], outs, left.shape[0], 256, count
    )


def norm_kernel(*refs, unit):
    *piece_refs, gain_ref, shift_ref, out_ref = refs
    step, at = pl.program_id(0), 0
    for piece_ref in piece_refs:
        for start in range(0, piece_ref.shape[0], unit):

            @pl.when(step == at)
            def _(piece_ref=piece_ref, start=start):
                normed, _ = norm_core(piece_ref[start : start + unit, :].astype(F32))
                out_ref[...] = (normed * gain_ref[...] + shift_ref[...]).astype(BF)

            at += 1


def norm_rows(pieces, gain, shift):
    rows, width = sum(piece.shape[0] for piece in pieces), pieces[0].shape[1]
    unit = min(min(piece.shape[0] for piece in pieces), 128)
    whole = [pl.BlockSpec(piece.shape, lambda i: (0, 0)) for piece in pieces]
    vector = pl.BlockSpec((1, width), lambda i: (0, 0))
    return pl.pallas_call(
        functools.partial(norm_kernel, unit=unit),
        grid=(rows // unit,),
        in_specs=whole + [vector, vector],
        out_specs=pl.BlockSpec((unit, width), lambda i: (i, 0)),
        out_shape=jax.ShapeDtypeStruct((rows, width), BF),
        compiler_params=pltpu.CompilerParams(dimension_semantics=("arbitrary",), vmem_limit_bytes=PRODUCT_GRANT),
        cost_estimate=light_cost(2000 * rows * width),
        name="norm_rows",
    )(*pieces, gain.reshape(1, -1), shift.reshape(1, -1))


def visible_scores(q_head, k_block, first, q_place, key_start, length):
    scores = dot_nt(q_head, k_block)
    k_place = key_start + lax.broadcasted_iota(jnp.int32, (1, length), 1)
    allowed = (k_place >= first) & (k_place <= q_place)
    return jnp.where(allowed, scores, NEG_FILL)


def storage_row(block, place, blocks, length):
    k = block ^ place
    return pl.multiple_of(((k >> 1) + (k & 1) * (blocks // 2)) * length, length)


def spread_heads(source_ref, target_ref, lanes, heads, length, blocks):
    def one(m, carry):
        rows = source_ref[pl.ds(pl.multiple_of(m * length, length), length), :]
        for h in range(heads):
            target = pl.ds(pl.multiple_of((m * heads + h) * length, length), length)
            target_ref[target, :] = jnp.where(lanes == h, rows, jnp.zeros_like(rows))
        return carry

    lax.fori_loop(0, blocks, one, 0)


def fold(values, op):
    out = values[:, :128]
    for start in range(128, values.shape[1], 128):
        out = op(out, values[:, start : start + 128])
    return out


def attend_forward_kernel(
    place_ref, low_ref, q_ref, k_ref, v_ref, first_ref, o_ref, lse_ref, s_scr, m_scr, l_scr, v_scr, *, heads, length, blocks
):
    i = pl.program_id(0)
    place = place_ref[0]
    low = low_ref[i]
    width = heads * HD
    lanes = lax.broadcasted_iota(jnp.int32, (length, width), 1) // HD
    q_all = q_ref[...]
    q_heads = [jnp.where(lanes == h, q_all, jnp.zeros_like(q_all)) for h in range(heads)]
    first = first_ref[...]
    q_place = i * length + lax.broadcasted_iota(jnp.int32, (length, 1), 0)
    m_scr[...] = jnp.full_like(m_scr, NEG_FILL)
    l_scr[...] = jnp.zeros_like(l_scr)

    @pl.when(i == 0)
    def _():
        spread_heads(v_ref, v_scr, lanes, heads, length, blocks)

    def score_step(j, carry):
        k_block = k_ref[pl.ds(storage_row(j, place, blocks, length), length), :]
        cols = pl.ds(pl.multiple_of(j * length, length), length)
        for h in range(heads):
            scores = visible_scores(q_heads[h], k_block, first, q_place, j * length, length)
            s_scr[h, :, cols] = scores
            m_scr[h] = jnp.maximum(m_scr[h], fold(scores, jnp.maximum))
        return carry

    lax.fori_loop(low, i + 1, score_step, 0)
    tops = [jnp.max(m_scr[h], axis=-1, keepdims=True) for h in range(heads)]

    def exp_step(j, carry):
        cols = pl.ds(pl.multiple_of(j * length, length), length)
        for h in range(heads):
            raised = jnp.exp(s_scr[h, :, cols] - tops[h])
            s_scr[h, :, cols] = raised
            l_scr[h] = l_scr[h] + fold(raised, jnp.add)
        return carry

    lax.fori_loop(low, i + 1, exp_step, 0)
    totals = [jnp.sum(l_scr[h], axis=-1, keepdims=True) for h in range(heads)]
    scales = [1.0 / total for total in totals]

    def mix_step(j, acc):
        rows = pl.ds(pl.multiple_of(storage_row(j, place, blocks, length) * heads, heads * length), heads * length)
        cols = pl.ds(pl.multiple_of(j * length, length), length)
        probs = [(s_scr[h, :, cols] * scales[h]).astype(BF) for h in range(heads)]
        return acc + dot(jnp.concatenate(probs, axis=1), v_scr[rows, :])

    mixed = lax.fori_loop(low, i + 1, mix_step, jnp.zeros((length, width), F32))
    o_ref[...] = mixed.astype(BF)
    cols = lax.broadcasted_iota(jnp.int32, (length, 128), 1)
    lse = jnp.zeros((length, 128), F32)
    for h in range(heads):
        lse = jnp.where(cols == h, tops[h] + jnp.log(totals[h]), lse)
    lse_ref[...] = lse


def attend_backward_kernel(
    place_ref, low_ref, q_ref, go_ref, o_ref, lse_ref, k_ref, v_ref, first_ref, even_ref, odd_ref, kt_scr, vt_scr, k_scr,
    *, heads, length, blocks
):
    i = pl.program_id(0)
    place = place_ref[0]
    low = low_ref[i]
    width = heads * HD
    lanes = lax.broadcasted_iota(jnp.int32, (length, width), 1) // HD
    first = first_ref[...]
    q_place = i * length + lax.broadcasted_iota(jnp.int32, (length, 1), 0)
    q_all, go_all = q_ref[...], go_ref[...]
    inner_all = go_all.astype(F32) * o_ref[...].astype(F32)
    q_turned, go_turned = q_all.astype(F32).T.astype(BF), go_all.astype(F32).T.astype(BF)
    lse_all = lse_ref[...]
    q_heads, go_heads, inner, lse = [], [], [], []
    for h in range(heads):
        mine = lanes == h
        q_heads.append(jnp.where(mine, q_all, jnp.zeros_like(q_all)))
        go_heads.append(jnp.where(mine, go_all, jnp.zeros_like(go_all)))
        inner.append(jnp.sum(jnp.where(mine, inner_all, 0.0), axis=-1, keepdims=True))
        lse.append(lse_all[:, h : h + 1])

    @pl.when(i == 0)
    def _():
        kt_scr[...] = jnp.zeros_like(kt_scr)
        vt_scr[...] = jnp.zeros_like(vt_scr)
        spread_heads(k_ref, k_scr, lanes, heads, length, blocks)

    def step(j, acc):
        start = storage_row(j, place, blocks, length)
        rows = pl.ds(start, length)
        k_block, v_block = k_ref[rows, :], v_ref[rows, :]
        k_place = j * length + lax.broadcasted_iota(jnp.int32, (1, length), 1)
        allowed = (k_place >= first) & (k_place <= q_place)
        every = range(heads)
        scores = [dot_nt(q_heads[h], k_block) for h in every]
        grad_probs = [dot_nt(go_heads[h], v_block) for h in every]
        probs = [jnp.exp(jnp.where(allowed, scores[h] - lse[h], NEG_FILL)) for h in every]
        grad_scores = [(probs[h] * (grad_probs[h] - inner[h])).astype(BF) for h in every]
        for h in every:
            part = slice(h * HD, (h + 1) * HD)
            vt_scr[part, rows] = vt_scr[part, rows] + dot(go_turned[part, :], probs[h].astype(BF))
            kt_scr[part, rows] = kt_scr[part, rows] + dot(q_turned[part, :], grad_scores[h])
        spread = pl.ds(pl.multiple_of(start * heads, heads * length), heads * length)
        return acc + dot(jnp.concatenate(grad_scores, axis=1), k_scr[spread, :])

    grad_q = lax.fori_loop(low, i + 1, step, jnp.zeros((length, width), F32))
    grad_q = (grad_q.astype(BF).astype(F32) * (HD**-0.5)).astype(BF)
    k = i ^ place
    own_rows = pl.ds(pl.multiple_of((k >> 1) * length, length), length)

    @pl.when((k & 1) == 0)
    def _():
        even_ref[own_rows, 0:width] = grad_q

    @pl.when((k & 1) == 1)
    def _():
        odd_ref[own_rows, 0:width] = grad_q

    @pl.when(i == blocks - 1)
    def _():
        for j in range(blocks):
            target, m = (even_ref, j) if j < blocks // 2 else (odd_ref, j - blocks // 2)
            source, rows = slice(j * length, (j + 1) * length), slice(m * length, (m + 1) * length)
            target[rows, width : 2 * width] = kt_scr[:, source].T.astype(BF)
            target[rows, 2 * width : 3 * width] = vt_scr[:, source].T.astype(BF)


def storage_map(length, blocks, column):
    def index(i, place_ref, low_ref):
        k = i ^ place_ref[0]
        return ((k >> 1) + (k & 1) * (blocks // 2), column)

    return index


def attend_forward(place, low, qkv, first, length):
    rows, triple = qkv.shape
    width, blocks = triple // 3, rows // length
    heads = width // HD
    return pl.pallas_call(
        functools.partial(attend_forward_kernel, heads=heads, length=length, blocks=blocks),
        grid_spec=pltpu.PrefetchScalarGridSpec(
            num_scalar_prefetch=2,
            grid=(blocks,),
            in_specs=[
                pl.BlockSpec((length, width), storage_map(length, blocks, 0)),
                pl.BlockSpec((rows, width), lambda i, p, w: (0, 1)),
                pl.BlockSpec((rows, width), lambda i, p, w: (0, 2)),
                pl.BlockSpec((length, 1), lambda i, p, w: (i, 0)),
            ],
            out_specs=[
                pl.BlockSpec((length, width), lambda i, p, w: (i, 0)),
                pl.BlockSpec((length, 128), lambda i, p, w: (i, 0)),
            ],
            scratch_shapes=[
                pltpu.VMEM((heads, length, rows), F32),
                pltpu.VMEM((heads, length, 128), F32),
                pltpu.VMEM((heads, length, 128), F32),
                pltpu.VMEM((heads * rows, width), BF),
            ],
        ),
        out_shape=[jax.ShapeDtypeStruct((rows, width), BF), jax.ShapeDtypeStruct((rows, 128), F32)],
        compiler_params=pltpu.CompilerParams(dimension_semantics=("arbitrary",), vmem_limit_bytes=LARGE_GRANT),
        cost_estimate=light_cost(24 * rows * rows * width),
        name="attend_forward",
    )(place, low, qkv, qkv, qkv, first)


def attend_backward(place, low, qkv, grad_out, mixed, lse, first, length):
    rows, triple = qkv.shape
    width, blocks = triple // 3, rows // length
    heads = width // HD
    return pl.pallas_call(
        functools.partial(attend_backward_kernel, heads=heads, length=length, blocks=blocks),
        grid_spec=pltpu.PrefetchScalarGridSpec(
            num_scalar_prefetch=2,
            grid=(blocks,),
            in_specs=[
                pl.BlockSpec((length, width), storage_map(length, blocks, 0)),
                pl.BlockSpec((length, width), lambda i, p, w: (i, 0)),
                pl.BlockSpec((length, width), lambda i, p, w: (i, 0)),
                pl.BlockSpec((length, 128), lambda i, p, w: (i, 0)),
                pl.BlockSpec((rows, width), lambda i, p, w: (0, 1)),
                pl.BlockSpec((rows, width), lambda i, p, w: (0, 2)),
                pl.BlockSpec((length, 1), lambda i, p, w: (i, 0)),
            ],
            out_specs=[pl.BlockSpec((rows // 2, triple), lambda i, p, w: (0, 0))] * 2,
            scratch_shapes=[
                pltpu.VMEM((width, rows), F32),
                pltpu.VMEM((width, rows), F32),
                pltpu.VMEM((heads * rows, width), BF),
            ],
        ),
        out_shape=[jax.ShapeDtypeStruct((rows // 2, triple), BF)] * 2,
        compiler_params=pltpu.CompilerParams(dimension_semantics=("arbitrary",), vmem_limit_bytes=LARGE_GRANT),
        cost_estimate=light_cost(36 * rows * rows * width),
        name="attend_backward",
    )(place, low, qkv, grad_out, mixed, lse, qkv, qkv, first)


def local(
    inputs,
    teacher,
    segment_ids,
    summary_start,
    valid_mask,
    attn_norm_gain,
    attn_norm_bias,
    query_weight,
    query_bias,
    key_weight,
    value_weight,
    value_bias,
    out_weight,
    out_bias,
    mlp_norm_gain,
    mlp_norm_bias,
    up_weight,
    up_bias,
    down_weight,
    down_bias,
):
    seqs, length = segment_ids.shape
    width = inputs.shape[-1]
    hidden_units = up_weight.shape[1]
    n, groups = lax.axis_size("seq"), lax.axis_size("dp")
    place, group = lax.axis_index("seq"), lax.axis_index("dp")
    both = ("dp", "seq")
    seq_len = length * n
    tokens_all = seqs * seq_len * groups
    scale = HD**-0.5
    own_rows = query_weight.shape[0]
    own_hidden = up_bias.shape[0]
    head_cols = width // n

    def out_of(value):
        return lax.all_to_all(value, "seq", split_axis=0, concat_axis=0, tiled=True)

    valid = valid_mask.astype(F32)
    order = Order()
    near = n == 8 and groups == 4
    out_steps = Steps(order, line_gather(out_weight)) if near else None
    cut = jnp.concatenate(
        [w.reshape(own_rows, n, head_cols).transpose(1, 0, 2) for w in (query_weight, key_weight, value_weight)], axis=2
    )
    qkv_cut = out_of(cut)
    small = [attn_norm_gain, attn_norm_bias, out_bias, mlp_norm_gain, mlp_norm_bias, down_bias, query_bias, value_bias, up_bias]
    pieces = [v.astype(F32) for v in small] + [segment_ids.astype(F32).reshape(-1), jnp.sum(valid).reshape(1)]
    starts, lines = [], []
    for piece in pieces:
        starts.append(sum(line.shape[0] for line in lines))
        short = -piece.shape[0] % 128
        lines.append(jnp.pad(piece, (0, short)).reshape(-1, 128))
    used = sum(line.shape[0] for line in lines)
    packed = jnp.pad(jnp.concatenate(lines, axis=0), ((0, -used % 8), (0, 0)))[None]
    small_steps = Steps(order, doubling(after(packed, cut), ("dp", "seq")))
    if near:
        out_steps.step()
    small_steps.step(2)
    if near:
        out_steps.step()
    small_steps.step(1)
    qkv_cut = order.pause(qkv_cut).reshape(n * own_rows, 3 * head_cols)
    w_qkv = lax.all_gather(qkv_cut, "dp", axis=0, tiled=True)
    if near:
        own_out = out_steps.finish()
    packed = small_steps.finish().reshape(n, groups, -1, 128).transpose(1, 0, 2, 3).reshape(groups * n, -1, 128)

    def zero_after(value):
        return jnp.minimum(jnp.abs(value.reshape(-1)[0].astype(F32)), 0.0).astype(jnp.int32)

    def rows_after(b, value):
        return lax.dynamic_index_in_dim(inputs, b + zero_after(value), 0, keepdims=False)

    state = [types.SimpleNamespace() for _ in range(seqs)]
    state[0].own = rows_after(0, packed)
    state[0].came = gather_start(state[0].own)
    parts = []
    for piece, at in zip(pieces, starts):
        count = -(-piece.shape[0] // 128)
        parts.append(packed[:, at : at + count].reshape(groups * n, -1)[:, : piece.shape[0]])
    gain_one, shift_one, b_out, gain_two, shift_two, b_down = [part.reshape(-1) for part in parts[:6]]
    b_query, b_value = [lax.dynamic_slice_in_dim(part.reshape(-1), place * head_cols, head_cols) for part in parts[6:8]]
    b_up = lax.dynamic_index_in_dim(parts[8].reshape(groups, n, -1), place, 1, keepdims=False).reshape(-1)
    ids = lax.dynamic_index_in_dim(parts[9].reshape(groups, n, seqs, length), group, 0, keepdims=False)
    ids = ids.transpose(1, 0, 2).reshape(seqs, seq_len)
    total_count = jnp.sum(parts[10])

    up_cut = up_weight.reshape(own_rows, groups, n, own_hidden).transpose(2, 0, 1, 3).reshape(n, own_rows, groups * own_hidden)
    b_qkv = jnp.concatenate([b_query, jnp.zeros_like(b_query), b_value])
    s_qkv = jnp.concatenate([jnp.full((head_cols,), scale, F32), jnp.ones((2 * head_cols,), F32)])

    place_arr = place.reshape(1).astype(jnp.int32)
    positions = jnp.arange(seq_len, dtype=jnp.int32)

    def add_all(terms):
        out = terms[0]
        for term in terms[1:]:
            out = out + term
        return out


    def spans(b):
        st = state[b]
        first = jnp.sum((ids[b][None, :] < ids[b][:, None]).astype(jnp.int32), axis=1)
        in_summary = (positions >= summary_start[b]) & (positions < summary_start[b] + NSUM)
        first = jnp.where(in_summary, 0, first)
        st.low = jnp.min(first.reshape(n, length), axis=1) // length
        st.first = first.reshape(seq_len, 1)

    def project(b):
        st = state[b]
        even, odd = order.tie((st.even, st.odd))
        parts = [project_product(part, w_qkv, b_qkv, s_qkv) for part in (even, odd)]
        st.qkv = order.mark(jnp.concatenate(parts, axis=0))

    def attend(b):
        st = state[b]
        qkv = order.tie(st.qkv)
        st.mixed, st.lse = attend_forward(place_arr, st.low, qkv, st.first, length)
        order.mark(st.mixed)

    def send_mixed(b):
        st = state[b]
        st.moved = out_of(st.mixed.reshape(n, length, head_cols))

    def middle(b):
        st = state[b]
        attended = order.tie(st.moved)
        st.attended = attended.transpose(1, 0, 2).reshape(length, width)
        rows = inputs[b].astype(F32)
        st.hidden = rows + (dot(st.attended, w_out) + b_out)
        st.normed_two, st.inverse_two = norm_core(st.hidden)
        st.own_two = order.mark((st.normed_two * gain_two + shift_two).astype(BF))
        st.came_two = gather_start(st.own_two)

    def up_even(b):
        st = state[b]
        st.act_even = order.mark(up_product(order.tie(st.even_two), w_up, b_up))

    def up_odd(b):
        st = state[b]
        st.act_odd = order.mark(up_product(order.tie(st.odd_two), w_up, b_up))

    def relay(b, own, came):
        st = state[b]
        came = order.pause(getattr(st, came))
        return came, gather_relay(getattr(st, own), came)

    def join(b, own, came_relayed):
        same = order.mark(gather_join(getattr(state[b], own), *order.tie(came_relayed)))
        return same, swap(same, 1)

    def down_odd(b):
        st = state[b]
        st.down_got = swap(order.mark(plain_product(order.tie(st.act_odd), w_down)), 1)

    def down_even(b):
        st = state[b]
        st.down_sums = order.mark(block_products(st.act_even, w_down, order.tie(st.down_got), n // 2))
        st.down_came = scatter_start(st.down_sums)

    def pass_on(b, sums, came):
        st = state[b]
        came = order.pause(getattr(st, came))
        return scatter_relay(order.mark(scatter_halves(getattr(st, sums), came)))

    def misfit(b):
        st = state[b]
        summed = scatter_join(st.down_sums, order.tie(st.down_sent))
        st.result = st.hidden + (summed + b_down)
        error = st.result - teacher[b].astype(F32)
        st.local_sq = jnp.sum(jnp.sum(error * error, axis=-1) * valid[b])
        st.grad_result = error * (valid[b] * (tokens_all / total_count))[:, None]
        st.own_grad = order.mark(st.grad_result.astype(BF))
        st.g_b_down = jnp.sum(st.own_grad.astype(F32), axis=0)
        st.came_grad = gather_start(st.own_grad)

    def act_back_even(b):
        st = state[b]
        st.pre_even, st.sums_even = masked_product(order.tie(st.gm_even), w_down, st.act_even)
        order.mark(st.pre_even)

    def act_back_odd(b):
        st = state[b]
        st.pre_odd, st.sums_odd = masked_product(order.tie(st.gm_odd), w_down, st.act_odd)
        order.mark(st.pre_odd)

    def up_back_odd(b):
        st = state[b]
        st.up_got = swap(order.mark(plain_product(order.tie(st.pre_odd), w_up, turned=True)), 1)

    def up_back_even(b):
        st = state[b]
        st.up_sums = order.mark(block_products(st.pre_even, w_up, order.tie(st.up_got), n // 2, turned=True))
        st.up_came = scatter_start(st.up_sums)

    def branch_back(b):
        st = state[b]
        grad_ready = scatter_join(st.up_sums, order.tie(st.up_sent))
        grad_norm, st.g_gain_two, st.g_shift_two = norm_back(grad_ready, st.normed_two, st.inverse_two, gain_two)
        st.grad_hidden = st.grad_result + grad_norm
        st.branch = st.grad_hidden.astype(BF)
        st.g_b_out = jnp.sum(st.branch.astype(F32), axis=0)
        grad_att = dot_nt(st.branch, w_out).astype(BF).reshape(length, n, head_cols).transpose(1, 0, 2)
        st.grad_mixed = out_of(order.mark(grad_att)).reshape(seq_len, head_cols)

    def attend_back(b):
        st = state[b]
        st.grad_qkv = attend_backward(
            place_arr, st.low, st.qkv, order.tie(st.grad_mixed), st.mixed, st.lse, st.first, length
        )
        order.mark(st.grad_qkv)
        st.g_b_qkv = sum(jnp.sum(part.astype(F32), axis=0) for part in st.grad_qkv)

    def project_back_odd(b):
        st = state[b]
        odd = order.tie(st.grad_qkv[1])
        st.one_got = swap(order.mark(plain_product(odd, w_qkv, turned=True)), 1)

    def project_back_even(b):
        st = state[b]
        st.one_sums = block_products(st.grad_qkv[0], w_qkv, order.tie(st.one_got), n // 2, turned=True)
        order.mark(st.one_sums)
        st.one_came = scatter_start(st.one_sums)

    def finish(b):
        st = state[b]
        grad_ready = scatter_join(st.one_sums, order.tie(st.one_sent))
        normed, inverse = norm_core(inputs[b].astype(F32))
        grad_norm, st.g_gain_one, st.g_shift_one = norm_back(grad_ready, normed, inverse, gain_one)
        st.grad_inputs = order.mark(st.grad_hidden + grad_norm)

    every, later = range(seqs), range(1, seqs)

    def whole_out_weight(own, came, relayed):
        whole = jnp.zeros((groups, n, own_rows, width), BF)
        half = groups // 2
        same = [(0, own, 0), (2, came[0], 0), (4, came[1], 0), (6, relayed[0], 0), (6, relayed[1], half)]
        other = [(k + 1, swap(piece, 1), first) for k, piece, first in same]
        for k, piece, first in same + other:
            whole = lax.dynamic_update_slice(whole, piece.reshape(-1, 1, own_rows, width), (first, place ^ k, 0, 0))
        return whole.reshape(width, width)

    def make_ready(b, came_relayed):
        st = state[b]
        st.even = order.mark(norm_rows(gather_pieces(st.own, *order.tie(came_relayed)), gain_one, shift_one))
        st.odd = swap(st.even, 1)

    for b in every:
        spans(b)
    came_relayed = relay(0, "own", "came")
    make_ready(0, came_relayed)
    up_cut = out_of(after(up_cut, qkv_cut))
    for b in later:
        state[b].own = rows_after(b, came_relayed[0][0] if near else packed)
        state[b].came = gather_start(state[b].own)
    up_cut = order.pause(up_cut)
    w_up = lax.all_gather(up_cut.reshape(n * own_rows, groups * own_hidden), "dp", axis=0, tiled=True)
    w_down = lax.all_gather(after(down_weight, up_cut), "dp", axis=0, tiled=True)
    if near:
        own_out = order.tie(own_out)
        out_came = gather_start(own_out)
    else:
        w_out = lax.all_gather(after(out_weight, up_cut), both, axis=0, tiled=True)
    w_qkv = order.pause(w_qkv)
    project(0)
    came_relayed = [relay(b, "own", "came") for b in later]
    if near:
        out_came = order.pause(out_came)
        out_relayed = gather_relay(own_out, out_came)
    attend(0)
    send_mixed(0)
    raw = came_relayed
    if near:
        w_out = whole_out_weight(own_out, out_came, order.pause(out_relayed))
    middle(0)
    for b in later:
        last, st = state[b - 1], state[b]
        make_ready(b, raw[b - 1])
        project(b)
        came_relayed = relay(b - 1, "own_two", "came_two")
        attend(b)
        send_mixed(b)
        last.even_two, last.odd_two = join(b - 1, "own_two", came_relayed)
        up_even(b - 1)
        middle(b)
        up_odd(b - 1)
        came_relayed = relay(b, "own_two", "came_two")
        down_odd(b - 1)
        st.even_two, st.odd_two = join(b, "own_two", came_relayed)
        up_even(b)
        down_even(b - 1)
        up_odd(b)
        last.down_sent = pass_on(b - 1, "down_sums", "down_came")
        down_odd(b)
        down_even(b)
        misfit(b - 1)
        st.down_sent = pass_on(b, "down_sums", "down_came")
        came_relayed = relay(b - 1, "own_grad", "came_grad")
        misfit(b)
        last.gm_even, last.gm_odd = join(b - 1, "own_grad", came_relayed)
        act_back_even(b - 1)
        act_back_odd(b - 1)
        came_relayed = relay(b, "own_grad", "came_grad")
        up_back_odd(b - 1)
        up_back_even(b - 1)
        st.gm_even, st.gm_odd = join(b, "own_grad", came_relayed)
        act_back_even(b)
        last.up_sent = pass_on(b - 1, "up_sums", "up_came")
        act_back_odd(b)
        up_back_odd(b)
        up_back_even(b)
    lefts = [part for st in state for part in (st.even_two, st.odd_two)]
    rights = [part for st in state for part in (st.pre_even, st.pre_odd)]
    g_w_up = order.mark(weight_grad(order.tie(lefts), rights, 512, 1024))
    g_up = lax.psum_scatter(g_w_up, "dp", scatter_dimension=0, tiled=True)
    for b in later:
        state[b].up_sent = pass_on(b, "up_sums", "up_came")
    branch_back(0)
    lefts = [part for st in state for part in (st.act_even, st.act_odd)]
    rights = [part for st in state for part in (st.gm_even, st.gm_odd)]
    g_w_down = order.mark(weight_grad(order.tie(lefts), rights, 256, 1024))
    g_down = lax.psum_scatter(g_w_down, "dp", scatter_dimension=0, tiled=True)
    for b in later:
        branch_back(b)
    turned = [
        st.attended.reshape(length, groups, n, own_rows).transpose(2, 0, 1, 3).reshape(n, length, groups * own_rows)
        for st in state
    ]

    def out_block(k):
        return add_all(
            [dot_tn(lax.dynamic_index_in_dim(t, place ^ k, 0, keepdims=False), st.branch) for t, st in zip(turned, state)]
        )

    out_rows = groups * own_rows
    turned = order.tie(turned)
    out_odd = order.mark(jnp.concatenate([out_block(k).astype(BF) for k in range(1, n, 2)], axis=0))
    out_got = swap(out_odd, 1)
    attend_back(0)
    out_got = order.tie(out_got)
    out_sums = [out_block(2 * m) + out_got[m * out_rows : (m + 1) * out_rows].astype(F32) for m in range(n // 2)]
    order.mark(out_sums)
    out_came = scatter_start(out_sums)
    project_back_odd(0)
    out_sent = scatter_relay(order.mark(scatter_halves(out_sums, order.pause(out_came))))
    project_back_even(0)
    for b in later:
        attend_back(b)
    out_sum = order.mark(scatter_join(out_sums, order.tie(out_sent)))
    out_group_steps = Steps(order, scatter_groups(out_sum))
    for b in later:
        state[b - 1].one_sent = pass_on(b - 1, "one_sums", "one_came")
        project_back_odd(b)
    out_group_steps.step()
    g_up, g_down = order.pause((g_up, g_down))
    g_up = out_of(g_up.reshape(n, own_rows, groups * own_hidden))
    lefts = [part for st in state for part in (st.even, st.odd)]
    rights = [part for st in state for part in st.grad_qkv]
    g_w_qkv = order.mark(weight_grad(order.tie(lefts), rights, 1024, 768))
    if near:
        qkv_steps = Steps(order, line_scatter(g_w_qkv.reshape(groups, n * own_rows, 3 * head_cols)))
    else:
        g_qkv = lax.psum_scatter(g_w_qkv, "dp", scatter_dimension=0, tiled=True)
    for b in later:
        project_back_even(b)
    if near:
        qkv_steps.step()
    for b in later:
        state[b].one_sent = pass_on(b, "one_sums", "one_came")
    g_out = out_group_steps.finish()
    if near:
        qkv_steps.step()
    g_up = order.pause(g_up)
    for b in later:
        finish(b - 1)
    if near:
        g_qkv = order.mark(qkv_steps.finish().astype(BF))
    g_qkv = out_of(g_qkv.reshape(n, own_rows, 3 * head_cols))
    for b in later:
        finish(b)

    def summed(name):
        return add_all([after(getattr(st, name), *state[-1].one_sums) for st in state])

    g_down = order.tie(g_down).astype(F32)
    g_up = g_up.reshape(n, own_rows, groups, own_hidden).transpose(1, 2, 0, 3).reshape(own_rows, hidden_units).astype(F32)
    g_qkv = g_qkv.reshape(n, own_rows, 3, head_cols).transpose(2, 1, 0, 3).reshape(3, own_rows, width).astype(F32)

    g_b_qkv = summed("g_b_qkv").reshape(3, head_cols)
    own_bias = jnp.zeros((2, width), F32)
    own_bias = lax.dynamic_update_slice(own_bias, jnp.stack([g_b_qkv[0], g_b_qkv[2]]), (0, place * head_cols))
    g_b_up = jnp.sum(summed("sums_even") + summed("sums_odd"), axis=0).reshape(groups, 1, own_hidden)
    spread_up = lax.dynamic_update_slice_in_dim(jnp.zeros((groups, n, own_hidden), F32), g_b_up, place, 1)
    names = ("g_gain_one", "g_shift_one", "g_b_out", "g_gain_two", "g_shift_two", "g_b_down")
    vectors = jnp.concatenate([jnp.stack([summed(name) for name in names]), own_bias], axis=0)
    count = vectors.shape[0]
    vectors = vectors.reshape(count, groups * n, own_rows).transpose(1, 0, 2).reshape(groups * n, count * own_rows)
    sq = jnp.broadcast_to(summed("local_sq"), (groups * n, 1))
    tail = jnp.concatenate([vectors, spread_up.reshape(groups * n, own_hidden), sq], axis=1)
    tail = scatter_small(tail)
    vectors = tail[: count * own_rows].reshape(count, own_rows)
    g_b_query, g_b_value, g_b_up = vectors[6], vectors[7], tail[count * own_rows : -1]
    mean_loss = tail[-1] / (total_count * width)
    return (
        jnp.stack([st.result.astype(BF) for st in state]),
        mean_loss,
        jnp.stack([st.grad_inputs for st in state]),
        vectors[0],
        vectors[1],
        g_qkv[0],
        g_b_query,
        g_qkv[1],
        g_qkv[2],
        g_b_value,
        g_out,
        vectors[2],
        vectors[3],
        vectors[4],
        g_up,
        g_b_up,
        g_down,
        vectors[5],
    )


def solution(mesh):
    rows3, rows2, flat, mat = P("dp", "seq", None), P("dp", "seq"), P(("dp", "seq")), P(("dp", "seq"), None)
    placed = (
        rows3, rows3, rows2, P("dp"), rows2, flat, flat, mat, flat, mat, mat, flat, mat, flat, flat, flat, mat, flat, mat, flat,
    )
    out = (rows3, P(), rows3, flat, flat, mat, flat, mat, mat, flat, mat, flat, flat, flat, mat, flat, mat, flat)
    return jax.shard_map(local, mesh=mesh, in_specs=placed, out_specs=out, check_vma=False)
```

```python
import functools
import types

import jax
import jax.numpy as jnp
from jax import lax
from jax.experimental import pallas as pl
from jax.experimental.pallas import tpu as pltpu
from jax.sharding import PartitionSpec as P

HD = 64
NSUM = 50
NORM_EPS = 1e-05
NEG_FILL = -1e30
PRODUCT_GRANT, LARGE_GRANT = 30 << 20, 56 << 20
BF = jnp.bfloat16
F32 = jnp.float32


def dot(left_in, right_in):
    return jnp.dot(left_in, right_in, preferred_element_type=F32)


def dot_tn(left_in, right_in):
    return lax.dot_general(left_in, right_in, (((0,), (0,)), ((), ())), preferred_element_type=F32)


def dot_nt(left_in, right_in):
    return lax.dot_general(left_in, right_in, (((1,), (1,)), ((), ())), preferred_element_type=F32)


def norm_core(values):
    center = values - jnp.mean(values, axis=-1, keepdims=True)
    inverse = lax.rsqrt(jnp.mean(center * center, axis=-1, keepdims=True) + NORM_EPS)
    return center * inverse, inverse


def norm_back(grad_out, normed, inverse, gain_in):
    grad_normed = grad_out * gain_in
    inner_one = jnp.mean(grad_normed, axis=-1, keepdims=True)
    inner_two = jnp.mean(grad_normed * normed, axis=-1, keepdims=True)
    grad_in = inverse * (grad_normed - inner_one - normed * inner_two)
    return grad_in, jnp.sum(grad_out * normed, axis=0), jnp.sum(grad_out, axis=0)


def swap(values, mask):
    n = lax.axis_size("seq")
    return lax.ppermute(values, "seq", [(i, i ^ mask) for i in range(n)])


def gather_start(own):
    return (swap(own, 2), swap(own, 4)) if lax.axis_size("seq") == 8 else ()


def gather_relay(own, came):
    if lax.axis_size("seq") != 8:
        return ()
    half = own.shape[0] // 2
    return swap(came[1][:half], 2), swap(came[0][half:], 4)


def gather_pieces(own, came, relayed):
    if lax.axis_size("seq") == 8:
        return [own, *came, *relayed]
    return [gather_join(own, came, relayed)]


def gather_join(own, came, relayed):
    if lax.axis_size("seq") == 8:
        return jnp.concatenate([own, *came, *relayed], axis=0)
    same, step = own, 2
    while step < lax.axis_size("seq"):
        same = jnp.concatenate([same, swap(same, step)], axis=0)
        step *= 2
    return same


def gather_rows(own):
    came = gather_start(own)
    same = gather_join(own, came, gather_relay(own, came))
    return same, swap(same, 1)


def scatter_start(blocks):
    if lax.axis_size("seq") != 8:
        return ()
    six = blocks[3].astype(BF)
    half = six.shape[0] // 2
    return swap(six[:half], 2), swap(six[half:], 4)


def scatter_halves(blocks, came):
    if lax.axis_size("seq") != 8:
        return ()
    _, two, four, _ = blocks
    half, width = two.shape[0] // 2, two.shape[1]
    which = lax.broadcasted_iota(jnp.int32, (2, half, width), 0)

    def with_half(block, part, side):
        part = jnp.where(which == side, part.astype(F32)[None], 0.0)
        return (block.reshape(2, half, width) + part).astype(BF).reshape(2 * half, width)

    return with_half(two, came[1], 1), with_half(four, came[0], 0)


def scatter_relay(halves):
    return (swap(halves[0], 2), swap(halves[1], 4)) if halves else ()


def scatter_join(blocks, relayed):
    n = lax.axis_size("seq")
    if n == 8:
        return blocks[0] + relayed[0].astype(F32) + relayed[1].astype(F32)
    step = n // 2
    while step > 1:
        keep = len(blocks) // 2
        sent = [swap(block.astype(BF), step).astype(F32) for block in blocks[keep:]]
        blocks = [block.astype(F32) + got for block, got in zip(blocks[:keep], sent)]
        step //= 2
    return blocks[0]


def scatter_groups(rows):
    bit, index = lax.axis_size("dp") // 2, lax.axis_index("dp")
    while bit > 0:
        half = rows.shape[0] // 2
        upper = (index & bit) != 0
        sent = jnp.where(upper, rows[:half], rows[half:]).astype(BF)
        other = yield exchange(sent, "dp", bit)
        rows = jnp.where(upper, rows[half:], rows[:half]) + other.astype(F32)
        bit //= 2
    return rows


def exchange(values, axis, bit):
    size = lax.axis_size(axis)
    return lax.ppermute(values, axis, [(i, i ^ bit) for i in range(size)])


class Order:
    def __init__(self):
        self.last = ()

    def tie(self, value):
        if not jax.tree.leaves(value) or not jax.tree.leaves(self.last):
            return value
        return lax.optimization_barrier((value, self.last))[0]

    def mark(self, value):
        if jax.tree.leaves(value):
            self.last = value
        return value

    def pause(self, value):
        return self.mark(self.tie(value))


def doubling(held, axes):
    for axis in axes:
        bit, index = 1, lax.axis_index(axis)
        while bit < lax.axis_size(axis):
            other = yield exchange(held, axis, bit)
            upper = (index & bit) != 0
            held = jnp.concatenate([jnp.where(upper, other, held), jnp.where(upper, held, other)], axis=0)
            bit *= 2
    return held


def line_gather(own):
    size, index = lax.axis_size("dp"), lax.axis_index("dp")
    below, above = [], []
    to_right, to_left = own, own
    for _ in range(size - 1):
        flight = (
            lax.ppermute(to_right, "dp", [(i, i + 1) for i in range(size - 1)]),
            lax.ppermute(to_left, "dp", [(i + 1, i) for i in range(size - 1)]),
        )
        to_right, to_left = yield flight
        below.insert(0, to_right)
        above.append(to_left)
    rows = jnp.concatenate(below + [own] + above, axis=0)
    return lax.dynamic_slice_in_dim(rows, (size - 1 - index) * own.shape[0], size * own.shape[0], axis=0)


def line_scatter(parts):
    size, index = lax.axis_size("dp"), lax.axis_index("dp")

    def part(which):
        return lax.dynamic_index_in_dim(parts, jnp.clip(which, 0, size - 1), 0, keepdims=False)

    right = left = None
    for step in range(size - 1):
        far = size - 1 - step
        up, down = part(index + far), part(index - far)
        if step:
            up, down = (up.astype(F32) + right.astype(F32)).astype(BF), (down.astype(F32) + left.astype(F32)).astype(BF)
        flight = (
            lax.ppermute(up, "dp", [(i, i + 1) for i in range(size - far)]),
            lax.ppermute(down, "dp", [(i, i - 1) for i in range(far, size)]),
        )
        right, left = yield flight
    return part(index).astype(F32) + right.astype(F32) + left.astype(F32)


class Steps:
    def __init__(self, order, generator):
        self.order, self.generator, self.flight, self.result = order, generator, next(generator), None

    def step(self, count=1):
        for _ in range(count):
            if self.flight is None:
                return
            try:
                self.flight = self.generator.send(self.order.pause(self.flight))
            except StopIteration as stop:
                self.flight, self.result = None, stop.value

    def finish(self):
        while self.flight is not None:
            self.step()
        return self.result


def scatter_small(table):
    count, width = table.shape
    length = -(-width // 1024) * 1024
    held = jnp.pad(table, ((0, 0), (0, length - width))).reshape(count, 8, length // 8)
    for axis in ("dp", "seq"):
        bit, index = lax.axis_size(axis) // 2, lax.axis_index(axis)
        while bit > 0:
            half = held.shape[0] // 2
            upper = (index & bit) != 0
            sent = jnp.where(upper, held[:half], held[half:])
            held = jnp.where(upper, held[half:], held[:half]) + exchange(sent, axis, bit)
            bit //= 2
    return held.reshape(length)[:width]


def after(value, *earlier):
    return lax.optimization_barrier((value, *earlier))[0]


def weight_grad_kernel(*refs):
    count = (len(refs) - 1) // 2
    total = dot_tn(refs[0][...], refs[count][...])
    for part in range(1, count):
        total = total + dot_tn(refs[part][...], refs[count + part][...])
    refs[-1][...] = total.astype(BF)


def weight_grad(lefts, rights, left_tile, right_tile):
    rows, left_width = lefts[0].shape
    right_width = rights[0].shape[1]
    left_tile, right_tile = min(left_tile, left_width), min(right_tile, right_width)
    count = len(lefts)
    return pl.pallas_call(
        weight_grad_kernel,
        grid=(right_width // right_tile, left_width // left_tile),
        in_specs=[pl.BlockSpec((rows, left_tile), lambda j, i: (0, i))] * count
        + [pl.BlockSpec((rows, right_tile), lambda j, i: (0, j))] * count,
        out_specs=pl.BlockSpec((left_tile, right_tile), lambda j, i: (i, j)),
        out_shape=jax.ShapeDtypeStruct((left_width, right_width), BF),
        compiler_params=pltpu.CompilerParams(dimension_semantics=("arbitrary", "arbitrary"), vmem_limit_bytes=LARGE_GRANT),
        cost_estimate=light_cost(2 * count * rows * left_width * right_width),
        name="weight_grad",
    )(*lefts, *rights)


def tile_dot(left, right, turned):
    return dot_nt(left, right) if turned else dot(left, right)


def plain_kernel(left_ref, right_ref, out_ref, *, turned):
    out_ref[...] = tile_dot(left_ref[...], right_ref[...], turned).astype(out_ref.dtype)


def project_kernel(left_ref, right_ref, bias_ref, scale_ref, out_ref):
    out_ref[...] = ((dot(left_ref[...], right_ref[...]) + bias_ref[...]) * scale_ref[...]).astype(BF)


def up_kernel(left_ref, right_ref, bias_ref, out_ref):
    out_ref[...] = jnp.maximum(dot(left_ref[...], right_ref[...]) + bias_ref[...], 0.0).astype(BF)


def masked_kernel(left_ref, right_ref, act_ref, out_ref, sums_ref):
    grad = jnp.where(act_ref[...] > 0, dot_nt(left_ref[...], right_ref[...]), 0.0).astype(BF)
    out_ref[...] = grad
    part = jnp.sum(grad.astype(F32).reshape(-1, 8, grad.shape[1]), axis=0)

    @pl.when(pl.program_id(1) == 0)
    def _():
        sums_ref[...] = part

    @pl.when(pl.program_id(1) > 0)
    def _():
        sums_ref[...] = sums_ref[...] + part


def blocks_kernel(left_ref, right_ref, got_ref, *out_refs, turned):
    rows = out_refs[0].shape[0]
    for m in range(len(out_refs) - 1, -1, -1):
        cut = slice(m * rows, (m + 1) * rows)
        total = tile_dot(left_ref[cut, :], right_ref[...], turned) + got_ref[cut, :].astype(F32)
        out_refs[m][...] = total.astype(out_refs[m].dtype)


def light_cost(flops):
    return pl.CostEstimate(flops=int(flops) // 8, bytes_accessed=1, transcendentals=0)


def tiled(kernel, name, left, right, turned, extras, outs, row_tile, col_tile, parts=1):
    rows, depth = left.shape
    cols = right.shape[0] if turned else right.shape[1]
    row_tile, col_tile = min(row_tile, rows), min(col_tile, cols)
    kinds = {
        "both": pl.BlockSpec((row_tile, col_tile), lambda j, m: (m, j)),
        "vector": pl.BlockSpec((1, col_tile), lambda j, m: (0, j)),
        "sums": pl.BlockSpec((8, col_tile), lambda j, m: (0, j)),
        "block": pl.BlockSpec((rows // parts, col_tile), lambda j, m: (0, j)),
    }
    shapes = {"both": (rows, cols), "sums": (8, cols), "block": (rows // parts, cols)}
    right_spec = (
        pl.BlockSpec((col_tile, depth), lambda j, m: (j, 0)) if turned else pl.BlockSpec((depth, col_tile), lambda j, m: (0, j))
    )
    return pl.pallas_call(
        kernel,
        grid=(cols // col_tile, rows // row_tile),
        in_specs=[pl.BlockSpec((row_tile, depth), lambda j, m: (m, 0)), right_spec] + [kinds[k] for k, _ in extras],
        out_specs=[kinds[k] for k, _ in outs],
        out_shape=[jax.ShapeDtypeStruct(shapes[k], dtype) for k, dtype in outs],
        compiler_params=pltpu.CompilerParams(dimension_semantics=("arbitrary", "arbitrary"), vmem_limit_bytes=PRODUCT_GRANT),
        cost_estimate=light_cost(2 * rows * cols * depth),
        name=name,
    )(left, right, *[value for _, value in extras])


def plain_product(left, right, turned=False):
    kernel = functools.partial(plain_kernel, turned=turned)
    return tiled(kernel, "product", left, right, turned, [], [("both", BF)], 1024, 256)[0]


def project_product(left, right, bias, scale):
    extras = [("vector", bias.reshape(1, -1)), ("vector", scale.reshape(1, -1))]
    return tiled(project_kernel, "project", left, right, False, extras, [("both", BF)], 1024, 256)[0]


def up_product(left, right, bias):
    return tiled(up_kernel, "up", left, right, False, [("vector", bias.reshape(1, -1))], [("both", BF)], 1024, 256)[0]


def masked_product(left, right, act):
    outs = [("both", BF), ("sums", F32)]
    return tiled(masked_kernel, "masked_product", left, right, True, [("both", act)], outs, 1024, 256)


def block_products(left, right, got, count, turned=False):
    kernel = functools.partial(blocks_kernel, turned=turned)
    outs = [("block", F32)] * (count - 1) + [("block", BF)]
    return tiled(
        kernel, "block_products", left, right, turned, [("both", got)], outs, left.shape[0], 256, count
    )


def norm_kernel(*refs, unit):
    *piece_refs, gain_ref, shift_ref, out_ref = refs
    step, at = pl.program_id(0), 0
    for piece_ref in piece_refs:
        for start in range(0, piece_ref.shape[0], unit):

            @pl.when(step == at)
            def _(piece_ref=piece_ref, start=start):
                normed, _ = norm_core(piece_ref[start : start + unit, :].astype(F32))
                out_ref[...] = (normed * gain_ref[...] + shift_ref[...]).astype(BF)

            at += 1


def norm_rows(pieces, gain, shift):
    rows, width = sum(piece.shape[0] for piece in pieces), pieces[0].shape[1]
    unit = min(min(piece.shape[0] for piece in pieces), 128)
    whole = [pl.BlockSpec(piece.shape, lambda i: (0, 0)) for piece in pieces]
    vector = pl.BlockSpec((1, width), lambda i: (0, 0))
    return pl.pallas_call(
        functools.partial(norm_kernel, unit=unit),
        grid=(rows // unit,),
        in_specs=whole + [vector, vector],
        out_specs=pl.BlockSpec((unit, width), lambda i: (i, 0)),
        out_shape=jax.ShapeDtypeStruct((rows, width), BF),
        compiler_params=pltpu.CompilerParams(dimension_semantics=("arbitrary",), vmem_limit_bytes=PRODUCT_GRANT),
        cost_estimate=light_cost(2000 * rows * width),
        name="norm_rows",
    )(*pieces, gain.reshape(1, -1), shift.reshape(1, -1))


def visible_scores(q_head, k_block, first, q_place, key_start, length):
    scores = dot_nt(q_head, k_block)
    k_place = key_start + lax.broadcasted_iota(jnp.int32, (1, length), 1)
    allowed = (k_place >= first) & (k_place <= q_place)
    return jnp.where(allowed, scores, NEG_FILL)


def storage_row(block, place, blocks, length):
    k = block ^ place
    return pl.multiple_of(((k >> 1) + (k & 1) * (blocks // 2)) * length, length)


def spread_heads(source_ref, target_ref, lanes, heads, length, blocks):
    def one(m, carry):
        rows = source_ref[pl.ds(pl.multiple_of(m * length, length), length), :]
        for h in range(heads):
            target = pl.ds(pl.multiple_of((m * heads + h) * length, length), length)
            target_ref[target, :] = jnp.where(lanes == h, rows, jnp.zeros_like(rows))
        return carry

    lax.fori_loop(0, blocks, one, 0)


def fold(values, op):
    out = values[:, :128]
    for start in range(128, values.shape[1], 128):
        out = op(out, values[:, start : start + 128])
    return out


def attend_forward_kernel(
    place_ref, low_ref, q_ref, k_ref, v_ref, first_ref, o_ref, lse_ref, s_scr, m_scr, l_scr, v_scr, *, heads, length, blocks
):
    i = pl.program_id(0)
    place = place_ref[0]
    low = low_ref[i]
    width = heads * HD
    lanes = lax.broadcasted_iota(jnp.int32, (length, width), 1) // HD
    q_all = q_ref[...]
    q_heads = [jnp.where(lanes == h, q_all, jnp.zeros_like(q_all)) for h in range(heads)]
    first = first_ref[...]
    q_place = i * length + lax.broadcasted_iota(jnp.int32, (length, 1), 0)
    m_scr[...] = jnp.full_like(m_scr, NEG_FILL)
    l_scr[...] = jnp.zeros_like(l_scr)

    @pl.when(i == 0)
    def _():
        spread_heads(v_ref, v_scr, lanes, heads, length, blocks)

    def score_step(j, carry):
        k_block = k_ref[pl.ds(storage_row(j, place, blocks, length), length), :]
        cols = pl.ds(pl.multiple_of(j * length, length), length)
        for h in range(heads):
            scores = visible_scores(q_heads[h], k_block, first, q_place, j * length, length)
            s_scr[h, :, cols] = scores
            m_scr[h] = jnp.maximum(m_scr[h], fold(scores, jnp.maximum))
        return carry

    lax.fori_loop(low, i + 1, score_step, 0)
    tops = [jnp.max(m_scr[h], axis=-1, keepdims=True) for h in range(heads)]

    def exp_step(j, carry):
        cols = pl.ds(pl.multiple_of(j * length, length), length)
        for h in range(heads):
            raised = jnp.exp(s_scr[h, :, cols] - tops[h])
            s_scr[h, :, cols] = raised
            l_scr[h] = l_scr[h] + fold(raised, jnp.add)
        return carry

    lax.fori_loop(low, i + 1, exp_step, 0)
    totals = [jnp.sum(l_scr[h], axis=-1, keepdims=True) for h in range(heads)]
    scales = [1.0 / total for total in totals]

    def mix_step(j, acc):
        rows = pl.ds(pl.multiple_of(storage_row(j, place, blocks, length) * heads, heads * length), heads * length)
        cols = pl.ds(pl.multiple_of(j * length, length), length)
        probs = [(s_scr[h, :, cols] * scales[h]).astype(BF) for h in range(heads)]
        return acc + dot(jnp.concatenate(probs, axis=1), v_scr[rows, :])

    mixed = lax.fori_loop(low, i + 1, mix_step, jnp.zeros((length, width), F32))
    o_ref[...] = mixed.astype(BF)
    cols = lax.broadcasted_iota(jnp.int32, (length, 128), 1)
    lse = jnp.zeros((length, 128), F32)
    for h in range(heads):
        lse = jnp.where(cols == h, tops[h] + jnp.log(totals[h]), lse)
    lse_ref[...] = lse


def attend_backward_kernel(
    place_ref, low_ref, q_ref, go_ref, o_ref, lse_ref, k_ref, v_ref, first_ref, even_ref, odd_ref, kt_scr, vt_scr, k_scr,
    *, heads, length, blocks
):
    i = pl.program_id(0)
    place = place_ref[0]
    low = low_ref[i]
    width = heads * HD
    lanes = lax.broadcasted_iota(jnp.int32, (length, width), 1) // HD
    first = first_ref[...]
    q_place = i * length + lax.broadcasted_iota(jnp.int32, (length, 1), 0)
    q_all, go_all = q_ref[...], go_ref[...]
    inner_all = go_all.astype(F32) * o_ref[...].astype(F32)
    q_turned, go_turned = q_all.astype(F32).T.astype(BF), go_all.astype(F32).T.astype(BF)
    lse_all = lse_ref[...]
    q_heads, go_heads, inner, lse = [], [], [], []
    for h in range(heads):
        mine = lanes == h
        q_heads.append(jnp.where(mine, q_all, jnp.zeros_like(q_all)))
        go_heads.append(jnp.where(mine, go_all, jnp.zeros_like(go_all)))
        inner.append(jnp.sum(jnp.where(mine, inner_all, 0.0), axis=-1, keepdims=True))
        lse.append(lse_all[:, h : h + 1])

    @pl.when(i == 0)
    def _():
        kt_scr[...] = jnp.zeros_like(kt_scr)
        vt_scr[...] = jnp.zeros_like(vt_scr)
        spread_heads(k_ref, k_scr, lanes, heads, length, blocks)

    def step(j, acc):
        start = storage_row(j, place, blocks, length)
        rows = pl.ds(start, length)
        k_block, v_block = k_ref[rows, :], v_ref[rows, :]
        k_place = j * length + lax.broadcasted_iota(jnp.int32, (1, length), 1)
        allowed = (k_place >= first) & (k_place <= q_place)
        every = range(heads)
        scores = [dot_nt(q_heads[h], k_block) for h in every]
        grad_probs = [dot_nt(go_heads[h], v_block) for h in every]
        probs = [jnp.exp(jnp.where(allowed, scores[h] - lse[h], NEG_FILL)) for h in every]
        grad_scores = [(probs[h] * (grad_probs[h] - inner[h])).astype(BF) for h in every]
        for h in every:
            part = slice(h * HD, (h + 1) * HD)
            vt_scr[part, rows] = vt_scr[part, rows] + dot(go_turned[part, :], probs[h].astype(BF))
            kt_scr[part, rows] = kt_scr[part, rows] + dot(q_turned[part, :], grad_scores[h])
        spread = pl.ds(pl.multiple_of(start * heads, heads * length), heads * length)
        return acc + dot(jnp.concatenate(grad_scores, axis=1), k_scr[spread, :])

    grad_q = lax.fori_loop(low, i + 1, step, jnp.zeros((length, width), F32))
    grad_q = (grad_q.astype(BF).astype(F32) * (HD**-0.5)).astype(BF)
    k = i ^ place
    own_rows = pl.ds(pl.multiple_of((k >> 1) * length, length), length)

    @pl.when((k & 1) == 0)
    def _():
        even_ref[own_rows, 0:width] = grad_q

    @pl.when((k & 1) == 1)
    def _():
        odd_ref[own_rows, 0:width] = grad_q

    @pl.when(i == blocks - 1)
    def _():
        for j in range(blocks):
            target, m = (even_ref, j) if j < blocks // 2 else (odd_ref, j - blocks // 2)
            source, rows = slice(j * length, (j + 1) * length), slice(m * length, (m + 1) * length)
            target[rows, width : 2 * width] = kt_scr[:, source].T.astype(BF)
            target[rows, 2 * width : 3 * width] = vt_scr[:, source].T.astype(BF)


def storage_map(length, blocks, column):
    def index(i, place_ref, low_ref):
        k = i ^ place_ref[0]
        return ((k >> 1) + (k & 1) * (blocks // 2), column)

    return index


def attend_forward(place, low, qkv, first, length):
    rows, triple = qkv.shape
    width, blocks = triple // 3, rows // length
    heads = width // HD
    return pl.pallas_call(
        functools.partial(attend_forward_kernel, heads=heads, length=length, blocks=blocks),
        grid_spec=pltpu.PrefetchScalarGridSpec(
            num_scalar_prefetch=2,
            grid=(blocks,),
            in_specs=[
                pl.BlockSpec((length, width), storage_map(length, blocks, 0)),
                pl.BlockSpec((rows, width), lambda i, p, w: (0, 1)),
                pl.BlockSpec((rows, width), lambda i, p, w: (0, 2)),
                pl.BlockSpec((length, 1), lambda i, p, w: (i, 0)),
            ],
            out_specs=[
                pl.BlockSpec((length, width), lambda i, p, w: (i, 0)),
                pl.BlockSpec((length, 128), lambda i, p, w: (i, 0)),
            ],
            scratch_shapes=[
                pltpu.VMEM((heads, length, rows), F32),
                pltpu.VMEM((heads, length, 128), F32),
                pltpu.VMEM((heads, length, 128), F32),
                pltpu.VMEM((heads * rows, width), BF),
            ],
        ),
        out_shape=[jax.ShapeDtypeStruct((rows, width), BF), jax.ShapeDtypeStruct((rows, 128), F32)],
        compiler_params=pltpu.CompilerParams(dimension_semantics=("arbitrary",), vmem_limit_bytes=LARGE_GRANT),
        cost_estimate=light_cost(24 * rows * rows * width),
        name="attend_forward",
    )(place, low, qkv, qkv, qkv, first)


def attend_backward(place, low, qkv, grad_out, mixed, lse, first, length):
    rows, triple = qkv.shape
    width, blocks = triple // 3, rows // length
    heads = width // HD
    return pl.pallas_call(
        functools.partial(attend_backward_kernel, heads=heads, length=length, blocks=blocks),
        grid_spec=pltpu.PrefetchScalarGridSpec(
            num_scalar_prefetch=2,
            grid=(blocks,),
            in_specs=[
                pl.BlockSpec((length, width), storage_map(length, blocks, 0)),
                pl.BlockSpec((length, width), lambda i, p, w: (i, 0)),
                pl.BlockSpec((length, width), lambda i, p, w: (i, 0)),
                pl.BlockSpec((length, 128), lambda i, p, w: (i, 0)),
                pl.BlockSpec((rows, width), lambda i, p, w: (0, 1)),
                pl.BlockSpec((rows, width), lambda i, p, w: (0, 2)),
                pl.BlockSpec((length, 1), lambda i, p, w: (i, 0)),
            ],
            out_specs=[pl.BlockSpec((rows // 2, triple), lambda i, p, w: (0, 0))] * 2,
            scratch_shapes=[
                pltpu.VMEM((width, rows), F32),
                pltpu.VMEM((width, rows), F32),
                pltpu.VMEM((heads * rows, width), BF),
            ],
        ),
        out_shape=[jax.ShapeDtypeStruct((rows // 2, triple), BF)] * 2,
        compiler_params=pltpu.CompilerParams(dimension_semantics=("arbitrary",), vmem_limit_bytes=LARGE_GRANT),
        cost_estimate=light_cost(36 * rows * rows * width),
        name="attend_backward",
    )(place, low, qkv, grad_out, mixed, lse, qkv, qkv, first)


def local(
    inputs,
    teacher,
    segment_ids,
    summary_start,
    valid_mask,
    attn_norm_gain,
    attn_norm_bias,
    query_weight,
    query_bias,
    key_weight,
    value_weight,
    value_bias,
    out_weight,
    out_bias,
    mlp_norm_gain,
    mlp_norm_bias,
    up_weight,
    up_bias,
    down_weight,
    down_bias,
):
    seqs, length = segment_ids.shape
    width = inputs.shape[-1]
    hidden_units = up_weight.shape[1]
    n, groups = lax.axis_size("seq"), lax.axis_size("dp")
    place, group = lax.axis_index("seq"), lax.axis_index("dp")
    both = ("dp", "seq")
    seq_len = length * n
    tokens_all = seqs * seq_len * groups
    scale = HD**-0.5
    own_rows = query_weight.shape[0]
    own_hidden = up_bias.shape[0]
    head_cols = width // n

    def out_of(value):
        return lax.all_to_all(value, "seq", split_axis=0, concat_axis=0, tiled=True)

    valid = valid_mask.astype(F32)
    order = Order()
    near = n == 8 and groups == 4
    out_steps = Steps(order, line_gather(out_weight)) if near else None
    cut = jnp.concatenate(
        [w.reshape(own_rows, n, head_cols).transpose(1, 0, 2) for w in (query_weight, key_weight, value_weight)], axis=2
    )
    qkv_cut = out_of(cut)
    small = [attn_norm_gain, attn_norm_bias, out_bias, mlp_norm_gain, mlp_norm_bias, down_bias, query_bias, value_bias, up_bias]
    pieces = [v.astype(F32) for v in small] + [segment_ids.astype(F32).reshape(-1), jnp.sum(valid).reshape(1)]
    starts, lines = [], []
    for piece in pieces:
        starts.append(sum(line.shape[0] for line in lines))
        short = -piece.shape[0] % 128
        lines.append(jnp.pad(piece, (0, short)).reshape(-1, 128))
    used = sum(line.shape[0] for line in lines)
    packed = jnp.pad(jnp.concatenate(lines, axis=0), ((0, -used % 8), (0, 0)))[None]
    small_steps = Steps(order, doubling(after(packed, cut), ("dp", "seq")))
    small_steps.step(1)
    qkv_cut = order.pause(qkv_cut).reshape(n * own_rows, 3 * head_cols)
    w_qkv = lax.all_gather(qkv_cut, "dp", axis=0, tiled=True)
    if near:
        out_steps.step()
    small_steps.step(1)
    if near:
        out_steps.step()
    small_steps.step(1)
    if near:
        own_out = out_steps.finish()
    packed = small_steps.finish().reshape(n, groups, -1, 128).transpose(1, 0, 2, 3).reshape(groups * n, -1, 128)

    def zero_after(value):
        return jnp.minimum(jnp.abs(value.reshape(-1)[0].astype(F32)), 0.0).astype(jnp.int32)

    def rows_after(b, value):
        return lax.dynamic_index_in_dim(inputs, b + zero_after(value), 0, keepdims=False)

    state = [types.SimpleNamespace() for _ in range(seqs)]
    state[0].own = rows_after(0, packed)
    state[0].came = gather_start(state[0].own)
    parts = []
    for piece, at in zip(pieces, starts):
        count = -(-piece.shape[0] // 128)
        parts.append(packed[:, at : at + count].reshape(groups * n, -1)[:, : piece.shape[0]])
    gain_one, shift_one, b_out, gain_two, shift_two, b_down = [part.reshape(-1) for part in parts[:6]]
    b_query, b_value = [lax.dynamic_slice_in_dim(part.reshape(-1), place * head_cols, head_cols) for part in parts[6:8]]
    b_up = lax.dynamic_index_in_dim(parts[8].reshape(groups, n, -1), place, 1, keepdims=False).reshape(-1)
    ids = lax.dynamic_index_in_dim(parts[9].reshape(groups, n, seqs, length), group, 0, keepdims=False)
    ids = ids.transpose(1, 0, 2).reshape(seqs, seq_len)
    total_count = jnp.sum(parts[10])

    up_cut = up_weight.reshape(own_rows, groups, n, own_hidden).transpose(2, 0, 1, 3).reshape(n, own_rows, groups * own_hidden)
    b_qkv = jnp.concatenate([b_query, jnp.zeros_like(b_query), b_value])
    s_qkv = jnp.concatenate([jnp.full((head_cols,), scale, F32), jnp.ones((2 * head_cols,), F32)])

    place_arr = place.reshape(1).astype(jnp.int32)
    positions = jnp.arange(seq_len, dtype=jnp.int32)

    def add_all(terms):
        out = terms[0]
        for term in terms[1:]:
            out = out + term
        return out


    def spans(b):
        st = state[b]
        first = jnp.sum((ids[b][None, :] < ids[b][:, None]).astype(jnp.int32), axis=1)
        in_summary = (positions >= summary_start[b]) & (positions < summary_start[b] + NSUM)
        first = jnp.where(in_summary, 0, first)
        st.low = jnp.min(first.reshape(n, length), axis=1) // length
        st.first = first.reshape(seq_len, 1)

    def project(b):
        st = state[b]
        even, odd = order.tie((st.even, st.odd))
        parts = [project_product(part, w_qkv, b_qkv, s_qkv) for part in (even, odd)]
        st.qkv = order.mark(jnp.concatenate(parts, axis=0))

    def attend(b):
        st = state[b]
        qkv = order.tie(st.qkv)
        st.mixed, st.lse = attend_forward(place_arr, st.low, qkv, st.first, length)
        order.mark(st.mixed)

    def send_mixed(b):
        st = state[b]
        st.moved = out_of(st.mixed.reshape(n, length, head_cols))

    def middle(b):
        st = state[b]
        attended = order.tie(st.moved)
        st.attended = attended.transpose(1, 0, 2).reshape(length, width)
        rows = inputs[b].astype(F32)
        st.hidden = rows + (dot(st.attended, w_out) + b_out)
        st.normed_two, st.inverse_two = norm_core(st.hidden)
        st.own_two = order.mark((st.normed_two * gain_two + shift_two).astype(BF))
        st.came_two = gather_start(st.own_two)

    def up_even(b):
        st = state[b]
        st.act_even = order.mark(up_product(order.tie(st.even_two), w_up, b_up))

    def up_odd(b):
        st = state[b]
        st.act_odd = order.mark(up_product(order.tie(st.odd_two), w_up, b_up))

    def relay(b, own, came):
        st = state[b]
        came = order.pause(getattr(st, came))
        return came, gather_relay(getattr(st, own), came)

    def join(b, own, came_relayed):
        same = order.mark(gather_join(getattr(state[b], own), *order.tie(came_relayed)))
        return same, swap(same, 1)

    def down_odd(b):
        st = state[b]
        st.down_got = swap(order.mark(plain_product(order.tie(st.act_odd), w_down)), 1)

    def down_even(b):
        st = state[b]
        st.down_sums = order.mark(block_products(st.act_even, w_down, order.tie(st.down_got), n // 2))
        st.down_came = scatter_start(st.down_sums)

    def pass_on(b, sums, came):
        st = state[b]
        came = order.pause(getattr(st, came))
        return scatter_relay(order.mark(scatter_halves(getattr(st, sums), came)))

    def misfit(b):
        st = state[b]
        summed = scatter_join(st.down_sums, order.tie(st.down_sent))
        st.result = st.hidden + (summed + b_down)
        error = st.result - teacher[b].astype(F32)
        st.local_sq = jnp.sum(jnp.sum(error * error, axis=-1) * valid[b])
        st.grad_result = error * (valid[b] * (tokens_all / total_count))[:, None]
        st.own_grad = order.mark(st.grad_result.astype(BF))
        st.g_b_down = jnp.sum(st.own_grad.astype(F32), axis=0)
        st.came_grad = gather_start(st.own_grad)

    def act_back_even(b):
        st = state[b]
        st.pre_even, st.sums_even = masked_product(order.tie(st.gm_even), w_down, st.act_even)
        order.mark(st.pre_even)

    def act_back_odd(b):
        st = state[b]
        st.pre_odd, st.sums_odd = masked_product(order.tie(st.gm_odd), w_down, st.act_odd)
        order.mark(st.pre_odd)

    def up_back_odd(b):
        st = state[b]
        st.up_got = swap(order.mark(plain_product(order.tie(st.pre_odd), w_up, turned=True)), 1)

    def up_back_even(b):
        st = state[b]
        st.up_sums = order.mark(block_products(st.pre_even, w_up, order.tie(st.up_got), n // 2, turned=True))
        st.up_came = scatter_start(st.up_sums)

    def branch_back(b):
        st = state[b]
        grad_ready = scatter_join(st.up_sums, order.tie(st.up_sent))
        grad_norm, st.g_gain_two, st.g_shift_two = norm_back(grad_ready, st.normed_two, st.inverse_two, gain_two)
        st.grad_hidden = st.grad_result + grad_norm
        st.branch = st.grad_hidden.astype(BF)
        st.g_b_out = jnp.sum(st.branch.astype(F32), axis=0)
        grad_att = dot_nt(st.branch, w_out).astype(BF).reshape(length, n, head_cols).transpose(1, 0, 2)
        st.grad_mixed = out_of(order.mark(grad_att)).reshape(seq_len, head_cols)

    def attend_back(b):
        st = state[b]
        st.grad_qkv = attend_backward(
            place_arr, st.low, st.qkv, order.tie(st.grad_mixed), st.mixed, st.lse, st.first, length
        )
        order.mark(st.grad_qkv)
        st.g_b_qkv = sum(jnp.sum(part.astype(F32), axis=0) for part in st.grad_qkv)

    def project_back_odd(b):
        st = state[b]
        odd = order.tie(st.grad_qkv[1])
        st.one_got = swap(order.mark(plain_product(odd, w_qkv, turned=True)), 1)

    def project_back_even(b):
        st = state[b]
        st.one_sums = block_products(st.grad_qkv[0], w_qkv, order.tie(st.one_got), n // 2, turned=True)
        order.mark(st.one_sums)
        st.one_came = scatter_start(st.one_sums)

    def finish(b):
        st = state[b]
        grad_ready = scatter_join(st.one_sums, order.tie(st.one_sent))
        normed, inverse = norm_core(inputs[b].astype(F32))
        grad_norm, st.g_gain_one, st.g_shift_one = norm_back(grad_ready, normed, inverse, gain_one)
        st.grad_inputs = order.mark(st.grad_hidden + grad_norm)

    every, later = range(seqs), range(1, seqs)

    def whole_out_weight(own, came, relayed):
        whole = jnp.zeros((groups, n, own_rows, width), BF)
        half = groups // 2
        same = [(0, own, 0), (2, came[0], 0), (4, came[1], 0), (6, relayed[0], 0), (6, relayed[1], half)]
        other = [(k + 1, swap(piece, 1), first) for k, piece, first in same]
        for k, piece, first in same + other:
            whole = lax.dynamic_update_slice(whole, piece.reshape(-1, 1, own_rows, width), (first, place ^ k, 0, 0))
        return whole.reshape(width, width)

    def make_ready(b, came_relayed):
        st = state[b]
        st.even = order.mark(norm_rows(gather_pieces(st.own, *order.tie(came_relayed)), gain_one, shift_one))
        st.odd = swap(st.even, 1)

    for b in every:
        spans(b)
    came_relayed = relay(0, "own", "came")
    for b in later:
        state[b].own = rows_after(b, came_relayed[0][0] if near else packed)
        state[b].came = gather_start(state[b].own)
    make_ready(0, came_relayed)
    up_cut = out_of(after(up_cut, qkv_cut))
    if near:
        own_out = order.tie(own_out)
        out_came = order.pause(gather_start(own_out))
        out_relayed = gather_relay(own_out, out_came)
    else:
        w_out = lax.all_gather(after(out_weight, qkv_cut), both, axis=0, tiled=True)
    up_cut = order.pause(up_cut)
    w_up = lax.all_gather(up_cut.reshape(n * own_rows, groups * own_hidden), "dp", axis=0, tiled=True)
    w_down = lax.all_gather(after(down_weight, up_cut), "dp", axis=0, tiled=True)
    w_qkv = order.pause(w_qkv)
    project(0)
    attend(0)
    send_mixed(0)
    came_relayed = [relay(b, "own", "came") for b in later]
    raw = came_relayed
    if near:
        w_out = whole_out_weight(own_out, out_came, order.pause(out_relayed))
    middle(0)
    for b in later:
        last, st = state[b - 1], state[b]
        make_ready(b, raw[b - 1])
        project(b)
        came_relayed = relay(b - 1, "own_two", "came_two")
        attend(b)
        send_mixed(b)
        last.even_two, last.odd_two = join(b - 1, "own_two", came_relayed)
        up_even(b - 1)
        middle(b)
        up_odd(b - 1)
        came_relayed = relay(b, "own_two", "came_two")
        down_odd(b - 1)
        st.even_two, st.odd_two = join(b, "own_two", came_relayed)
        up_even(b)
        down_even(b - 1)
        up_odd(b)
        last.down_sent = pass_on(b - 1, "down_sums", "down_came")
        down_odd(b)
        down_even(b)
        misfit(b - 1)
        st.down_sent = pass_on(b, "down_sums", "down_came")
        came_relayed = relay(b - 1, "own_grad", "came_grad")
        misfit(b)
        last.gm_even, last.gm_odd = join(b - 1, "own_grad", came_relayed)
        act_back_even(b - 1)
        act_back_odd(b - 1)
        came_relayed = relay(b, "own_grad", "came_grad")
        up_back_odd(b - 1)
        up_back_even(b - 1)
        st.gm_even, st.gm_odd = join(b, "own_grad", came_relayed)
        act_back_even(b)
        last.up_sent = pass_on(b - 1, "up_sums", "up_came")
        act_back_odd(b)
        up_back_odd(b)
        up_back_even(b)
    lefts = [part for st in state for part in (st.even_two, st.odd_two)]
    rights = [part for st in state for part in (st.pre_even, st.pre_odd)]
    g_w_up = order.mark(weight_grad(order.tie(lefts), rights, 512, 1024))
    g_up = lax.psum_scatter(g_w_up, "dp", scatter_dimension=0, tiled=True)
    for b in later:
        state[b].up_sent = pass_on(b, "up_sums", "up_came")
    branch_back(0)
    lefts = [part for st in state for part in (st.act_even, st.act_odd)]
    rights = [part for st in state for part in (st.gm_even, st.gm_odd)]
    g_w_down = order.mark(weight_grad(order.tie(lefts), rights, 256, 1024))
    g_down = lax.psum_scatter(g_w_down, "dp", scatter_dimension=0, tiled=True)
    state[0].grad_mixed = order.pause(state[0].grad_mixed)
    for b in later:
        branch_back(b)
    turned = [
        st.attended.reshape(length, groups, n, own_rows).transpose(2, 0, 1, 3).reshape(n, length, groups * own_rows)
        for st in state
    ]

    def out_block(k):
        return add_all(
            [dot_tn(lax.dynamic_index_in_dim(t, place ^ k, 0, keepdims=False), st.branch) for t, st in zip(turned, state)]
        )

    out_rows = groups * own_rows
    turned = order.tie(turned)
    out_odd = order.mark(jnp.concatenate([out_block(k).astype(BF) for k in range(1, n, 2)], axis=0))
    out_got = swap(out_odd, 1)
    attend_back(0)
    out_got = order.tie(out_got)
    out_sums = [out_block(2 * m) + out_got[m * out_rows : (m + 1) * out_rows].astype(F32) for m in range(n // 2)]
    order.mark(out_sums)
    out_came = scatter_start(out_sums)
    project_back_odd(0)
    out_sent = scatter_relay(order.mark(scatter_halves(out_sums, order.pause(out_came))))
    project_back_even(0)
    g_up, g_down = order.pause((g_up, g_down))
    g_up = out_of(g_up.reshape(n, own_rows, groups * own_hidden))
    for b in later:
        attend_back(b)
    for b in later:
        state[b - 1].one_sent = pass_on(b - 1, "one_sums", "one_came")
        project_back_odd(b)
    out_sum = order.mark(scatter_join(out_sums, order.tie(out_sent)))
    out_group_steps = Steps(order, scatter_groups(out_sum))
    lefts = [part for st in state for part in (st.even, st.odd)]
    rights = [part for st in state for part in st.grad_qkv]
    g_w_qkv = order.mark(weight_grad(order.tie(lefts), rights, 1024, 768))
    if near:
        qkv_steps = Steps(order, line_scatter(g_w_qkv.reshape(groups, n * own_rows, 3 * head_cols)))
    else:
        g_qkv = lax.psum_scatter(g_w_qkv, "dp", scatter_dimension=0, tiled=True)
    g_up = order.pause(g_up)
    for b in later:
        state[b - 1].one_sent = order.pause(state[b - 1].one_sent)
        project_back_even(b)
    if near:
        qkv_steps.step()
    out_group_steps.step()
    for b in later:
        state[b].one_sent = pass_on(b, "one_sums", "one_came")
        finish(b - 1)
    if near:
        qkv_steps.step()
    g_out = out_group_steps.finish()
    for b in later:
        state[b].one_sent = order.pause(state[b].one_sent)
    if near:
        g_qkv = order.mark(qkv_steps.finish().astype(BF))
    g_qkv = out_of(g_qkv.reshape(n, own_rows, 3 * head_cols))
    for b in later:
        finish(b)

    def summed(name):
        return add_all([after(getattr(st, name), *state[-1].one_sums) for st in state])

    g_down = order.tie(g_down).astype(F32)
    g_up = g_up.reshape(n, own_rows, groups, own_hidden).transpose(1, 2, 0, 3).reshape(own_rows, hidden_units).astype(F32)
    g_qkv_came = g_qkv
    g_qkv = g_qkv.reshape(n, own_rows, 3, head_cols).transpose(2, 1, 0, 3).reshape(3, own_rows, width).astype(F32)

    g_b_qkv = summed("g_b_qkv").reshape(3, head_cols)
    own_bias = jnp.zeros((2, width), F32)
    own_bias = lax.dynamic_update_slice(own_bias, jnp.stack([g_b_qkv[0], g_b_qkv[2]]), (0, place * head_cols))
    g_b_up = jnp.sum(summed("sums_even") + summed("sums_odd"), axis=0).reshape(groups, 1, own_hidden)
    spread_up = lax.dynamic_update_slice_in_dim(jnp.zeros((groups, n, own_hidden), F32), g_b_up, place, 1)
    names = ("g_gain_one", "g_shift_one", "g_b_out", "g_gain_two", "g_shift_two", "g_b_down")
    vectors = jnp.concatenate([jnp.stack([summed(name) for name in names]), own_bias], axis=0)
    count = vectors.shape[0]
    vectors = vectors.reshape(count, groups * n, own_rows).transpose(1, 0, 2).reshape(groups * n, count * own_rows)
    sq = jnp.broadcast_to(summed("local_sq"), (groups * n, 1))
    tail = jnp.concatenate([vectors, spread_up.reshape(groups * n, own_hidden), sq], axis=1)
    tail = scatter_small(after(tail, g_qkv_came))
    vectors = tail[: count * own_rows].reshape(count, own_rows)
    g_b_query, g_b_value, g_b_up = vectors[6], vectors[7], tail[count * own_rows : -1]
    mean_loss = tail[-1] / (total_count * width)
    return (
        jnp.stack([st.result.astype(BF) for st in state]),
        mean_loss,
        jnp.stack([st.grad_inputs for st in state]),
        vectors[0],
        vectors[1],
        g_qkv[0],
        g_b_query,
        g_qkv[1],
        g_qkv[2],
        g_b_value,
        g_out,
        vectors[2],
        vectors[3],
        vectors[4],
        g_up,
        g_b_up,
        g_down,
        vectors[5],
    )


def solution(mesh):
    rows3, rows2, flat, mat = P("dp", "seq", None), P("dp", "seq"), P(("dp", "seq")), P(("dp", "seq"), None)
    placed = (
        rows3, rows3, rows2, P("dp"), rows2, flat, flat, mat, flat, mat, mat, flat, mat, flat, flat, flat, mat, flat, mat, flat,
    )
    out = (rows3, P(), rows3, flat, flat, mat, flat, mat, mat, flat, mat, flat, flat, flat, mat, flat, mat, flat)
    return jax.shard_map(local, mesh=mesh, in_specs=placed, out_specs=out, check_vma=False)
```

```python
import functools
import types

import jax
import jax.numpy as jnp
from jax import lax
from jax.experimental import pallas as pl
from jax.experimental.pallas import tpu as pltpu
from jax.sharding import PartitionSpec as P

HD = 64
NSUM = 50
NORM_EPS = 1e-05
NEG_FILL = -1e30
PRODUCT_GRANT, LARGE_GRANT = 30 << 20, 56 << 20
BF = jnp.bfloat16
F32 = jnp.float32


def dot(left_in, right_in):
    return jnp.dot(left_in, right_in, preferred_element_type=F32)


def dot_tn(left_in, right_in):
    return lax.dot_general(left_in, right_in, (((0,), (0,)), ((), ())), preferred_element_type=F32)


def dot_nt(left_in, right_in):
    return lax.dot_general(left_in, right_in, (((1,), (1,)), ((), ())), preferred_element_type=F32)


def norm_core(values):
    center = values - jnp.mean(values, axis=-1, keepdims=True)
    inverse = lax.rsqrt(jnp.mean(center * center, axis=-1, keepdims=True) + NORM_EPS)
    return center * inverse, inverse


def norm_back(grad_out, normed, inverse, gain_in):
    grad_normed = grad_out * gain_in
    inner_one = jnp.mean(grad_normed, axis=-1, keepdims=True)
    inner_two = jnp.mean(grad_normed * normed, axis=-1, keepdims=True)
    grad_in = inverse * (grad_normed - inner_one - normed * inner_two)
    return grad_in, jnp.sum(grad_out * normed, axis=0), jnp.sum(grad_out, axis=0)


def swap(values, mask):
    n = lax.axis_size("seq")
    return lax.ppermute(values, "seq", [(i, i ^ mask) for i in range(n)])


def gather_start(own):
    return (swap(own, 2), swap(own, 4)) if lax.axis_size("seq") == 8 else ()


def gather_relay(own, came):
    if lax.axis_size("seq") != 8:
        return ()
    half = own.shape[0] // 2
    return swap(came[1][:half], 2), swap(came[0][half:], 4)


def gather_pieces(own, came, relayed):
    if lax.axis_size("seq") == 8:
        return [own, *came, *relayed]
    return [gather_join(own, came, relayed)]


def gather_join(own, came, relayed):
    if lax.axis_size("seq") == 8:
        return jnp.concatenate([own, *came, *relayed], axis=0)
    same, step = own, 2
    while step < lax.axis_size("seq"):
        same = jnp.concatenate([same, swap(same, step)], axis=0)
        step *= 2
    return same


def gather_rows(own):
    came = gather_start(own)
    same = gather_join(own, came, gather_relay(own, came))
    return same, swap(same, 1)


def scatter_start(blocks):
    if lax.axis_size("seq") != 8:
        return ()
    six = blocks[3].astype(BF)
    half = six.shape[0] // 2
    return swap(six[:half], 2), swap(six[half:], 4)


def scatter_halves(blocks, came):
    if lax.axis_size("seq") != 8:
        return ()
    _, two, four, _ = blocks
    half, width = two.shape[0] // 2, two.shape[1]
    which = lax.broadcasted_iota(jnp.int32, (2, half, width), 0)

    def with_half(block, part, side):
        part = jnp.where(which == side, part.astype(F32)[None], 0.0)
        return (block.reshape(2, half, width) + part).astype(BF).reshape(2 * half, width)

    return with_half(two, came[1], 1), with_half(four, came[0], 0)


def scatter_relay(halves):
    return (swap(halves[0], 2), swap(halves[1], 4)) if halves else ()


def scatter_join(blocks, relayed):
    n = lax.axis_size("seq")
    if n == 8:
        return blocks[0] + relayed[0].astype(F32) + relayed[1].astype(F32)
    step = n // 2
    while step > 1:
        keep = len(blocks) // 2
        sent = [swap(block.astype(BF), step).astype(F32) for block in blocks[keep:]]
        blocks = [block.astype(F32) + got for block, got in zip(blocks[:keep], sent)]
        step //= 2
    return blocks[0]


def exchange(values, axis, bit):
    size = lax.axis_size(axis)
    return lax.ppermute(values, axis, [(i, i ^ bit) for i in range(size)])


class Order:
    def __init__(self):
        self.last = ()

    def tie(self, value):
        if not jax.tree.leaves(value) or not jax.tree.leaves(self.last):
            return value
        return lax.optimization_barrier((value, self.last))[0]

    def mark(self, value):
        if jax.tree.leaves(value):
            self.last = value
        return value

    def pause(self, value):
        return self.mark(self.tie(value))


def doubling(held, axes):
    for axis in axes:
        bit, index = 1, lax.axis_index(axis)
        while bit < lax.axis_size(axis):
            other = yield exchange(held, axis, bit)
            upper = (index & bit) != 0
            held = jnp.concatenate([jnp.where(upper, other, held), jnp.where(upper, held, other)], axis=0)
            bit *= 2
    return held


def line_gather(own):
    size, index = lax.axis_size("dp"), lax.axis_index("dp")
    below, above = [], []
    to_right, to_left = own, own
    for _ in range(size - 1):
        flight = (
            lax.ppermute(to_right, "dp", [(i, i + 1) for i in range(size - 1)]),
            lax.ppermute(to_left, "dp", [(i + 1, i) for i in range(size - 1)]),
        )
        to_right, to_left = yield flight
        below.insert(0, to_right)
        above.append(to_left)
    rows = jnp.concatenate(below + [own] + above, axis=0)
    return lax.dynamic_slice_in_dim(rows, (size - 1 - index) * own.shape[0], size * own.shape[0], axis=0)


def line_scatter(parts):
    size, index = lax.axis_size("dp"), lax.axis_index("dp")

    def part(which):
        return lax.dynamic_index_in_dim(parts, jnp.clip(which, 0, size - 1), 0, keepdims=False)

    right = left = None
    for step in range(size - 1):
        far = size - 1 - step
        up, down = part(index + far), part(index - far)
        if step:
            up, down = (up.astype(F32) + right.astype(F32)).astype(BF), (down.astype(F32) + left.astype(F32)).astype(BF)
        flight = (
            lax.ppermute(up, "dp", [(i, i + 1) for i in range(size - far)]),
            lax.ppermute(down, "dp", [(i, i - 1) for i in range(far, size)]),
        )
        right, left = yield flight
    return part(index).astype(F32) + right.astype(F32) + left.astype(F32)


class Steps:
    def __init__(self, order, generator):
        self.order, self.generator, self.flight, self.result = order, generator, next(generator), None

    def step(self, count=1):
        for _ in range(count):
            if self.flight is None:
                return
            try:
                self.flight = self.generator.send(self.order.pause(self.flight))
            except StopIteration as stop:
                self.flight, self.result = None, stop.value

    def finish(self):
        while self.flight is not None:
            self.step()
        return self.result


def scatter_small(table, awaited):
    count, width = table.shape
    length = -(-width // 1024) * 1024
    held = jnp.pad(table, ((0, 0), (0, length - width))).reshape(count, 8, length // 8)
    for axis in ("dp", "seq"):
        bit, index = lax.axis_size(axis) // 2, lax.axis_index(axis)
        while bit > 0:
            half = held.shape[0] // 2
            upper = (index & bit) != 0
            sent = jnp.where(upper, held[:half], held[half:])
            held = jnp.where(upper, held[half:], held[:half]) + exchange(sent, axis, bit)
            bit //= 2
        if axis == "dp":
            held = after(held, awaited)
    return held.reshape(length)[:width]


def after(value, *earlier):
    return lax.optimization_barrier((value, *earlier))[0]


def weight_grad_kernel(*refs):
    count = (len(refs) - 1) // 2
    total = dot_tn(refs[0][...], refs[count][...])
    for part in range(1, count):
        total = total + dot_tn(refs[part][...], refs[count + part][...])
    refs[-1][...] = total.astype(BF)


def weight_grad(lefts, rights, left_tile, right_tile):
    rows, left_width = lefts[0].shape
    right_width = rights[0].shape[1]
    left_tile, right_tile = min(left_tile, left_width), min(right_tile, right_width)
    count = len(lefts)
    return pl.pallas_call(
        weight_grad_kernel,
        grid=(right_width // right_tile, left_width // left_tile),
        in_specs=[pl.BlockSpec((rows, left_tile), lambda j, i: (0, i))] * count
        + [pl.BlockSpec((rows, right_tile), lambda j, i: (0, j))] * count,
        out_specs=pl.BlockSpec((left_tile, right_tile), lambda j, i: (i, j)),
        out_shape=jax.ShapeDtypeStruct((left_width, right_width), BF),
        compiler_params=pltpu.CompilerParams(dimension_semantics=("arbitrary", "arbitrary"), vmem_limit_bytes=LARGE_GRANT),
        cost_estimate=light_cost(2 * count * rows * left_width * right_width),
        name="weight_grad",
    )(*lefts, *rights)


def tile_dot(left, right, turned):
    return dot_nt(left, right) if turned else dot(left, right)


def plain_kernel(left_ref, right_ref, out_ref, *, turned):
    out_ref[...] = tile_dot(left_ref[...], right_ref[...], turned).astype(out_ref.dtype)


def project_kernel(left_ref, right_ref, bias_ref, scale_ref, out_ref):
    out_ref[...] = ((dot(left_ref[...], right_ref[...]) + bias_ref[...]) * scale_ref[...]).astype(BF)


def up_kernel(left_ref, right_ref, bias_ref, out_ref):
    out_ref[...] = jnp.maximum(dot(left_ref[...], right_ref[...]) + bias_ref[...], 0.0).astype(BF)


def masked_kernel(left_ref, right_ref, act_ref, out_ref, sums_ref):
    grad = jnp.where(act_ref[...] > 0, dot_nt(left_ref[...], right_ref[...]), 0.0).astype(BF)
    out_ref[...] = grad
    part = jnp.sum(grad.astype(F32).reshape(-1, 8, grad.shape[1]), axis=0)

    @pl.when(pl.program_id(1) == 0)
    def _():
        sums_ref[...] = part

    @pl.when(pl.program_id(1) > 0)
    def _():
        sums_ref[...] = sums_ref[...] + part


def blocks_kernel(left_ref, right_ref, got_ref, *out_refs, turned):
    rows = out_refs[0].shape[0]
    for m in range(len(out_refs) - 1, -1, -1):
        cut = slice(m * rows, (m + 1) * rows)
        total = tile_dot(left_ref[cut, :], right_ref[...], turned) + got_ref[cut, :].astype(F32)
        out_refs[m][...] = total.astype(out_refs[m].dtype)


def light_cost(flops):
    return pl.CostEstimate(flops=int(flops) // 8, bytes_accessed=1, transcendentals=0)


def tiled(kernel, name, left, right, turned, extras, outs, row_tile, col_tile, parts=1):
    rows, depth = left.shape
    cols = right.shape[0] if turned else right.shape[1]
    row_tile, col_tile = min(row_tile, rows), min(col_tile, cols)
    kinds = {
        "both": pl.BlockSpec((row_tile, col_tile), lambda j, m: (m, j)),
        "vector": pl.BlockSpec((1, col_tile), lambda j, m: (0, j)),
        "sums": pl.BlockSpec((8, col_tile), lambda j, m: (0, j)),
        "block": pl.BlockSpec((rows // parts, col_tile), lambda j, m: (0, j)),
    }
    shapes = {"both": (rows, cols), "sums": (8, cols), "block": (rows // parts, cols)}
    right_spec = (
        pl.BlockSpec((col_tile, depth), lambda j, m: (j, 0)) if turned else pl.BlockSpec((depth, col_tile), lambda j, m: (0, j))
    )
    return pl.pallas_call(
        kernel,
        grid=(cols // col_tile, rows // row_tile),
        in_specs=[pl.BlockSpec((row_tile, depth), lambda j, m: (m, 0)), right_spec] + [kinds[k] for k, _ in extras],
        out_specs=[kinds[k] for k, _ in outs],
        out_shape=[jax.ShapeDtypeStruct(shapes[k], dtype) for k, dtype in outs],
        compiler_params=pltpu.CompilerParams(dimension_semantics=("arbitrary", "arbitrary"), vmem_limit_bytes=PRODUCT_GRANT),
        cost_estimate=light_cost(2 * rows * cols * depth),
        name=name,
    )(left, right, *[value for _, value in extras])


def plain_product(left, right, turned=False):
    kernel = functools.partial(plain_kernel, turned=turned)
    return tiled(kernel, "product", left, right, turned, [], [("both", BF)], 1024, 256)[0]


def project_product(left, right, bias, scale):
    extras = [("vector", bias.reshape(1, -1)), ("vector", scale.reshape(1, -1))]
    return tiled(project_kernel, "project", left, right, False, extras, [("both", BF)], 1024, 256)[0]


def up_product(left, right, bias):
    return tiled(up_kernel, "up", left, right, False, [("vector", bias.reshape(1, -1))], [("both", BF)], 1024, 256)[0]


def masked_product(left, right, act):
    outs = [("both", BF), ("sums", F32)]
    return tiled(masked_kernel, "masked_product", left, right, True, [("both", act)], outs, 1024, 256)


def block_products(left, right, got, count, turned=False):
    kernel = functools.partial(blocks_kernel, turned=turned)
    outs = [("block", F32)] * (count - 1) + [("block", BF)]
    return tiled(
        kernel, "block_products", left, right, turned, [("both", got)], outs, left.shape[0], 256, count
    )


def norm_kernel(*refs, unit):
    *piece_refs, gain_ref, shift_ref, out_ref = refs
    step, at = pl.program_id(0), 0
    for piece_ref in piece_refs:
        for start in range(0, piece_ref.shape[0], unit):

            @pl.when(step == at)
            def _(piece_ref=piece_ref, start=start):
                normed, _ = norm_core(piece_ref[start : start + unit, :].astype(F32))
                out_ref[...] = (normed * gain_ref[...] + shift_ref[...]).astype(BF)

            at += 1


def norm_rows(pieces, gain, shift):
    rows, width = sum(piece.shape[0] for piece in pieces), pieces[0].shape[1]
    unit = min(min(piece.shape[0] for piece in pieces), 128)
    whole = [pl.BlockSpec(piece.shape, lambda i: (0, 0)) for piece in pieces]
    vector = pl.BlockSpec((1, width), lambda i: (0, 0))
    return pl.pallas_call(
        functools.partial(norm_kernel, unit=unit),
        grid=(rows // unit,),
        in_specs=whole + [vector, vector],
        out_specs=pl.BlockSpec((unit, width), lambda i: (i, 0)),
        out_shape=jax.ShapeDtypeStruct((rows, width), BF),
        compiler_params=pltpu.CompilerParams(dimension_semantics=("arbitrary",), vmem_limit_bytes=PRODUCT_GRANT),
        cost_estimate=light_cost(2000 * rows * width),
        name="norm_rows",
    )(*pieces, gain.reshape(1, -1), shift.reshape(1, -1))


def visible_scores(q_head, k_block, first, q_place, key_start, length):
    scores = dot_nt(q_head, k_block)
    k_place = key_start + lax.broadcasted_iota(jnp.int32, (1, length), 1)
    allowed = (k_place >= first) & (k_place <= q_place)
    return jnp.where(allowed, scores, NEG_FILL)


def storage_row(block, place, blocks, length):
    k = block ^ place
    return pl.multiple_of(((k >> 1) + (k & 1) * (blocks // 2)) * length, length)


def spread_heads(source_ref, target_ref, lanes, heads, length, blocks):
    def one(m, carry):
        rows = source_ref[pl.ds(pl.multiple_of(m * length, length), length), :]
        for h in range(heads):
            target = pl.ds(pl.multiple_of((m * heads + h) * length, length), length)
            target_ref[target, :] = jnp.where(lanes == h, rows, jnp.zeros_like(rows))
        return carry

    lax.fori_loop(0, blocks, one, 0)


def fold(values, op):
    out = values[:, :128]
    for start in range(128, values.shape[1], 128):
        out = op(out, values[:, start : start + 128])
    return out


def attend_forward_kernel(
    place_ref, low_ref, q_ref, k_ref, v_ref, first_ref, o_ref, lse_ref, s_scr, m_scr, l_scr, v_scr, *, heads, length, blocks
):
    i = pl.program_id(0)
    place = place_ref[0]
    low = low_ref[i]
    width = heads * HD
    lanes = lax.broadcasted_iota(jnp.int32, (length, width), 1) // HD
    q_all = q_ref[...]
    q_heads = [jnp.where(lanes == h, q_all, jnp.zeros_like(q_all)) for h in range(heads)]
    first = first_ref[...]
    q_place = i * length + lax.broadcasted_iota(jnp.int32, (length, 1), 0)
    m_scr[...] = jnp.full_like(m_scr, NEG_FILL)
    l_scr[...] = jnp.zeros_like(l_scr)

    @pl.when(i == 0)
    def _():
        spread_heads(v_ref, v_scr, lanes, heads, length, blocks)

    def score_step(j, carry):
        k_block = k_ref[pl.ds(storage_row(j, place, blocks, length), length), :]
        cols = pl.ds(pl.multiple_of(j * length, length), length)
        for h in range(heads):
            scores = visible_scores(q_heads[h], k_block, first, q_place, j * length, length)
            s_scr[h, :, cols] = scores
            m_scr[h] = jnp.maximum(m_scr[h], fold(scores, jnp.maximum))
        return carry

    lax.fori_loop(low, i + 1, score_step, 0)
    tops = [jnp.max(m_scr[h], axis=-1, keepdims=True) for h in range(heads)]

    def exp_step(j, carry):
        cols = pl.ds(pl.multiple_of(j * length, length), length)
        for h in range(heads):
            raised = jnp.exp(s_scr[h, :, cols] - tops[h])
            s_scr[h, :, cols] = raised
            l_scr[h] = l_scr[h] + fold(raised, jnp.add)
        return carry

    lax.fori_loop(low, i + 1, exp_step, 0)
    totals = [jnp.sum(l_scr[h], axis=-1, keepdims=True) for h in range(heads)]
    scales = [1.0 / total for total in totals]

    def mix_step(j, acc):
        rows = pl.ds(pl.multiple_of(storage_row(j, place, blocks, length) * heads, heads * length), heads * length)
        cols = pl.ds(pl.multiple_of(j * length, length), length)
        probs = [(s_scr[h, :, cols] * scales[h]).astype(BF) for h in range(heads)]
        return acc + dot(jnp.concatenate(probs, axis=1), v_scr[rows, :])

    mixed = lax.fori_loop(low, i + 1, mix_step, jnp.zeros((length, width), F32))
    o_ref[...] = mixed.astype(BF)
    cols = lax.broadcasted_iota(jnp.int32, (length, 128), 1)
    lse = jnp.zeros((length, 128), F32)
    for h in range(heads):
        lse = jnp.where(cols == h, tops[h] + jnp.log(totals[h]), lse)
    lse_ref[...] = lse


def attend_backward_kernel(
    place_ref, low_ref, q_ref, go_ref, o_ref, lse_ref, k_ref, v_ref, first_ref, even_ref, odd_ref, kt_scr, vt_scr, k_scr,
    *, heads, length, blocks
):
    i = pl.program_id(0)
    place = place_ref[0]
    low = low_ref[i]
    width = heads * HD
    lanes = lax.broadcasted_iota(jnp.int32, (length, width), 1) // HD
    first = first_ref[...]
    q_place = i * length + lax.broadcasted_iota(jnp.int32, (length, 1), 0)
    q_all, go_all = q_ref[...], go_ref[...]
    inner_all = go_all.astype(F32) * o_ref[...].astype(F32)
    q_turned, go_turned = q_all.astype(F32).T.astype(BF), go_all.astype(F32).T.astype(BF)
    lse_all = lse_ref[...]
    q_heads, go_heads, inner, lse = [], [], [], []
    for h in range(heads):
        mine = lanes == h
        q_heads.append(jnp.where(mine, q_all, jnp.zeros_like(q_all)))
        go_heads.append(jnp.where(mine, go_all, jnp.zeros_like(go_all)))
        inner.append(jnp.sum(jnp.where(mine, inner_all, 0.0), axis=-1, keepdims=True))
        lse.append(lse_all[:, h : h + 1])

    @pl.when(i == 0)
    def _():
        kt_scr[...] = jnp.zeros_like(kt_scr)
        vt_scr[...] = jnp.zeros_like(vt_scr)
        spread_heads(k_ref, k_scr, lanes, heads, length, blocks)

    def step(j, acc):
        start = storage_row(j, place, blocks, length)
        rows = pl.ds(start, length)
        k_block, v_block = k_ref[rows, :], v_ref[rows, :]
        k_place = j * length + lax.broadcasted_iota(jnp.int32, (1, length), 1)
        allowed = (k_place >= first) & (k_place <= q_place)
        every = range(heads)
        scores = [dot_nt(q_heads[h], k_block) for h in every]
        grad_probs = [dot_nt(go_heads[h], v_block) for h in every]
        probs = [jnp.exp(jnp.where(allowed, scores[h] - lse[h], NEG_FILL)) for h in every]
        grad_scores = [(probs[h] * (grad_probs[h] - inner[h])).astype(BF) for h in every]
        for h in every:
            part = slice(h * HD, (h + 1) * HD)
            vt_scr[part, rows] = vt_scr[part, rows] + dot(go_turned[part, :], probs[h].astype(BF))
            kt_scr[part, rows] = kt_scr[part, rows] + dot(q_turned[part, :], grad_scores[h])
        spread = pl.ds(pl.multiple_of(start * heads, heads * length), heads * length)
        return acc + dot(jnp.concatenate(grad_scores, axis=1), k_scr[spread, :])

    grad_q = lax.fori_loop(low, i + 1, step, jnp.zeros((length, width), F32))
    grad_q = (grad_q.astype(BF).astype(F32) * (HD**-0.5)).astype(BF)
    k = i ^ place
    own_rows = pl.ds(pl.multiple_of((k >> 1) * length, length), length)

    @pl.when((k & 1) == 0)
    def _():
        even_ref[own_rows, 0:width] = grad_q

    @pl.when((k & 1) == 1)
    def _():
        odd_ref[own_rows, 0:width] = grad_q

    @pl.when(i == blocks - 1)
    def _():
        for j in range(blocks):
            target, m = (even_ref, j) if j < blocks // 2 else (odd_ref, j - blocks // 2)
            source, rows = slice(j * length, (j + 1) * length), slice(m * length, (m + 1) * length)
            target[rows, width : 2 * width] = kt_scr[:, source].T.astype(BF)
            target[rows, 2 * width : 3 * width] = vt_scr[:, source].T.astype(BF)


def storage_map(length, blocks, column):
    def index(i, place_ref, low_ref):
        k = i ^ place_ref[0]
        return ((k >> 1) + (k & 1) * (blocks // 2), column)

    return index


def attend_forward(place, low, qkv, first, length):
    rows, triple = qkv.shape
    width, blocks = triple // 3, rows // length
    heads = width // HD
    return pl.pallas_call(
        functools.partial(attend_forward_kernel, heads=heads, length=length, blocks=blocks),
        grid_spec=pltpu.PrefetchScalarGridSpec(
            num_scalar_prefetch=2,
            grid=(blocks,),
            in_specs=[
                pl.BlockSpec((length, width), storage_map(length, blocks, 0)),
                pl.BlockSpec((rows, width), lambda i, p, w: (0, 1)),
                pl.BlockSpec((rows, width), lambda i, p, w: (0, 2)),
                pl.BlockSpec((length, 1), lambda i, p, w: (i, 0)),
            ],
            out_specs=[
                pl.BlockSpec((length, width), lambda i, p, w: (i, 0)),
                pl.BlockSpec((length, 128), lambda i, p, w: (i, 0)),
            ],
            scratch_shapes=[
                pltpu.VMEM((heads, length, rows), F32),
                pltpu.VMEM((heads, length, 128), F32),
                pltpu.VMEM((heads, length, 128), F32),
                pltpu.VMEM((heads * rows, width), BF),
            ],
        ),
        out_shape=[jax.ShapeDtypeStruct((rows, width), BF), jax.ShapeDtypeStruct((rows, 128), F32)],
        compiler_params=pltpu.CompilerParams(dimension_semantics=("arbitrary",), vmem_limit_bytes=LARGE_GRANT),
        cost_estimate=light_cost(24 * rows * rows * width),
        name="attend_forward",
    )(place, low, qkv, qkv, qkv, first)


def attend_backward(place, low, qkv, grad_out, mixed, lse, first, length):
    rows, triple = qkv.shape
    width, blocks = triple // 3, rows // length
    heads = width // HD
    return pl.pallas_call(
        functools.partial(attend_backward_kernel, heads=heads, length=length, blocks=blocks),
        grid_spec=pltpu.PrefetchScalarGridSpec(
            num_scalar_prefetch=2,
            grid=(blocks,),
            in_specs=[
                pl.BlockSpec((length, width), storage_map(length, blocks, 0)),
                pl.BlockSpec((length, width), lambda i, p, w: (i, 0)),
                pl.BlockSpec((length, width), lambda i, p, w: (i, 0)),
                pl.BlockSpec((length, 128), lambda i, p, w: (i, 0)),
                pl.BlockSpec((rows, width), lambda i, p, w: (0, 1)),
                pl.BlockSpec((rows, width), lambda i, p, w: (0, 2)),
                pl.BlockSpec((length, 1), lambda i, p, w: (i, 0)),
            ],
            out_specs=[pl.BlockSpec((rows // 2, triple), lambda i, p, w: (0, 0))] * 2,
            scratch_shapes=[
                pltpu.VMEM((width, rows), F32),
                pltpu.VMEM((width, rows), F32),
                pltpu.VMEM((heads * rows, width), BF),
            ],
        ),
        out_shape=[jax.ShapeDtypeStruct((rows // 2, triple), BF)] * 2,
        compiler_params=pltpu.CompilerParams(dimension_semantics=("arbitrary",), vmem_limit_bytes=LARGE_GRANT),
        cost_estimate=light_cost(36 * rows * rows * width),
        name="attend_backward",
    )(place, low, qkv, grad_out, mixed, lse, qkv, qkv, first)


def local(
    inputs,
    teacher,
    segment_ids,
    summary_start,
    valid_mask,
    attn_norm_gain,
    attn_norm_bias,
    query_weight,
    query_bias,
    key_weight,
    value_weight,
    value_bias,
    out_weight,
    out_bias,
    mlp_norm_gain,
    mlp_norm_bias,
    up_weight,
    up_bias,
    down_weight,
    down_bias,
):
    seqs, length = segment_ids.shape
    width = inputs.shape[-1]
    hidden_units = up_weight.shape[1]
    n, groups = lax.axis_size("seq"), lax.axis_size("dp")
    place, group = lax.axis_index("seq"), lax.axis_index("dp")
    both = ("dp", "seq")
    seq_len = length * n
    tokens_all = seqs * seq_len * groups
    scale = HD**-0.5
    own_rows = query_weight.shape[0]
    own_hidden = up_bias.shape[0]
    head_cols = width // n

    def out_of(value):
        return lax.all_to_all(value, "seq", split_axis=0, concat_axis=0, tiled=True)

    valid = valid_mask.astype(F32)
    order = Order()
    near = n == 8 and groups == 4
    out_steps = Steps(order, line_gather(out_weight)) if near else None
    cut = jnp.concatenate(
        [w.reshape(own_rows, n, head_cols).transpose(1, 0, 2) for w in (query_weight, key_weight, value_weight)], axis=2
    )
    qkv_cut = out_of(cut)
    small = [attn_norm_gain, attn_norm_bias, out_bias, mlp_norm_gain, mlp_norm_bias, down_bias, query_bias, value_bias, up_bias]
    pieces = [v.astype(F32) for v in small] + [segment_ids.astype(F32).reshape(-1), jnp.sum(valid).reshape(1)]
    starts, lines = [], []
    for piece in pieces:
        starts.append(sum(line.shape[0] for line in lines))
        short = -piece.shape[0] % 128
        lines.append(jnp.pad(piece, (0, short)).reshape(-1, 128))
    used = sum(line.shape[0] for line in lines)
    packed = jnp.pad(jnp.concatenate(lines, axis=0), ((0, -used % 8), (0, 0)))[None]
    small_steps = Steps(order, doubling(after(packed, cut), ("dp", "seq")))
    small_steps.step(1)
    qkv_cut = order.pause(qkv_cut).reshape(n * own_rows, 3 * head_cols)
    w_qkv = lax.all_gather(qkv_cut, "dp", axis=0, tiled=True)
    if near:
        out_steps.step()
    small_steps.step(1)
    if near:
        out_steps.step()
    small_steps.step(1)
    if near:
        own_out = out_steps.finish()
    packed = small_steps.finish().reshape(n, groups, -1, 128).transpose(1, 0, 2, 3).reshape(groups * n, -1, 128)

    def zero_after(value):
        return jnp.minimum(jnp.abs(value.reshape(-1)[0].astype(F32)), 0.0).astype(jnp.int32)

    def rows_after(b, value):
        return lax.dynamic_index_in_dim(inputs, b + zero_after(value), 0, keepdims=False)

    state = [types.SimpleNamespace() for _ in range(seqs)]
    state[0].own = rows_after(0, packed)
    state[0].came = gather_start(state[0].own)
    parts = []
    for piece, at in zip(pieces, starts):
        count = -(-piece.shape[0] // 128)
        parts.append(packed[:, at : at + count].reshape(groups * n, -1)[:, : piece.shape[0]])
    gain_one, shift_one, b_out, gain_two, shift_two, b_down = [part.reshape(-1) for part in parts[:6]]
    b_query, b_value = [lax.dynamic_slice_in_dim(part.reshape(-1), place * head_cols, head_cols) for part in parts[6:8]]
    b_up = lax.dynamic_index_in_dim(parts[8].reshape(groups, n, -1), place, 1, keepdims=False).reshape(-1)
    ids = lax.dynamic_index_in_dim(parts[9].reshape(groups, n, seqs, length), group, 0, keepdims=False)
    ids = ids.transpose(1, 0, 2).reshape(seqs, seq_len)
    total_count = jnp.sum(parts[10])

    up_cut = up_weight.reshape(own_rows, groups, n, own_hidden).transpose(2, 0, 1, 3).reshape(n, own_rows, groups * own_hidden)
    b_qkv = jnp.concatenate([b_query, jnp.zeros_like(b_query), b_value])
    s_qkv = jnp.concatenate([jnp.full((head_cols,), scale, F32), jnp.ones((2 * head_cols,), F32)])

    place_arr = place.reshape(1).astype(jnp.int32)
    positions = jnp.arange(seq_len, dtype=jnp.int32)

    def add_all(terms):
        out = terms[0]
        for term in terms[1:]:
            out = out + term
        return out


    def spans(b):
        st = state[b]
        first = jnp.sum((ids[b][None, :] < ids[b][:, None]).astype(jnp.int32), axis=1)
        in_summary = (positions >= summary_start[b]) & (positions < summary_start[b] + NSUM)
        first = jnp.where(in_summary, 0, first)
        st.low = jnp.min(first.reshape(n, length), axis=1) // length
        st.first = first.reshape(seq_len, 1)

    def project(b):
        st = state[b]
        even, odd = order.tie((st.even, st.odd))
        parts = [project_product(part, w_qkv, b_qkv, s_qkv) for part in (even, odd)]
        st.qkv = order.mark(jnp.concatenate(parts, axis=0))

    def attend(b):
        st = state[b]
        qkv = order.tie(st.qkv)
        st.mixed, st.lse = attend_forward(place_arr, st.low, qkv, st.first, length)
        order.mark(st.mixed)

    def send_mixed(b):
        st = state[b]
        st.moved = out_of(st.mixed.reshape(n, length, head_cols))

    def middle(b):
        st = state[b]
        attended = order.tie(st.moved)
        st.attended = attended.transpose(1, 0, 2).reshape(length, width)
        rows = inputs[b].astype(F32)
        st.hidden = rows + (dot(st.attended, w_out) + b_out)
        st.normed_two, st.inverse_two = norm_core(st.hidden)
        st.own_two = order.mark((st.normed_two * gain_two + shift_two).astype(BF))
        st.came_two = gather_start(st.own_two)

    def up_even(b):
        st = state[b]
        st.act_even = order.mark(up_product(order.tie(st.even_two), w_up, b_up))

    def up_odd(b):
        st = state[b]
        st.act_odd = order.mark(up_product(order.tie(st.odd_two), w_up, b_up))

    def relay(b, own, came):
        st = state[b]
        came = order.pause(getattr(st, came))
        return came, gather_relay(getattr(st, own), came)

    def join(b, own, came_relayed):
        same = order.mark(gather_join(getattr(state[b], own), *order.tie(came_relayed)))
        return same, swap(same, 1)

    def down_odd(b):
        st = state[b]
        st.down_got = swap(order.mark(plain_product(order.tie(st.act_odd), w_down)), 1)

    def down_even(b):
        st = state[b]
        st.down_sums = order.mark(block_products(st.act_even, w_down, order.tie(st.down_got), n // 2))
        st.down_came = scatter_start(st.down_sums)

    def pass_on(b, sums, came):
        st = state[b]
        came = order.pause(getattr(st, came))
        return scatter_relay(order.mark(scatter_halves(getattr(st, sums), came)))

    def misfit(b):
        st = state[b]
        summed = scatter_join(st.down_sums, order.tie(st.down_sent))
        st.result = st.hidden + (summed + b_down)
        error = st.result - teacher[b].astype(F32)
        st.local_sq = jnp.sum(jnp.sum(error * error, axis=-1) * valid[b])
        st.grad_result = error * (valid[b] * (tokens_all / total_count))[:, None]
        st.own_grad = order.mark(st.grad_result.astype(BF))
        st.g_b_down = jnp.sum(st.own_grad.astype(F32), axis=0)
        st.came_grad = gather_start(st.own_grad)

    def act_back_even(b):
        st = state[b]
        st.pre_even, st.sums_even = masked_product(order.tie(st.gm_even), w_down, st.act_even)
        order.mark(st.pre_even)

    def act_back_odd(b):
        st = state[b]
        st.pre_odd, st.sums_odd = masked_product(order.tie(st.gm_odd), w_down, st.act_odd)
        order.mark(st.pre_odd)

    def up_back_odd(b):
        st = state[b]
        st.up_got = swap(order.mark(plain_product(order.tie(st.pre_odd), w_up, turned=True)), 1)

    def up_back_even(b):
        st = state[b]
        st.up_sums = order.mark(block_products(st.pre_even, w_up, order.tie(st.up_got), n // 2, turned=True))
        st.up_came = scatter_start(st.up_sums)

    def branch_back(b):
        st = state[b]
        grad_ready = scatter_join(st.up_sums, order.tie(st.up_sent))
        grad_norm, st.g_gain_two, st.g_shift_two = norm_back(grad_ready, st.normed_two, st.inverse_two, gain_two)
        st.grad_hidden = st.grad_result + grad_norm
        st.branch = st.grad_hidden.astype(BF)
        st.g_b_out = jnp.sum(st.branch.astype(F32), axis=0)
        grad_att = dot_nt(st.branch, w_out).astype(BF).reshape(length, n, head_cols).transpose(1, 0, 2)
        st.grad_mixed = out_of(order.mark(grad_att)).reshape(seq_len, head_cols)

    def attend_back(b):
        st = state[b]
        st.grad_qkv = attend_backward(
            place_arr, st.low, st.qkv, order.tie(st.grad_mixed), st.mixed, st.lse, st.first, length
        )
        order.mark(st.grad_qkv)
        st.g_b_qkv = sum(jnp.sum(part.astype(F32), axis=0) for part in st.grad_qkv)

    def project_back_odd(b):
        st = state[b]
        odd = order.tie(st.grad_qkv[1])
        st.one_got = swap(order.mark(plain_product(odd, w_qkv, turned=True)), 1)

    def project_back_even(b):
        st = state[b]
        st.one_sums = block_products(st.grad_qkv[0], w_qkv, order.tie(st.one_got), n // 2, turned=True)
        order.mark(st.one_sums)
        st.one_came = scatter_start(st.one_sums)

    def finish(b):
        st = state[b]
        grad_ready = scatter_join(st.one_sums, order.tie(st.one_sent))
        normed, inverse = norm_core(inputs[b].astype(F32))
        grad_norm, st.g_gain_one, st.g_shift_one = norm_back(grad_ready, normed, inverse, gain_one)
        st.grad_inputs = order.mark(st.grad_hidden + grad_norm)

    every, later = range(seqs), range(1, seqs)

    def whole_out_weight(own, came, relayed):
        whole = jnp.zeros((groups, n, own_rows, width), BF)
        half = groups // 2
        same = [(0, own, 0), (2, came[0], 0), (4, came[1], 0), (6, relayed[0], 0), (6, relayed[1], half)]
        other = [(k + 1, swap(piece, 1), first) for k, piece, first in same]
        for k, piece, first in same + other:
            whole = lax.dynamic_update_slice(whole, piece.reshape(-1, 1, own_rows, width), (first, place ^ k, 0, 0))
        return whole.reshape(width, width)

    def make_ready(b, came_relayed):
        st = state[b]
        st.even = order.mark(norm_rows(gather_pieces(st.own, *order.tie(came_relayed)), gain_one, shift_one))
        st.odd = swap(st.even, 1)

    for b in every:
        spans(b)
    came_relayed = relay(0, "own", "came")
    for b in later:
        state[b].own = rows_after(b, came_relayed[0][0] if near else packed)
        state[b].came = gather_start(state[b].own)
    if near:
        own_out = order.tie(own_out)
        out_came = gather_start(own_out)
    else:
        w_out = lax.all_gather(after(out_weight, qkv_cut), both, axis=0, tiled=True)
    make_ready(0, came_relayed)
    up_cut = out_of(after(up_cut, qkv_cut))
    if near:
        out_came = order.pause(out_came)
        out_relayed = gather_relay(own_out, out_came)
    up_cut = order.pause(up_cut)
    w_up = lax.all_gather(up_cut.reshape(n * own_rows, groups * own_hidden), "dp", axis=0, tiled=True)
    w_down = lax.all_gather(after(down_weight, up_cut), "dp", axis=0, tiled=True)
    w_qkv = order.pause(w_qkv)
    if near:
        out_relayed = order.pause(out_relayed)
    project(0)
    attend(0)
    send_mixed(0)
    came_relayed = [relay(b, "own", "came") for b in later]
    raw = came_relayed
    if near:
        w_out = whole_out_weight(own_out, out_came, out_relayed)
    middle(0)
    for b in later:
        last, st = state[b - 1], state[b]
        make_ready(b, raw[b - 1])
        project(b)
        came_relayed = relay(b - 1, "own_two", "came_two")
        attend(b)
        send_mixed(b)
        last.even_two, last.odd_two = join(b - 1, "own_two", came_relayed)
        up_even(b - 1)
        middle(b)
        up_odd(b - 1)
        came_relayed = relay(b, "own_two", "came_two")
        down_odd(b - 1)
        st.even_two, st.odd_two = join(b, "own_two", came_relayed)
        up_even(b)
        down_even(b - 1)
        up_odd(b)
        last.down_sent = pass_on(b - 1, "down_sums", "down_came")
        down_odd(b)
        down_even(b)
        misfit(b - 1)
        st.down_sent = pass_on(b, "down_sums", "down_came")
        came_relayed = relay(b - 1, "own_grad", "came_grad")
        misfit(b)
        last.gm_even, last.gm_odd = join(b - 1, "own_grad", came_relayed)
        act_back_even(b - 1)
        act_back_odd(b - 1)
        came_relayed = relay(b, "own_grad", "came_grad")
        up_back_odd(b - 1)
        up_back_even(b - 1)
        st.gm_even, st.gm_odd = join(b, "own_grad", came_relayed)
        act_back_even(b)
        last.up_sent = pass_on(b - 1, "up_sums", "up_came")
        act_back_odd(b)
        up_back_odd(b)
        up_back_even(b)
    lefts = [part for st in state for part in (st.even_two, st.odd_two)]
    rights = [part for st in state for part in (st.pre_even, st.pre_odd)]
    g_w_up = order.mark(weight_grad(order.tie(lefts), rights, 512, 1024))
    g_up = lax.psum_scatter(g_w_up, "dp", scatter_dimension=0, tiled=True)
    for b in later:
        state[b].up_sent = pass_on(b, "up_sums", "up_came")
    branch_back(0)
    lefts = [part for st in state for part in (st.act_even, st.act_odd)]
    rights = [part for st in state for part in (st.gm_even, st.gm_odd)]
    g_w_down = order.mark(weight_grad(order.tie(lefts), rights, 256, 1024))
    g_down = lax.psum_scatter(g_w_down, "dp", scatter_dimension=0, tiled=True)
    state[0].grad_mixed = order.pause(state[0].grad_mixed)
    for b in later:
        branch_back(b)
    turned = [
        st.attended.reshape(length, groups, n, own_rows).transpose(2, 0, 1, 3).reshape(n, length, groups * own_rows)
        for st in state
    ]

    def out_block(k):
        return add_all(
            [dot_tn(lax.dynamic_index_in_dim(t, place ^ k, 0, keepdims=False), st.branch) for t, st in zip(turned, state)]
        )

    out_rows = groups * own_rows
    turned = order.tie(turned)
    out_odd = order.mark(jnp.concatenate([out_block(k).astype(BF) for k in range(1, n, 2)], axis=0))
    out_got = swap(out_odd, 1)
    attend_back(0)
    out_got = order.tie(out_got)
    out_sums = [out_block(2 * m) + out_got[m * out_rows : (m + 1) * out_rows].astype(F32) for m in range(n // 2)]
    order.mark(out_sums)
    out_came = scatter_start(out_sums)
    project_back_odd(0)
    out_sent = scatter_relay(order.mark(scatter_halves(out_sums, order.pause(out_came))))
    project_back_even(0)
    g_up, g_down = order.pause((g_up, g_down))
    g_up = out_of(g_up.reshape(n, own_rows, groups * own_hidden))
    for b in later:
        attend_back(b)
        state[b - 1].one_came, out_sent = order.pause((state[b - 1].one_came, out_sent))
    for b in later:
        state[b - 1].one_sent = pass_on(b - 1, "one_sums", "one_came")
    out_sum = order.mark(scatter_join(out_sums, order.tie(out_sent)).astype(BF))
    out_parts = out_sum.reshape(groups, own_rows, width)
    out_line = Steps(order, line_scatter(out_parts)) if near else None
    for b in later:
        project_back_odd(b)
    lefts = [part for st in state for part in (st.even, st.odd)]
    rights = [part for st in state for part in st.grad_qkv]
    g_w_qkv = order.mark(weight_grad(order.tie(lefts), rights, 1024, 768))
    if near:
        out_line.step()
        qkv_line = Steps(order, line_scatter(g_w_qkv.reshape(groups, n * own_rows, 3 * head_cols)))
    else:
        g_qkv = lax.psum_scatter(g_w_qkv, "dp", scatter_dimension=0, tiled=True)
        g_out = lax.psum_scatter(out_sum, "dp", scatter_dimension=0, tiled=True)
    g_up = order.pause(g_up)
    for b in later:
        state[b - 1].one_sent = order.pause(state[b - 1].one_sent)
        project_back_even(b)
    if near:
        out_line.step()
        qkv_line.step()
    for b in later:
        state[b].one_sent = pass_on(b, "one_sums", "one_came")
        finish(b - 1)
    if near:
        g_out = out_line.finish()
        qkv_line.step()
    for b in later:
        state[b].one_sent = order.pause(state[b].one_sent)
    if near:
        g_qkv = order.mark(qkv_line.finish().astype(BF))
    g_qkv = out_of(g_qkv.reshape(n, own_rows, 3 * head_cols))
    for b in later:
        finish(b)
    g_out = g_out.astype(F32)

    def summed(name):
        return add_all([after(getattr(st, name), *state[-1].one_sums) for st in state])

    g_down = order.tie(g_down).astype(F32)
    g_up = g_up.reshape(n, own_rows, groups, own_hidden).transpose(1, 2, 0, 3).reshape(own_rows, hidden_units).astype(F32)
    g_qkv_came = g_qkv
    g_qkv = g_qkv.reshape(n, own_rows, 3, head_cols).transpose(2, 1, 0, 3).reshape(3, own_rows, width).astype(F32)

    g_b_qkv = summed("g_b_qkv").reshape(3, head_cols)
    own_bias = jnp.zeros((2, width), F32)
    own_bias = lax.dynamic_update_slice(own_bias, jnp.stack([g_b_qkv[0], g_b_qkv[2]]), (0, place * head_cols))
    g_b_up = jnp.sum(summed("sums_even") + summed("sums_odd"), axis=0).reshape(groups, 1, own_hidden)
    spread_up = lax.dynamic_update_slice_in_dim(jnp.zeros((groups, n, own_hidden), F32), g_b_up, place, 1)
    names = ("g_gain_one", "g_shift_one", "g_b_out", "g_gain_two", "g_shift_two", "g_b_down")
    vectors = jnp.concatenate([jnp.stack([summed(name) for name in names]), own_bias], axis=0)
    count = vectors.shape[0]
    vectors = vectors.reshape(count, groups * n, own_rows).transpose(1, 0, 2).reshape(groups * n, count * own_rows)
    sq = jnp.broadcast_to(summed("local_sq"), (groups * n, 1))
    tail = jnp.concatenate([vectors, spread_up.reshape(groups * n, own_hidden), sq], axis=1)
    tail = scatter_small(tail, g_qkv_came)
    vectors = tail[: count * own_rows].reshape(count, own_rows)
    g_b_query, g_b_value, g_b_up = vectors[6], vectors[7], tail[count * own_rows : -1]
    mean_loss = tail[-1] / (total_count * width)
    return (
        jnp.stack([st.result.astype(BF) for st in state]),
        mean_loss,
        jnp.stack([st.grad_inputs for st in state]),
        vectors[0],
        vectors[1],
        g_qkv[0],
        g_b_query,
        g_qkv[1],
        g_qkv[2],
        g_b_value,
        g_out,
        vectors[2],
        vectors[3],
        vectors[4],
        g_up,
        g_b_up,
        g_down,
        vectors[5],
    )


def solution(mesh):
    rows3, rows2, flat, mat = P("dp", "seq", None), P("dp", "seq"), P(("dp", "seq")), P(("dp", "seq"), None)
    placed = (
        rows3, rows3, rows2, P("dp"), rows2, flat, flat, mat, flat, mat, mat, flat, mat, flat, flat, flat, mat, flat, mat, flat,
    )
    out = (rows3, P(), rows3, flat, flat, mat, flat, mat, mat, flat, mat, flat, flat, flat, mat, flat, mat, flat)
    return jax.shard_map(local, mesh=mesh, in_specs=placed, out_specs=out, check_vma=False)
```

```python
import functools
import types

import jax
import jax.numpy as jnp
from jax import lax
from jax.experimental import pallas as pl
from jax.experimental.pallas import tpu as pltpu
from jax.sharding import PartitionSpec as P

HD = 64
NSUM = 50
NORM_EPS = 1e-05
NEG_FILL = -1e30
PRODUCT_GRANT, LARGE_GRANT = 30 << 20, 56 << 20
BF = jnp.bfloat16
F32 = jnp.float32


def dot(left_in, right_in):
    return jnp.dot(left_in, right_in, preferred_element_type=F32)


def dot_tn(left_in, right_in):
    return lax.dot_general(left_in, right_in, (((0,), (0,)), ((), ())), preferred_element_type=F32)


def dot_nt(left_in, right_in):
    return lax.dot_general(left_in, right_in, (((1,), (1,)), ((), ())), preferred_element_type=F32)


def norm_core(values):
    center = values - jnp.mean(values, axis=-1, keepdims=True)
    inverse = lax.rsqrt(jnp.mean(center * center, axis=-1, keepdims=True) + NORM_EPS)
    return center * inverse, inverse


def norm_back(grad_out, normed, inverse, gain_in):
    grad_normed = grad_out * gain_in
    inner_one = jnp.mean(grad_normed, axis=-1, keepdims=True)
    inner_two = jnp.mean(grad_normed * normed, axis=-1, keepdims=True)
    grad_in = inverse * (grad_normed - inner_one - normed * inner_two)
    return grad_in, jnp.sum(grad_out * normed, axis=0), jnp.sum(grad_out, axis=0)


def swap(values, mask):
    n = lax.axis_size("seq")
    return lax.ppermute(values, "seq", [(i, i ^ mask) for i in range(n)])


def gather_start(own):
    return (swap(own, 2), swap(own, 4)) if lax.axis_size("seq") == 8 else ()


def gather_relay(own, came):
    if lax.axis_size("seq") != 8:
        return ()
    half = own.shape[0] // 2
    return swap(came[1][:half], 2), swap(came[0][half:], 4)


def gather_pieces(own, came, relayed):
    if lax.axis_size("seq") == 8:
        return [own, *came, *relayed]
    return [gather_join(own, came, relayed)]


def gather_join(own, came, relayed):
    if lax.axis_size("seq") == 8:
        return jnp.concatenate([own, *came, *relayed], axis=0)
    same, step = own, 2
    while step < lax.axis_size("seq"):
        same = jnp.concatenate([same, swap(same, step)], axis=0)
        step *= 2
    return same


def gather_rows(own):
    came = gather_start(own)
    same = gather_join(own, came, gather_relay(own, came))
    return same, swap(same, 1)


def scatter_start(blocks):
    if lax.axis_size("seq") != 8:
        return ()
    six = blocks[3].astype(BF)
    half = six.shape[0] // 2
    return swap(six[:half], 2), swap(six[half:], 4)


def scatter_halves(blocks, came):
    if lax.axis_size("seq") != 8:
        return ()
    _, two, four, _ = blocks
    half, width = two.shape[0] // 2, two.shape[1]
    which = lax.broadcasted_iota(jnp.int32, (2, half, width), 0)

    def with_half(block, part, side):
        part = jnp.where(which == side, part.astype(F32)[None], 0.0)
        return (block.reshape(2, half, width) + part).astype(BF).reshape(2 * half, width)

    return with_half(two, came[1], 1), with_half(four, came[0], 0)


def scatter_relay(halves):
    return (swap(halves[0], 2), swap(halves[1], 4)) if halves else ()


def scatter_join(blocks, relayed):
    n = lax.axis_size("seq")
    if n == 8:
        return blocks[0] + relayed[0].astype(F32) + relayed[1].astype(F32)
    step = n // 2
    while step > 1:
        keep = len(blocks) // 2
        sent = [swap(block.astype(BF), step).astype(F32) for block in blocks[keep:]]
        blocks = [block.astype(F32) + got for block, got in zip(blocks[:keep], sent)]
        step //= 2
    return blocks[0]


def exchange(values, axis, bit):
    size = lax.axis_size(axis)
    return lax.ppermute(values, axis, [(i, i ^ bit) for i in range(size)])


class Order:
    def __init__(self):
        self.last = ()

    def tie(self, value):
        if not jax.tree.leaves(value) or not jax.tree.leaves(self.last):
            return value
        return lax.optimization_barrier((value, self.last))[0]

    def mark(self, value):
        if jax.tree.leaves(value):
            self.last = value
        return value

    def pause(self, value):
        return self.mark(self.tie(value))


def doubling(held, axes):
    for axis in axes:
        bit, index = 1, lax.axis_index(axis)
        while bit < lax.axis_size(axis):
            other = yield exchange(held, axis, bit)
            upper = (index & bit) != 0
            held = jnp.concatenate([jnp.where(upper, other, held), jnp.where(upper, held, other)], axis=0)
            bit *= 2
    return held


def line_gather(own):
    size, index = lax.axis_size("dp"), lax.axis_index("dp")
    below, above = [], []
    to_right, to_left = own, own
    for _ in range(size - 1):
        flight = (
            lax.ppermute(to_right, "dp", [(i, i + 1) for i in range(size - 1)]),
            lax.ppermute(to_left, "dp", [(i + 1, i) for i in range(size - 1)]),
        )
        to_right, to_left = yield flight
        below.insert(0, to_right)
        above.append(to_left)
    rows = jnp.concatenate(below + [own] + above, axis=0)
    return lax.dynamic_slice_in_dim(rows, (size - 1 - index) * own.shape[0], size * own.shape[0], axis=0)


def line_scatter(parts):
    size, index = lax.axis_size("dp"), lax.axis_index("dp")

    def part(which):
        return lax.dynamic_index_in_dim(parts, jnp.clip(which, 0, size - 1), 0, keepdims=False)

    right = left = None
    for step in range(size - 1):
        far = size - 1 - step
        up, down = part(index + far), part(index - far)
        if step:
            up, down = (up.astype(F32) + right.astype(F32)).astype(BF), (down.astype(F32) + left.astype(F32)).astype(BF)
        flight = (
            lax.ppermute(up, "dp", [(i, i + 1) for i in range(size - far)]),
            lax.ppermute(down, "dp", [(i, i - 1) for i in range(far, size)]),
        )
        right, left = yield flight
    return part(index).astype(F32) + right.astype(F32) + left.astype(F32)


class Steps:
    def __init__(self, order, generator):
        self.order, self.generator, self.flight, self.result = order, generator, next(generator), None

    def step(self, count=1):
        for _ in range(count):
            if self.flight is None:
                return
            try:
                self.flight = self.generator.send(self.order.pause(self.flight))
            except StopIteration as stop:
                self.flight, self.result = None, stop.value

    def finish(self):
        while self.flight is not None:
            self.step()
        return self.result


def scatter_small(table, awaited):
    count, width = table.shape
    length = -(-width // 1024) * 1024
    held = jnp.pad(table, ((0, 0), (0, length - width))).reshape(count, 8, length // 8)
    for axis in ("dp", "seq"):
        bit, index = lax.axis_size(axis) // 2, lax.axis_index(axis)
        while bit > 0:
            half = held.shape[0] // 2
            upper = (index & bit) != 0
            sent = jnp.where(upper, held[:half], held[half:])
            held = jnp.where(upper, held[half:], held[:half]) + exchange(sent, axis, bit)
            bit //= 2
        if axis == "dp":
            held = after(held, awaited)
    return held.reshape(length)[:width]


def after(value, *earlier):
    return lax.optimization_barrier((value, *earlier))[0]


def weight_grad_kernel(*refs):
    count = (len(refs) - 1) // 2
    total = dot_tn(refs[0][...], refs[count][...])
    for part in range(1, count):
        total = total + dot_tn(refs[part][...], refs[count + part][...])
    refs[-1][...] = total.astype(BF)


def weight_grad(lefts, rights, left_tile, right_tile):
    rows, left_width = lefts[0].shape
    right_width = rights[0].shape[1]
    left_tile, right_tile = min(left_tile, left_width), min(right_tile, right_width)
    count = len(lefts)
    return pl.pallas_call(
        weight_grad_kernel,
        grid=(right_width // right_tile, left_width // left_tile),
        in_specs=[pl.BlockSpec((rows, left_tile), lambda j, i: (0, i))] * count
        + [pl.BlockSpec((rows, right_tile), lambda j, i: (0, j))] * count,
        out_specs=pl.BlockSpec((left_tile, right_tile), lambda j, i: (i, j)),
        out_shape=jax.ShapeDtypeStruct((left_width, right_width), BF),
        compiler_params=pltpu.CompilerParams(dimension_semantics=("arbitrary", "arbitrary"), vmem_limit_bytes=LARGE_GRANT),
        cost_estimate=light_cost(2 * count * rows * left_width * right_width),
        name="weight_grad",
    )(*lefts, *rights)


def tile_dot(left, right, turned):
    return dot_nt(left, right) if turned else dot(left, right)


def plain_kernel(left_ref, right_ref, out_ref, *, turned):
    out_ref[...] = tile_dot(left_ref[...], right_ref[...], turned).astype(out_ref.dtype)


def project_kernel(left_ref, right_ref, bias_ref, scale_ref, out_ref):
    out_ref[...] = ((dot(left_ref[...], right_ref[...]) + bias_ref[...]) * scale_ref[...]).astype(BF)


def up_kernel(left_ref, right_ref, bias_ref, out_ref):
    out_ref[...] = jnp.maximum(dot(left_ref[...], right_ref[...]) + bias_ref[...], 0.0).astype(BF)


def masked_kernel(left_ref, right_ref, act_ref, out_ref, sums_ref):
    grad = jnp.where(act_ref[...] > 0, dot_nt(left_ref[...], right_ref[...]), 0.0).astype(BF)
    out_ref[...] = grad
    part = jnp.sum(grad.astype(F32).reshape(-1, 8, grad.shape[1]), axis=0)

    @pl.when(pl.program_id(1) == 0)
    def _():
        sums_ref[...] = part

    @pl.when(pl.program_id(1) > 0)
    def _():
        sums_ref[...] = sums_ref[...] + part


def blocks_kernel(left_ref, right_ref, got_ref, *out_refs, turned):
    rows = out_refs[0].shape[0]
    for m in range(len(out_refs) - 1, -1, -1):
        cut = slice(m * rows, (m + 1) * rows)
        total = tile_dot(left_ref[cut, :], right_ref[...], turned) + got_ref[cut, :].astype(F32)
        out_refs[m][...] = total.astype(out_refs[m].dtype)


def light_cost(flops):
    return pl.CostEstimate(flops=int(flops) // 8, bytes_accessed=1, transcendentals=0)


def tiled(kernel, name, left, right, turned, extras, outs, row_tile, col_tile, parts=1):
    rows, depth = left.shape
    cols = right.shape[0] if turned else right.shape[1]
    row_tile, col_tile = min(row_tile, rows), min(col_tile, cols)
    kinds = {
        "both": pl.BlockSpec((row_tile, col_tile), lambda j, m: (m, j)),
        "vector": pl.BlockSpec((1, col_tile), lambda j, m: (0, j)),
        "sums": pl.BlockSpec((8, col_tile), lambda j, m: (0, j)),
        "block": pl.BlockSpec((rows // parts, col_tile), lambda j, m: (0, j)),
    }
    shapes = {"both": (rows, cols), "sums": (8, cols), "block": (rows // parts, cols)}
    right_spec = (
        pl.BlockSpec((col_tile, depth), lambda j, m: (j, 0)) if turned else pl.BlockSpec((depth, col_tile), lambda j, m: (0, j))
    )
    return pl.pallas_call(
        kernel,
        grid=(cols // col_tile, rows // row_tile),
        in_specs=[pl.BlockSpec((row_tile, depth), lambda j, m: (m, 0)), right_spec] + [kinds[k] for k, _ in extras],
        out_specs=[kinds[k] for k, _ in outs],
        out_shape=[jax.ShapeDtypeStruct(shapes[k], dtype) for k, dtype in outs],
        compiler_params=pltpu.CompilerParams(dimension_semantics=("arbitrary", "arbitrary"), vmem_limit_bytes=PRODUCT_GRANT),
        cost_estimate=light_cost(2 * rows * cols * depth),
        name=name,
    )(left, right, *[value for _, value in extras])


def plain_product(left, right, turned=False):
    kernel = functools.partial(plain_kernel, turned=turned)
    return tiled(kernel, "product", left, right, turned, [], [("both", BF)], 1024, 256)[0]


def project_product(left, right, bias, scale):
    extras = [("vector", bias.reshape(1, -1)), ("vector", scale.reshape(1, -1))]
    return tiled(project_kernel, "project", left, right, False, extras, [("both", BF)], 1024, 256)[0]


def up_product(left, right, bias):
    return tiled(up_kernel, "up", left, right, False, [("vector", bias.reshape(1, -1))], [("both", BF)], 1024, 256)[0]


def masked_product(left, right, act):
    outs = [("both", BF), ("sums", F32)]
    return tiled(masked_kernel, "masked_product", left, right, True, [("both", act)], outs, 1024, 256)


def block_products(left, right, got, count, turned=False):
    kernel = functools.partial(blocks_kernel, turned=turned)
    outs = [("block", F32)] * (count - 1) + [("block", BF)]
    return tiled(
        kernel, "block_products", left, right, turned, [("both", got)], outs, left.shape[0], 256, count
    )


def norm_kernel(*refs, unit):
    *piece_refs, gain_ref, shift_ref, out_ref = refs
    step, at = pl.program_id(0), 0
    for piece_ref in piece_refs:
        for start in range(0, piece_ref.shape[0], unit):

            @pl.when(step == at)
            def _(piece_ref=piece_ref, start=start):
                normed, _ = norm_core(piece_ref[start : start + unit, :].astype(F32))
                out_ref[...] = (normed * gain_ref[...] + shift_ref[...]).astype(BF)

            at += 1


def norm_rows(pieces, gain, shift):
    rows, width = sum(piece.shape[0] for piece in pieces), pieces[0].shape[1]
    unit = min(min(piece.shape[0] for piece in pieces), 128)
    whole = [pl.BlockSpec(piece.shape, lambda i: (0, 0)) for piece in pieces]
    vector = pl.BlockSpec((1, width), lambda i: (0, 0))
    return pl.pallas_call(
        functools.partial(norm_kernel, unit=unit),
        grid=(rows // unit,),
        in_specs=whole + [vector, vector],
        out_specs=pl.BlockSpec((unit, width), lambda i: (i, 0)),
        out_shape=jax.ShapeDtypeStruct((rows, width), BF),
        compiler_params=pltpu.CompilerParams(dimension_semantics=("arbitrary",), vmem_limit_bytes=PRODUCT_GRANT),
        cost_estimate=light_cost(2000 * rows * width),
        name="norm_rows",
    )(*pieces, gain.reshape(1, -1), shift.reshape(1, -1))


def visible_scores(q_head, k_block, first, q_place, key_start, length):
    scores = dot_nt(q_head, k_block)
    k_place = key_start + lax.broadcasted_iota(jnp.int32, (1, length), 1)
    allowed = (k_place >= first) & (k_place <= q_place)
    return jnp.where(allowed, scores, NEG_FILL)


def storage_row(block, place, blocks, length):
    k = block ^ place
    return pl.multiple_of(((k >> 1) + (k & 1) * (blocks // 2)) * length, length)


def spread_heads(source_ref, target_ref, lanes, heads, length, blocks):
    def one(m, carry):
        rows = source_ref[pl.ds(pl.multiple_of(m * length, length), length), :]
        for h in range(heads):
            target = pl.ds(pl.multiple_of((m * heads + h) * length, length), length)
            target_ref[target, :] = jnp.where(lanes == h, rows, jnp.zeros_like(rows))
        return carry

    lax.fori_loop(0, blocks, one, 0)


def fold(values, op):
    out = values[:, :128]
    for start in range(128, values.shape[1], 128):
        out = op(out, values[:, start : start + 128])
    return out


def attend_forward_kernel(
    place_ref, low_ref, q_ref, k_ref, v_ref, first_ref, o_ref, lse_ref, s_scr, m_scr, l_scr, v_scr, *, heads, length, blocks
):
    i = pl.program_id(0)
    place = place_ref[0]
    low = low_ref[i]
    width = heads * HD
    lanes = lax.broadcasted_iota(jnp.int32, (length, width), 1) // HD
    q_all = q_ref[...]
    q_heads = [jnp.where(lanes == h, q_all, jnp.zeros_like(q_all)) for h in range(heads)]
    first = first_ref[...]
    q_place = i * length + lax.broadcasted_iota(jnp.int32, (length, 1), 0)
    m_scr[...] = jnp.full_like(m_scr, NEG_FILL)
    l_scr[...] = jnp.zeros_like(l_scr)

    @pl.when(i == 0)
    def _():
        spread_heads(v_ref, v_scr, lanes, heads, length, blocks)

    def score_step(j, carry):
        k_block = k_ref[pl.ds(storage_row(j, place, blocks, length), length), :]
        cols = pl.ds(pl.multiple_of(j * length, length), length)
        for h in range(heads):
            scores = visible_scores(q_heads[h], k_block, first, q_place, j * length, length)
            s_scr[h, :, cols] = scores
            m_scr[h] = jnp.maximum(m_scr[h], fold(scores, jnp.maximum))
        return carry

    lax.fori_loop(low, i + 1, score_step, 0)
    tops = [jnp.max(m_scr[h], axis=-1, keepdims=True) for h in range(heads)]

    def exp_step(j, carry):
        cols = pl.ds(pl.multiple_of(j * length, length), length)
        for h in range(heads):
            raised = jnp.exp(s_scr[h, :, cols] - tops[h])
            s_scr[h, :, cols] = raised
            l_scr[h] = l_scr[h] + fold(raised, jnp.add)
        return carry

    lax.fori_loop(low, i + 1, exp_step, 0)
    totals = [jnp.sum(l_scr[h], axis=-1, keepdims=True) for h in range(heads)]
    scales = [1.0 / total for total in totals]

    def mix_step(j, acc):
        rows = pl.ds(pl.multiple_of(storage_row(j, place, blocks, length) * heads, heads * length), heads * length)
        cols = pl.ds(pl.multiple_of(j * length, length), length)
        probs = [(s_scr[h, :, cols] * scales[h]).astype(BF) for h in range(heads)]
        return acc + dot(jnp.concatenate(probs, axis=1), v_scr[rows, :])

    mixed = lax.fori_loop(low, i + 1, mix_step, jnp.zeros((length, width), F32))
    o_ref[...] = mixed.astype(BF)
    cols = lax.broadcasted_iota(jnp.int32, (length, 128), 1)
    lse = jnp.zeros((length, 128), F32)
    for h in range(heads):
        lse = jnp.where(cols == h, tops[h] + jnp.log(totals[h]), lse)
    lse_ref[...] = lse


def attend_backward_kernel(
    place_ref, low_ref, q_ref, go_ref, o_ref, lse_ref, k_ref, v_ref, first_ref, even_ref, odd_ref, kt_scr, vt_scr, k_scr,
    *, heads, length, blocks
):
    i = pl.program_id(0)
    place = place_ref[0]
    low = low_ref[i]
    width = heads * HD
    lanes = lax.broadcasted_iota(jnp.int32, (length, width), 1) // HD
    first = first_ref[...]
    q_place = i * length + lax.broadcasted_iota(jnp.int32, (length, 1), 0)
    q_all, go_all = q_ref[...], go_ref[...]
    inner_all = go_all.astype(F32) * o_ref[...].astype(F32)
    q_turned, go_turned = q_all.astype(F32).T.astype(BF), go_all.astype(F32).T.astype(BF)
    lse_all = lse_ref[...]
    q_heads, go_heads, inner, lse = [], [], [], []
    for h in range(heads):
        mine = lanes == h
        q_heads.append(jnp.where(mine, q_all, jnp.zeros_like(q_all)))
        go_heads.append(jnp.where(mine, go_all, jnp.zeros_like(go_all)))
        inner.append(jnp.sum(jnp.where(mine, inner_all, 0.0), axis=-1, keepdims=True))
        lse.append(lse_all[:, h : h + 1])

    @pl.when(i == 0)
    def _():
        kt_scr[...] = jnp.zeros_like(kt_scr)
        vt_scr[...] = jnp.zeros_like(vt_scr)
        spread_heads(k_ref, k_scr, lanes, heads, length, blocks)

    def step(j, acc):
        start = storage_row(j, place, blocks, length)
        rows = pl.ds(start, length)
        k_block, v_block = k_ref[rows, :], v_ref[rows, :]
        k_place = j * length + lax.broadcasted_iota(jnp.int32, (1, length), 1)
        allowed = (k_place >= first) & (k_place <= q_place)
        every = range(heads)
        scores = [dot_nt(q_heads[h], k_block) for h in every]
        grad_probs = [dot_nt(go_heads[h], v_block) for h in every]
        probs = [jnp.exp(jnp.where(allowed, scores[h] - lse[h], NEG_FILL)) for h in every]
        grad_scores = [(probs[h] * (grad_probs[h] - inner[h])).astype(BF) for h in every]
        for h in every:
            part = slice(h * HD, (h + 1) * HD)
            vt_scr[part, rows] = vt_scr[part, rows] + dot(go_turned[part, :], probs[h].astype(BF))
            kt_scr[part, rows] = kt_scr[part, rows] + dot(q_turned[part, :], grad_scores[h])
        spread = pl.ds(pl.multiple_of(start * heads, heads * length), heads * length)
        return acc + dot(jnp.concatenate(grad_scores, axis=1), k_scr[spread, :])

    grad_q = lax.fori_loop(low, i + 1, step, jnp.zeros((length, width), F32))
    grad_q = (grad_q.astype(BF).astype(F32) * (HD**-0.5)).astype(BF)
    k = i ^ place
    own_rows = pl.ds(pl.multiple_of((k >> 1) * length, length), length)

    @pl.when((k & 1) == 0)
    def _():
        even_ref[own_rows, 0:width] = grad_q

    @pl.when((k & 1) == 1)
    def _():
        odd_ref[own_rows, 0:width] = grad_q

    @pl.when(i == blocks - 1)
    def _():
        for j in range(blocks):
            target, m = (even_ref, j) if j < blocks // 2 else (odd_ref, j - blocks // 2)
            source, rows = slice(j * length, (j + 1) * length), slice(m * length, (m + 1) * length)
            target[rows, width : 2 * width] = kt_scr[:, source].T.astype(BF)
            target[rows, 2 * width : 3 * width] = vt_scr[:, source].T.astype(BF)


def storage_map(length, blocks, column):
    def index(i, place_ref, low_ref):
        k = i ^ place_ref[0]
        return ((k >> 1) + (k & 1) * (blocks // 2), column)

    return index


def attend_forward(place, low, qkv, first, length):
    rows, triple = qkv.shape
    width, blocks = triple // 3, rows // length
    heads = width // HD
    return pl.pallas_call(
        functools.partial(attend_forward_kernel, heads=heads, length=length, blocks=blocks),
        grid_spec=pltpu.PrefetchScalarGridSpec(
            num_scalar_prefetch=2,
            grid=(blocks,),
            in_specs=[
                pl.BlockSpec((length, width), storage_map(length, blocks, 0)),
                pl.BlockSpec((rows, width), lambda i, p, w: (0, 1)),
                pl.BlockSpec((rows, width), lambda i, p, w: (0, 2)),
                pl.BlockSpec((length, 1), lambda i, p, w: (i, 0)),
            ],
            out_specs=[
                pl.BlockSpec((length, width), lambda i, p, w: (i, 0)),
                pl.BlockSpec((length, 128), lambda i, p, w: (i, 0)),
            ],
            scratch_shapes=[
                pltpu.VMEM((heads, length, rows), F32),
                pltpu.VMEM((heads, length, 128), F32),
                pltpu.VMEM((heads, length, 128), F32),
                pltpu.VMEM((heads * rows, width), BF),
            ],
        ),
        out_shape=[jax.ShapeDtypeStruct((rows, width), BF), jax.ShapeDtypeStruct((rows, 128), F32)],
        compiler_params=pltpu.CompilerParams(dimension_semantics=("arbitrary",), vmem_limit_bytes=LARGE_GRANT),
        cost_estimate=light_cost(24 * rows * rows * width),
        name="attend_forward",
    )(place, low, qkv, qkv, qkv, first)


def attend_backward(place, low, qkv, grad_out, mixed, lse, first, length):
    rows, triple = qkv.shape
    width, blocks = triple // 3, rows // length
    heads = width // HD
    return pl.pallas_call(
        functools.partial(attend_backward_kernel, heads=heads, length=length, blocks=blocks),
        grid_spec=pltpu.PrefetchScalarGridSpec(
            num_scalar_prefetch=2,
            grid=(blocks,),
            in_specs=[
                pl.BlockSpec((length, width), storage_map(length, blocks, 0)),
                pl.BlockSpec((length, width), lambda i, p, w: (i, 0)),
                pl.BlockSpec((length, width), lambda i, p, w: (i, 0)),
                pl.BlockSpec((length, 128), lambda i, p, w: (i, 0)),
                pl.BlockSpec((rows, width), lambda i, p, w: (0, 1)),
                pl.BlockSpec((rows, width), lambda i, p, w: (0, 2)),
                pl.BlockSpec((length, 1), lambda i, p, w: (i, 0)),
            ],
            out_specs=[pl.BlockSpec((rows // 2, triple), lambda i, p, w: (0, 0))] * 2,
            scratch_shapes=[
                pltpu.VMEM((width, rows), F32),
                pltpu.VMEM((width, rows), F32),
                pltpu.VMEM((heads * rows, width), BF),
            ],
        ),
        out_shape=[jax.ShapeDtypeStruct((rows // 2, triple), BF)] * 2,
        compiler_params=pltpu.CompilerParams(dimension_semantics=("arbitrary",), vmem_limit_bytes=LARGE_GRANT),
        cost_estimate=light_cost(36 * rows * rows * width),
        name="attend_backward",
    )(place, low, qkv, grad_out, mixed, lse, qkv, qkv, first)


def local(
    inputs,
    teacher,
    segment_ids,
    summary_start,
    valid_mask,
    attn_norm_gain,
    attn_norm_bias,
    query_weight,
    query_bias,
    key_weight,
    value_weight,
    value_bias,
    out_weight,
    out_bias,
    mlp_norm_gain,
    mlp_norm_bias,
    up_weight,
    up_bias,
    down_weight,
    down_bias,
):
    seqs, length = segment_ids.shape
    width = inputs.shape[-1]
    hidden_units = up_weight.shape[1]
    n, groups = lax.axis_size("seq"), lax.axis_size("dp")
    place, group = lax.axis_index("seq"), lax.axis_index("dp")
    both = ("dp", "seq")
    seq_len = length * n
    tokens_all = seqs * seq_len * groups
    scale = HD**-0.5
    own_rows = query_weight.shape[0]
    own_hidden = up_bias.shape[0]
    head_cols = width // n

    def out_of(value):
        return lax.all_to_all(value, "seq", split_axis=0, concat_axis=0, tiled=True)

    valid = valid_mask.astype(F32)
    order = Order()
    near = n == 8 and groups == 4
    out_steps = Steps(order, line_gather(out_weight)) if near else None
    cut = jnp.concatenate(
        [w.reshape(own_rows, n, head_cols).transpose(1, 0, 2) for w in (query_weight, key_weight, value_weight)], axis=2
    )
    qkv_cut = out_of(cut)
    small = [attn_norm_gain, attn_norm_bias, out_bias, mlp_norm_gain, mlp_norm_bias, down_bias, query_bias, value_bias, up_bias]
    pieces = [v.astype(F32) for v in small] + [segment_ids.astype(F32).reshape(-1), jnp.sum(valid).reshape(1)]
    starts, lines = [], []
    for piece in pieces:
        starts.append(sum(line.shape[0] for line in lines))
        short = -piece.shape[0] % 128
        lines.append(jnp.pad(piece, (0, short)).reshape(-1, 128))
    used = sum(line.shape[0] for line in lines)
    packed = jnp.pad(jnp.concatenate(lines, axis=0), ((0, -used % 8), (0, 0)))[None]
    small_steps = Steps(order, doubling(after(packed, cut), ("dp", "seq")))
    small_steps.step(1)
    qkv_cut = order.pause(qkv_cut).reshape(n * own_rows, 3 * head_cols)
    w_qkv = lax.all_gather(qkv_cut, "dp", axis=0, tiled=True)
    if near:
        out_steps.step()
    small_steps.step(1)
    if near:
        out_steps.step()
    small_steps.step(1)
    if near:
        own_out = out_steps.finish()
    packed = small_steps.finish().reshape(n, groups, -1, 128).transpose(1, 0, 2, 3).reshape(groups * n, -1, 128)

    def zero_after(value):
        return jnp.minimum(jnp.abs(value.reshape(-1)[0].astype(F32)), 0.0).astype(jnp.int32)

    def rows_after(b, value):
        return lax.dynamic_index_in_dim(inputs, b + zero_after(value), 0, keepdims=False)

    state = [types.SimpleNamespace() for _ in range(seqs)]
    state[0].own = rows_after(0, packed)
    state[0].came = gather_start(state[0].own)
    parts = []
    for piece, at in zip(pieces, starts):
        count = -(-piece.shape[0] // 128)
        parts.append(packed[:, at : at + count].reshape(groups * n, -1)[:, : piece.shape[0]])
    gain_one, shift_one, b_out, gain_two, shift_two, b_down = [part.reshape(-1) for part in parts[:6]]
    b_query, b_value = [lax.dynamic_slice_in_dim(part.reshape(-1), place * head_cols, head_cols) for part in parts[6:8]]
    b_up = lax.dynamic_index_in_dim(parts[8].reshape(groups, n, -1), place, 1, keepdims=False).reshape(-1)
    ids = lax.dynamic_index_in_dim(parts[9].reshape(groups, n, seqs, length), group, 0, keepdims=False)
    ids = ids.transpose(1, 0, 2).reshape(seqs, seq_len)
    total_count = jnp.sum(parts[10])

    up_cut = up_weight.reshape(own_rows, groups, n, own_hidden).transpose(2, 0, 1, 3).reshape(n, own_rows, groups * own_hidden)
    b_qkv = jnp.concatenate([b_query, jnp.zeros_like(b_query), b_value])
    s_qkv = jnp.concatenate([jnp.full((head_cols,), scale, F32), jnp.ones((2 * head_cols,), F32)])

    place_arr = place.reshape(1).astype(jnp.int32)
    positions = jnp.arange(seq_len, dtype=jnp.int32)

    def add_all(terms):
        out = terms[0]
        for term in terms[1:]:
            out = out + term
        return out


    def spans(b):
        st = state[b]
        first = jnp.sum((ids[b][None, :] < ids[b][:, None]).astype(jnp.int32), axis=1)
        in_summary = (positions >= summary_start[b]) & (positions < summary_start[b] + NSUM)
        first = jnp.where(in_summary, 0, first)
        st.low = jnp.min(first.reshape(n, length), axis=1) // length
        st.first = first.reshape(seq_len, 1)

    def project(b):
        st = state[b]
        even, odd = order.tie((st.even, st.odd))
        parts = [project_product(part, w_qkv, b_qkv, s_qkv) for part in (even, odd)]
        st.qkv = order.mark(jnp.concatenate(parts, axis=0))

    def attend(b):
        st = state[b]
        qkv = order.tie(st.qkv)
        st.mixed, st.lse = attend_forward(place_arr, st.low, qkv, st.first, length)
        order.mark(st.mixed)

    def send_mixed(b):
        st = state[b]
        st.moved = out_of(st.mixed.reshape(n, length, head_cols))

    def middle(b):
        st = state[b]
        attended = order.tie(st.moved)
        st.attended = attended.transpose(1, 0, 2).reshape(length, width)
        rows = inputs[b].astype(F32)
        st.hidden = rows + (dot(st.attended, w_out) + b_out)
        st.normed_two, st.inverse_two = norm_core(st.hidden)
        st.own_two = order.mark((st.normed_two * gain_two + shift_two).astype(BF))
        st.came_two = gather_start(st.own_two)

    def up_even(b):
        st = state[b]
        st.act_even = order.mark(up_product(order.tie(st.even_two), w_up, b_up))

    def up_odd(b):
        st = state[b]
        st.act_odd = order.mark(up_product(order.tie(st.odd_two), w_up, b_up))

    def relay(b, own, came):
        st = state[b]
        came = order.pause(getattr(st, came))
        return came, gather_relay(getattr(st, own), came)

    def join(b, own, came_relayed):
        same = order.mark(gather_join(getattr(state[b], own), *order.tie(came_relayed)))
        return same, swap(same, 1)

    def down_odd(b):
        st = state[b]
        st.down_got = swap(order.mark(plain_product(order.tie(st.act_odd), w_down)), 1)

    def down_even(b):
        st = state[b]
        st.down_sums = order.mark(block_products(st.act_even, w_down, order.tie(st.down_got), n // 2))
        st.down_came = scatter_start(st.down_sums)

    def pass_on(b, sums, came):
        st = state[b]
        came = order.pause(getattr(st, came))
        return scatter_relay(order.mark(scatter_halves(getattr(st, sums), came)))

    def misfit(b):
        st = state[b]
        summed = scatter_join(st.down_sums, order.tie(st.down_sent))
        st.result = st.hidden + (summed + b_down)
        error = st.result - teacher[b].astype(F32)
        st.local_sq = jnp.sum(jnp.sum(error * error, axis=-1) * valid[b])
        st.grad_result = error * (valid[b] * (tokens_all / total_count))[:, None]
        st.own_grad = order.mark(st.grad_result.astype(BF))
        st.g_b_down = jnp.sum(st.own_grad.astype(F32), axis=0)
        st.came_grad = gather_start(st.own_grad)

    def act_back_even(b):
        st = state[b]
        st.pre_even, st.sums_even = masked_product(order.tie(st.gm_even), w_down, st.act_even)
        order.mark(st.pre_even)

    def act_back_odd(b):
        st = state[b]
        st.pre_odd, st.sums_odd = masked_product(order.tie(st.gm_odd), w_down, st.act_odd)
        order.mark(st.pre_odd)

    def up_back_odd(b):
        st = state[b]
        st.up_got = swap(order.mark(plain_product(order.tie(st.pre_odd), w_up, turned=True)), 1)

    def up_back_even(b):
        st = state[b]
        st.up_sums = order.mark(block_products(st.pre_even, w_up, order.tie(st.up_got), n // 2, turned=True))
        st.up_came = scatter_start(st.up_sums)

    def branch_back(b):
        st = state[b]
        grad_ready = scatter_join(st.up_sums, order.tie(st.up_sent))
        grad_norm, st.g_gain_two, st.g_shift_two = norm_back(grad_ready, st.normed_two, st.inverse_two, gain_two)
        st.grad_hidden = st.grad_result + grad_norm
        st.branch = st.grad_hidden.astype(BF)
        st.g_b_out = jnp.sum(st.branch.astype(F32), axis=0)
        grad_att = dot_nt(st.branch, w_out).astype(BF).reshape(length, n, head_cols).transpose(1, 0, 2)
        st.grad_mixed = out_of(order.mark(grad_att)).reshape(seq_len, head_cols)

    def attend_back(b):
        st = state[b]
        st.grad_qkv = attend_backward(
            place_arr, st.low, st.qkv, order.tie(st.grad_mixed), st.mixed, st.lse, st.first, length
        )
        order.mark(st.grad_qkv)
        st.g_b_qkv = sum(jnp.sum(part.astype(F32), axis=0) for part in st.grad_qkv)

    def project_back_odd(b):
        st = state[b]
        odd = order.tie(st.grad_qkv[1])
        st.one_got = swap(order.mark(plain_product(odd, w_qkv, turned=True)), 1)

    def project_back_even(b):
        st = state[b]
        st.one_sums = block_products(st.grad_qkv[0], w_qkv, order.tie(st.one_got), n // 2, turned=True)
        order.mark(st.one_sums)
        st.one_came = scatter_start(st.one_sums)

    def finish(b):
        st = state[b]
        grad_ready = scatter_join(st.one_sums, order.tie(st.one_sent))
        normed, inverse = norm_core(inputs[b].astype(F32))
        grad_norm, st.g_gain_one, st.g_shift_one = norm_back(grad_ready, normed, inverse, gain_one)
        st.grad_inputs = order.mark(st.grad_hidden + grad_norm)

    every, later = range(seqs), range(1, seqs)

    def whole_out_weight(own, came, relayed):
        whole = jnp.zeros((groups, n, own_rows, width), BF)
        half = groups // 2
        same = [(0, own, 0), (2, came[0], 0), (4, came[1], 0), (6, relayed[0], 0), (6, relayed[1], half)]
        other = [(k + 1, swap(piece, 1), first) for k, piece, first in same]
        for k, piece, first in same + other:
            whole = lax.dynamic_update_slice(whole, piece.reshape(-1, 1, own_rows, width), (first, place ^ k, 0, 0))
        return whole.reshape(width, width)

    def make_ready(b, came_relayed):
        st = state[b]
        st.even = order.mark(norm_rows(gather_pieces(st.own, *order.tie(came_relayed)), gain_one, shift_one))
        st.odd = swap(st.even, 1)

    for b in every:
        spans(b)
    came_relayed = relay(0, "own", "came")
    for b in later:
        state[b].own = rows_after(b, came_relayed[0][0] if near else packed)
        state[b].came = gather_start(state[b].own)
    make_ready(0, came_relayed)
    up_cut = out_of(after(up_cut, qkv_cut))
    if near:
        own_out = order.tie(own_out)
        out_came = order.pause(gather_start(own_out))
        out_relayed = gather_relay(own_out, out_came)
    else:
        w_out = lax.all_gather(after(out_weight, qkv_cut), both, axis=0, tiled=True)
    up_cut = order.pause(up_cut)
    w_up = lax.all_gather(up_cut.reshape(n * own_rows, groups * own_hidden), "dp", axis=0, tiled=True)
    w_down = lax.all_gather(after(down_weight, up_cut), "dp", axis=0, tiled=True)
    w_qkv = order.pause(w_qkv)
    project(0)
    attend(0)
    send_mixed(0)
    came_relayed = [relay(b, "own", "came") for b in later]
    raw = came_relayed
    if near:
        w_out = whole_out_weight(own_out, out_came, order.pause(out_relayed))
    w_up = order.pause(w_up)
    middle(0)
    for b in later:
        last, st = state[b - 1], state[b]
        make_ready(b, raw[b - 1])
        project(b)
        came_relayed = relay(b - 1, "own_two", "came_two")
        attend(b)
        send_mixed(b)
        last.even_two, last.odd_two = join(b - 1, "own_two", came_relayed)
        up_even(b - 1)
        middle(b)
        up_odd(b - 1)
        came_relayed = relay(b, "own_two", "came_two")
        down_odd(b - 1)
        st.even_two, st.odd_two = join(b, "own_two", came_relayed)
        up_even(b)
        down_even(b - 1)
        up_odd(b)
        last.down_sent = pass_on(b - 1, "down_sums", "down_came")
        down_odd(b)
        down_even(b)
        misfit(b - 1)
        st.down_sent = pass_on(b, "down_sums", "down_came")
        came_relayed = relay(b - 1, "own_grad", "came_grad")
        misfit(b)
        last.gm_even, last.gm_odd = join(b - 1, "own_grad", came_relayed)
        act_back_even(b - 1)
        act_back_odd(b - 1)
        came_relayed = relay(b, "own_grad", "came_grad")
        up_back_odd(b - 1)
        up_back_even(b - 1)
        st.gm_even, st.gm_odd = join(b, "own_grad", came_relayed)
        act_back_even(b)
        last.up_sent = pass_on(b - 1, "up_sums", "up_came")
        act_back_odd(b)
        up_back_odd(b)
        up_back_even(b)
    lefts = [part for st in state for part in (st.even_two, st.odd_two)]
    rights = [part for st in state for part in (st.pre_even, st.pre_odd)]
    g_w_up = order.mark(weight_grad(order.tie(lefts), rights, 512, 1024))
    g_up = lax.psum_scatter(g_w_up, "dp", scatter_dimension=0, tiled=True)
    for b in later:
        state[b].up_sent = pass_on(b, "up_sums", "up_came")
    branch_back(0)
    lefts = [part for st in state for part in (st.act_even, st.act_odd)]
    rights = [part for st in state for part in (st.gm_even, st.gm_odd)]
    g_w_down = order.mark(weight_grad(order.tie(lefts), rights, 256, 1024))
    g_down = lax.psum_scatter(g_w_down, "dp", scatter_dimension=0, tiled=True)
    state[0].grad_mixed = order.pause(state[0].grad_mixed)
    for b in later:
        branch_back(b)
    turned = [
        st.attended.reshape(length, groups, n, own_rows).transpose(2, 0, 1, 3).reshape(n, length, groups * own_rows)
        for st in state
    ]

    def out_block(k):
        return add_all(
            [dot_tn(lax.dynamic_index_in_dim(t, place ^ k, 0, keepdims=False), st.branch) for t, st in zip(turned, state)]
        )

    out_rows = groups * own_rows
    turned = order.tie(turned)
    out_odd = order.mark(jnp.concatenate([out_block(k).astype(BF) for k in range(1, n, 2)], axis=0))
    out_got = swap(out_odd, 1)
    attend_back(0)
    out_got = order.tie(out_got)
    out_sums = [out_block(2 * m) + out_got[m * out_rows : (m + 1) * out_rows].astype(F32) for m in range(n // 2)]
    order.mark(out_sums)
    out_came = scatter_start(out_sums)
    project_back_odd(0)
    out_sent = scatter_relay(order.mark(scatter_halves(out_sums, order.pause(out_came))))
    project_back_even(0)
    g_up, g_down = order.pause((g_up, g_down))
    g_up = out_of(g_up.reshape(n, own_rows, groups * own_hidden))
    for b in later:
        attend_back(b)
        state[b - 1].one_came, out_sent = order.pause((state[b - 1].one_came, out_sent))
    for b in later:
        state[b - 1].one_sent = pass_on(b - 1, "one_sums", "one_came")
    out_sum = order.mark(scatter_join(out_sums, order.tie(out_sent)).astype(BF))
    out_parts = out_sum.reshape(groups, own_rows, width)
    out_line = Steps(order, line_scatter(out_parts)) if near else None
    for b in later:
        project_back_odd(b)
    lefts = [part for st in state for part in (st.even, st.odd)]
    rights = [part for st in state for part in st.grad_qkv]
    g_w_qkv = order.mark(weight_grad(order.tie(lefts), rights, 1024, 768))
    if near:
        out_line.step()
        qkv_line = Steps(order, line_scatter(g_w_qkv.reshape(groups, n * own_rows, 3 * head_cols)))
    else:
        g_qkv = lax.psum_scatter(g_w_qkv, "dp", scatter_dimension=0, tiled=True)
        g_out = lax.psum_scatter(out_sum, "dp", scatter_dimension=0, tiled=True)
    g_up = order.pause(g_up)
    for b in later:
        state[b - 1].one_sent = order.pause(state[b - 1].one_sent)
        project_back_even(b)
    if near:
        out_line.step()
        qkv_line.step()
    for b in later:
        state[b].one_sent = pass_on(b, "one_sums", "one_came")
        finish(b - 1)
    if near:
        g_out = out_line.finish()
        qkv_line.step()
    for b in later:
        state[b].one_sent = order.pause(state[b].one_sent)
    if near:
        g_qkv = order.mark(qkv_line.finish().astype(BF))
    g_qkv = out_of(g_qkv.reshape(n, own_rows, 3 * head_cols))
    for b in later:
        finish(b)
    g_out = g_out.astype(F32)

    def summed(name):
        return add_all([after(getattr(st, name), *state[-1].one_sums) for st in state])

    g_down = order.tie(g_down).astype(F32)
    g_up = g_up.reshape(n, own_rows, groups, own_hidden).transpose(1, 2, 0, 3).reshape(own_rows, hidden_units).astype(F32)
    g_qkv_came = g_qkv
    g_qkv = g_qkv.reshape(n, own_rows, 3, head_cols).transpose(2, 1, 0, 3).reshape(3, own_rows, width).astype(F32)

    g_b_qkv = summed("g_b_qkv").reshape(3, head_cols)
    own_bias = jnp.zeros((2, width), F32)
    own_bias = lax.dynamic_update_slice(own_bias, jnp.stack([g_b_qkv[0], g_b_qkv[2]]), (0, place * head_cols))
    g_b_up = jnp.sum(summed("sums_even") + summed("sums_odd"), axis=0).reshape(groups, 1, own_hidden)
    spread_up = lax.dynamic_update_slice_in_dim(jnp.zeros((groups, n, own_hidden), F32), g_b_up, place, 1)
    names = ("g_gain_one", "g_shift_one", "g_b_out", "g_gain_two", "g_shift_two", "g_b_down")
    vectors = jnp.concatenate([jnp.stack([summed(name) for name in names]), own_bias], axis=0)
    count = vectors.shape[0]
    vectors = vectors.reshape(count, groups * n, own_rows).transpose(1, 0, 2).reshape(groups * n, count * own_rows)
    sq = jnp.broadcast_to(summed("local_sq"), (groups * n, 1))
    tail = jnp.concatenate([vectors, spread_up.reshape(groups * n, own_hidden), sq], axis=1)
    tail = scatter_small(tail, g_qkv_came)
    vectors = tail[: count * own_rows].reshape(count, own_rows)
    g_b_query, g_b_value, g_b_up = vectors[6], vectors[7], tail[count * own_rows : -1]
    mean_loss = tail[-1] / (total_count * width)
    return (
        jnp.stack([st.result.astype(BF) for st in state]),
        mean_loss,
        jnp.stack([st.grad_inputs for st in state]),
        vectors[0],
        vectors[1],
        g_qkv[0],
        g_b_query,
        g_qkv[1],
        g_qkv[2],
        g_b_value,
        g_out,
        vectors[2],
        vectors[3],
        vectors[4],
        g_up,
        g_b_up,
        g_down,
        vectors[5],
    )


def solution(mesh):
    rows3, rows2, flat, mat = P("dp", "seq", None), P("dp", "seq"), P(("dp", "seq")), P(("dp", "seq"), None)
    placed = (
        rows3, rows3, rows2, P("dp"), rows2, flat, flat, mat, flat, mat, mat, flat, mat, flat, flat, flat, mat, flat, mat, flat,
    )
    out = (rows3, P(), rows3, flat, flat, mat, flat, mat, mat, flat, mat, flat, flat, flat, mat, flat, mat, flat)
    return jax.shard_map(local, mesh=mesh, in_specs=placed, out_specs=out, check_vma=False)
```

```python
import functools
import types

import jax
import jax.numpy as jnp
from jax import lax
from jax.experimental import pallas as pl
from jax.experimental.pallas import tpu as pltpu
from jax.sharding import PartitionSpec as P

HD = 64
NSUM = 50
NORM_EPS = 1e-05
NEG_FILL = -1e30
PRODUCT_GRANT, LARGE_GRANT = 30 << 20, 56 << 20
BF = jnp.bfloat16
F32 = jnp.float32


def dot(left_in, right_in):
    return jnp.dot(left_in, right_in, preferred_element_type=F32)


def dot_tn(left_in, right_in):
    return lax.dot_general(left_in, right_in, (((0,), (0,)), ((), ())), preferred_element_type=F32)


def dot_nt(left_in, right_in):
    return lax.dot_general(left_in, right_in, (((1,), (1,)), ((), ())), preferred_element_type=F32)


def norm_core(values):
    center = values - jnp.mean(values, axis=-1, keepdims=True)
    inverse = lax.rsqrt(jnp.mean(center * center, axis=-1, keepdims=True) + NORM_EPS)
    return center * inverse, inverse


def norm_back(grad_out, normed, inverse, gain_in):
    grad_normed = grad_out * gain_in
    inner_one = jnp.mean(grad_normed, axis=-1, keepdims=True)
    inner_two = jnp.mean(grad_normed * normed, axis=-1, keepdims=True)
    grad_in = inverse * (grad_normed - inner_one - normed * inner_two)
    return grad_in, jnp.sum(grad_out * normed, axis=0), jnp.sum(grad_out, axis=0)


def swap(values, mask):
    n = lax.axis_size("seq")
    return lax.ppermute(values, "seq", [(i, i ^ mask) for i in range(n)])


def gather_start(own):
    return (swap(own, 2), swap(own, 4)) if lax.axis_size("seq") == 8 else ()


def gather_relay(own, came):
    if lax.axis_size("seq") != 8:
        return ()
    half = own.shape[0] // 2
    return swap(came[1][:half], 2), swap(came[0][half:], 4)


def gather_pieces(own, came, relayed):
    if lax.axis_size("seq") == 8:
        return [own, *came, *relayed]
    return [gather_join(own, came, relayed)]


def gather_join(own, came, relayed):
    if lax.axis_size("seq") == 8:
        return jnp.concatenate([own, *came, *relayed], axis=0)
    same, step = own, 2
    while step < lax.axis_size("seq"):
        same = jnp.concatenate([same, swap(same, step)], axis=0)
        step *= 2
    return same


def gather_rows(own):
    came = gather_start(own)
    same = gather_join(own, came, gather_relay(own, came))
    return same, swap(same, 1)


def scatter_start(blocks):
    if lax.axis_size("seq") != 8:
        return ()
    six = blocks[3].astype(BF)
    half = six.shape[0] // 2
    return swap(six[:half], 2), swap(six[half:], 4)


def scatter_halves(blocks, came):
    if lax.axis_size("seq") != 8:
        return ()
    _, two, four, _ = blocks
    half, width = two.shape[0] // 2, two.shape[1]
    which = lax.broadcasted_iota(jnp.int32, (2, half, width), 0)

    def with_half(block, part, side):
        part = jnp.where(which == side, part.astype(F32)[None], 0.0)
        return (block.reshape(2, half, width) + part).astype(BF).reshape(2 * half, width)

    return with_half(two, came[1], 1), with_half(four, came[0], 0)


def scatter_relay(halves):
    return (swap(halves[0], 2), swap(halves[1], 4)) if halves else ()


def scatter_join(blocks, relayed):
    n = lax.axis_size("seq")
    if n == 8:
        return blocks[0] + relayed[0].astype(F32) + relayed[1].astype(F32)
    step = n // 2
    while step > 1:
        keep = len(blocks) // 2
        sent = [swap(block.astype(BF), step).astype(F32) for block in blocks[keep:]]
        blocks = [block.astype(F32) + got for block, got in zip(blocks[:keep], sent)]
        step //= 2
    return blocks[0]


def exchange(values, axis, bit):
    size = lax.axis_size(axis)
    return lax.ppermute(values, axis, [(i, i ^ bit) for i in range(size)])


class Order:
    def __init__(self):
        self.last = ()

    def tie(self, value):
        if not jax.tree.leaves(value) or not jax.tree.leaves(self.last):
            return value
        return lax.optimization_barrier((value, self.last))[0]

    def mark(self, value):
        if jax.tree.leaves(value):
            self.last = value
        return value

    def pause(self, value):
        return self.mark(self.tie(value))


def doubling(held, axes):
    for axis in axes:
        bit, index = 1, lax.axis_index(axis)
        while bit < lax.axis_size(axis):
            other = yield exchange(held, axis, bit)
            upper = (index & bit) != 0
            held = jnp.concatenate([jnp.where(upper, other, held), jnp.where(upper, held, other)], axis=0)
            bit *= 2
    return held


def line_gather(own):
    size, index = lax.axis_size("dp"), lax.axis_index("dp")
    below, above = [], []
    to_right, to_left = own, own
    for _ in range(size - 1):
        flight = (
            lax.ppermute(to_right, "dp", [(i, i + 1) for i in range(size - 1)]),
            lax.ppermute(to_left, "dp", [(i + 1, i) for i in range(size - 1)]),
        )
        to_right, to_left = yield flight
        below.insert(0, to_right)
        above.append(to_left)
    rows = jnp.concatenate(below + [own] + above, axis=0)
    return lax.dynamic_slice_in_dim(rows, (size - 1 - index) * own.shape[0], size * own.shape[0], axis=0)


def line_scatter(parts):
    size, index = lax.axis_size("dp"), lax.axis_index("dp")

    def part(which):
        return lax.dynamic_index_in_dim(parts, jnp.clip(which, 0, size - 1), 0, keepdims=False)

    right = left = None
    for step in range(size - 1):
        far = size - 1 - step
        up, down = part(index + far), part(index - far)
        if step:
            up, down = (up.astype(F32) + right.astype(F32)).astype(BF), (down.astype(F32) + left.astype(F32)).astype(BF)
        flight = (
            lax.ppermute(up, "dp", [(i, i + 1) for i in range(size - far)]),
            lax.ppermute(down, "dp", [(i, i - 1) for i in range(far, size)]),
        )
        right, left = yield flight
    return part(index).astype(F32) + right.astype(F32) + left.astype(F32)


class Steps:
    def __init__(self, order, generator):
        self.order, self.generator, self.flight, self.result = order, generator, next(generator), None

    def step(self, count=1):
        for _ in range(count):
            if self.flight is None:
                return
            try:
                self.flight = self.generator.send(self.order.pause(self.flight))
            except StopIteration as stop:
                self.flight, self.result = None, stop.value

    def finish(self):
        while self.flight is not None:
            self.step()
        return self.result


def scatter_small(table, awaited):
    count, width = table.shape
    length = -(-width // 1024) * 1024
    held = jnp.pad(table, ((0, 0), (0, length - width))).reshape(count, 8, length // 8)
    for axis in ("dp", "seq"):
        bit, index = lax.axis_size(axis) // 2, lax.axis_index(axis)
        while bit > 0:
            half = held.shape[0] // 2
            upper = (index & bit) != 0
            sent = jnp.where(upper, held[:half], held[half:])
            held = jnp.where(upper, held[half:], held[:half]) + exchange(sent, axis, bit)
            bit //= 2
        if axis == "dp":
            held = after(held, awaited)
    return held.reshape(length)[:width]


def after(value, *earlier):
    return lax.optimization_barrier((value, *earlier))[0]


def weight_grad_kernel(*refs):
    count = (len(refs) - 1) // 2
    total = dot_tn(refs[0][...], refs[count][...])
    for part in range(1, count):
        total = total + dot_tn(refs[part][...], refs[count + part][...])
    refs[-1][...] = total.astype(BF)


def weight_grad(lefts, rights, left_tile, right_tile):
    rows, left_width = lefts[0].shape
    right_width = rights[0].shape[1]
    left_tile, right_tile = min(left_tile, left_width), min(right_tile, right_width)
    count = len(lefts)
    return pl.pallas_call(
        weight_grad_kernel,
        grid=(right_width // right_tile, left_width // left_tile),
        in_specs=[pl.BlockSpec((rows, left_tile), lambda j, i: (0, i))] * count
        + [pl.BlockSpec((rows, right_tile), lambda j, i: (0, j))] * count,
        out_specs=pl.BlockSpec((left_tile, right_tile), lambda j, i: (i, j)),
        out_shape=jax.ShapeDtypeStruct((left_width, right_width), BF),
        compiler_params=pltpu.CompilerParams(dimension_semantics=("arbitrary", "arbitrary"), vmem_limit_bytes=LARGE_GRANT),
        cost_estimate=light_cost(2 * count * rows * left_width * right_width),
        name="weight_grad",
    )(*lefts, *rights)


def tile_dot(left, right, turned):
    return dot_nt(left, right) if turned else dot(left, right)


def plain_kernel(left_ref, right_ref, out_ref, *, turned):
    out_ref[...] = tile_dot(left_ref[...], right_ref[...], turned).astype(out_ref.dtype)


def project_kernel(left_ref, right_ref, bias_ref, scale_ref, out_ref):
    out_ref[...] = ((dot(left_ref[...], right_ref[...]) + bias_ref[...]) * scale_ref[...]).astype(BF)


def up_kernel(left_ref, right_ref, bias_ref, out_ref):
    out_ref[...] = jnp.maximum(dot(left_ref[...], right_ref[...]) + bias_ref[...], 0.0).astype(BF)


def masked_kernel(left_ref, right_ref, act_ref, out_ref, sums_ref):
    grad = jnp.where(act_ref[...] > 0, dot_nt(left_ref[...], right_ref[...]), 0.0).astype(BF)
    out_ref[...] = grad
    part = jnp.sum(grad.astype(F32).reshape(-1, 8, grad.shape[1]), axis=0)

    @pl.when(pl.program_id(1) == 0)
    def _():
        sums_ref[...] = part

    @pl.when(pl.program_id(1) > 0)
    def _():
        sums_ref[...] = sums_ref[...] + part


def blocks_kernel(left_ref, right_ref, got_ref, *out_refs, turned):
    rows = out_refs[0].shape[0]
    for m in range(len(out_refs) - 1, -1, -1):
        cut = slice(m * rows, (m + 1) * rows)
        total = tile_dot(left_ref[cut, :], right_ref[...], turned) + got_ref[cut, :].astype(F32)
        out_refs[m][...] = total.astype(out_refs[m].dtype)


def light_cost(flops):
    return pl.CostEstimate(flops=int(flops) // 8, bytes_accessed=1, transcendentals=0)


def tiled(kernel, name, left, right, turned, extras, outs, row_tile, col_tile, parts=1):
    rows, depth = left.shape
    cols = right.shape[0] if turned else right.shape[1]
    row_tile, col_tile = min(row_tile, rows), min(col_tile, cols)
    kinds = {
        "both": pl.BlockSpec((row_tile, col_tile), lambda j, m: (m, j)),
        "vector": pl.BlockSpec((1, col_tile), lambda j, m: (0, j)),
        "sums": pl.BlockSpec((8, col_tile), lambda j, m: (0, j)),
        "block": pl.BlockSpec((rows // parts, col_tile), lambda j, m: (0, j)),
    }
    shapes = {"both": (rows, cols), "sums": (8, cols), "block": (rows // parts, cols)}
    right_spec = (
        pl.BlockSpec((col_tile, depth), lambda j, m: (j, 0)) if turned else pl.BlockSpec((depth, col_tile), lambda j, m: (0, j))
    )
    return pl.pallas_call(
        kernel,
        grid=(cols // col_tile, rows // row_tile),
        in_specs=[pl.BlockSpec((row_tile, depth), lambda j, m: (m, 0)), right_spec] + [kinds[k] for k, _ in extras],
        out_specs=[kinds[k] for k, _ in outs],
        out_shape=[jax.ShapeDtypeStruct(shapes[k], dtype) for k, dtype in outs],
        compiler_params=pltpu.CompilerParams(dimension_semantics=("arbitrary", "arbitrary"), vmem_limit_bytes=PRODUCT_GRANT),
        cost_estimate=light_cost(2 * rows * cols * depth),
        name=name,
    )(left, right, *[value for _, value in extras])


def plain_product(left, right, turned=False):
    kernel = functools.partial(plain_kernel, turned=turned)
    return tiled(kernel, "product", left, right, turned, [], [("both", BF)], 1024, 256)[0]


def project_product(left, right, bias, scale):
    extras = [("vector", bias.reshape(1, -1)), ("vector", scale.reshape(1, -1))]
    return tiled(project_kernel, "project", left, right, False, extras, [("both", BF)], 1024, 256)[0]


def up_product(left, right, bias):
    return tiled(up_kernel, "up", left, right, False, [("vector", bias.reshape(1, -1))], [("both", BF)], 1024, 256)[0]


def masked_product(left, right, act):
    outs = [("both", BF), ("sums", F32)]
    return tiled(masked_kernel, "masked_product", left, right, True, [("both", act)], outs, 1024, 256)


def block_products(left, right, got, count, turned=False):
    kernel = functools.partial(blocks_kernel, turned=turned)
    outs = [("block", F32)] * (count - 1) + [("block", BF)]
    return tiled(
        kernel, "block_products", left, right, turned, [("both", got)], outs, left.shape[0], 256, count
    )


def norm_kernel(*refs, unit):
    *piece_refs, gain_ref, shift_ref, out_ref = refs
    step, at = pl.program_id(0), 0
    for piece_ref in piece_refs:
        for start in range(0, piece_ref.shape[0], unit):

            @pl.when(step == at)
            def _(piece_ref=piece_ref, start=start):
                normed, _ = norm_core(piece_ref[start : start + unit, :].astype(F32))
                out_ref[...] = (normed * gain_ref[...] + shift_ref[...]).astype(BF)

            at += 1


def norm_rows(pieces, gain, shift):
    rows, width = sum(piece.shape[0] for piece in pieces), pieces[0].shape[1]
    unit = min(min(piece.shape[0] for piece in pieces), 128)
    whole = [pl.BlockSpec(piece.shape, lambda i: (0, 0)) for piece in pieces]
    vector = pl.BlockSpec((1, width), lambda i: (0, 0))
    return pl.pallas_call(
        functools.partial(norm_kernel, unit=unit),
        grid=(rows // unit,),
        in_specs=whole + [vector, vector],
        out_specs=pl.BlockSpec((unit, width), lambda i: (i, 0)),
        out_shape=jax.ShapeDtypeStruct((rows, width), BF),
        compiler_params=pltpu.CompilerParams(dimension_semantics=("arbitrary",), vmem_limit_bytes=PRODUCT_GRANT),
        cost_estimate=light_cost(2000 * rows * width),
        name="norm_rows",
    )(*pieces, gain.reshape(1, -1), shift.reshape(1, -1))


def visible_scores(q_head, k_block, first, q_place, key_start, length):
    scores = dot_nt(q_head, k_block)
    k_place = key_start + lax.broadcasted_iota(jnp.int32, (1, length), 1)
    allowed = (k_place >= first) & (k_place <= q_place)
    return jnp.where(allowed, scores, NEG_FILL)


def storage_row(block, place, blocks, length):
    k = block ^ place
    return pl.multiple_of(((k >> 1) + (k & 1) * (blocks // 2)) * length, length)


def spread_heads(source_ref, target_ref, lanes, heads, length, blocks):
    def one(m, carry):
        rows = source_ref[pl.ds(pl.multiple_of(m * length, length), length), :]
        for h in range(heads):
            target = pl.ds(pl.multiple_of((m * heads + h) * length, length), length)
            target_ref[target, :] = jnp.where(lanes == h, rows, jnp.zeros_like(rows))
        return carry

    lax.fori_loop(0, blocks, one, 0)


def fold(values, op):
    out = values[:, :128]
    for start in range(128, values.shape[1], 128):
        out = op(out, values[:, start : start + 128])
    return out


def attend_forward_kernel(
    place_ref, low_ref, q_ref, k_ref, v_ref, first_ref, o_ref, lse_ref, s_scr, m_scr, l_scr, v_scr, *, heads, length, blocks
):
    i = pl.program_id(0)
    place = place_ref[0]
    low = low_ref[i]
    width = heads * HD
    lanes = lax.broadcasted_iota(jnp.int32, (length, width), 1) // HD
    q_all = q_ref[...]
    q_heads = [jnp.where(lanes == h, q_all, jnp.zeros_like(q_all)) for h in range(heads)]
    first = first_ref[...]
    q_place = i * length + lax.broadcasted_iota(jnp.int32, (length, 1), 0)
    m_scr[...] = jnp.full_like(m_scr, NEG_FILL)
    l_scr[...] = jnp.zeros_like(l_scr)

    @pl.when(i == 0)
    def _():
        spread_heads(v_ref, v_scr, lanes, heads, length, blocks)

    def score_step(j, carry):
        k_block = k_ref[pl.ds(storage_row(j, place, blocks, length), length), :]
        cols = pl.ds(pl.multiple_of(j * length, length), length)
        for h in range(heads):
            scores = visible_scores(q_heads[h], k_block, first, q_place, j * length, length)
            s_scr[h, :, cols] = scores
            m_scr[h] = jnp.maximum(m_scr[h], fold(scores, jnp.maximum))
        return carry

    lax.fori_loop(low, i + 1, score_step, 0)
    tops = [jnp.max(m_scr[h], axis=-1, keepdims=True) for h in range(heads)]

    def exp_step(j, carry):
        cols = pl.ds(pl.multiple_of(j * length, length), length)
        for h in range(heads):
            raised = jnp.exp(s_scr[h, :, cols] - tops[h])
            s_scr[h, :, cols] = raised
            l_scr[h] = l_scr[h] + fold(raised, jnp.add)
        return carry

    lax.fori_loop(low, i + 1, exp_step, 0)
    totals = [jnp.sum(l_scr[h], axis=-1, keepdims=True) for h in range(heads)]
    scales = [1.0 / total for total in totals]

    def mix_step(j, acc):
        rows = pl.ds(pl.multiple_of(storage_row(j, place, blocks, length) * heads, heads * length), heads * length)
        cols = pl.ds(pl.multiple_of(j * length, length), length)
        probs = [(s_scr[h, :, cols] * scales[h]).astype(BF) for h in range(heads)]
        return acc + dot(jnp.concatenate(probs, axis=1), v_scr[rows, :])

    mixed = lax.fori_loop(low, i + 1, mix_step, jnp.zeros((length, width), F32))
    o_ref[...] = mixed.astype(BF)
    cols = lax.broadcasted_iota(jnp.int32, (length, 128), 1)
    lse = jnp.zeros((length, 128), F32)
    for h in range(heads):
        lse = jnp.where(cols == h, tops[h] + jnp.log(totals[h]), lse)
    lse_ref[...] = lse


def attend_backward_kernel(
    place_ref, low_ref, q_ref, go_ref, o_ref, lse_ref, k_ref, v_ref, first_ref, even_ref, odd_ref, kt_scr, vt_scr, k_scr,
    *, heads, length, blocks
):
    i = pl.program_id(0)
    place = place_ref[0]
    low = low_ref[i]
    width = heads * HD
    lanes = lax.broadcasted_iota(jnp.int32, (length, width), 1) // HD
    first = first_ref[...]
    q_place = i * length + lax.broadcasted_iota(jnp.int32, (length, 1), 0)
    q_all, go_all = q_ref[...], go_ref[...]
    inner_all = go_all.astype(F32) * o_ref[...].astype(F32)
    q_turned, go_turned = q_all.astype(F32).T.astype(BF), go_all.astype(F32).T.astype(BF)
    lse_all = lse_ref[...]
    q_heads, go_heads, inner, lse = [], [], [], []
    for h in range(heads):
        mine = lanes == h
        q_heads.append(jnp.where(mine, q_all, jnp.zeros_like(q_all)))
        go_heads.append(jnp.where(mine, go_all, jnp.zeros_like(go_all)))
        inner.append(jnp.sum(jnp.where(mine, inner_all, 0.0), axis=-1, keepdims=True))
        lse.append(lse_all[:, h : h + 1])

    @pl.when(i == 0)
    def _():
        kt_scr[...] = jnp.zeros_like(kt_scr)
        vt_scr[...] = jnp.zeros_like(vt_scr)
        spread_heads(k_ref, k_scr, lanes, heads, length, blocks)

    def step(j, acc):
        start = storage_row(j, place, blocks, length)
        rows = pl.ds(start, length)
        k_block, v_block = k_ref[rows, :], v_ref[rows, :]
        k_place = j * length + lax.broadcasted_iota(jnp.int32, (1, length), 1)
        allowed = (k_place >= first) & (k_place <= q_place)
        every = range(heads)
        scores = [dot_nt(q_heads[h], k_block) for h in every]
        grad_probs = [dot_nt(go_heads[h], v_block) for h in every]
        probs = [jnp.exp(jnp.where(allowed, scores[h] - lse[h], NEG_FILL)) for h in every]
        grad_scores = [(probs[h] * (grad_probs[h] - inner[h])).astype(BF) for h in every]
        for h in every:
            part = slice(h * HD, (h + 1) * HD)
            vt_scr[part, rows] = vt_scr[part, rows] + dot(go_turned[part, :], probs[h].astype(BF))
            kt_scr[part, rows] = kt_scr[part, rows] + dot(q_turned[part, :], grad_scores[h])
        spread = pl.ds(pl.multiple_of(start * heads, heads * length), heads * length)
        return acc + dot(jnp.concatenate(grad_scores, axis=1), k_scr[spread, :])

    grad_q = lax.fori_loop(low, i + 1, step, jnp.zeros((length, width), F32))
    grad_q = (grad_q.astype(BF).astype(F32) * (HD**-0.5)).astype(BF)
    k = i ^ place
    own_rows = pl.ds(pl.multiple_of((k >> 1) * length, length), length)

    @pl.when((k & 1) == 0)
    def _():
        even_ref[own_rows, 0:width] = grad_q

    @pl.when((k & 1) == 1)
    def _():
        odd_ref[own_rows, 0:width] = grad_q

    @pl.when(i == blocks - 1)
    def _():
        for j in range(blocks):
            target, m = (even_ref, j) if j < blocks // 2 else (odd_ref, j - blocks // 2)
            source, rows = slice(j * length, (j + 1) * length), slice(m * length, (m + 1) * length)
            target[rows, width : 2 * width] = kt_scr[:, source].T.astype(BF)
            target[rows, 2 * width : 3 * width] = vt_scr[:, source].T.astype(BF)


def storage_map(length, blocks, column):
    def index(i, place_ref, low_ref):
        k = i ^ place_ref[0]
        return ((k >> 1) + (k & 1) * (blocks // 2), column)

    return index


def attend_forward(place, low, qkv, first, length):
    rows, triple = qkv.shape
    width, blocks = triple // 3, rows // length
    heads = width // HD
    return pl.pallas_call(
        functools.partial(attend_forward_kernel, heads=heads, length=length, blocks=blocks),
        grid_spec=pltpu.PrefetchScalarGridSpec(
            num_scalar_prefetch=2,
            grid=(blocks,),
            in_specs=[
                pl.BlockSpec((length, width), storage_map(length, blocks, 0)),
                pl.BlockSpec((rows, width), lambda i, p, w: (0, 1)),
                pl.BlockSpec((rows, width), lambda i, p, w: (0, 2)),
                pl.BlockSpec((length, 1), lambda i, p, w: (i, 0)),
            ],
            out_specs=[
                pl.BlockSpec((length, width), lambda i, p, w: (i, 0)),
                pl.BlockSpec((length, 128), lambda i, p, w: (i, 0)),
            ],
            scratch_shapes=[
                pltpu.VMEM((heads, length, rows), F32),
                pltpu.VMEM((heads, length, 128), F32),
                pltpu.VMEM((heads, length, 128), F32),
                pltpu.VMEM((heads * rows, width), BF),
            ],
        ),
        out_shape=[jax.ShapeDtypeStruct((rows, width), BF), jax.ShapeDtypeStruct((rows, 128), F32)],
        compiler_params=pltpu.CompilerParams(dimension_semantics=("arbitrary",), vmem_limit_bytes=LARGE_GRANT),
        cost_estimate=light_cost(24 * rows * rows * width),
        name="attend_forward",
    )(place, low, qkv, qkv, qkv, first)


def attend_backward(place, low, qkv, grad_out, mixed, lse, first, length):
    rows, triple = qkv.shape
    width, blocks = triple // 3, rows // length
    heads = width // HD
    return pl.pallas_call(
        functools.partial(attend_backward_kernel, heads=heads, length=length, blocks=blocks),
        grid_spec=pltpu.PrefetchScalarGridSpec(
            num_scalar_prefetch=2,
            grid=(blocks,),
            in_specs=[
                pl.BlockSpec((length, width), storage_map(length, blocks, 0)),
                pl.BlockSpec((length, width), lambda i, p, w: (i, 0)),
                pl.BlockSpec((length, width), lambda i, p, w: (i, 0)),
                pl.BlockSpec((length, 128), lambda i, p, w: (i, 0)),
                pl.BlockSpec((rows, width), lambda i, p, w: (0, 1)),
                pl.BlockSpec((rows, width), lambda i, p, w: (0, 2)),
                pl.BlockSpec((length, 1), lambda i, p, w: (i, 0)),
            ],
            out_specs=[pl.BlockSpec((rows // 2, triple), lambda i, p, w: (0, 0))] * 2,
            scratch_shapes=[
                pltpu.VMEM((width, rows), F32),
                pltpu.VMEM((width, rows), F32),
                pltpu.VMEM((heads * rows, width), BF),
            ],
        ),
        out_shape=[jax.ShapeDtypeStruct((rows // 2, triple), BF)] * 2,
        compiler_params=pltpu.CompilerParams(dimension_semantics=("arbitrary",), vmem_limit_bytes=LARGE_GRANT),
        cost_estimate=light_cost(36 * rows * rows * width),
        name="attend_backward",
    )(place, low, qkv, grad_out, mixed, lse, qkv, qkv, first)


def local(
    inputs,
    teacher,
    segment_ids,
    summary_start,
    valid_mask,
    attn_norm_gain,
    attn_norm_bias,
    query_weight,
    query_bias,
    key_weight,
    value_weight,
    value_bias,
    out_weight,
    out_bias,
    mlp_norm_gain,
    mlp_norm_bias,
    up_weight,
    up_bias,
    down_weight,
    down_bias,
):
    seqs, length = segment_ids.shape
    width = inputs.shape[-1]
    hidden_units = up_weight.shape[1]
    n, groups = lax.axis_size("seq"), lax.axis_size("dp")
    place, group = lax.axis_index("seq"), lax.axis_index("dp")
    both = ("dp", "seq")
    seq_len = length * n
    tokens_all = seqs * seq_len * groups
    scale = HD**-0.5
    own_rows = query_weight.shape[0]
    own_hidden = up_bias.shape[0]
    head_cols = width // n

    def out_of(value):
        return lax.all_to_all(value, "seq", split_axis=0, concat_axis=0, tiled=True)

    valid = valid_mask.astype(F32)
    order = Order()
    near = n == 8 and groups == 4
    out_steps = Steps(order, line_gather(out_weight)) if near else None
    cut = jnp.concatenate(
        [w.reshape(own_rows, n, head_cols).transpose(1, 0, 2) for w in (query_weight, key_weight, value_weight)], axis=2
    )
    qkv_cut = out_of(cut)
    small = [attn_norm_gain, attn_norm_bias, out_bias, mlp_norm_gain, mlp_norm_bias, down_bias, query_bias, value_bias, up_bias]
    pieces = [v.astype(F32) for v in small] + [segment_ids.astype(F32).reshape(-1), jnp.sum(valid).reshape(1)]
    starts, lines = [], []
    for piece in pieces:
        starts.append(sum(line.shape[0] for line in lines))
        short = -piece.shape[0] % 128
        lines.append(jnp.pad(piece, (0, short)).reshape(-1, 128))
    used = sum(line.shape[0] for line in lines)
    packed = jnp.pad(jnp.concatenate(lines, axis=0), ((0, -used % 8), (0, 0)))[None]
    small_steps = Steps(order, doubling(after(packed, cut), ("dp", "seq")))
    small_steps.step(1)
    qkv_cut = order.pause(qkv_cut).reshape(n * own_rows, 3 * head_cols)
    w_qkv = lax.all_gather(qkv_cut, "dp", axis=0, tiled=True)
    if near:
        out_steps.step()
    small_steps.step(1)
    if near:
        out_steps.step()
    small_steps.step(1)
    if near:
        own_out = out_steps.finish()
    packed = small_steps.finish().reshape(n, groups, -1, 128).transpose(1, 0, 2, 3).reshape(groups * n, -1, 128)

    def zero_after(value):
        return jnp.minimum(jnp.abs(value.reshape(-1)[0].astype(F32)), 0.0).astype(jnp.int32)

    def rows_after(b, value):
        return lax.dynamic_index_in_dim(inputs, b + zero_after(value), 0, keepdims=False)

    state = [types.SimpleNamespace() for _ in range(seqs)]
    state[0].own = rows_after(0, packed)
    state[0].came = gather_start(state[0].own)
    parts = []
    for piece, at in zip(pieces, starts):
        count = -(-piece.shape[0] // 128)
        parts.append(packed[:, at : at + count].reshape(groups * n, -1)[:, : piece.shape[0]])
    gain_one, shift_one, b_out, gain_two, shift_two, b_down = [part.reshape(-1) for part in parts[:6]]
    b_query, b_value = [lax.dynamic_slice_in_dim(part.reshape(-1), place * head_cols, head_cols) for part in parts[6:8]]
    b_up = lax.dynamic_index_in_dim(parts[8].reshape(groups, n, -1), place, 1, keepdims=False).reshape(-1)
    ids = lax.dynamic_index_in_dim(parts[9].reshape(groups, n, seqs, length), group, 0, keepdims=False)
    ids = ids.transpose(1, 0, 2).reshape(seqs, seq_len)
    total_count = jnp.sum(parts[10])

    up_cut = up_weight.reshape(own_rows, groups, n, own_hidden).transpose(2, 0, 1, 3).reshape(n, own_rows, groups * own_hidden)
    b_qkv = jnp.concatenate([b_query, jnp.zeros_like(b_query), b_value])
    s_qkv = jnp.concatenate([jnp.full((head_cols,), scale, F32), jnp.ones((2 * head_cols,), F32)])

    place_arr = place.reshape(1).astype(jnp.int32)
    positions = jnp.arange(seq_len, dtype=jnp.int32)

    def add_all(terms):
        out = terms[0]
        for term in terms[1:]:
            out = out + term
        return out


    def spans(b):
        st = state[b]
        first = jnp.sum((ids[b][None, :] < ids[b][:, None]).astype(jnp.int32), axis=1)
        in_summary = (positions >= summary_start[b]) & (positions < summary_start[b] + NSUM)
        first = jnp.where(in_summary, 0, first)
        st.low = jnp.min(first.reshape(n, length), axis=1) // length
        st.first = first.reshape(seq_len, 1)

    def project(b):
        st = state[b]
        even, odd = order.tie((st.even, st.odd))
        parts = [project_product(part, w_qkv, b_qkv, s_qkv) for part in (even, odd)]
        st.qkv = order.mark(jnp.concatenate(parts, axis=0))

    def attend(b):
        st = state[b]
        qkv = order.tie(st.qkv)
        st.mixed, st.lse = attend_forward(place_arr, st.low, qkv, st.first, length)
        order.mark(st.mixed)

    def send_mixed(b):
        st = state[b]
        st.moved = out_of(st.mixed.reshape(n, length, head_cols))

    def middle(b):
        st = state[b]
        attended = order.tie(st.moved)
        st.attended = attended.transpose(1, 0, 2).reshape(length, width)
        rows = inputs[b].astype(F32)
        st.hidden = rows + (dot(st.attended, w_out) + b_out)
        st.normed_two, st.inverse_two = norm_core(st.hidden)
        st.own_two = order.mark((st.normed_two * gain_two + shift_two).astype(BF))
        st.came_two = gather_start(st.own_two)

    def up_even(b):
        st = state[b]
        st.act_even = order.mark(up_product(order.tie(st.even_two), w_up, b_up))

    def up_odd(b):
        st = state[b]
        st.act_odd = order.mark(up_product(order.tie(st.odd_two), w_up, b_up))

    def relay(b, own, came):
        st = state[b]
        came = order.pause(getattr(st, came))
        return came, gather_relay(getattr(st, own), came)

    def join(b, own, came_relayed):
        same = order.mark(gather_join(getattr(state[b], own), *order.tie(came_relayed)))
        return same, swap(same, 1)

    def down_odd(b):
        st = state[b]
        st.down_got = swap(order.mark(plain_product(order.tie(st.act_odd), w_down)), 1)

    def down_even(b):
        st = state[b]
        st.down_sums = order.mark(block_products(st.act_even, w_down, order.tie(st.down_got), n // 2))
        st.down_came = scatter_start(st.down_sums)

    def pass_on(b, sums, came):
        st = state[b]
        came = order.pause(getattr(st, came))
        return scatter_relay(order.mark(scatter_halves(getattr(st, sums), came)))

    def misfit(b):
        st = state[b]
        summed = scatter_join(st.down_sums, order.tie(st.down_sent))
        st.result = st.hidden + (summed + b_down)
        error = st.result - teacher[b].astype(F32)
        st.local_sq = jnp.sum(jnp.sum(error * error, axis=-1) * valid[b])
        st.grad_result = error * (valid[b] * (tokens_all / total_count))[:, None]
        st.own_grad = order.mark(st.grad_result.astype(BF))
        st.g_b_down = jnp.sum(st.own_grad.astype(F32), axis=0)
        st.came_grad = gather_start(st.own_grad)

    def act_back_even(b):
        st = state[b]
        st.pre_even, st.sums_even = masked_product(order.tie(st.gm_even), w_down, st.act_even)
        order.mark(st.pre_even)

    def act_back_odd(b):
        st = state[b]
        st.pre_odd, st.sums_odd = masked_product(order.tie(st.gm_odd), w_down, st.act_odd)
        order.mark(st.pre_odd)

    def up_back_odd(b):
        st = state[b]
        st.up_got = swap(order.mark(plain_product(order.tie(st.pre_odd), w_up, turned=True)), 1)

    def up_back_even(b):
        st = state[b]
        st.up_sums = order.mark(block_products(st.pre_even, w_up, order.tie(st.up_got), n // 2, turned=True))
        st.up_came = scatter_start(st.up_sums)

    def branch_back(b):
        st = state[b]
        grad_ready = scatter_join(st.up_sums, order.tie(st.up_sent))
        grad_norm, st.g_gain_two, st.g_shift_two = norm_back(grad_ready, st.normed_two, st.inverse_two, gain_two)
        st.grad_hidden = st.grad_result + grad_norm
        st.branch = st.grad_hidden.astype(BF)
        st.g_b_out = jnp.sum(st.branch.astype(F32), axis=0)
        grad_att = dot_nt(st.branch, w_out).astype(BF).reshape(length, n, head_cols).transpose(1, 0, 2)
        st.grad_mixed = out_of(order.mark(grad_att)).reshape(seq_len, head_cols)

    def attend_back(b):
        st = state[b]
        st.grad_qkv = attend_backward(
            place_arr, st.low, st.qkv, order.tie(st.grad_mixed), st.mixed, st.lse, st.first, length
        )
        order.mark(st.grad_qkv)
        st.g_b_qkv = sum(jnp.sum(part.astype(F32), axis=0) for part in st.grad_qkv)

    def project_back_odd(b):
        st = state[b]
        odd = order.tie(st.grad_qkv[1])
        st.one_got = swap(order.mark(plain_product(odd, w_qkv, turned=True)), 1)

    def project_back_even(b):
        st = state[b]
        st.one_sums = block_products(st.grad_qkv[0], w_qkv, order.tie(st.one_got), n // 2, turned=True)
        order.mark(st.one_sums)
        st.one_came = scatter_start(st.one_sums)

    def finish(b):
        st = state[b]
        grad_ready = scatter_join(st.one_sums, order.tie(st.one_sent))
        normed, inverse = norm_core(inputs[b].astype(F32))
        grad_norm, st.g_gain_one, st.g_shift_one = norm_back(grad_ready, normed, inverse, gain_one)
        st.grad_inputs = order.mark(st.grad_hidden + grad_norm)

    every, later = range(seqs), range(1, seqs)

    def whole_out_weight(own, came, relayed):
        whole = jnp.zeros((groups, n, own_rows, width), BF)
        half = groups // 2
        same = [(0, own, 0), (2, came[0], 0), (4, came[1], 0), (6, relayed[0], 0), (6, relayed[1], half)]
        other = [(k + 1, swap(piece, 1), first) for k, piece, first in same]
        for k, piece, first in same + other:
            whole = lax.dynamic_update_slice(whole, piece.reshape(-1, 1, own_rows, width), (first, place ^ k, 0, 0))
        return whole.reshape(width, width)

    def make_ready(b, came_relayed):
        st = state[b]
        st.even = order.mark(norm_rows(gather_pieces(st.own, *order.tie(came_relayed)), gain_one, shift_one))
        st.odd = swap(st.even, 1)

    for b in every:
        spans(b)
    came_relayed = relay(0, "own", "came")
    for b in later:
        state[b].own = rows_after(b, came_relayed[0][0] if near else packed)
        state[b].came = gather_start(state[b].own)
    make_ready(0, came_relayed)
    if near:
        own_out = order.tie(own_out)
        out_came = gather_start(own_out)
    else:
        w_out = lax.all_gather(after(out_weight, qkv_cut), both, axis=0, tiled=True)
    up_cut = order.pause(out_of(after(up_cut, qkv_cut)))
    w_up = lax.all_gather(up_cut.reshape(n * own_rows, groups * own_hidden), "dp", axis=0, tiled=True)
    w_down = lax.all_gather(after(down_weight, up_cut), "dp", axis=0, tiled=True)
    w_qkv = order.pause(w_qkv)
    project(0)
    attend(0)
    send_mixed(0)
    if near:
        out_came = order.pause(out_came)
        out_relayed = gather_relay(own_out, out_came)
    raw = [relay(b, "own", "came") for b in later]
    if near:
        w_out = whole_out_weight(own_out, out_came, order.pause(out_relayed))
    middle(0)
    for b in later:
        last, st = state[b - 1], state[b]
        w_up = order.pause(w_up)
        make_ready(b, raw[b - 1])
        project(b)
        came_relayed = relay(b - 1, "own_two", "came_two")
        attend(b)
        send_mixed(b)
        last.even_two, last.odd_two = join(b - 1, "own_two", came_relayed)
        up_even(b - 1)
        middle(b)
        up_odd(b - 1)
        came_relayed = relay(b, "own_two", "came_two")
        down_odd(b - 1)
        st.even_two, st.odd_two = join(b, "own_two", came_relayed)
        up_even(b)
        down_even(b - 1)
        up_odd(b)
        last.down_sent = pass_on(b - 1, "down_sums", "down_came")
        down_odd(b)
        down_even(b)
        misfit(b - 1)
        st.down_sent = pass_on(b, "down_sums", "down_came")
        came_relayed = relay(b - 1, "own_grad", "came_grad")
        misfit(b)
        last.gm_even, last.gm_odd = join(b - 1, "own_grad", came_relayed)
        act_back_even(b - 1)
        act_back_odd(b - 1)
        came_relayed = relay(b, "own_grad", "came_grad")
        up_back_odd(b - 1)
        up_back_even(b - 1)
        st.gm_even, st.gm_odd = join(b, "own_grad", came_relayed)
        act_back_even(b)
        last.up_sent = pass_on(b - 1, "up_sums", "up_came")
        act_back_odd(b)
        up_back_odd(b)
        up_back_even(b)
    lefts = [part for st in state for part in (st.even_two, st.odd_two)]
    rights = [part for st in state for part in (st.pre_even, st.pre_odd)]
    g_w_up = order.mark(weight_grad(order.tie(lefts), rights, 512, 1024))
    g_up = lax.psum_scatter(g_w_up, "dp", scatter_dimension=0, tiled=True)
    for b in later:
        state[b].up_sent = pass_on(b, "up_sums", "up_came")
    branch_back(0)
    lefts = [part for st in state for part in (st.act_even, st.act_odd)]
    rights = [part for st in state for part in (st.gm_even, st.gm_odd)]
    g_w_down = order.mark(weight_grad(order.tie(lefts), rights, 256, 1024))
    g_down = lax.psum_scatter(g_w_down, "dp", scatter_dimension=0, tiled=True)
    state[0].grad_mixed = order.pause(state[0].grad_mixed)
    for b in later:
        branch_back(b)
    turned = [
        st.attended.reshape(length, groups, n, own_rows).transpose(2, 0, 1, 3).reshape(n, length, groups * own_rows)
        for st in state
    ]

    def out_block(k):
        return add_all(
            [dot_tn(lax.dynamic_index_in_dim(t, place ^ k, 0, keepdims=False), st.branch) for t, st in zip(turned, state)]
        )

    out_rows = groups * own_rows
    turned = order.tie(turned)
    out_odd = order.mark(jnp.concatenate([out_block(k).astype(BF) for k in range(1, n, 2)], axis=0))
    out_got = swap(out_odd, 1)
    attend_back(0)
    out_got = order.tie(out_got)
    out_sums = [out_block(2 * m) + out_got[m * out_rows : (m + 1) * out_rows].astype(F32) for m in range(n // 2)]
    order.mark(out_sums)
    out_came = scatter_start(out_sums)
    project_back_odd(0)
    out_sent = scatter_relay(order.mark(scatter_halves(out_sums, order.pause(out_came))))
    project_back_even(0)
    g_up, g_down = order.pause((g_up, g_down))
    g_up = out_of(g_up.reshape(n, own_rows, groups * own_hidden))
    for b in later:
        attend_back(b)
        state[b - 1].one_came, out_sent = order.pause((state[b - 1].one_came, out_sent))
    for b in later:
        state[b - 1].one_sent = pass_on(b - 1, "one_sums", "one_came")
    out_sum = order.mark(scatter_join(out_sums, order.tie(out_sent)).astype(BF))
    out_parts = out_sum.reshape(groups, own_rows, width)
    out_line = Steps(order, line_scatter(out_parts)) if near else None
    for b in later:
        project_back_odd(b)
    lefts = [part for st in state for part in (st.even, st.odd)]
    rights = [part for st in state for part in st.grad_qkv]
    g_w_qkv = order.mark(weight_grad(order.tie(lefts), rights, 1024, 768))
    if near:
        out_line.step()
        qkv_line = Steps(order, line_scatter(g_w_qkv.reshape(groups, n * own_rows, 3 * head_cols)))
    else:
        g_qkv = lax.psum_scatter(g_w_qkv, "dp", scatter_dimension=0, tiled=True)
        g_out = lax.psum_scatter(out_sum, "dp", scatter_dimension=0, tiled=True)
    g_up = order.pause(g_up)
    for b in later:
        state[b - 1].one_sent = order.pause(state[b - 1].one_sent)
        project_back_even(b)
    if near:
        out_line.step()
        qkv_line.step()
    for b in later:
        state[b].one_sent = pass_on(b, "one_sums", "one_came")
        finish(b - 1)
    if near:
        g_out = out_line.finish()
        qkv_line.step()
    for b in later:
        state[b].one_sent = order.pause(state[b].one_sent)
    if near:
        g_qkv = order.mark(qkv_line.finish().astype(BF))
    g_qkv = out_of(g_qkv.reshape(n, own_rows, 3 * head_cols))
    for b in later:
        finish(b)
    g_out = g_out.astype(F32)

    def summed(name):
        return add_all([after(getattr(st, name), *state[-1].one_sums) for st in state])

    g_down = order.tie(g_down).astype(F32)
    g_up = g_up.reshape(n, own_rows, groups, own_hidden).transpose(1, 2, 0, 3).reshape(own_rows, hidden_units).astype(F32)
    g_qkv_came = g_qkv
    g_qkv = g_qkv.reshape(n, own_rows, 3, head_cols).transpose(2, 1, 0, 3).reshape(3, own_rows, width).astype(F32)

    g_b_qkv = summed("g_b_qkv").reshape(3, head_cols)
    own_bias = jnp.zeros((2, width), F32)
    own_bias = lax.dynamic_update_slice(own_bias, jnp.stack([g_b_qkv[0], g_b_qkv[2]]), (0, place * head_cols))
    g_b_up = jnp.sum(summed("sums_even") + summed("sums_odd"), axis=0).reshape(groups, 1, own_hidden)
    spread_up = lax.dynamic_update_slice_in_dim(jnp.zeros((groups, n, own_hidden), F32), g_b_up, place, 1)
    names = ("g_gain_one", "g_shift_one", "g_b_out", "g_gain_two", "g_shift_two", "g_b_down")
    vectors = jnp.concatenate([jnp.stack([summed(name) for name in names]), own_bias], axis=0)
    count = vectors.shape[0]
    vectors = vectors.reshape(count, groups * n, own_rows).transpose(1, 0, 2).reshape(groups * n, count * own_rows)
    sq = jnp.broadcast_to(summed("local_sq"), (groups * n, 1))
    tail = jnp.concatenate([vectors, spread_up.reshape(groups * n, own_hidden), sq], axis=1)
    tail = scatter_small(tail, g_qkv_came)
    vectors = tail[: count * own_rows].reshape(count, own_rows)
    g_b_query, g_b_value, g_b_up = vectors[6], vectors[7], tail[count * own_rows : -1]
    mean_loss = tail[-1] / (total_count * width)
    return (
        jnp.stack([st.result.astype(BF) for st in state]),
        mean_loss,
        jnp.stack([st.grad_inputs for st in state]),
        vectors[0],
        vectors[1],
        g_qkv[0],
        g_b_query,
        g_qkv[1],
        g_qkv[2],
        g_b_value,
        g_out,
        vectors[2],
        vectors[3],
        vectors[4],
        g_up,
        g_b_up,
        g_down,
        vectors[5],
    )


def solution(mesh):
    rows3, rows2, flat, mat = P("dp", "seq", None), P("dp", "seq"), P(("dp", "seq")), P(("dp", "seq"), None)
    placed = (
        rows3, rows3, rows2, P("dp"), rows2, flat, flat, mat, flat, mat, mat, flat, mat, flat, flat, flat, mat, flat, mat, flat,
    )
    out = (rows3, P(), rows3, flat, flat, mat, flat, mat, mat, flat, mat, flat, flat, flat, mat, flat, mat, flat)
    return jax.shard_map(local, mesh=mesh, in_specs=placed, out_specs=out, check_vma=False)
```

```python
import functools
import types

import jax
import jax.numpy as jnp
from jax import lax
from jax.experimental import pallas as pl
from jax.experimental.pallas import tpu as pltpu
from jax.sharding import PartitionSpec as P

HD = 64
NSUM = 50
NORM_EPS = 1e-05
NEG_FILL = -1e30
PRODUCT_GRANT, LARGE_GRANT = 30 << 20, 56 << 20
BF = jnp.bfloat16
F32 = jnp.float32


def dot(left_in, right_in):
    return jnp.dot(left_in, right_in, preferred_element_type=F32)


def dot_tn(left_in, right_in):
    return lax.dot_general(left_in, right_in, (((0,), (0,)), ((), ())), preferred_element_type=F32)


def dot_nt(left_in, right_in):
    return lax.dot_general(left_in, right_in, (((1,), (1,)), ((), ())), preferred_element_type=F32)


def norm_core(values):
    center = values - jnp.mean(values, axis=-1, keepdims=True)
    inverse = lax.rsqrt(jnp.mean(center * center, axis=-1, keepdims=True) + NORM_EPS)
    return center * inverse, inverse


def norm_back(grad_out, normed, inverse, gain_in):
    grad_normed = grad_out * gain_in
    inner_one = jnp.mean(grad_normed, axis=-1, keepdims=True)
    inner_two = jnp.mean(grad_normed * normed, axis=-1, keepdims=True)
    grad_in = inverse * (grad_normed - inner_one - normed * inner_two)
    return grad_in, jnp.sum(grad_out * normed, axis=0), jnp.sum(grad_out, axis=0)


def swap(values, mask):
    n = lax.axis_size("seq")
    return lax.ppermute(values, "seq", [(i, i ^ mask) for i in range(n)])


def gather_start(own):
    return (swap(own, 2), swap(own, 4)) if lax.axis_size("seq") == 8 else ()


def gather_relay(own, came):
    if lax.axis_size("seq") != 8:
        return ()
    half = own.shape[0] // 2
    return swap(came[1][:half], 2), swap(came[0][half:], 4)


def gather_pieces(own, came, relayed):
    if lax.axis_size("seq") == 8:
        return [own, *came, *relayed]
    return [gather_join(own, came, relayed)]


def gather_join(own, came, relayed):
    if lax.axis_size("seq") == 8:
        return jnp.concatenate([own, *came, *relayed], axis=0)
    same, step = own, 2
    while step < lax.axis_size("seq"):
        same = jnp.concatenate([same, swap(same, step)], axis=0)
        step *= 2
    return same


def gather_rows(own):
    came = gather_start(own)
    same = gather_join(own, came, gather_relay(own, came))
    return same, swap(same, 1)


def scatter_start(blocks):
    if lax.axis_size("seq") != 8:
        return ()
    six = blocks[3].astype(BF)
    half = six.shape[0] // 2
    return swap(six[:half], 2), swap(six[half:], 4)


def scatter_halves(blocks, came):
    if lax.axis_size("seq") != 8:
        return ()
    _, two, four, _ = blocks
    half, width = two.shape[0] // 2, two.shape[1]
    which = lax.broadcasted_iota(jnp.int32, (2, half, width), 0)

    def with_half(block, part, side):
        part = jnp.where(which == side, part.astype(F32)[None], 0.0)
        return (block.reshape(2, half, width) + part).astype(BF).reshape(2 * half, width)

    return with_half(two, came[1], 1), with_half(four, came[0], 0)


def scatter_relay(halves):
    return (swap(halves[0], 2), swap(halves[1], 4)) if halves else ()


def scatter_join(blocks, relayed):
    n = lax.axis_size("seq")
    if n == 8:
        return blocks[0] + relayed[0].astype(F32) + relayed[1].astype(F32)
    step = n // 2
    while step > 1:
        keep = len(blocks) // 2
        sent = [swap(block.astype(BF), step).astype(F32) for block in blocks[keep:]]
        blocks = [block.astype(F32) + got for block, got in zip(blocks[:keep], sent)]
        step //= 2
    return blocks[0]


def exchange(values, axis, bit):
    size = lax.axis_size(axis)
    return lax.ppermute(values, axis, [(i, i ^ bit) for i in range(size)])


class Order:
    def __init__(self):
        self.last = ()

    def tie(self, value):
        if not jax.tree.leaves(value) or not jax.tree.leaves(self.last):
            return value
        return lax.optimization_barrier((value, self.last))[0]

    def mark(self, value):
        if jax.tree.leaves(value):
            self.last = value
        return value

    def pause(self, value):
        return self.mark(self.tie(value))


def doubling(held, axes):
    for axis in axes:
        bit, index = 1, lax.axis_index(axis)
        while bit < lax.axis_size(axis):
            other = yield exchange(held, axis, bit)
            upper = (index & bit) != 0
            held = jnp.concatenate([jnp.where(upper, other, held), jnp.where(upper, held, other)], axis=0)
            bit *= 2
    return held


def line_gather(own):
    size, index = lax.axis_size("dp"), lax.axis_index("dp")
    below, above = [], []
    to_right, to_left = own, own
    for _ in range(size - 1):
        flight = (
            lax.ppermute(to_right, "dp", [(i, i + 1) for i in range(size - 1)]),
            lax.ppermute(to_left, "dp", [(i + 1, i) for i in range(size - 1)]),
        )
        to_right, to_left = yield flight
        below.insert(0, to_right)
        above.append(to_left)
    rows = jnp.concatenate(below + [own] + above, axis=0)
    return lax.dynamic_slice_in_dim(rows, (size - 1 - index) * own.shape[0], size * own.shape[0], axis=0)


def line_scatter(parts):
    size, index = lax.axis_size("dp"), lax.axis_index("dp")

    def part(which):
        return lax.dynamic_index_in_dim(parts, jnp.clip(which, 0, size - 1), 0, keepdims=False)

    right = left = None
    for step in range(size - 1):
        far = size - 1 - step
        up, down = part(index + far), part(index - far)
        if step:
            up, down = (up.astype(F32) + right.astype(F32)).astype(BF), (down.astype(F32) + left.astype(F32)).astype(BF)
        flight = (
            lax.ppermute(up, "dp", [(i, i + 1) for i in range(size - far)]),
            lax.ppermute(down, "dp", [(i, i - 1) for i in range(far, size)]),
        )
        right, left = yield flight
    return part(index).astype(F32) + right.astype(F32) + left.astype(F32)


class Steps:
    def __init__(self, order, generator):
        self.order, self.generator, self.flight, self.result = order, generator, next(generator), None

    def step(self, count=1):
        for _ in range(count):
            if self.flight is None:
                return
            try:
                self.flight = self.generator.send(self.order.pause(self.flight))
            except StopIteration as stop:
                self.flight, self.result = None, stop.value

    def finish(self):
        while self.flight is not None:
            self.step()
        return self.result


def scatter_small(table, awaited):
    count, width = table.shape
    length = -(-width // 1024) * 1024
    held = jnp.pad(table, ((0, 0), (0, length - width))).reshape(count, 8, length // 8)
    for axis in ("dp", "seq"):
        bit, index = lax.axis_size(axis) // 2, lax.axis_index(axis)
        while bit > 0:
            half = held.shape[0] // 2
            upper = (index & bit) != 0
            sent = jnp.where(upper, held[:half], held[half:])
            held = jnp.where(upper, held[half:], held[:half]) + exchange(sent, axis, bit)
            bit //= 2
        if axis == "dp":
            held = after(held, awaited)
    return held.reshape(length)[:width]


def after(value, *earlier):
    return lax.optimization_barrier((value, *earlier))[0]


def weight_grad_kernel(*refs):
    count = (len(refs) - 1) // 2
    total = dot_tn(refs[0][...], refs[count][...])
    for part in range(1, count):
        total = total + dot_tn(refs[part][...], refs[count + part][...])
    refs[-1][...] = total.astype(BF)


def weight_grad(lefts, rights, left_tile, right_tile):
    rows, left_width = lefts[0].shape
    right_width = rights[0].shape[1]
    left_tile, right_tile = min(left_tile, left_width), min(right_tile, right_width)
    count = len(lefts)
    return pl.pallas_call(
        weight_grad_kernel,
        grid=(right_width // right_tile, left_width // left_tile),
        in_specs=[pl.BlockSpec((rows, left_tile), lambda j, i: (0, i))] * count
        + [pl.BlockSpec((rows, right_tile), lambda j, i: (0, j))] * count,
        out_specs=pl.BlockSpec((left_tile, right_tile), lambda j, i: (i, j)),
        out_shape=jax.ShapeDtypeStruct((left_width, right_width), BF),
        compiler_params=pltpu.CompilerParams(dimension_semantics=("arbitrary", "arbitrary"), vmem_limit_bytes=LARGE_GRANT),
        cost_estimate=light_cost(2 * count * rows * left_width * right_width),
        name="weight_grad",
    )(*lefts, *rights)


def tile_dot(left, right, turned):
    return dot_nt(left, right) if turned else dot(left, right)


def plain_kernel(left_ref, right_ref, out_ref, *, turned):
    out_ref[...] = tile_dot(left_ref[...], right_ref[...], turned).astype(out_ref.dtype)


def project_kernel(left_ref, right_ref, bias_ref, scale_ref, out_ref):
    out_ref[...] = ((dot(left_ref[...], right_ref[...]) + bias_ref[...]) * scale_ref[...]).astype(BF)


def up_kernel(left_ref, right_ref, bias_ref, out_ref):
    out_ref[...] = jnp.maximum(dot(left_ref[...], right_ref[...]) + bias_ref[...], 0.0).astype(BF)


def masked_kernel(left_ref, right_ref, act_ref, out_ref, sums_ref):
    grad = jnp.where(act_ref[...] > 0, dot_nt(left_ref[...], right_ref[...]), 0.0).astype(BF)
    out_ref[...] = grad
    part = jnp.sum(grad.astype(F32).reshape(-1, 8, grad.shape[1]), axis=0)

    @pl.when(pl.program_id(1) == 0)
    def _():
        sums_ref[...] = part

    @pl.when(pl.program_id(1) > 0)
    def _():
        sums_ref[...] = sums_ref[...] + part


def blocks_kernel(left_ref, right_ref, got_ref, *out_refs, turned):
    rows = out_refs[0].shape[0]
    for m in range(len(out_refs) - 1, -1, -1):
        cut = slice(m * rows, (m + 1) * rows)
        total = tile_dot(left_ref[cut, :], right_ref[...], turned) + got_ref[cut, :].astype(F32)
        out_refs[m][...] = total.astype(out_refs[m].dtype)


def light_cost(flops):
    return pl.CostEstimate(flops=int(flops) // 8, bytes_accessed=1, transcendentals=0)


def tiled(kernel, name, left, right, turned, extras, outs, row_tile, col_tile, parts=1):
    rows, depth = left.shape
    cols = right.shape[0] if turned else right.shape[1]
    row_tile, col_tile = min(row_tile, rows), min(col_tile, cols)
    kinds = {
        "both": pl.BlockSpec((row_tile, col_tile), lambda j, m: (m, j)),
        "vector": pl.BlockSpec((1, col_tile), lambda j, m: (0, j)),
        "sums": pl.BlockSpec((8, col_tile), lambda j, m: (0, j)),
        "block": pl.BlockSpec((rows // parts, col_tile), lambda j, m: (0, j)),
    }
    shapes = {"both": (rows, cols), "sums": (8, cols), "block": (rows // parts, cols)}
    right_spec = (
        pl.BlockSpec((col_tile, depth), lambda j, m: (j, 0)) if turned else pl.BlockSpec((depth, col_tile), lambda j, m: (0, j))
    )
    return pl.pallas_call(
        kernel,
        grid=(cols // col_tile, rows // row_tile),
        in_specs=[pl.BlockSpec((row_tile, depth), lambda j, m: (m, 0)), right_spec] + [kinds[k] for k, _ in extras],
        out_specs=[kinds[k] for k, _ in outs],
        out_shape=[jax.ShapeDtypeStruct(shapes[k], dtype) for k, dtype in outs],
        compiler_params=pltpu.CompilerParams(dimension_semantics=("arbitrary", "arbitrary"), vmem_limit_bytes=PRODUCT_GRANT),
        cost_estimate=light_cost(2 * rows * cols * depth),
        name=name,
    )(left, right, *[value for _, value in extras])


def plain_product(left, right, turned=False):
    kernel = functools.partial(plain_kernel, turned=turned)
    return tiled(kernel, "product", left, right, turned, [], [("both", BF)], 1024, 256)[0]


def project_product(left, right, bias, scale):
    extras = [("vector", bias.reshape(1, -1)), ("vector", scale.reshape(1, -1))]
    return tiled(project_kernel, "project", left, right, False, extras, [("both", BF)], 1024, 256)[0]


def up_product(left, right, bias):
    return tiled(up_kernel, "up", left, right, False, [("vector", bias.reshape(1, -1))], [("both", BF)], 1024, 256)[0]


def masked_product(left, right, act):
    outs = [("both", BF), ("sums", F32)]
    return tiled(masked_kernel, "masked_product", left, right, True, [("both", act)], outs, 1024, 256)


def block_products(left, right, got, count, turned=False):
    kernel = functools.partial(blocks_kernel, turned=turned)
    outs = [("block", F32)] * (count - 1) + [("block", BF)]
    return tiled(
        kernel, "block_products", left, right, turned, [("both", got)], outs, left.shape[0], 256, count
    )


def norm_kernel(*refs, unit):
    *piece_refs, gain_ref, shift_ref, out_ref = refs
    step, at = pl.program_id(0), 0
    for piece_ref in piece_refs:
        for start in range(0, piece_ref.shape[0], unit):

            @pl.when(step == at)
            def _(piece_ref=piece_ref, start=start):
                normed, _ = norm_core(piece_ref[start : start + unit, :].astype(F32))
                out_ref[...] = (normed * gain_ref[...] + shift_ref[...]).astype(BF)

            at += 1


def norm_rows(pieces, gain, shift):
    rows, width = sum(piece.shape[0] for piece in pieces), pieces[0].shape[1]
    unit = min(min(piece.shape[0] for piece in pieces), 128)
    whole = [pl.BlockSpec(piece.shape, lambda i: (0, 0)) for piece in pieces]
    vector = pl.BlockSpec((1, width), lambda i: (0, 0))
    return pl.pallas_call(
        functools.partial(norm_kernel, unit=unit),
        grid=(rows // unit,),
        in_specs=whole + [vector, vector],
        out_specs=pl.BlockSpec((unit, width), lambda i: (i, 0)),
        out_shape=jax.ShapeDtypeStruct((rows, width), BF),
        compiler_params=pltpu.CompilerParams(dimension_semantics=("arbitrary",), vmem_limit_bytes=PRODUCT_GRANT),
        cost_estimate=light_cost(2000 * rows * width),
        name="norm_rows",
    )(*pieces, gain.reshape(1, -1), shift.reshape(1, -1))


def visible_scores(q_head, k_block, first, q_place, key_start, length):
    scores = dot_nt(q_head, k_block)
    k_place = key_start + lax.broadcasted_iota(jnp.int32, (1, length), 1)
    allowed = (k_place >= first) & (k_place <= q_place)
    return jnp.where(allowed, scores, NEG_FILL)


def storage_row(block, place, blocks, length):
    k = block ^ place
    return pl.multiple_of(((k >> 1) + (k & 1) * (blocks // 2)) * length, length)


def spread_heads(source_ref, target_ref, lanes, heads, length, blocks):
    def one(m, carry):
        rows = source_ref[pl.ds(pl.multiple_of(m * length, length), length), :]
        for h in range(heads):
            target = pl.ds(pl.multiple_of((m * heads + h) * length, length), length)
            target_ref[target, :] = jnp.where(lanes == h, rows, jnp.zeros_like(rows))
        return carry

    lax.fori_loop(0, blocks, one, 0)


def fold(values, op):
    out = values[:, :128]
    for start in range(128, values.shape[1], 128):
        out = op(out, values[:, start : start + 128])
    return out


def attend_forward_kernel(
    place_ref, low_ref, q_ref, k_ref, v_ref, first_ref, o_ref, lse_ref, s_scr, m_scr, l_scr, v_scr, *, heads, length, blocks
):
    i = pl.program_id(0)
    place = place_ref[0]
    low = low_ref[i]
    width = heads * HD
    lanes = lax.broadcasted_iota(jnp.int32, (length, width), 1) // HD
    q_all = q_ref[...]
    q_heads = [jnp.where(lanes == h, q_all, jnp.zeros_like(q_all)) for h in range(heads)]
    first = first_ref[...]
    q_place = i * length + lax.broadcasted_iota(jnp.int32, (length, 1), 0)
    m_scr[...] = jnp.full_like(m_scr, NEG_FILL)
    l_scr[...] = jnp.zeros_like(l_scr)

    @pl.when(i == 0)
    def _():
        spread_heads(v_ref, v_scr, lanes, heads, length, blocks)

    def score_step(j, carry):
        k_block = k_ref[pl.ds(storage_row(j, place, blocks, length), length), :]
        cols = pl.ds(pl.multiple_of(j * length, length), length)
        for h in range(heads):
            scores = visible_scores(q_heads[h], k_block, first, q_place, j * length, length)
            s_scr[h, :, cols] = scores
            m_scr[h] = jnp.maximum(m_scr[h], fold(scores, jnp.maximum))
        return carry

    lax.fori_loop(low, i + 1, score_step, 0)
    tops = [jnp.max(m_scr[h], axis=-1, keepdims=True) for h in range(heads)]

    def exp_step(j, carry):
        cols = pl.ds(pl.multiple_of(j * length, length), length)
        for h in range(heads):
            raised = jnp.exp(s_scr[h, :, cols] - tops[h])
            s_scr[h, :, cols] = raised
            l_scr[h] = l_scr[h] + fold(raised, jnp.add)
        return carry

    lax.fori_loop(low, i + 1, exp_step, 0)
    totals = [jnp.sum(l_scr[h], axis=-1, keepdims=True) for h in range(heads)]
    scales = [1.0 / total for total in totals]

    def mix_step(j, acc):
        rows = pl.ds(pl.multiple_of(storage_row(j, place, blocks, length) * heads, heads * length), heads * length)
        cols = pl.ds(pl.multiple_of(j * length, length), length)
        probs = [(s_scr[h, :, cols] * scales[h]).astype(BF) for h in range(heads)]
        return acc + dot(jnp.concatenate(probs, axis=1), v_scr[rows, :])

    mixed = lax.fori_loop(low, i + 1, mix_step, jnp.zeros((length, width), F32))
    o_ref[...] = mixed.astype(BF)
    cols = lax.broadcasted_iota(jnp.int32, (length, 128), 1)
    lse = jnp.zeros((length, 128), F32)
    for h in range(heads):
        lse = jnp.where(cols == h, tops[h] + jnp.log(totals[h]), lse)
    lse_ref[...] = lse


def attend_backward_kernel(
    place_ref, low_ref, q_ref, go_ref, o_ref, lse_ref, k_ref, v_ref, first_ref, even_ref, odd_ref, kt_scr, vt_scr, k_scr,
    *, heads, length, blocks
):
    i = pl.program_id(0)
    place = place_ref[0]
    low = low_ref[i]
    width = heads * HD
    lanes = lax.broadcasted_iota(jnp.int32, (length, width), 1) // HD
    first = first_ref[...]
    q_place = i * length + lax.broadcasted_iota(jnp.int32, (length, 1), 0)
    q_all, go_all = q_ref[...], go_ref[...]
    inner_all = go_all.astype(F32) * o_ref[...].astype(F32)
    q_turned, go_turned = q_all.astype(F32).T.astype(BF), go_all.astype(F32).T.astype(BF)
    lse_all = lse_ref[...]
    q_heads, go_heads, inner, lse = [], [], [], []
    for h in range(heads):
        mine = lanes == h
        q_heads.append(jnp.where(mine, q_all, jnp.zeros_like(q_all)))
        go_heads.append(jnp.where(mine, go_all, jnp.zeros_like(go_all)))
        inner.append(jnp.sum(jnp.where(mine, inner_all, 0.0), axis=-1, keepdims=True))
        lse.append(lse_all[:, h : h + 1])

    @pl.when(i == 0)
    def _():
        kt_scr[...] = jnp.zeros_like(kt_scr)
        vt_scr[...] = jnp.zeros_like(vt_scr)
        spread_heads(k_ref, k_scr, lanes, heads, length, blocks)

    def step(j, acc):
        start = storage_row(j, place, blocks, length)
        rows = pl.ds(start, length)
        k_block, v_block = k_ref[rows, :], v_ref[rows, :]
        k_place = j * length + lax.broadcasted_iota(jnp.int32, (1, length), 1)
        allowed = (k_place >= first) & (k_place <= q_place)
        every = range(heads)
        scores = [dot_nt(q_heads[h], k_block) for h in every]
        grad_probs = [dot_nt(go_heads[h], v_block) for h in every]
        probs = [jnp.exp(jnp.where(allowed, scores[h] - lse[h], NEG_FILL)) for h in every]
        grad_scores = [(probs[h] * (grad_probs[h] - inner[h])).astype(BF) for h in every]
        for h in every:
            part = slice(h * HD, (h + 1) * HD)
            vt_scr[part, rows] = vt_scr[part, rows] + dot(go_turned[part, :], probs[h].astype(BF))
            kt_scr[part, rows] = kt_scr[part, rows] + dot(q_turned[part, :], grad_scores[h])
        spread = pl.ds(pl.multiple_of(start * heads, heads * length), heads * length)
        return acc + dot(jnp.concatenate(grad_scores, axis=1), k_scr[spread, :])

    grad_q = lax.fori_loop(low, i + 1, step, jnp.zeros((length, width), F32))
    grad_q = (grad_q.astype(BF).astype(F32) * (HD**-0.5)).astype(BF)
    k = i ^ place
    own_rows = pl.ds(pl.multiple_of((k >> 1) * length, length), length)

    @pl.when((k & 1) == 0)
    def _():
        even_ref[own_rows, 0:width] = grad_q

    @pl.when((k & 1) == 1)
    def _():
        odd_ref[own_rows, 0:width] = grad_q

    @pl.when(i == blocks - 1)
    def _():
        for j in range(blocks):
            target, m = (even_ref, j) if j < blocks // 2 else (odd_ref, j - blocks // 2)
            source, rows = slice(j * length, (j + 1) * length), slice(m * length, (m + 1) * length)
            target[rows, width : 2 * width] = kt_scr[:, source].T.astype(BF)
            target[rows, 2 * width : 3 * width] = vt_scr[:, source].T.astype(BF)


def storage_map(length, blocks, column):
    def index(i, place_ref, low_ref):
        k = i ^ place_ref[0]
        return ((k >> 1) + (k & 1) * (blocks // 2), column)

    return index


def attend_forward(place, low, qkv, first, length):
    rows, triple = qkv.shape
    width, blocks = triple // 3, rows // length
    heads = width // HD
    return pl.pallas_call(
        functools.partial(attend_forward_kernel, heads=heads, length=length, blocks=blocks),
        grid_spec=pltpu.PrefetchScalarGridSpec(
            num_scalar_prefetch=2,
            grid=(blocks,),
            in_specs=[
                pl.BlockSpec((length, width), storage_map(length, blocks, 0)),
                pl.BlockSpec((rows, width), lambda i, p, w: (0, 1)),
                pl.BlockSpec((rows, width), lambda i, p, w: (0, 2)),
                pl.BlockSpec((length, 1), lambda i, p, w: (i, 0)),
            ],
            out_specs=[
                pl.BlockSpec((length, width), lambda i, p, w: (i, 0)),
                pl.BlockSpec((length, 128), lambda i, p, w: (i, 0)),
            ],
            scratch_shapes=[
                pltpu.VMEM((heads, length, rows), F32),
                pltpu.VMEM((heads, length, 128), F32),
                pltpu.VMEM((heads, length, 128), F32),
                pltpu.VMEM((heads * rows, width), BF),
            ],
        ),
        out_shape=[jax.ShapeDtypeStruct((rows, width), BF), jax.ShapeDtypeStruct((rows, 128), F32)],
        compiler_params=pltpu.CompilerParams(dimension_semantics=("arbitrary",), vmem_limit_bytes=LARGE_GRANT),
        cost_estimate=light_cost(24 * rows * rows * width),
        name="attend_forward",
    )(place, low, qkv, qkv, qkv, first)


def attend_backward(place, low, qkv, grad_out, mixed, lse, first, length):
    rows, triple = qkv.shape
    width, blocks = triple // 3, rows // length
    heads = width // HD
    return pl.pallas_call(
        functools.partial(attend_backward_kernel, heads=heads, length=length, blocks=blocks),
        grid_spec=pltpu.PrefetchScalarGridSpec(
            num_scalar_prefetch=2,
            grid=(blocks,),
            in_specs=[
                pl.BlockSpec((length, width), storage_map(length, blocks, 0)),
                pl.BlockSpec((length, width), lambda i, p, w: (i, 0)),
                pl.BlockSpec((length, width), lambda i, p, w: (i, 0)),
                pl.BlockSpec((length, 128), lambda i, p, w: (i, 0)),
                pl.BlockSpec((rows, width), lambda i, p, w: (0, 1)),
                pl.BlockSpec((rows, width), lambda i, p, w: (0, 2)),
                pl.BlockSpec((length, 1), lambda i, p, w: (i, 0)),
            ],
            out_specs=[pl.BlockSpec((rows // 2, triple), lambda i, p, w: (0, 0))] * 2,
            scratch_shapes=[
                pltpu.VMEM((width, rows), F32),
                pltpu.VMEM((width, rows), F32),
                pltpu.VMEM((heads * rows, width), BF),
            ],
        ),
        out_shape=[jax.ShapeDtypeStruct((rows // 2, triple), BF)] * 2,
        compiler_params=pltpu.CompilerParams(dimension_semantics=("arbitrary",), vmem_limit_bytes=LARGE_GRANT),
        cost_estimate=light_cost(36 * rows * rows * width),
        name="attend_backward",
    )(place, low, qkv, grad_out, mixed, lse, qkv, qkv, first)


def local(
    inputs,
    teacher,
    segment_ids,
    summary_start,
    valid_mask,
    attn_norm_gain,
    attn_norm_bias,
    query_weight,
    query_bias,
    key_weight,
    value_weight,
    value_bias,
    out_weight,
    out_bias,
    mlp_norm_gain,
    mlp_norm_bias,
    up_weight,
    up_bias,
    down_weight,
    down_bias,
):
    seqs, length = segment_ids.shape
    width = inputs.shape[-1]
    hidden_units = up_weight.shape[1]
    n, groups = lax.axis_size("seq"), lax.axis_size("dp")
    place, group = lax.axis_index("seq"), lax.axis_index("dp")
    both = ("dp", "seq")
    seq_len = length * n
    tokens_all = seqs * seq_len * groups
    scale = HD**-0.5
    own_rows = query_weight.shape[0]
    own_hidden = up_bias.shape[0]
    head_cols = width // n

    def out_of(value):
        return lax.all_to_all(value, "seq", split_axis=0, concat_axis=0, tiled=True)

    valid = valid_mask.astype(F32)
    order = Order()
    near = n == 8 and groups == 4
    out_steps = Steps(order, line_gather(out_weight)) if near else None
    cut = jnp.concatenate(
        [w.reshape(own_rows, n, head_cols).transpose(1, 0, 2) for w in (query_weight, key_weight, value_weight)], axis=2
    )
    qkv_cut = out_of(cut)
    small = [attn_norm_gain, attn_norm_bias, out_bias, mlp_norm_gain, mlp_norm_bias, down_bias, query_bias, value_bias, up_bias]
    pieces = [v.astype(F32) for v in small] + [segment_ids.astype(F32).reshape(-1), jnp.sum(valid).reshape(1)]
    starts, lines = [], []
    for piece in pieces:
        starts.append(sum(line.shape[0] for line in lines))
        short = -piece.shape[0] % 128
        lines.append(jnp.pad(piece, (0, short)).reshape(-1, 128))
    used = sum(line.shape[0] for line in lines)
    packed = jnp.pad(jnp.concatenate(lines, axis=0), ((0, -used % 8), (0, 0)))[None]
    small_steps = Steps(order, doubling(after(packed, cut), ("dp", "seq")))
    small_steps.step(1)
    qkv_cut = order.pause(qkv_cut).reshape(n * own_rows, 3 * head_cols)
    w_qkv = lax.all_gather(qkv_cut, "dp", axis=0, tiled=True)
    if near:
        out_steps.step()
    small_steps.step(1)
    if near:
        out_steps.step()
    small_steps.step(1)
    if near:
        own_out = out_steps.finish()
    packed = small_steps.finish().reshape(n, groups, -1, 128).transpose(1, 0, 2, 3).reshape(groups * n, -1, 128)

    def zero_after(value):
        return jnp.minimum(jnp.abs(value.reshape(-1)[0].astype(F32)), 0.0).astype(jnp.int32)

    def rows_after(b, value):
        return lax.dynamic_index_in_dim(inputs, b + zero_after(value), 0, keepdims=False)

    state = [types.SimpleNamespace() for _ in range(seqs)]
    state[0].own = rows_after(0, packed)
    state[0].came = gather_start(state[0].own)
    parts = []
    for piece, at in zip(pieces, starts):
        count = -(-piece.shape[0] // 128)
        parts.append(packed[:, at : at + count].reshape(groups * n, -1)[:, : piece.shape[0]])
    gain_one, shift_one, b_out, gain_two, shift_two, b_down = [part.reshape(-1) for part in parts[:6]]
    b_query, b_value = [lax.dynamic_slice_in_dim(part.reshape(-1), place * head_cols, head_cols) for part in parts[6:8]]
    b_up = lax.dynamic_index_in_dim(parts[8].reshape(groups, n, -1), place, 1, keepdims=False).reshape(-1)
    ids = lax.dynamic_index_in_dim(parts[9].reshape(groups, n, seqs, length), group, 0, keepdims=False)
    ids = ids.transpose(1, 0, 2).reshape(seqs, seq_len)
    total_count = jnp.sum(parts[10])

    up_cut = up_weight.reshape(own_rows, groups, n, own_hidden).transpose(2, 0, 1, 3).reshape(n, own_rows, groups * own_hidden)
    b_qkv = jnp.concatenate([b_query, jnp.zeros_like(b_query), b_value])
    s_qkv = jnp.concatenate([jnp.full((head_cols,), scale, F32), jnp.ones((2 * head_cols,), F32)])

    place_arr = place.reshape(1).astype(jnp.int32)
    positions = jnp.arange(seq_len, dtype=jnp.int32)

    def add_all(terms):
        out = terms[0]
        for term in terms[1:]:
            out = out + term
        return out


    def spans(b):
        st = state[b]
        first = jnp.sum((ids[b][None, :] < ids[b][:, None]).astype(jnp.int32), axis=1)
        in_summary = (positions >= summary_start[b]) & (positions < summary_start[b] + NSUM)
        first = jnp.where(in_summary, 0, first)
        st.low = jnp.min(first.reshape(n, length), axis=1) // length
        st.first = first.reshape(seq_len, 1)

    def project(b):
        st = state[b]
        even, odd = order.tie((st.even, st.odd))
        parts = [project_product(part, w_qkv, b_qkv, s_qkv) for part in (even, odd)]
        st.qkv = order.mark(jnp.concatenate(parts, axis=0))

    def attend(b):
        st = state[b]
        qkv = order.tie(st.qkv)
        st.mixed, st.lse = attend_forward(place_arr, st.low, qkv, st.first, length)
        order.mark(st.mixed)

    def send_mixed(b):
        st = state[b]
        st.moved = out_of(st.mixed.reshape(n, length, head_cols))

    def middle(b):
        st = state[b]
        attended = order.tie(st.moved)
        st.attended = attended.transpose(1, 0, 2).reshape(length, width)
        rows = inputs[b].astype(F32)
        st.hidden = rows + (dot(st.attended, w_out) + b_out)
        st.normed_two, st.inverse_two = norm_core(st.hidden)
        st.own_two = order.mark((st.normed_two * gain_two + shift_two).astype(BF))
        st.came_two = gather_start(st.own_two)

    def up_even(b):
        st = state[b]
        st.act_even = order.mark(up_product(order.tie(st.even_two), w_up, b_up))

    def up_odd(b):
        st = state[b]
        st.act_odd = order.mark(up_product(order.tie(st.odd_two), w_up, b_up))

    def relay(b, own, came):
        st = state[b]
        came = order.pause(getattr(st, came))
        return came, gather_relay(getattr(st, own), came)

    def join(b, own, came_relayed):
        same = order.mark(gather_join(getattr(state[b], own), *order.tie(came_relayed)))
        return same, swap(same, 1)

    def down_odd(b):
        st = state[b]
        st.down_got = swap(order.mark(plain_product(order.tie(st.act_odd), w_down)), 1)

    def down_even(b):
        st = state[b]
        st.down_sums = order.mark(block_products(st.act_even, w_down, order.tie(st.down_got), n // 2))
        st.down_came = scatter_start(st.down_sums)

    def pass_on(b, sums, came):
        st = state[b]
        came = order.pause(getattr(st, came))
        return scatter_relay(order.mark(scatter_halves(getattr(st, sums), came)))

    def misfit(b):
        st = state[b]
        summed = scatter_join(st.down_sums, order.tie(st.down_sent))
        st.result = st.hidden + (summed + b_down)
        error = st.result - teacher[b].astype(F32)
        st.local_sq = jnp.sum(jnp.sum(error * error, axis=-1) * valid[b])
        st.grad_result = error * (valid[b] * (tokens_all / total_count))[:, None]
        st.own_grad = order.mark(st.grad_result.astype(BF))
        st.g_b_down = jnp.sum(st.own_grad.astype(F32), axis=0)
        st.came_grad = gather_start(st.own_grad)

    def act_back_even(b):
        st = state[b]
        st.pre_even, st.sums_even = masked_product(order.tie(st.gm_even), w_down, st.act_even)
        order.mark(st.pre_even)

    def act_back_odd(b):
        st = state[b]
        st.pre_odd, st.sums_odd = masked_product(order.tie(st.gm_odd), w_down, st.act_odd)
        order.mark(st.pre_odd)

    def up_back_odd(b):
        st = state[b]
        st.up_got = swap(order.mark(plain_product(order.tie(st.pre_odd), w_up, turned=True)), 1)

    def up_back_even(b):
        st = state[b]
        st.up_sums = order.mark(block_products(st.pre_even, w_up, order.tie(st.up_got), n // 2, turned=True))
        st.up_came = scatter_start(st.up_sums)

    def branch_back(b):
        st = state[b]
        grad_ready = scatter_join(st.up_sums, order.tie(st.up_sent))
        grad_norm, st.g_gain_two, st.g_shift_two = norm_back(grad_ready, st.normed_two, st.inverse_two, gain_two)
        st.grad_hidden = st.grad_result + grad_norm
        st.branch = st.grad_hidden.astype(BF)
        st.g_b_out = jnp.sum(st.branch.astype(F32), axis=0)
        grad_att = dot_nt(st.branch, w_out).astype(BF).reshape(length, n, head_cols).transpose(1, 0, 2)
        st.grad_mixed = out_of(order.mark(grad_att)).reshape(seq_len, head_cols)

    def attend_back(b):
        st = state[b]
        st.grad_qkv = attend_backward(
            place_arr, st.low, st.qkv, order.tie(st.grad_mixed), st.mixed, st.lse, st.first, length
        )
        order.mark(st.grad_qkv)
        st.g_b_qkv = sum(jnp.sum(part.astype(F32), axis=0) for part in st.grad_qkv)

    def project_back_odd(b):
        st = state[b]
        odd = order.tie(st.grad_qkv[1])
        st.one_got = swap(order.mark(plain_product(odd, w_qkv, turned=True)), 1)

    def project_back_even(b):
        st = state[b]
        st.one_sums = block_products(st.grad_qkv[0], w_qkv, order.tie(st.one_got), n // 2, turned=True)
        order.mark(st.one_sums)
        st.one_came = scatter_start(st.one_sums)

    def finish(b):
        st = state[b]
        grad_ready = scatter_join(st.one_sums, order.tie(st.one_sent))
        normed, inverse = norm_core(inputs[b].astype(F32))
        grad_norm, st.g_gain_one, st.g_shift_one = norm_back(grad_ready, normed, inverse, gain_one)
        st.grad_inputs = order.mark(st.grad_hidden + grad_norm)

    every, later = range(seqs), range(1, seqs)

    def whole_out_weight(own, came, relayed):
        whole = jnp.zeros((groups, n, own_rows, width), BF)
        half = groups // 2
        same = [(0, own, 0), (2, came[0], 0), (4, came[1], 0), (6, relayed[0], 0), (6, relayed[1], half)]
        other = [(k + 1, swap(piece, 1), first) for k, piece, first in same]
        for k, piece, first in same + other:
            whole = lax.dynamic_update_slice(whole, piece.reshape(-1, 1, own_rows, width), (first, place ^ k, 0, 0))
        return whole.reshape(width, width)

    def make_ready(b, came_relayed):
        st = state[b]
        st.even = order.mark(norm_rows(gather_pieces(st.own, *order.tie(came_relayed)), gain_one, shift_one))
        st.odd = swap(st.even, 1)

    for b in every:
        spans(b)
    came_relayed = relay(0, "own", "came")
    for b in later:
        state[b].own = rows_after(b, came_relayed[0][0] if near else packed)
        state[b].came = gather_start(state[b].own)
    make_ready(0, came_relayed)
    up_cut = out_of(after(up_cut, qkv_cut))
    if near:
        own_out = order.tie(own_out)
        out_came = order.pause(gather_start(own_out))
        out_relayed = gather_relay(own_out, out_came)
    else:
        w_out = lax.all_gather(after(out_weight, qkv_cut), both, axis=0, tiled=True)
    up_cut = order.pause(up_cut)
    w_up = lax.all_gather(up_cut.reshape(n * own_rows, groups * own_hidden), "dp", axis=0, tiled=True)
    w_down = lax.all_gather(after(down_weight, up_cut), "dp", axis=0, tiled=True)
    w_qkv = order.pause(w_qkv)
    project(0)
    attend(0)
    send_mixed(0)
    came_relayed = [relay(b, "own", "came") for b in later]
    raw = came_relayed
    if near:
        w_out = whole_out_weight(own_out, out_came, order.pause(out_relayed))
    middle(0)
    for b in later:
        last, st = state[b - 1], state[b]
        make_ready(b, raw[b - 1])
        project(b)
        came_relayed = relay(b - 1, "own_two", "came_two")
        attend(b)
        send_mixed(b)
        last.even_two, last.odd_two = join(b - 1, "own_two", came_relayed)
        up_even(b - 1)
        middle(b)
        up_odd(b - 1)
        came_relayed = relay(b, "own_two", "came_two")
        down_odd(b - 1)
        st.even_two, st.odd_two = join(b, "own_two", came_relayed)
        up_even(b)
        down_even(b - 1)
        up_odd(b)
        last.down_sent = pass_on(b - 1, "down_sums", "down_came")
        down_odd(b)
        down_even(b)
        misfit(b - 1)
        st.down_sent = pass_on(b, "down_sums", "down_came")
        came_relayed = relay(b - 1, "own_grad", "came_grad")
        misfit(b)
        last.gm_even, last.gm_odd = join(b - 1, "own_grad", came_relayed)
        act_back_even(b - 1)
        act_back_odd(b - 1)
        came_relayed = relay(b, "own_grad", "came_grad")
        up_back_odd(b - 1)
        up_back_even(b - 1)
        st.gm_even, st.gm_odd = join(b, "own_grad", came_relayed)
        act_back_even(b)
        last.up_sent = pass_on(b - 1, "up_sums", "up_came")
        act_back_odd(b)
        up_back_odd(b)
        up_back_even(b)
    lefts = [part for st in state for part in (st.even_two, st.odd_two)]
    rights = [part for st in state for part in (st.pre_even, st.pre_odd)]
    g_w_up = order.mark(weight_grad(order.tie(lefts), rights, 512, 1024))
    g_up = lax.psum_scatter(g_w_up, "dp", scatter_dimension=0, tiled=True)
    for b in later:
        state[b].up_sent = pass_on(b, "up_sums", "up_came")
    branch_back(0)
    lefts = [part for st in state for part in (st.act_even, st.act_odd)]
    rights = [part for st in state for part in (st.gm_even, st.gm_odd)]
    g_w_down = order.mark(weight_grad(order.tie(lefts), rights, 256, 1024))
    g_down = lax.psum_scatter(g_w_down, "dp", scatter_dimension=0, tiled=True)
    state[0].grad_mixed = order.pause(state[0].grad_mixed)
    for b in later:
        branch_back(b)
    turned = [
        st.attended.reshape(length, groups, n, own_rows).transpose(2, 0, 1, 3).reshape(n, length, groups * own_rows)
        for st in state
    ]

    def out_block(k):
        return add_all(
            [dot_tn(lax.dynamic_index_in_dim(t, place ^ k, 0, keepdims=False), st.branch) for t, st in zip(turned, state)]
        )

    out_rows = groups * own_rows
    turned = order.tie(turned)
    out_odd = order.mark(jnp.concatenate([out_block(k).astype(BF) for k in range(1, n, 2)], axis=0))
    out_got = swap(out_odd, 1)
    attend_back(0)
    out_got = order.tie(out_got)
    out_sums = [out_block(2 * m) + out_got[m * out_rows : (m + 1) * out_rows].astype(F32) for m in range(n // 2)]
    order.mark(out_sums)
    out_came = scatter_start(out_sums)
    project_back_odd(0)
    out_sent = scatter_relay(order.mark(scatter_halves(out_sums, order.pause(out_came))))
    project_back_even(0)
    g_up, g_down = order.pause((g_up, g_down))
    g_up = out_of(g_up.reshape(n, own_rows, groups * own_hidden))
    for b in later:
        attend_back(b)
        state[b - 1].one_came, out_sent = order.pause((state[b - 1].one_came, out_sent))
    for b in later:
        state[b - 1].one_sent = pass_on(b - 1, "one_sums", "one_came")
    out_sum = order.mark(scatter_join(out_sums, order.tie(out_sent)).astype(BF))
    out_parts = out_sum.reshape(groups, own_rows, width)
    out_line = Steps(order, line_scatter(out_parts)) if near else None
    for b in later:
        project_back_odd(b)
    lefts = [part for st in state for part in (st.even, st.odd)]
    rights = [part for st in state for part in st.grad_qkv]
    g_w_qkv = order.mark(weight_grad(order.tie(lefts), rights, 1024, 768))
    if near:
        out_line.step()
        qkv_line = Steps(order, line_scatter(g_w_qkv.reshape(groups, n * own_rows, 3 * head_cols)))
    else:
        g_qkv = lax.psum_scatter(g_w_qkv, "dp", scatter_dimension=0, tiled=True)
        g_out = lax.psum_scatter(out_sum, "dp", scatter_dimension=0, tiled=True)
    g_up = order.pause(g_up)
    for b in later:
        state[b - 1].one_sent = order.pause(state[b - 1].one_sent)
        project_back_even(b)
    if near:
        out_line.step()
        qkv_line.step()
    for b in later:
        state[b].one_sent = pass_on(b, "one_sums", "one_came")
        finish(b - 1)
    if near:
        g_out = out_line.finish()
        qkv_line.step()
    for b in later:
        state[b].one_sent = order.pause(state[b].one_sent)
    if near:
        g_qkv = order.mark(qkv_line.finish().astype(BF))
    g_qkv = out_of(g_qkv.reshape(n, own_rows, 3 * head_cols))
    for b in later:
        finish(b)
    g_out = g_out.astype(F32)

    def summed(name):
        return add_all([after(getattr(st, name), *state[-1].one_sums) for st in state])

    g_down = order.tie(g_down).astype(F32)
    g_up = g_up.reshape(n, own_rows, groups, own_hidden).transpose(1, 2, 0, 3).reshape(own_rows, hidden_units).astype(F32)
    g_qkv_came = g_qkv
    g_qkv = g_qkv.reshape(n, own_rows, 3, head_cols).transpose(2, 1, 0, 3).reshape(3, own_rows, width).astype(F32)

    g_b_qkv = summed("g_b_qkv").reshape(3, head_cols)
    own_bias = jnp.zeros((2, width), F32)
    own_bias = lax.dynamic_update_slice(own_bias, jnp.stack([g_b_qkv[0], g_b_qkv[2]]), (0, place * head_cols))
    g_b_up = jnp.sum(summed("sums_even") + summed("sums_odd"), axis=0).reshape(groups, 1, own_hidden)
    spread_up = lax.dynamic_update_slice_in_dim(jnp.zeros((groups, n, own_hidden), F32), g_b_up, place, 1)
    names = ("g_gain_one", "g_shift_one", "g_b_out", "g_gain_two", "g_shift_two", "g_b_down")
    vectors = jnp.concatenate([jnp.stack([summed(name) for name in names]), own_bias], axis=0)
    count = vectors.shape[0]
    vectors = vectors.reshape(count, groups * n, own_rows).transpose(1, 0, 2).reshape(groups * n, count * own_rows)
    sq = jnp.broadcast_to(summed("local_sq"), (groups * n, 1))
    tail = jnp.concatenate([vectors, spread_up.reshape(groups * n, own_hidden), sq], axis=1)
    tail = scatter_small(tail, g_qkv_came)
    vectors = tail[: count * own_rows].reshape(count, own_rows)
    g_b_query, g_b_value, g_b_up = vectors[6], vectors[7], tail[count * own_rows : -1]
    mean_loss = tail[-1] / (total_count * width)
    return (
        jnp.stack([st.result.astype(BF) for st in state]),
        mean_loss,
        jnp.stack([st.grad_inputs for st in state]),
        vectors[0],
        vectors[1],
        g_qkv[0],
        g_b_query,
        g_qkv[1],
        g_qkv[2],
        g_b_value,
        g_out,
        vectors[2],
        vectors[3],
        vectors[4],
        g_up,
        g_b_up,
        g_down,
        vectors[5],
    )


def solution(mesh):
    rows3, rows2, flat, mat = P("dp", "seq", None), P("dp", "seq"), P(("dp", "seq")), P(("dp", "seq"), None)
    placed = (
        rows3, rows3, rows2, P("dp"), rows2, flat, flat, mat, flat, mat, mat, flat, mat, flat, flat, flat, mat, flat, mat, flat,
    )
    out = (rows3, P(), rows3, flat, flat, mat, flat, mat, mat, flat, mat, flat, flat, flat, mat, flat, mat, flat)
    return jax.shard_map(local, mesh=mesh, in_specs=placed, out_specs=out, check_vma=False)
```
